32 devices in a mesh: img: 2 (over x), row: 4 (over y, core), col: 4 (over z).
Axes of the slice: x: 2, y: 2, z: 4, core: 2. Of those that a mesh axis runs over, the one named last changes fastest.
Arguments:
- image_in: bfloat16 [4, 64, 64, 768], P('img', 'row', 'col'), may hold values from -6 to 6
- cotangent: bfloat16 [4, 64, 64, 768], P('img', 'row', 'col'), may hold values from -6 to 6
- qkv_weight: bfloat16 [768, 2304], P(('row', 'col'), 'img'), may hold values from -0.21875 to 0.21875
- out_weight: bfloat16 [768, 768], P(('row', 'col'), 'img'), may hold values from -0.875 to 0.875
- up_weight: bfloat16 [768, 3072], P(('row', 'col'), 'img'), may hold values from -0.21875 to 0.21875
- down_weight: bfloat16 [3072, 768], P(('row', 'col'), 'img'), may hold values from -0.109375 to 0.109375
- query_bias: float32 [768], replicated, may hold values from -4 to 4
- value_bias: float32 [768], replicated, may hold values from -4 to 4
- out_bias: float32 [768], replicated, may hold values from -4 to 4
- up_bias: float32 [3072], replicated, may hold values from -4 to 4
- down_bias: float32 [768], replicated, may hold values from -4 to 4
- first_gain: float32 [768], replicated, may hold values from 0.25 to 1.75
- first_shift: float32 [768], replicated, may hold values from -4 to 4
- second_gain: float32 [768], replicated, may hold values from 0.25 to 1.75
- second_shift: float32 [768], replicated, may hold values from -4 to 4
- rows_table: bfloat16 [27, 64], replicated, may hold values from -2 to 2
- cols_table: bfloat16 [27, 64], replicated, may hold values from -2 to 2
Outputs:
- image_out: bfloat16 [4, 64, 64, 768], P('img', 'row', 'col')
- image_grad: float32 [4, 64, 64, 768], P('img', 'row', 'col')
- grad_qkv_weight: float32 [768, 2304], P(('row', 'col'), 'img')
- grad_out_weight: float32 [768, 768], P(('row', 'col'), 'img')
- grad_up_weight: float32 [768, 3072], P(('row', 'col'), 'img')
- grad_down_weight: float32 [3072, 768], P(('row', 'col'), 'img')
- grad_query_bias: float32 [768], replicated
- grad_value_bias: float32 [768], replicated
- grad_out_bias: float32 [768], replicated
- grad_up_bias: float32 [3072], replicated
- grad_down_bias: float32 [768], replicated
- grad_first_gain: float32 [768], replicated
- grad_first_shift: float32 [768], replicated
- grad_second_gain: float32 [768], replicated
- grad_second_shift: float32 [768], replicated
- grad_rows_table: float32 [27, 64], replicated
- grad_cols_table: float32 [27, 64], replicated
The draws below stay inside these ranges and needn't reach their ends.
All inputs are finite; a program needn't handle non-finite values.
Results may differ from the reference program's by a relative error of at most 0.018.
Values may be sent and summed in bfloat16 or wider, within the bound.
A program may use at most 256 MiB of HBM per device.

```python
import jax
import jax.numpy as jnp
from jax import lax

D = 768
HEADS = 12
HEAD_DIM = 64
FF = 3072
GRID = 64
WIN = 14
IMAGES = 4
REL = 27


def steps_of(stream_key, shape, shards, least, largest):
    level = 1.0
    for position, shards_of in shards:
        draws = jax.random.uniform(jax.random.fold_in(jax.random.fold_in(stream_key, 6), position), (shards_of,), jnp.float32, least / len(shards), largest / len(shards))
        level = level * jnp.repeat(jnp.exp(draws), shape[position] // shards_of).reshape((-1,) + (1,) * (len(shape) - 1 - position))
    return level


def bell_draw(key, extent, scale, limit, pieces=(), kind=jnp.bfloat16):
    array = jax.random.normal(key, extent, jnp.float32) * scale
    if len(pieces) > 0:
        array = steps_of(key, extent, pieces, -0.22, 0.18) * array
    return jnp.clip(array, min=-limit, max=limit).astype(kind)


def setup_inputs(seed: int = 0) -> dict:
    arg_keys = jax.random.split(jax.random.key(seed), 18)
    return {
        "image_in": bell_draw(arg_keys[0], (IMAGES, GRID, GRID, D), 1.0, 6.0, ((0, 2), (1, 4), (2, 4))),
        "cotangent": bell_draw(arg_keys[1], (IMAGES, GRID, GRID, D), 1.0, 6.0, ((0, 2), (1, 4), (2, 4))),
        "qkv_weight": bell_draw(arg_keys[2], (D, 3 * D), D ** -0.5, 0.21875, ((0, 16), (1, 2))),
        "out_weight": bell_draw(arg_keys[3], (D, D), (D // 16) ** -0.5, 0.875, ((0, 16), (1, 2))),
        "up_weight": bell_draw(arg_keys[4], (D, FF), D ** -0.5, 0.21875, ((0, 16), (1, 2))),
        "down_weight": bell_draw(arg_keys[5], (FF, D), FF ** -0.5, 0.109375, ((0, 16), (1, 2))),
        "query_bias": bell_draw(arg_keys[6], (D,), 0.3, 4.0, (), jnp.float32),
        "value_bias": bell_draw(arg_keys[7], (D,), 0.3, 4.0, (), jnp.float32),
        "out_bias": bell_draw(arg_keys[8], (D,), 0.3, 4.0, (), jnp.float32),
        "up_bias": bell_draw(arg_keys[9], (FF,), 0.3, 4.0, (), jnp.float32),
        "down_bias": bell_draw(arg_keys[10], (D,), 0.3, 4.0, (), jnp.float32),
        "first_gain": jnp.clip(1.0 + 0.15 * jax.random.normal(arg_keys[11], (D,), jnp.float32), 0.25, 1.75),
        "first_shift": bell_draw(arg_keys[12], (D,), 0.3, 4.0, (), jnp.float32),
        "second_gain": jnp.clip(1.0 + 0.15 * jax.random.normal(arg_keys[13], (D,), jnp.float32), 0.25, 1.75),
        "second_shift": bell_draw(arg_keys[14], (D,), 0.3, 4.0, (), jnp.float32),
        "rows_table": bell_draw(arg_keys[15], (REL, HEAD_DIM), 0.15, 2.0),
        "cols_table": bell_draw(arg_keys[16], (REL, HEAD_DIM), 0.15, 2.0),
    }


exact_mode = lax.Precision.HIGHEST

@jax.custom_vjp
def low(v):
    return lax.optimization_barrier(v.astype(jnp.bfloat16)).astype(jnp.float32)

@jax.custom_vjp
def low_back(v):
    return v

def low_keep(v):
    return (low(v), None)

def low_pass(kept, grad):
    return (grad,)

def back_keep(v):
    return (v, None)

def back_low(kept, grad):
    return (low(grad),)
low.defvjp(low_keep, low_pass)
low_back.defvjp(back_keep, back_low)

def layer_norm(values, gain_vector, shift_vector):
    center = values - lax.optimization_barrier(jnp.mean(values, axis=-1, keepdims=True))
    spread = lax.optimization_barrier(jnp.mean(center * center, axis=-1, keepdims=True))
    return center * lax.rsqrt(spread + 1e-06) * gain_vector + shift_vector

def encoder_block(picture, qkv_weight, out_weight, up_weight, down_weight, query_bias, value_bias, out_bias, up_bias, down_bias, first_gain, first_shift, second_gain, second_shift, rows_table, cols_table):
    padded_side = WIN * ((GRID + WIN - 1) // WIN)
    window_count = padded_side // WIN
    window_total = window_count * window_count
    normed = low_back(low(layer_norm(picture, first_gain, first_shift)))
    padded = jnp.pad(normed, ((0, padded_side - GRID), (0, padded_side - GRID), (0, 0)))
    windows = padded.reshape(window_count, WIN, window_count, WIN, D).transpose(0, 2, 1, 3, 4).reshape(window_total, WIN * WIN, D)
    bias_all = jnp.concatenate([query_bias, jnp.zeros_like(query_bias), value_bias])
    packed = jnp.einsum('tpd,de->tpe', windows, qkv_weight, precision=exact_mode) + bias_all
    packed = low_back(low(packed))
    queries = packed[:, :, :D].reshape(window_total, WIN * WIN, HEADS, HEAD_DIM)
    key_rows = packed[:, :, D:2 * D].reshape(window_total, WIN * WIN, HEADS, HEAD_DIM)
    value_rows = packed[:, :, 2 * D:].reshape(window_total, WIN * WIN, HEADS, HEAD_DIM)
    grid_q = queries.reshape(window_total, WIN, WIN, HEADS, HEAD_DIM)
    places = jnp.arange(WIN)
    offset = places[:, None] - places[None, :] + WIN - 1
    near_rows = rows_table[offset]
    near_cols = cols_table[offset]
    products = jnp.einsum('tqnc,tknc->tnqk', queries, key_rows, precision=exact_mode) * HEAD_DIM ** (-0.5)
    along_rows = jnp.einsum('thwnc,hkc->tnhwk', grid_q, near_rows, precision=exact_mode)
    along_cols = jnp.einsum('thwnc,wkc->tnhwk', grid_q, near_cols, precision=exact_mode)
    scores = products.reshape(window_total, HEADS, WIN, WIN, WIN, WIN) + along_rows[:, :, :, :, :, None] + along_cols[:, :, :, :, None, :]
    scores = low_back(scores.reshape(window_total, HEADS, WIN * WIN, WIN * WIN))
    attention = jax.nn.softmax(scores, axis=-1)
    blended = jnp.einsum('tnqk,tknc->tqnc', low(attention), value_rows, precision=exact_mode)
    blended = low_back(low(blended.reshape(window_total, WIN * WIN, D)))
    placed = blended.reshape(window_count, window_count, WIN, WIN, D).transpose(0, 2, 1, 3, 4).reshape(padded_side, padded_side, D)
    mixed_rows = placed[:GRID, :GRID].reshape(GRID * GRID, D)
    branch = jnp.dot(mixed_rows, out_weight, precision=exact_mode, preferred_element_type=jnp.float32) + out_bias
    middle = picture.reshape(GRID * GRID, D) + low_back(branch)
    second_normed = low_back(low(layer_norm(middle, second_gain, second_shift)))
    hidden = low_back(jnp.dot(second_normed, up_weight, precision=exact_mode, preferred_element_type=jnp.float32) + up_bias)
    active = low(jax.nn.gelu(hidden, approximate=False))
    result = middle + low_back(jnp.dot(active, down_weight, precision=exact_mode, preferred_element_type=jnp.float32) + down_bias)
    return result.reshape(GRID, GRID, D)

def reference(image_in, cotangent, qkv_weight, out_weight, up_weight, down_weight, query_bias, value_bias, out_bias, up_bias, down_bias, first_gain, first_shift, second_gain, second_shift, rows_table, cols_table):
    weights = (qkv_weight.astype(jnp.float32), out_weight.astype(jnp.float32), up_weight.astype(jnp.float32), down_weight.astype(jnp.float32), query_bias.astype(jnp.float32), value_bias.astype(jnp.float32), out_bias.astype(jnp.float32), up_bias.astype(jnp.float32), down_bias.astype(jnp.float32), first_gain.astype(jnp.float32), first_shift.astype(jnp.float32), second_gain.astype(jnp.float32), second_shift.astype(jnp.float32), rows_table.astype(jnp.float32), cols_table.astype(jnp.float32))

    def one_image(totals, inputs_pair):
        picture, upstream = inputs_pair
        result, backward = jax.vjp(encoder_block, picture.astype(jnp.float32), *weights)
        gradients = backward(upstream.astype(jnp.float32))
        totals = tuple((carried + fresh for carried, fresh in zip(totals, gradients[1:])))
        return (totals, (result.astype(jnp.bfloat16), gradients[0]))
    initial = tuple((jnp.zeros(weight.shape, jnp.float32) for weight in weights))
    totals, outputs_pair = lax.scan(one_image, initial, (image_in, cotangent))
    return (outputs_pair[0], outputs_pair[1], totals[0], totals[1], totals[2], totals[3], totals[4], totals[5], totals[6], totals[7], totals[8], totals[9], totals[10], totals[11], totals[12], totals[13], totals[14])
```

```python
import functools

import jax
import jax.numpy as jnp
import numpy as np
from jax import lax
from jax.experimental import pallas as pl
from jax.experimental.pallas import tpu as pltpu
from jax.sharding import PartitionSpec as P

MESH = pl.DeviceIdType.MESH


def place():
    return lax.axis_index("img"), lax.axis_index("row"), lax.axis_index("col")


def side_owner(window_row, image):
    return lax.rem(window_row, 2), 3 - image - 2 * (window_row // 2)


def piece_target(kind, image, row, col):
    last_row, last_col = row == 3, col == 3
    side_row, side_col = side_owner(row, image)
    next_row, next_col = side_owner(lax.rem(row + 1, 4), image)
    if kind == 0:
        return (jnp.where(last_row, 3 - image, row + 1), col, jnp.where(last_row, 2, image))
    if kind == 1:
        return (jnp.where(last_col, side_row, row), jnp.where(last_col, side_col, col + 1), jnp.where(last_col, 2, image))
    target_row = jnp.where(last_row, 3 - image, jnp.where(last_col, next_row, row + 1))
    target_col = jnp.where(last_col, jnp.where(last_row, 3, next_col), col + 1)
    slot = jnp.where(last_row & last_col, 3, jnp.where(last_row | last_col, 2, image))
    return (target_row, target_col, slot)


def arrivals(row, col):
    wide = row >= 2
    side_row = row + 2 * (1 - col // 2)
    table = []
    for image in range(2):
        table.append((image, 0, row > 0))
        table.append((image, 1, col > 0))
        table.append((image, 2, (row > 0) & (col > 0)))
    table.append((2, 0, wide))
    table.append((2, 1, jnp.logical_not(wide)))
    table.append((2, 2, jnp.where(wide, col, side_row) > 0))
    table.append((3, 2, wide & (col == 3)))
    return table


def tile_part(ref, image, kind):
    if kind == 0:
        return ref.at[image, pl.ds(8, 8), pl.ds(0, 2)]
    if kind == 1:
        return ref.at[image, pl.ds(0, 14), pl.ds(1, 1)]
    return ref.at[image, pl.ds(8, 8), pl.ds(1, 1)]


def window_part(ref, slot, kind):
    if kind == 0:
        return ref.at[slot, pl.ds(0, 8), pl.ds(1, 2)]
    if kind == 1:
        return ref.at[slot, pl.ds(8, 14), pl.ds(0, 1)]
    return ref.at[slot, pl.ds(0, 8), pl.ds(0, 1)]


def greet(img, row, col, pairs=True):
    barrier = pltpu.get_barrier_semaphore()
    for row_step in range(4):
        for col_step in range(4):
            if row_step or col_step:
                pl.semaphore_signal(
                    barrier,
                    inc=1,
                    device_id={"row": lax.rem(row + row_step, 4), "col": lax.rem(col + col_step, 4)},
                    device_id_type=MESH,
                )
    if pairs:
        pl.semaphore_signal(barrier, inc=1, device_id={"img": 1 - img}, device_id_type=MESH)
    pl.semaphore_wait(barrier, 16 if pairs else 15)


CHUNKS = ((0, 0, 640), (0, 640, 1152), (1, 0, 384), (2, 0, 768), (2, 768, 1536), (3, 0, 128), (3, 128, 384))


def links(shards, fulls, wsend, wrecv, wloc):
    img, row, col = place()
    y_row = lax.rem(row + 2, 4)
    core_row = row + 1 - 2 * lax.rem(row, 2)
    other = 1 - img
    sent = []

    def rows_of(w, rw, half=None):
        kb = fulls[w].shape[0] // 4
        if half is None:
            return pl.ds(pl.multiple_of(rw * kb, kb), kb)
        return pl.ds(pl.multiple_of(rw * kb + half * (kb // 2), kb // 2), kb // 2)

    def cols_of(n, im):
        w, lo, hi = CHUNKS[n]
        nb = fulls[w].shape[1] // 2
        return pl.ds(pl.multiple_of(im * nb + lo, 128), hi - lo)

    def block(n, rw, im, half=None):
        w = CHUNKS[n][0]
        return fulls[w].at[rows_of(w, rw, half), cols_of(n, im)]

    def slot(n, cl):
        w = CHUNKS[n][0]
        k16 = fulls[w].shape[0] // 16
        return fulls[w].at[pl.ds(pl.multiple_of((row * 4 + cl) * k16, k16), k16), cols_of(n, img)]

    def source(n):
        w, lo, hi = CHUNKS[n]
        return shards[w].at[:, pl.ds(lo, hi - lo)]

    def push(n, k, where, target, start=None):
        def copy():
            ref = block(n, *where)
            return pltpu.make_async_remote_copy(
                src_ref=source(n) if start else ref,
                dst_ref=slot(n, col) if start else ref,
                send_sem=wsend.at[n, k],
                recv_sem=wrecv.at[n, k],
                device_id=target(),
                device_id_type=MESH,
            )

        copy().start()
        sent.append(copy)

    def arrive(n, k, ref):
        pltpu.make_async_copy(ref, ref, wrecv.at[n, k]).wait()

    def along_col(n):
        pltpu.make_async_copy(source(n), slot(n, col), wloc.at[n]).start()
        for d in range(1, 4):
            push(n, d - 1, (row, img), lambda d=d: {"col": lax.rem(col + d, 4)}, True)

    def first(n):
        pltpu.make_async_copy(source(n), slot(n, col), wloc.at[n]).wait()
        for d in range(1, 4):
            arrive(n, d - 1, slot(n, lax.rem(col + 4 - d, 4)))
        push(n, 3, (row, img, 0), lambda: {"img": other})
        push(n, 4, (row, img, 1), lambda: {"row": y_row})
        push(n, 5, (row, img), lambda: {"row": core_row})

    def second(n):
        arrive(n, 3, block(n, row, other, 0))
        arrive(n, 4, block(n, y_row, img, 1))
        push(n, 6, (row, img, 0), lambda: {"row": y_row})
        push(n, 7, (row, other, 0), lambda: {"row": y_row})
        push(n, 8, (row, img, 1), lambda: {"img": other})
        push(n, 9, (y_row, img, 1), lambda: {"img": other})
        push(n, 10, (row, other, 0), lambda: {"row": core_row})
        push(n, 11, (y_row, img, 1), lambda: {"row": core_row})

    def third(n):
        arrive(n, 6, block(n, y_row, img, 0))
        arrive(n, 7, block(n, y_row, other, 0))
        arrive(n, 8, block(n, row, other, 1))
        arrive(n, 9, block(n, y_row, other, 1))
        push(n, 12, (y_row, img, 0), lambda: {"row": core_row})
        push(n, 13, (y_row, other, 0), lambda: {"row": core_row})
        push(n, 14, (row, other, 1), lambda: {"row": core_row})
        push(n, 15, (y_row, other, 1), lambda: {"row": core_row})

    def last(n):
        core_y = lax.rem(core_row + 2, 4)
        arrive(n, 5, block(n, core_row, img))
        arrive(n, 10, block(n, core_row, other, 0))
        arrive(n, 11, block(n, core_y, img, 1))
        arrive(n, 12, block(n, core_y, img, 0))
        arrive(n, 13, block(n, core_y, other, 0))
        arrive(n, 14, block(n, core_row, other, 1))
        arrive(n, 15, block(n, core_y, other, 1))

    return along_col, first, second, third, last, sent


def window_moves(tiles, raws, send, recv, loc):
    img, row, col = place()

    def each(t, act):
        for image in range(2):
            for kind in range(3):
                target_row, target_col, target_slot = piece_target(kind, image, row, col)
                here = (target_row == row) & (target_col == col)
                part = tile_part(tiles[t], image, kind)
                goal = window_part(raws[t], target_slot, kind)
                act(here, part, goal, send.at[t, image, kind], recv.at[t, target_slot, kind], target_row, target_col)

    def remote(part, goal, leave, arrival, target_row, target_col):
        return pltpu.make_async_remote_copy(
            src_ref=part,
            dst_ref=goal,
            send_sem=leave,
            recv_sem=arrival,
            device_id={"row": target_row, "col": target_col},
            device_id_type=MESH,
        )

    def own(t, image):
        return pltpu.make_async_copy(tiles[t].at[image, pl.ds(0, 14)], raws[t].at[image, pl.ds(8, 14), pl.ds(1, 2)], loc.at[t, image])

    def start(t):
        for image in range(2):
            own(t, image).start()

        def act(here, part, goal, leave, arrival, target_row, target_col):
            @pl.when(here)
            def _():
                pltpu.make_async_copy(part, goal, arrival).start()

            @pl.when(jnp.logical_not(here))
            def _():
                remote(part, goal, leave, arrival, target_row, target_col).start()

        each(t, act)

    def arrived(t):
        for image in range(2):
            own(t, image).wait()
        for slot_index, kind, present in arrivals(row, col):
            part = window_part(raws[t], slot_index, kind)

            @pl.when(present)
            def _():
                pltpu.make_async_copy(part, part, recv.at[t, slot_index, kind]).wait()

    def left(t):
        def act(here, part, goal, leave, arrival, target_row, target_col):
            @pl.when(jnp.logical_not(here))
            def _():
                remote(part, goal, leave, arrival, target_row, target_col).wait_send()

        each(t, act)

    return start, arrived, left


BF = jnp.bfloat16
F32 = jnp.float32
ROWS = 704
SPAN = 800
FEATURES = 768
EPS = 1e-06


def row_params(step, row, col):
    wide = row >= 2
    side_row = row + 2 * (1 - col // 2)
    third_step = step - 28
    in_corner = wide & (third_step >= 8)
    slot = jnp.where(step < 14, 0, jnp.where(step < 28, 1, jnp.where(in_corner, 3, 2)))
    place_row = jnp.where(step < 14, step, jnp.where(step < 28, step - 14, jnp.where(in_corner, third_step - 8, third_step)))
    full = step < 28
    row_start = jnp.where(full, 8 - 2 * row, jnp.where(wide, 0, 8 - 2 * side_row))
    col_start = jnp.where(full, 8 - 2 * col, jnp.where(wide & jnp.logical_not(in_corner), 8 - 2 * col, 0))
    width = jnp.where(full, 14, jnp.where(wide & jnp.logical_not(in_corner), 14, 8))
    alive = jnp.where(full, True, jnp.where(in_corner, col == 3, jnp.where(wide, True, third_step < 14)))
    return slot, jnp.minimum(place_row + row_start, 21), col_start, jnp.where(alive, width, 0)


def window_params(window, row, col):
    wide = row >= 2
    start = jnp.where(window < 2, 14 * window, jnp.where(window == 2, 28, 36))
    tall = jnp.where(window < 2, 14, jnp.where((window == 2) & jnp.logical_not(wide), 14, 8))
    width = jnp.where(window < 2, 14, jnp.where((window == 2) & wide, 14, 8))
    return start, tall, width


def window_count(row, col):
    return jnp.where((row >= 2) & (col == 3), 4, 3)


def unit_of(values):
    center = values - jnp.mean(values, axis=-1, keepdims=True)
    inverse = lax.rsqrt(jnp.mean(center * center, axis=-1, keepdims=True) + EPS)
    return center * inverse, inverse


def relative_layout(backward):
    take = np.zeros((2, 2, 27, 128), np.float32)
    for parity in range(2):
        base = 64 if parity == 0 else 0
        for j in range(27):
            for copy in (0,) if backward else (0, 32):
                take[parity, 0, 26 - j, (base - 13 + j + copy) % 128] = 1
                if backward:
                    take[parity, 1, j, base + 16 + j] = 1
                else:
                    take[parity, 1, 26 - j, (base + 3 + j + copy) % 128] = 1
    return take


def table_operand(rows_table, cols_table, backward):
    take = jnp.asarray(relative_layout(backward), BF)
    parts = []
    for parity in range(2):
        both = []
        for which, table in ((0, rows_table), (1, cols_table)):
            both.append(lax.dot_general(table, take[parity, which], (((0,), (0,)), ((), ())), preferred_element_type=F32).astype(BF))
        block = jnp.concatenate(both, axis=1)
        zero = jnp.zeros_like(block)
        parts.append(jnp.concatenate([block, zero] if parity == 0 else [zero, block], axis=0))
    return jnp.concatenate(parts, axis=1)


def table_grads(sums):
    take = jnp.asarray(relative_layout(True), F32)
    grads = []
    for which in range(2):
        total = 0.0
        for parity in range(2):
            part = sums[64 * parity : 64 * parity + 64, 256 * parity + 128 * which : 256 * parity + 128 * which + 128]
            total = total + lax.dot_general(take[parity, which], part, (((1,), (1,)), ((), ())), precision=lax.Precision.HIGHEST)
        grads.append(total)
    return grads


def run_all(act):
    for i in range(0, len(act), 2):
        act[i](act[i + 1])


def open_kernel(weights, x_ref, c_ref, gain, shift, bias, tab, *refs):
    img, row, col = place()
    greet(img, row, col, weights)
    if weights:
        shards, refs = refs[:4], refs[4:]
    else:
        wq, refs = refs[0], refs[1:]
    xw, cw, n1_turned, qkv_s, probs, o, o_turned = refs[:7]
    refs = refs[7:]
    if weights:
        fulls, refs = refs[:4], refs[4:]
        wq = fulls[0]
    rawx, rawc, n1, send, recv, loc = refs[:6]
    if weights:
        along_col, first, second, third, last, sent = links(shards, fulls, *refs[6:])
    window_start, window_arrived, window_left = window_moves((x_ref, c_ref), (rawx, rawc), send, recv, loc)
    places = lax.broadcasted_iota(jnp.int32, (16, 1), 0)

    def cut_one(raw, step):
        slot, raw_row, col_start, width = row_params(step, row, col)
        wide_rows = raw[slot, raw_row].reshape(24, FEATURES).astype(F32)
        keep = places < width
        return keep, jnp.where(keep, pltpu.roll(wide_rows, lax.rem(24 - col_start, 24), 0)[:16], 0.0)

    def cut_x(step, _):
        at = pl.ds(pl.multiple_of(step * 16, 16), 16)
        keep, x = cut_one(rawx, step)
        xw[at, :] = x.astype(BF)
        unit, _inverse = unit_of(x)
        n1[at, :] = jnp.where(keep, unit * gain[...] + shift[...], 0.0).astype(BF)
        return 0

    def cut_c(step, _):
        at = pl.ds(pl.multiple_of(step * 16, 16), 16)
        _keep, c = cut_one(rawc, step)
        cw[at, :] = c.astype(BF)
        return 0

    def project(step, _):
        at = pl.ds(pl.multiple_of(step * 352, 32), 352)
        for part_index in range(3):
            lanes = slice(part_index * FEATURES, (part_index + 1) * FEATURES)
            part = jnp.dot(n1[at, :], wq[:, lanes], preferred_element_type=F32) + bias[:, lanes]
            qkv_s[at, lanes] = part.astype(BF)
        return 0

    def turn(source, goal):
        def step(i, _):
            lanes = pl.ds(pl.multiple_of(i * 128, 128), 128)
            goal[lanes, :] = source[0:ROWS, lanes].T
            return 0

        lax.fori_loop(0, FEATURES // 128, step, 0)

    if weights:
        along_col(0)
    window_start(0)
    if weights:
        along_col(1)
    else:
        window_start(1)
    o[...] = jnp.zeros_like(o)
    if weights:
        first(0)
        along_col(2)
        first(1)
        along_col(3)
        second(0)
    window_arrived(0)
    lax.fori_loop(0, 44, cut_x, 0)
    steps = []
    if weights:
        first(2)
        along_col(4)
        second(1)
        third(0)
        first(3)
        along_col(5)
        third(1)
        last(0)
        last(1)
        steps = [
            (second, 2),
            (first, 4, along_col, 6),
            (second, 3),
            (third, 2),
            (first, 5, window_start, 1),
            (second, 4),
            (third, 3),
            (first, 6),
            (second, 5),
            (third, 4),
            (second, 6),
            (third, 5),
            (third, 6),
        ]
    lax.fori_loop(0, 2, project, 0)
    row_of = lax.broadcasted_iota(jnp.int32, (224, 1), 0)
    lane = lax.broadcasted_iota(jnp.int32, (1, 128), 1)
    key_place = lax.broadcasted_iota(jnp.int32, (224, 128), 0)
    key_lane = lax.broadcasted_iota(jnp.int32, (224, 128), 1)
    key_a, key_b = key_place // 16, key_place % 16

    def pair(index, _):
        for turn_index, act in enumerate(steps):
            pl.when(index == turn_index)(functools.partial(run_all, act))
        window, pair_index = index // 6, index % 6
        start, tall, width = window_params(window, row, col)
        at = pl.ds(pl.multiple_of(start * 16, 16), 224)
        alive = (row_of // 16 < tall) & (row_of % 16 < width)
        lanes = lambda third: pl.ds(pl.multiple_of(third * FEATURES + pair_index * 128, 128), 128)
        q = jnp.where(alive, qkv_s[at, lanes(0)].astype(F32), 0.0)
        k = jnp.where(alive, qkv_s[at, lanes(1)].astype(F32), 0.0)
        v = jnp.where(alive, qkv_s[at, lanes(2)].astype(F32), bias[:, lanes(2)].astype(BF).astype(F32)).astype(BF)
        terms = jnp.dot(q.astype(BF), tab[...], preferred_element_type=F32)
        outs = []
        for parity in range(2):
            base = 64 if parity == 0 else 0
            own = (lane < 64) if parity == 0 else (lane >= 64)
            rel_rows = jnp.concatenate(
                [pltpu.roll(terms[16 * a : 16 * a + 16, 256 * parity : 256 * parity + 128], a, 1) for a in range(14)], axis=0
            )
            rel_cols = jnp.concatenate(
                [
                    pltpu.roll(terms[16 * a : 16 * a + 16, 256 * parity + 128 : 256 * parity + 256], 0, 1, stride=1, stride_axis=0)
                    for a in range(14)
                ],
                axis=0,
            )
            on = lane - base
            in_rows = ((on >= 0) & (on < 14)) | ((on >= 32) & (on < 46))
            in_cols = ((on >= 16) & (on < 30)) | ((on >= 48) & (on < 62))
            rel = jnp.where(in_rows, rel_rows, jnp.where(in_cols, rel_cols, 0.0))
            rough = rel.astype(BF).astype(F32)
            fine = jnp.where(on >= 32, rel - rough, rough)
            fine = jnp.where(on == 14, -1e30, fine)
            q_side = jnp.where(own, q * 0.125, fine).astype(BF)
            key_on = key_lane - base
            hot = jnp.where(
                key_on == 14,
                jnp.where(key_b >= 14, 1.0, 0.0),
                jnp.where(
                    (key_on % 32 < 14) & (key_a == key_on % 32),
                    1.0,
                    jnp.where((key_on % 32 >= 16) & (key_on % 32 < 30) & (key_b == key_on % 32 - 16), 1.0, 0.0),
                ),
            )
            k_side = jnp.where(own, k, hot).astype(BF)
            scores = lax.dot_general(q_side, k_side, (((1,), (1,)), ((), ())), preferred_element_type=F32)
            exponent = jnp.exp(scores - jnp.max(scores, axis=-1, keepdims=True))
            p = (exponent * (1.0 / jnp.sum(exponent, axis=-1, keepdims=True))).astype(BF)
            probs[window, 2 * pair_index + parity] = p
            outs.append(jnp.dot(p, v, preferred_element_type=F32))
        blended = jnp.where(lane < 64, outs[0], outs[1])
        out_lanes = pl.ds(pl.multiple_of(pair_index * 128, 128), 128)
        o_at = pl.ds(pl.multiple_of(start * 16, 16), 224)
        o[o_at, out_lanes] = jnp.where(alive, blended, 0.0).astype(BF)
        return 0

    lax.fori_loop(0, window_count(row, col) * 6, pair, 0)
    turn(n1, n1_turned)
    turn(o, o_turned)
    window_arrived(1)
    lax.fori_loop(0, 44, cut_c, 0)
    if weights:
        for n in range(2, len(CHUNKS)):
            last(n)
        for copy in sent:
            copy().wait_send()
    window_left(0)
    window_left(1)


def open_windows(x, c, shards, gain, shift, bias, tab):
    vm = pl.BlockSpec(memory_space=pltpu.VMEM)
    an = pl.BlockSpec(memory_space=pl.ANY)
    shape = jax.ShapeDtypeStruct
    dma = pltpu.SemaphoreType.DMA
    chunks = len(CHUNKS)
    weights = lax.axis_size("img") == 2
    if weights:
        given, wholes = list(shards), [(768, 2304), (768, 768), (768, 3072), (3072, 768)]
    else:
        widened = [lax.all_gather(w, "img", axis=1, tiled=True) for w in shards]
        gathered = [lax.all_gather(w, ("row", "col"), axis=0, tiled=True) for w in widened]
        given, wholes = gathered[:1], []
    raw = pltpu.VMEM((4, 22, 3, 8, FEATURES), BF)
    outs = pl.pallas_call(
        functools.partial(open_kernel, weights),
        out_shape=[
            shape((ROWS, FEATURES), BF),
            shape((ROWS, FEATURES), BF),
            shape((FEATURES, ROWS), BF),
            shape((SPAN, 3 * FEATURES), BF),
            shape((4, 12, 224, 224), BF),
            shape((SPAN, FEATURES), BF),
            shape((FEATURES, ROWS), BF),
        ]
        + [shape(s, BF) for s in wholes],
        in_specs=[vm] * (6 + len(given)),
        out_specs=[vm] * 7 + ([vm, an, an, an] if weights else []),
        scratch_shapes=[raw, raw, pltpu.VMEM((ROWS, FEATURES), BF), dma((2, 2, 3)), dma((2, 4, 3)), dma((2, 2))]
        + ([dma((chunks, 16)), dma((chunks, 16)), dma((chunks,))] if weights else []),
        compiler_params=pltpu.CompilerParams(collective_id=0, has_side_effects=True, vmem_limit_bytes=67043328),
    )(x.reshape(2, 16, 2, 8, 768), c.reshape(2, 16, 2, 8, 768), gain, shift, bias, tab, *given)
    return list(outs) if weights else list(outs) + gathered


BLOCK = 176
FF = 3072
CHUNK = 512


def nt(a, b):
    return lax.dot_general(a, b, (((1,), (1,)), ((), ())), preferred_element_type=F32)


def norm_back(grad, unit, inverse, gain):
    scaled = grad * gain
    first_mean = jnp.mean(scaled, axis=-1, keepdims=True)
    second_mean = jnp.mean(scaled * unit, axis=-1, keepdims=True)
    return inverse * (scaled - first_mean - unit * second_mean)


def fold_rows(values):
    total = values[0:8]
    for i in range(1, values.shape[0] // 8):
        total = total + values[8 * i : 8 * i + 8]
    return total


def middle_kernel(o, xw, cw, wo, wu, wd, out_bias, up_bias, down_bias, gain, shift, result, n2, g, dh, da, do, dm, sums, up_sum, y_s, d_s):
    @pl.when(pl.program_id(0) == 0)
    def _():
        sums[...] = jnp.zeros_like(sums)
        up_sum[...] = jnp.zeros_like(up_sum)

    mid = xw[...].astype(F32) + (jnp.dot(o[...], wo[...], preferred_element_type=F32) + out_bias[...])
    unit, inverse = unit_of(mid)
    low = (unit * gain[...] + shift[...]).astype(BF)
    n2[...] = low
    y_s[...] = mid + down_bias[...]
    d_s[...] = jnp.zeros_like(d_s)
    dz = cw[...]

    def hidden(step, _):
        lanes = pl.ds(pl.multiple_of(step * CHUNK, CHUNK), CHUNK)
        h = jnp.dot(n2[...], wu[:, lanes], preferred_element_type=F32) + up_bias[:, lanes]
        up = nt(cw[...], wd[lanes, :])
        phi = 0.5 * (1.0 + lax.erf(h * 0.7071067811865476))
        slope = phi + h * (jnp.exp(-0.5 * h * h) * 0.3989422804014327)
        active = (h * phi).astype(BF)
        back = (up * slope).astype(BF)
        g[:, lanes] = active
        dh[:, lanes] = back
        up_sum[:, lanes] += fold_rows(back.astype(F32))
        y_s[...] += jnp.dot(active, wd[lanes, :], preferred_element_type=F32)
        d_s[...] += nt(back, wu[:, lanes])
        return 0

    lax.fori_loop(0, FF // CHUNK, hidden, 0)
    result[...] = y_s[...].astype(BF)
    mid = xw[...].astype(F32) + (jnp.dot(o[...], wo[...], preferred_element_type=F32) + out_bias[...])
    unit, inverse = unit_of(mid)
    grad = d_s[...].astype(BF).astype(F32)
    up = cw[...].astype(F32)
    grad_mid = up + norm_back(grad, unit, inverse, gain[...])
    low_grad = grad_mid.astype(BF)
    dm[...] = grad_mid
    da[...] = low_grad
    do[...] = nt(low_grad, wo[...]).astype(BF)
    sums[0] += fold_rows(low_grad.astype(F32))
    sums[1] += fold_rows(up)
    sums[2] += fold_rows(grad * unit)
    sums[3] += fold_rows(grad)


def middle(o, xw, cw, wo, wu, wd, out_bias, up_bias, down_bias, gain, shift):
    vm = pl.BlockSpec(memory_space=pltpu.VMEM)
    shape = jax.ShapeDtypeStruct
    rows = lambda n: pl.BlockSpec((BLOCK, n), lambda i: (i, 0))
    whole = lambda s: pl.BlockSpec(s, lambda i: (0,) * len(s), pipeline_mode=pl.Buffered(1))
    return pl.pallas_call(
        middle_kernel,
        grid=(ROWS // BLOCK,),
        out_shape=[
            shape((ROWS, FEATURES), BF),
            shape((ROWS, FEATURES), BF),
            shape((ROWS, FF), BF),
            shape((ROWS, FF), BF),
            shape((ROWS, FEATURES), BF),
            shape((ROWS, FEATURES), BF),
            shape((ROWS, FEATURES), F32),
            shape((4, 8, FEATURES), F32),
            shape((8, FF), F32),
        ],
        in_specs=[rows(FEATURES)] * 3
        + [whole((FEATURES, FEATURES)), whole((FEATURES, FF)), whole((FF, FEATURES))]
        + [whole((1, FEATURES)), whole((1, FF)), whole((1, FEATURES)), whole((1, FEATURES)), whole((1, FEATURES))],
        out_specs=[rows(FEATURES), rows(FEATURES), rows(FF), rows(FF), rows(FEATURES), rows(FEATURES), rows(FEATURES)]
        + [pl.BlockSpec((4, 8, FEATURES), lambda i: (0, 0, 0)), pl.BlockSpec((8, FF), lambda i: (0, 0))],
        scratch_shapes=[pltpu.VMEM((BLOCK, FEATURES), F32)] * 2,
        compiler_params=pltpu.CompilerParams(vmem_limit_bytes=62 << 20),
    )(o, xw, cw, wo, wu, wd, out_bias, up_bias, down_bias, gain, shift)


def back_kernel(do, probs, qkv_s, o, xw, dm, result, wq, tab, bias, gain, dqkv, raw_r, raw_g, bias_sums, norm_sums, table_sums, do_s, dqkv_s, image_grad):
    row, col = lax.axis_index("row"), lax.axis_index("col")
    do_s[0:ROWS, :] = do[...]
    dqkv_s[...] = jnp.zeros_like(dqkv_s)
    bias_sums[...] = jnp.zeros_like(bias_sums)
    norm_sums[...] = jnp.zeros_like(norm_sums)
    table_sums[...] = jnp.zeros_like(table_sums)
    row_of = lax.broadcasted_iota(jnp.int32, (224, 1), 0)
    lane = lax.broadcasted_iota(jnp.int32, (1, 128), 1)
    key_place = lax.broadcasted_iota(jnp.int32, (224, 128), 0)
    key_lane = lax.broadcasted_iota(jnp.int32, (224, 128), 1)
    key_a, key_b = key_place // 16, key_place % 16

    def pair(index, _):
        window, pair_index = index // 6, index % 6
        start, tall, width = window_params(window, row, col)
        at = pl.ds(pl.multiple_of(start * 16, 16), 224)
        alive = (row_of // 16 < tall) & (row_of % 16 < width)
        lanes = lambda third: pl.ds(pl.multiple_of(third * FEATURES + pair_index * 128, 128), 128)
        q = jnp.where(alive, qkv_s[at, lanes(0)].astype(F32), 0.0)
        k = jnp.where(alive, qkv_s[at, lanes(1)].astype(F32), 0.0)
        v = jnp.where(alive, qkv_s[at, lanes(2)].astype(F32), bias[:, lanes(2)].astype(BF).astype(F32))
        grad = jnp.where(alive, do_s[at, lanes(0)].astype(F32), 0.0)
        product = grad * jnp.where(alive, o[at, lanes(0)].astype(F32), 0.0)
        q_turned = q.T.astype(BF)
        grad_turned = grad.T.astype(BF)
        value_parts, key_parts, query_parts, table_parts = [], [], [], []
        for parity in range(2):
            base = 64 if parity == 0 else 0
            own = (lane < 64) if parity == 0 else (lane >= 64)
            half = slice(64 * parity, 64 * parity + 64)
            inner = jnp.sum(jnp.where(own, product, 0.0), axis=-1, keepdims=True)
            rough = inner.astype(BF).astype(F32)
            on = lane - base
            grad_side = jnp.where(own, grad, jnp.where(on == 0, rough, jnp.where(on == 1, inner - rough, 0.0))).astype(BF)
            v_side = jnp.where(own, v, jnp.where((on == 0) | (on == 1), -1.0, 0.0)).astype(BF)
            centered = nt(grad_side, v_side)
            p = probs[window, 2 * pair_index + parity]
            ds = (p.astype(F32) * centered).astype(BF)
            value_parts.append(jnp.dot(grad_turned[half], p, preferred_element_type=F32))
            key_parts.append(jnp.dot(q_turned[half], ds, preferred_element_type=F32))
            key_on = key_lane - base
            hot = jnp.where(
                (key_on >= 0) & (key_on < 14) & (key_a == key_on),
                1.0,
                jnp.where((key_on >= 16) & (key_on < 30) & (key_b == 29 - key_on), 1.0, 0.0),
            )
            k_side = jnp.where(own, k * 0.125, hot).astype(BF)
            wide = jnp.dot(ds, k_side, preferred_element_type=F32)
            query_parts.append(wide)
            by_rows = jnp.where((on >= 0) & (on < 14), wide, 0.0)
            by_cols = jnp.where((on >= 16) & (on < 30), wide, 0.0)
            table_parts.append(
                jnp.concatenate([pltpu.roll(by_rows[16 * a : 16 * a + 16], (128 - a) % 128, 1) for a in range(14)], axis=0)
            )
            table_parts.append(
                jnp.concatenate(
                    [pltpu.roll(by_cols[16 * a : 16 * a + 16], 0, 1, stride=1, stride_axis=0) for a in range(14)], axis=0
                )
            )
        turned = jnp.concatenate(table_parts, axis=1).astype(BF)
        dq = jnp.where(lane < 64, query_parts[0], query_parts[1]) + nt(turned, tab[...])
        table_sums[...] += jnp.dot(q_turned, turned, preferred_element_type=F32)
        dk = jnp.concatenate(key_parts, axis=0).T * 0.125
        dv = jnp.concatenate(value_parts, axis=0).T
        dq = jnp.where(alive, dq, 0.0).astype(BF)
        dv = dv.astype(BF)
        bias_sums[0, :, lanes(0)] += fold_rows(dq.astype(F32))
        bias_sums[1, :, lanes(0)] += fold_rows(dv.astype(F32))
        dqkv_s[at, lanes(0)] = dq
        dqkv_s[at, lanes(1)] = jnp.where(alive, dk, 0.0).astype(BF)
        dqkv_s[at, lanes(2)] = jnp.where(alive, dv.astype(F32), 0.0).astype(BF)
        return 0

    lax.fori_loop(0, window_count(row, col) * 6, pair, 0)
    dqkv[...] = dqkv_s[0:ROWS, :]

    def finish(step, _):
        at = pl.ds(pl.multiple_of(step * 176, 16), 176)
        grad = nt(dqkv_s[at, :], wq[...]).astype(BF).astype(F32)
        unit, inverse = unit_of(xw[at, :].astype(F32))
        image_grad[at, :] = dm[at, :] + norm_back(grad, unit, inverse, gain[...])
        norm_sums[0] += fold_rows(grad * unit)
        norm_sums[1] += fold_rows(grad)
        return 0

    lax.fori_loop(0, 4, finish, 0)

    def spread(step, _):
        slot, raw_row, col_start, width = row_params(step, row, col)
        at = pl.ds(pl.multiple_of(step * 16, 16), 16)

        @pl.when(width > 0)
        def _():
            for source, raw in ((result, raw_r), (image_grad, raw_g)):
                values = source[at, :].astype(F32)
                values = jnp.concatenate([values, jnp.zeros((8, FEATURES), F32)], axis=0)
                raw[slot, raw_row] = pltpu.roll(values, col_start, 0).astype(BF).reshape(3, 8, FEATURES)

        return 0

    lax.fori_loop(0, 44, spread, 0)


def back(do, probs, qkv, o, xw, dm, result, wq, tab, bias, gain):
    vm = pl.BlockSpec(memory_space=pltpu.VMEM)
    shape = jax.ShapeDtypeStruct
    return pl.pallas_call(
        back_kernel,
        out_shape=[
            shape((ROWS, 3 * FEATURES), BF),
            shape((4, 22, 3, 8, FEATURES), BF),
            shape((4, 22, 3, 8, FEATURES), BF),
            shape((2, 8, FEATURES), F32),
            shape((2, 8, FEATURES), F32),
            shape((128, 512), F32),
        ],
        in_specs=[vm] * 11,
        out_specs=[vm] * 6,
        scratch_shapes=[pltpu.VMEM((SPAN, FEATURES), BF), pltpu.VMEM((SPAN, 3 * FEATURES), BF), pltpu.VMEM((ROWS, FEATURES), F32)],
        compiler_params=pltpu.CompilerParams(vmem_limit_bytes=62 << 20),
    )(do, probs, qkv, o, xw, dm, result, wq, tab, bias, gain)


def source_tiles(row, col):
    wide = row >= 2
    side_row = row + 2 * (1 - col // 2)
    table = []
    for image in range(2):
        table.append((image, 0, image, row - 1, col, row > 0))
        table.append((image, 1, image, row, col - 1, col > 0))
        table.append((image, 2, image, row - 1, col - 1, (row > 0) & (col > 0)))
    third_image = jnp.where(wide, 3 - row, 1 - lax.rem(col, 2))
    table.append((2, 0, third_image, 3, col, wide))
    table.append((2, 1, third_image, side_row, 3, jnp.logical_not(wide)))
    table.append((2, 2, third_image, jnp.where(wide, 3, side_row - 1), jnp.where(wide, col - 1, 3), jnp.where(wide, col, side_row) > 0))
    table.append((3, 2, 3 - row, 3, 3, wide & (col == 3)))
    return table


def return_kernel(raw_r, raw_g, out, grad_out, below_r, right_r, both_r, below_g, right_g, both_g, send, recv):
    img, row, col = place()
    greet(img, row, col, False)
    raws = (raw_r, raw_g)
    landing = ((below_r, right_r, both_r), (below_g, right_g, both_g))

    for t in range(2):
        for slot, kind, image, tile_row, tile_col, present in source_tiles(row, col):
            part = window_part(raws[t], slot, kind)
            goal = landing[t][kind].at[image]
            arrival = recv.at[t, image, kind]
            here = (tile_row == row) & (tile_col == col)

            @pl.when(present & here)
            def _():
                pltpu.make_async_copy(part, goal, arrival).start()

            @pl.when(present & jnp.logical_not(here))
            def _():
                pltpu.make_async_remote_copy(
                    src_ref=part,
                    dst_ref=goal,
                    send_sem=send.at[t, slot, kind],
                    recv_sem=arrival,
                    device_id={"row": jnp.maximum(tile_row, 0), "col": jnp.maximum(tile_col, 0)},
                    device_id_type=MESH,
                ).start()

    for t in range(2):
        for image in range(2):
            for kind in range(3):
                goal = landing[t][kind].at[image]
                pltpu.make_async_copy(goal, goal, recv.at[t, image, kind]).wait()
    places = lax.broadcasted_iota(jnp.int32, (16, 1), 0)
    left = places < 14 - 2 * col

    def rows16(values):
        return values.reshape(16, FEATURES).astype(F32)

    def right_half(values):
        low = values.reshape(8, FEATURES).astype(F32)
        return jnp.concatenate([low, low], axis=0)

    for image in range(2):

        def merge(tile_row, _):
            top = tile_row < 14 - 2 * row
            upper = jnp.minimum(tile_row, 13)
            lower = jnp.maximum(tile_row - 8, 0)
            for t, goal in ((0, out), (1, grad_out)):
                below, right, both = landing[t]
                own = jnp.where(top, rows16(raws[t][image, 8 + upper, 1:3]), rows16(below[image, lower]))
                beside = jnp.where(top, right_half(right[image, upper]), right_half(both[image, lower]))
                goal[image, tile_row] = jnp.where(left, own, beside).astype(goal.dtype)
            return 0

        lax.fori_loop(0, 16, merge, 0)
    for t in range(2):
        for slot, kind, image, tile_row, tile_col, present in source_tiles(row, col):
            here = (tile_row == row) & (tile_col == col)

            @pl.when(present & jnp.logical_not(here))
            def _():
                pltpu.make_async_remote_copy(
                    src_ref=window_part(raws[t], slot, kind),
                    dst_ref=landing[t][kind].at[image],
                    send_sem=send.at[t, slot, kind],
                    recv_sem=recv.at[t, image, kind],
                    device_id={"row": jnp.maximum(tile_row, 0), "col": jnp.maximum(tile_col, 0)},
                    device_id_type=MESH,
                ).wait_send()


def give_back(raw_r, raw_g):
    vm = pl.BlockSpec(memory_space=pltpu.VMEM)
    shape = jax.ShapeDtypeStruct
    dma = pltpu.SemaphoreType.DMA
    pieces = [pltpu.VMEM((2, 8, 2, 8, FEATURES), BF), pltpu.VMEM((2, 14, 1, 8, FEATURES), BF), pltpu.VMEM((2, 8, 1, 8, FEATURES), BF)]
    return pl.pallas_call(
        return_kernel,
        out_shape=[shape((2, 16, 16, FEATURES), BF), shape((2, 16, 16, FEATURES), F32)],
        in_specs=[vm] * 2,
        out_specs=[vm] * 2,
        scratch_shapes=pieces + pieces + [dma((2, 4, 3)), dma((2, 2, 3))],
        compiler_params=pltpu.CompilerParams(collective_id=2, has_side_effects=True, vmem_limit_bytes=62 << 20),
    )(raw_r, raw_g)


SUM_CHUNKS = ((1, 0, 384), (3, 0, 128), (3, 128, 384), (2, 0, 768), (2, 768, 1536), (0, 0, 640), (0, 640, 1152))
WHOLES = ((768, 2304), (768, 768), (768, 3072), (3072, 768))


def table_taker():
    take = relative_layout(True)
    out = np.zeros((4, 128, 128), np.float32)
    for parity in range(2):
        for which in range(2):
            out[2 * parity + which, :, 64 * which : 64 * which + 27] = take[parity, which].T
    return out


def finish_kernel(turned_n1, dqkv, turned_o, da, n2, dh, g, dz, raw_r, raw_g, sums, up_sum, bias_sums, norm_sums, table_sums, taker, *refs):
    out, grad_out, gq, go, gu, gd, small_out, table_out = refs[:8]
    below_r, right_r, both_r, below_g, right_g, both_g, own_r, own_g = refs[8:16]
    turned_n2, turned_g = refs[16:18]
    full = refs[18:22]
    small, table, small_land, table_land, small_z, table_z = refs[22:28]
    chunks = len(SUM_CHUNKS)
    lands = [refs[28 + 5 * n : 33 + 5 * n] for n in range(chunks)]
    send, recv, own_sem, wsend, wrecv, ssend, srecv = refs[28 + 5 * chunks :]
    img, row, col = place()
    greet(img, row, col)
    raws = (raw_r, raw_g)
    landing = ((below_r, right_r, both_r), (below_g, right_g, both_g))
    owns = (own_r, own_g)
    y_row = lax.rem(row + 2, 4)
    core_row = row + 1 - 2 * lax.rem(row, 2)
    core_y = lax.rem(core_row + 2, 4)
    other = 1 - img
    left_turned = (turned_n1, turned_o, turned_n2, turned_g)
    left_side = (None, None, n2, g)
    right_side = (dqkv, da, dh, dz)
    grads = (gq, go, gu, gd)
    copies = []

    for t in range(2):
        for image in range(2):
            pltpu.make_async_copy(raws[t].at[image, pl.ds(8, 14), pl.ds(1, 2)], owns[t].at[image], own_sem.at[t, image]).start()
        for slot, kind, image, tile_row, tile_col, present in source_tiles(row, col):
            part = window_part(raws[t], slot, kind)
            goal = landing[t][kind].at[image]
            arrival = recv.at[t, image, kind]
            here = (tile_row == row) & (tile_col == col)

            @pl.when(present & here)
            def _():
                pltpu.make_async_copy(part, goal, arrival).start()

            @pl.when(present & jnp.logical_not(here))
            def _():
                pltpu.make_async_remote_copy(
                    src_ref=part,
                    dst_ref=goal,
                    send_sem=send.at[t, slot, kind],
                    recv_sem=arrival,
                    device_id={"row": jnp.maximum(tile_row, 0), "col": jnp.maximum(tile_col, 0)},
                    device_id_type=MESH,
                ).start()

    def turn(w):
        source, goal = left_side[w], left_turned[w]

        def step(i, _):
            lanes = pl.ds(pl.multiple_of(i * 128, 128), 128)
            goal[lanes, :] = source[0:ROWS, lanes].T
            return 0

        lax.fori_loop(0, WHOLES[w][0] // 128, step, 0)

    def size(n):
        w, lo, hi = SUM_CHUNKS[n]
        return WHOLES[w][0] // 4, WHOLES[w][1] // 2, lo, hi - lo

    def block(n, rw, im, half=None):
        kb, nb, lo, width = size(n)
        cols = pl.ds(pl.multiple_of(im * nb + lo, 128), width)
        if half is None:
            return full[SUM_CHUNKS[n][0]].at[pl.ds(pl.multiple_of(rw * kb, kb), kb), cols]
        return full[SUM_CHUNKS[n][0]].at[pl.ds(pl.multiple_of(rw * kb + half * (kb // 2), kb // 2), kb // 2), cols]

    def push(n, k, src, dst, target):
        c = pltpu.make_async_remote_copy(
            src_ref=src, dst_ref=dst, send_sem=wsend.at[n, k], recv_sem=wrecv.at[n, k], device_id=target, device_id_type=MESH
        )
        c.start()
        copies.append(c)

    def arrive(n, k, ref):
        pltpu.make_async_copy(ref, ref, wrecv.at[n, k]).wait()

    def add(goal, part, rows):
        step_rows = 48

        def step(i, _):
            at = pl.ds(pl.multiple_of(i * step_rows, 16), step_rows)
            goal[at, :] = (goal[at, :].astype(F32) + part[at, :].astype(F32)).astype(BF)
            return 0

        lax.fori_loop(0, rows // step_rows, step, 0)

    def product(n, rw):
        w = SUM_CHUNKS[n][0]
        kb, nb, lo, width = size(n)
        rows = pl.ds(pl.multiple_of(rw * kb, kb), kb)
        for im in range(2):
            at = slice(im * nb + lo, im * nb + lo + width)
            full[w][rows, at] = jnp.dot(left_turned[w][rows, :], right_side[w][0:ROWS, at], preferred_element_type=F32).astype(BF)

    def pair_stage(n):
        land = lands[n][0]
        for j, rw in enumerate((core_row, core_y)):
            product(n, rw)
            for im in range(2):
                push(n, 2 * j + im, block(n, rw, im), land.at[j, im], {"row": core_row})
        for rw in (row, y_row):
            product(n, rw)

    def first(n):
        kb, nb, lo, width = size(n)
        for j, rw in enumerate((row, y_row)):
            for im in range(2):
                arrive(n, 2 * j + im, lands[n][0].at[j, im])
                add(block(n, rw, im), lands[n][0].at[j, im], kb)
        land = lands[n][1]
        for im in range(2):
            push(n, 4 + im, block(n, y_row, im, 0), land.at[im], {"row": y_row})
        land = lands[n][2]
        push(n, 6, block(n, row, other, 1), land.at[0], {"img": other})
        push(n, 7, block(n, y_row, other, 1), land.at[1], {"img": other})

    def second(n):
        kb, nb, lo, width = size(n)
        for im in range(2):
            arrive(n, 4 + im, lands[n][1].at[im])
            add(block(n, row, im, 0), lands[n][1].at[im], kb // 2)
        push(n, 8, block(n, row, other, 0), lands[n][3].at[0], {"img": other})
        for j, rw in enumerate((row, y_row)):
            arrive(n, 6 + j, lands[n][2].at[j])
            add(block(n, rw, img, 1), lands[n][2].at[j], kb // 2)
        push(n, 9, block(n, y_row, img, 1), lands[n][3].at[1], {"row": y_row})

    def shard(n, cl):
        kb, nb, lo, width = size(n)
        cols = pl.ds(pl.multiple_of(img * nb + lo, 128), width)
        return full[SUM_CHUNKS[n][0]].at[pl.ds(pl.multiple_of(row * kb + cl * (kb // 4), kb // 4), kb // 4), cols]

    def third(n):
        kb, nb, lo, width = size(n)
        for half in range(2):
            arrive(n, 8 + half, lands[n][3].at[half])
            add(block(n, row, img, half), lands[n][3].at[half], kb // 2)
        for d in range(1, 4):
            cl = lax.rem(col + d, 4)
            push(n, 9 + d, shard(n, cl), lands[n][4].at[d - 1], {"col": cl})

    def fourth(n):
        w, lo, hi = SUM_CHUNKS[n]
        for d in range(1, 4):
            arrive(n, 9 + d, lands[n][4].at[d - 1])
        mine = shard(n, col)

        def step(i, _):
            at = pl.ds(pl.multiple_of(i * 48, 16), 48)
            total = mine[at, :].astype(F32)
            for d in range(3):
                total = total + lands[n][4][d, at, :].astype(F32)
            grads[w][at, lo:hi] = total
            return 0

        lax.fori_loop(0, WHOLES[w][0] // 16 // 48, step, 0)

    def over_rows(values):
        return jnp.sum(values, axis=0, keepdims=True)

    small[0] = jnp.zeros((16, FEATURES), F32)
    lines = [bias_sums[0], bias_sums[1], sums[0], sums[1], norm_sums[0], norm_sums[1], sums[2], sums[3]]
    for i, values in enumerate(lines):
        small[0, i : i + 1, :] = over_rows(values)
    for i in range(4):
        small[0, 8 + i : 9 + i, :] = over_rows(up_sum[:, i * FEATURES : (i + 1) * FEATURES])
    exact = lax.Precision.HIGHEST
    total = jnp.zeros((64, 128), F32)
    for parity in range(2):
        for which in range(2):
            part = table_sums[64 * parity : 64 * parity + 64, 256 * parity + 128 * which : 256 * parity + 128 * which + 128]
            total = total + jnp.dot(part, taker[2 * parity + which], precision=exact, preferred_element_type=F32)
    table[0] = total
    hops = ({"row": core_row}, {"row": y_row}, {"img": other})

    def small_push(k, src, dst, target):
        c = pltpu.make_async_remote_copy(
            src_ref=src, dst_ref=dst, send_sem=ssend.at[k], recv_sem=srecv.at[k], device_id=target, device_id_type=MESH
        )
        c.start()
        copies.append(c)
        return c

    def small_step(i):
        if 0 < i <= 3:
            for k, (acc, land) in enumerate(((small, small_land), (table, table_land))):
                pltpu.make_async_copy(land.at[i - 1], land.at[i - 1], srecv.at[2 * (i - 1) + k]).wait()
                acc[i] = acc[i - 1] + land[i - 1]
        if i < 3:
            for k, (acc, land) in enumerate(((small, small_land), (table, table_land))):
                small_push(2 * i + k, acc.at[i], land.at[i], hops[i])
        if i == 3:
            small_z[col] = small[3]
            table_z[col] = table[3]
            for d in range(1, 4):
                cl = lax.rem(col + d, 4)
                small_push(4 + 2 * d, small.at[3], small_z.at[col], {"col": cl})
                small_push(5 + 2 * d, table.at[3], table_z.at[col], {"col": cl})
        if i == 4:
            for d in range(1, 4):
                cl = lax.rem(col + 4 - d, 4)
                pltpu.make_async_copy(small_z.at[cl], small_z.at[cl], srecv.at[4 + 2 * d]).wait()
                pltpu.make_async_copy(table_z.at[cl], table_z.at[cl], srecv.at[5 + 2 * d]).wait()
            small_out[...] = (small_z[0] + small_z[1]) + (small_z[2] + small_z[3])
            table_out[...] = (table_z[0] + table_z[1]) + (table_z[2] + table_z[3])

    turned = {0, 1}
    for n in range(chunks + 4):
        if n < chunks:
            w = SUM_CHUNKS[n][0]
            if w not in turned:
                turned.add(w)
                turn(w)
            pair_stage(n)
        if n < 5:
            small_step(n)
        if 0 <= n - 1 < chunks:
            first(n - 1)
        if 0 <= n - 2 < chunks:
            second(n - 2)
        if 0 <= n - 3 < chunks:
            third(n - 3)
        if 0 <= n - 4 < chunks:
            fourth(n - 4)

    for t in range(2):
        for image in range(2):
            pltpu.make_async_copy(owns[t].at[image], owns[t].at[image], own_sem.at[t, image]).wait()
            for kind in range(3):
                goal = landing[t][kind].at[image]
                pltpu.make_async_copy(goal, goal, recv.at[t, image, kind]).wait()
    places = lax.broadcasted_iota(jnp.int32, (16, 1), 0)
    left = places < 14 - 2 * col

    def rows16(values):
        return values.reshape(16, FEATURES).astype(F32)

    def right_half(values):
        low = values.reshape(8, FEATURES).astype(F32)
        return jnp.concatenate([low, low], axis=0)

    for image in range(2):

        def merge(tile_row, _):
            top = tile_row < 14 - 2 * row
            upper = jnp.minimum(tile_row, 13)
            lower = jnp.maximum(tile_row - 8, 0)
            for t, goal in ((0, out), (1, grad_out)):
                below, right, both = landing[t]
                own = jnp.where(top, rows16(owns[t][image, upper]), rows16(below[image, lower]))
                beside = jnp.where(top, right_half(right[image, upper]), right_half(both[image, lower]))
                goal[image, tile_row] = jnp.where(left, own, beside).astype(goal.dtype)
            return 0

        lax.fori_loop(0, 16, merge, 0)
    for t in range(2):
        for slot, kind, image, tile_row, tile_col, present in source_tiles(row, col):
            here = (tile_row == row) & (tile_col == col)

            @pl.when(present & jnp.logical_not(here))
            def _():
                pltpu.make_async_remote_copy(
                    src_ref=window_part(raws[t], slot, kind),
                    dst_ref=landing[t][kind].at[image],
                    send_sem=send.at[t, slot, kind],
                    recv_sem=recv.at[t, image, kind],
                    device_id={"row": jnp.maximum(tile_row, 0), "col": jnp.maximum(tile_col, 0)},
                    device_id_type=MESH,
                ).wait_send()

    for c in copies:
        c.wait_send()


def finish(n1, dqkv, o, da, n2, dh, g, dz, raw_r, raw_g, sums, up_sum, bias_sums, norm_sums, table_sums):
    vm = pl.BlockSpec(memory_space=pltpu.VMEM)
    an = pl.BlockSpec(memory_space=pl.ANY)
    shape = jax.ShapeDtypeStruct
    dma = pltpu.SemaphoreType.DMA
    pieces = [pltpu.VMEM((2, 8, 2, 8, FEATURES), BF), pltpu.VMEM((2, 14, 1, 8, FEATURES), BF), pltpu.VMEM((2, 8, 1, 8, FEATURES), BF)]
    lands = []
    for w, lo, hi in SUM_CHUNKS:
        kb, width = WHOLES[w][0] // 4, hi - lo
        lands += [
            pltpu.VMEM((2, 2, kb, width), BF),
            pltpu.VMEM((2, kb // 2, width), BF),
            pltpu.VMEM((2, kb // 2, width), BF),
            pltpu.VMEM((2, kb // 2, width), BF),
            pltpu.VMEM((3, kb // 4, width), BF),
        ]
    chunks = len(SUM_CHUNKS)
    return pl.pallas_call(
        finish_kernel,
        out_shape=[shape((2, 16, 16, FEATURES), BF), shape((2, 16, 16, FEATURES), F32)]
        + [shape((k // 16, n // 2), F32) for k, n in WHOLES]
        + [shape((16, FEATURES), F32), shape((64, 128), F32)],
        in_specs=[vm] * 8 + [an] * 2 + [vm] * 6,
        out_specs=[vm] * 8,
        scratch_shapes=pieces
        + pieces
        + [pltpu.VMEM((2, 14, 2, 8, FEATURES), BF)] * 2
        + [pltpu.VMEM((k, ROWS), BF) for k, _n in WHOLES[2:]]
        + [pltpu.VMEM(s, BF) for s in WHOLES]
        + [
            pltpu.VMEM((4, 16, FEATURES), F32),
            pltpu.VMEM((4, 64, 128), F32),
            pltpu.VMEM((3, 16, FEATURES), F32),
            pltpu.VMEM((3, 64, 128), F32),
            pltpu.VMEM((4, 16, FEATURES), F32),
            pltpu.VMEM((4, 64, 128), F32),
        ]
        + lands
        + [dma((2, 4, 3)), dma((2, 2, 3)), dma((2, 2)), dma((chunks, 13)), dma((chunks, 13)), dma((12,)), dma((12,))],
        compiler_params=pltpu.CompilerParams(collective_id=1, has_side_effects=True, vmem_limit_bytes=67043328),
    )(n1, dqkv, o, da, n2, dh, g, dz, raw_r, raw_g, sums, up_sum, bias_sums, norm_sums, table_sums, jnp.asarray(table_taker()))


def dot_rows(a, b):
    return lax.dot_general(a, b, (((0,), (0,)), ((), ())), preferred_element_type=F32)


def on_device(
    image_in,
    cotangent,
    qkv_weight,
    out_weight,
    up_weight,
    down_weight,
    query_bias,
    value_bias,
    out_bias,
    up_bias,
    down_bias,
    first_gain,
    first_shift,
    second_gain,
    second_shift,
    rows_table,
    cols_table,
):
    line = lambda v: v.reshape(1, -1)
    bias_all = line(jnp.concatenate([query_bias, jnp.zeros_like(query_bias), value_bias]))
    tab = table_operand(rows_table, cols_table, False)
    tab_back = table_operand(rows_table, cols_table, True)
    xw, cw, n1_turned, qkv, probs, o, o_turned, wq, wo, wu, wd = open_windows(
        image_in, cotangent, (qkv_weight, out_weight, up_weight, down_weight), line(first_gain), line(first_shift), bias_all, tab
    )
    result, n2, g, dh, da, do, dm, sums, up_sum = middle(
        o, xw, cw, wo, wu, wd, line(out_bias), line(up_bias), line(down_bias), line(second_gain), line(second_shift)
    )
    dqkv, raw_r, raw_g, bias_sums, norm_sums, table_sums = back(
        do, probs, qkv, o, xw, dm, result, wq, tab_back, bias_all, line(first_gain)
    )
    if lax.axis_size("img") == 2:
        *large, small, table = finish(n1_turned, dqkv, o_turned, da, n2, dh, g, cw, raw_r, raw_g, sums, up_sum, bias_sums, norm_sums, table_sums)
        return (
            *large,
            small[0],
            small[1],
            small[2],
            small[8:12].reshape(-1),
            *(small[i] for i in range(3, 8)),
            table[:, :27].T,
            table[:, 64:91].T,
        )
    image_out, image_grad = give_back(raw_r, raw_g)
    totals = (jnp.dot(n1_turned, dqkv, preferred_element_type=F32), jnp.dot(o_turned, da, preferred_element_type=F32), dot_rows(n2, dh), dot_rows(g, cw))
    shard_sums = []
    for total in totals:
        part = lax.psum_scatter(total.astype(BF), ("row", "col"), scatter_dimension=0, tiled=True)
        shard_sums.append(lax.psum_scatter(part, "img", scatter_dimension=1, tiled=True).astype(F32))
    rows_grad, cols_grad = table_grads(table_sums)
    small_sums = lax.psum(
        tuple(jnp.sum(bias_sums, axis=1))
        + (jnp.sum(sums[0], axis=0), jnp.sum(up_sum, axis=0), jnp.sum(sums[1], axis=0))
        + tuple(jnp.sum(norm_sums, axis=1))
        + (jnp.sum(sums[2], axis=0), jnp.sum(sums[3], axis=0), rows_grad, cols_grad),
        ("img", "row", "col"),
    )
    return (image_out, image_grad, *shard_sums, *small_sums)


def solution(mesh):
    tiles = P("img", "row", "col", None)
    shards = P(("row", "col"), "img")
    return jax.shard_map(
        on_device,
        mesh=mesh,
        in_specs=(tiles,) * 2 + (shards,) * 4 + (P(),) * 11,
        out_specs=(tiles,) * 2 + (shards,) * 4 + (P(),) * 11,
        check_vma=False,
    )
```

```python
import functools

import jax
import jax.numpy as jnp
import numpy as np
from jax import lax
from jax.experimental import pallas as pl
from jax.experimental.pallas import tpu as pltpu
from jax.sharding import PartitionSpec as P

MESH = pl.DeviceIdType.MESH


def place():
    return lax.axis_index("img"), lax.axis_index("row"), lax.axis_index("col")


def side_owner(window_row, image):
    return lax.rem(window_row, 2), 3 - image - 2 * (window_row // 2)


def piece_target(kind, image, row, col):
    last_row, last_col = row == 3, col == 3
    side_row, side_col = side_owner(row, image)
    next_row, next_col = side_owner(lax.rem(row + 1, 4), image)
    if kind == 0:
        return (jnp.where(last_row, 3 - image, row + 1), col, jnp.where(last_row, 2, image))
    if kind == 1:
        return (jnp.where(last_col, side_row, row), jnp.where(last_col, side_col, col + 1), jnp.where(last_col, 2, image))
    target_row = jnp.where(last_row, 3 - image, jnp.where(last_col, next_row, row + 1))
    target_col = jnp.where(last_col, jnp.where(last_row, 3, next_col), col + 1)
    slot = jnp.where(last_row & last_col, 3, jnp.where(last_row | last_col, 2, image))
    return (target_row, target_col, slot)


def arrivals(row, col):
    wide = row >= 2
    side_row = row + 2 * (1 - col // 2)
    table = []
    for image in range(2):
        table.append((image, 0, row > 0))
        table.append((image, 1, col > 0))
        table.append((image, 2, (row > 0) & (col > 0)))
    table.append((2, 0, wide))
    table.append((2, 1, jnp.logical_not(wide)))
    table.append((2, 2, jnp.where(wide, col, side_row) > 0))
    table.append((3, 2, wide & (col == 3)))
    return table


def tile_part(ref, image, kind):
    if kind == 0:
        return ref.at[image, pl.ds(8, 8), pl.ds(0, 2)]
    if kind == 1:
        return ref.at[image, pl.ds(0, 14), pl.ds(1, 1)]
    return ref.at[image, pl.ds(8, 8), pl.ds(1, 1)]


def window_part(ref, slot, kind):
    if kind == 0:
        return ref.at[pl.ds(slot * 22, 8), pl.ds(1, 2)]
    if kind == 1:
        return ref.at[pl.ds(slot * 22 + 8, 14), pl.ds(0, 1)]
    return ref.at[pl.ds(slot * 22, 8), pl.ds(0, 1)]


def greet(img, row, col, pairs=True):
    barrier = pltpu.get_barrier_semaphore()
    for row_step in range(4):
        for col_step in range(4):
            if row_step or col_step:
                pl.semaphore_signal(
                    barrier,
                    inc=1,
                    device_id={"row": lax.rem(row + row_step, 4), "col": lax.rem(col + col_step, 4)},
                    device_id_type=MESH,
                )
    if pairs:
        pl.semaphore_signal(barrier, inc=1, device_id={"img": 1 - img}, device_id_type=MESH)
    pl.semaphore_wait(barrier, 16 if pairs else 15)


CHUNKS = ((0, 0, 640), (0, 640, 1152), (1, 0, 384), (2, 0, 768), (2, 768, 1536), (3, 0, 128), (3, 128, 384))


def links(shards, fulls, wsend, wrecv, wloc):
    img, row, col = place()
    y_row = lax.rem(row + 2, 4)
    core_row = row + 1 - 2 * lax.rem(row, 2)
    other = 1 - img
    sent = []

    def rows_of(w, rw, half=None):
        kb = fulls[w].shape[0] // 4
        if half is None:
            return pl.ds(pl.multiple_of(rw * kb, kb), kb)
        return pl.ds(pl.multiple_of(rw * kb + half * (kb // 2), kb // 2), kb // 2)

    def cols_of(n, im):
        w, lo, hi = CHUNKS[n]
        nb = fulls[w].shape[1] // 2
        return pl.ds(pl.multiple_of(im * nb + lo, 128), hi - lo)

    def block(n, rw, im, half=None):
        w = CHUNKS[n][0]
        return fulls[w].at[rows_of(w, rw, half), cols_of(n, im)]

    def slot(n, cl):
        w = CHUNKS[n][0]
        k16 = fulls[w].shape[0] // 16
        return fulls[w].at[pl.ds(pl.multiple_of((row * 4 + cl) * k16, k16), k16), cols_of(n, img)]

    def source(n):
        w, lo, hi = CHUNKS[n]
        return shards[w].at[:, pl.ds(lo, hi - lo)]

    def push(n, k, where, target, start=None):
        def copy():
            ref = block(n, *where)
            return pltpu.make_async_remote_copy(
                src_ref=source(n) if start else ref,
                dst_ref=slot(n, col) if start else ref,
                send_sem=wsend.at[n, k],
                recv_sem=wrecv.at[n, k],
                device_id=target(),
                device_id_type=MESH,
            )

        copy().start()
        sent.append(copy)

    def arrive(n, k, ref):
        pltpu.make_async_copy(ref, ref, wrecv.at[n, k]).wait()

    def along_col(n):
        pltpu.make_async_copy(source(n), slot(n, col), wloc.at[n]).start()
        for d in range(1, 4):
            push(n, d - 1, (row, img), lambda d=d: {"col": lax.rem(col + d, 4)}, True)

    def first(n):
        pltpu.make_async_copy(source(n), slot(n, col), wloc.at[n]).wait()
        for d in range(1, 4):
            arrive(n, d - 1, slot(n, lax.rem(col + 4 - d, 4)))
        push(n, 3, (row, img, 0), lambda: {"img": other})
        push(n, 4, (row, img, 1), lambda: {"row": y_row})
        push(n, 5, (row, img), lambda: {"row": core_row})

    def second(n):
        arrive(n, 3, block(n, row, other, 0))
        arrive(n, 4, block(n, y_row, img, 1))
        push(n, 6, (row, img, 0), lambda: {"row": y_row})
        push(n, 7, (row, other, 0), lambda: {"row": y_row})
        push(n, 8, (row, img, 1), lambda: {"img": other})
        push(n, 9, (y_row, img, 1), lambda: {"img": other})
        push(n, 10, (row, other, 0), lambda: {"row": core_row})
        push(n, 11, (y_row, img, 1), lambda: {"row": core_row})

    def third(n):
        arrive(n, 6, block(n, y_row, img, 0))
        arrive(n, 7, block(n, y_row, other, 0))
        arrive(n, 8, block(n, row, other, 1))
        arrive(n, 9, block(n, y_row, other, 1))
        push(n, 12, (y_row, img, 0), lambda: {"row": core_row})
        push(n, 13, (y_row, other, 0), lambda: {"row": core_row})
        push(n, 14, (row, other, 1), lambda: {"row": core_row})
        push(n, 15, (y_row, other, 1), lambda: {"row": core_row})

    def last(n):
        core_y = lax.rem(core_row + 2, 4)
        arrive(n, 5, block(n, core_row, img))
        arrive(n, 10, block(n, core_row, other, 0))
        arrive(n, 11, block(n, core_y, img, 1))
        arrive(n, 12, block(n, core_y, img, 0))
        arrive(n, 13, block(n, core_y, other, 0))
        arrive(n, 14, block(n, core_row, other, 1))
        arrive(n, 15, block(n, core_y, other, 1))

    return along_col, first, second, third, last, sent


def window_moves(tiles, raws, send, recv, loc):
    img, row, col = place()

    def each(t, act):
        for image in range(2):
            for kind in range(3):
                target_row, target_col, target_slot = piece_target(kind, image, row, col)
                here = (target_row == row) & (target_col == col)
                part = tile_part(tiles[t], image, kind)
                goal = window_part(raws[t], target_slot, kind)
                act(here, part, goal, send.at[t, image, kind], recv.at[t, target_slot, kind], target_row, target_col)

    def remote(part, goal, leave, arrival, target_row, target_col):
        return pltpu.make_async_remote_copy(
            src_ref=part,
            dst_ref=goal,
            send_sem=leave,
            recv_sem=arrival,
            device_id={"row": target_row, "col": target_col},
            device_id_type=MESH,
        )

    def own(t, image):
        return pltpu.make_async_copy(tiles[t].at[image, pl.ds(0, 14)], raws[t].at[pl.ds(image * 22 + 8, 14), pl.ds(1, 2)], loc.at[t, image])

    def start(t):
        for image in range(2):
            own(t, image).start()

        def act(here, part, goal, leave, arrival, target_row, target_col):
            @pl.when(here)
            def _():
                pltpu.make_async_copy(part, goal, arrival).start()

            @pl.when(jnp.logical_not(here))
            def _():
                remote(part, goal, leave, arrival, target_row, target_col).start()

        each(t, act)

    def arrived(t):
        for image in range(2):
            own(t, image).wait()
        for slot_index, kind, present in arrivals(row, col):
            part = window_part(raws[t], slot_index, kind)

            @pl.when(present)
            def _():
                pltpu.make_async_copy(part, part, recv.at[t, slot_index, kind]).wait()

    def left(t):
        def act(here, part, goal, leave, arrival, target_row, target_col):
            @pl.when(jnp.logical_not(here))
            def _():
                remote(part, goal, leave, arrival, target_row, target_col).wait_send()

        each(t, act)

    return start, arrived, left


BF = jnp.bfloat16
F32 = jnp.float32
ROWS = 704
SPAN = 800
FEATURES = 768
EPS = 1e-06


def row_params(step, row, col):
    wide = row >= 2
    side_row = row + 2 * (1 - col // 2)
    third_step = step - 28
    in_corner = wide & (third_step >= 8)
    slot = jnp.where(step < 14, 0, jnp.where(step < 28, 1, jnp.where(in_corner, 3, 2)))
    place_row = jnp.where(step < 14, step, jnp.where(step < 28, step - 14, jnp.where(in_corner, third_step - 8, third_step)))
    full = step < 28
    row_start = jnp.where(full, 8 - 2 * row, jnp.where(wide, 0, 8 - 2 * side_row))
    col_start = jnp.where(full, 8 - 2 * col, jnp.where(wide & jnp.logical_not(in_corner), 8 - 2 * col, 0))
    width = jnp.where(full, 14, jnp.where(wide & jnp.logical_not(in_corner), 14, 8))
    alive = jnp.where(full, True, jnp.where(in_corner, col == 3, jnp.where(wide, True, third_step < 14)))
    return slot, jnp.minimum(place_row + row_start, 21), col_start, jnp.where(alive, width, 0)


def window_params(window, row, col):
    wide = row >= 2
    start = jnp.where(window < 2, 14 * window, jnp.where(window == 2, 28, 36))
    tall = jnp.where(window < 2, 14, jnp.where((window == 2) & jnp.logical_not(wide), 14, 8))
    width = jnp.where(window < 2, 14, jnp.where((window == 2) & wide, 14, 8))
    return start, tall, width


def window_count(row, col):
    return jnp.where((row >= 2) & (col == 3), 4, 3)


def unit_of(values):
    center = values - jnp.mean(values, axis=-1, keepdims=True)
    inverse = lax.rsqrt(jnp.mean(center * center, axis=-1, keepdims=True) + EPS)
    return center * inverse, inverse


def relative_layout(backward):
    take = np.zeros((2, 2, 27, 128), np.float32)
    for parity in range(2):
        base = 64 if parity == 0 else 0
        for j in range(27):
            for copy in (0,) if backward else (0, 32):
                take[parity, 0, 26 - j, (base - 13 + j + copy) % 128] = 1
                if backward:
                    take[parity, 1, j, base + 16 + j] = 1
                else:
                    take[parity, 1, 26 - j, (base + 3 + j + copy) % 128] = 1
    return take


def table_operand(rows_table, cols_table, backward):
    take = jnp.asarray(relative_layout(backward), BF)
    parts = []
    for parity in range(2):
        both = []
        for which, table in ((0, rows_table), (1, cols_table)):
            both.append(lax.dot_general(table, take[parity, which], (((0,), (0,)), ((), ())), preferred_element_type=F32).astype(BF))
        block = jnp.concatenate(both, axis=1)
        zero = jnp.zeros_like(block)
        parts.append(jnp.concatenate([block, zero] if parity == 0 else [zero, block], axis=0))
    return jnp.concatenate(parts, axis=1)


def table_grads(sums):
    take = jnp.asarray(relative_layout(True), F32)
    grads = []
    for which in range(2):
        total = 0.0
        for parity in range(2):
            part = sums[64 * parity : 64 * parity + 64, 256 * parity + 128 * which : 256 * parity + 128 * which + 128]
            total = total + lax.dot_general(take[parity, which], part, (((1,), (1,)), ((), ())), precision=lax.Precision.HIGHEST)
        grads.append(total)
    return grads


def run_all(act):
    for i in range(0, len(act), 2):
        act[i](act[i + 1])


def open_kernel(weights, x_ref, c_ref, gain, shift, bias, tab, *refs):
    img, row, col = place()
    greet(img, row, col, weights)
    if weights:
        shards, refs = refs[:4], refs[4:]
    else:
        wq, refs = refs[0], refs[1:]
    xw, cw, n1_turned, qkv_s, probs, o, o_turned = refs[:7]
    refs = refs[7:]
    if weights:
        fulls, refs = refs[:4], refs[4:]
        wq = fulls[0]
    rawx, rawc, n1, send, recv, loc = refs[:6]
    if weights:
        along_col, first, second, third, last, sent = links(shards, fulls, *refs[6:])
    window_start, window_arrived, window_left = window_moves((x_ref, c_ref), (rawx, rawc), send, recv, loc)
    places = lax.broadcasted_iota(jnp.int32, (16, 1), 0)

    def cut_one(raw, step):
        slot, raw_row, col_start, width = row_params(step, row, col)
        wide_rows = raw[slot * 22 + raw_row].reshape(24, FEATURES).astype(F32)
        keep = places < width
        return keep, jnp.where(keep, pltpu.roll(wide_rows, lax.rem(24 - col_start, 24), 0)[:16], 0.0)

    def cut_x(step, _):
        at = pl.ds(pl.multiple_of(step * 16, 16), 16)
        keep, x = cut_one(rawx, step)
        xw[at, :] = x.astype(BF)
        unit, _inverse = unit_of(x)
        n1[at, :] = jnp.where(keep, unit * gain[...] + shift[...], 0.0).astype(BF)
        return 0

    def cut_c(step, _):
        at = pl.ds(pl.multiple_of(step * 16, 16), 16)
        _keep, c = cut_one(rawc, step)
        cw[at, :] = c.astype(BF)
        return 0

    def project(step, _):
        at = pl.ds(pl.multiple_of(step * 352, 32), 352)
        for part_index in range(3):
            lanes = slice(part_index * FEATURES, (part_index + 1) * FEATURES)
            part = jnp.dot(n1[at, :], wq[:, lanes], preferred_element_type=F32) + bias[:, lanes]
            qkv_s[at, lanes] = part.astype(BF)
        return 0

    def turn(source, goal):
        def step(i, _):
            lanes = pl.ds(pl.multiple_of(i * 128, 128), 128)
            goal[lanes, :] = source[0:ROWS, lanes].T
            return 0

        lax.fori_loop(0, FEATURES // 128, step, 0)

    if weights:
        along_col(0)
        along_col(1)
    else:
        window_start(0)
        window_start(1)
    o[...] = jnp.zeros_like(o)
    if weights:
        first(0)
        first(1)
        window_start(0)
        along_col(2)
        second(0)
        second(1)
        along_col(3)
    window_arrived(0)
    lax.fori_loop(0, 44, cut_x, 0)
    steps = []
    if weights:
        first(2)
        along_col(4)
        third(0)
        third(1)
        first(3)
        along_col(5)
        last(0)
        last(1)
        steps = [
            (second, 2),
            (first, 4, along_col, 6),
            (second, 3),
            (third, 2),
            (first, 5, window_start, 1),
            (second, 4),
            (third, 3),
            (first, 6),
            (second, 5),
            (third, 4),
            (second, 6),
            (third, 5),
            (third, 6),
        ]
    lax.fori_loop(0, 2, project, 0)
    row_of = lax.broadcasted_iota(jnp.int32, (224, 1), 0)
    lane = lax.broadcasted_iota(jnp.int32, (1, 128), 1)
    key_place = lax.broadcasted_iota(jnp.int32, (224, 128), 0)
    key_lane = lax.broadcasted_iota(jnp.int32, (224, 128), 1)
    key_a, key_b = key_place // 16, key_place % 16

    def pair(index, _):
        for turn_index, act in enumerate(steps):
            pl.when(index == turn_index)(functools.partial(run_all, act))
        window, pair_index = index // 6, index % 6
        start, tall, width = window_params(window, row, col)
        at = pl.ds(pl.multiple_of(start * 16, 16), 224)
        alive = (row_of // 16 < tall) & (row_of % 16 < width)
        lanes = lambda third: pl.ds(pl.multiple_of(third * FEATURES + pair_index * 128, 128), 128)
        q = jnp.where(alive, qkv_s[at, lanes(0)].astype(F32), 0.0)
        k = jnp.where(alive, qkv_s[at, lanes(1)].astype(F32), 0.0)
        v = jnp.where(alive, qkv_s[at, lanes(2)].astype(F32), bias[:, lanes(2)].astype(BF).astype(F32)).astype(BF)
        terms = jnp.dot(q.astype(BF), tab[...], preferred_element_type=F32)
        outs = []
        for parity in range(2):
            base = 64 if parity == 0 else 0
            own = (lane < 64) if parity == 0 else (lane >= 64)
            rel_rows = jnp.concatenate(
                [pltpu.roll(terms[16 * a : 16 * a + 16, 256 * parity : 256 * parity + 128], a, 1) for a in range(14)], axis=0
            )
            rel_cols = jnp.concatenate(
                [
                    pltpu.roll(terms[16 * a : 16 * a + 16, 256 * parity + 128 : 256 * parity + 256], 0, 1, stride=1, stride_axis=0)
                    for a in range(14)
                ],
                axis=0,
            )
            on = lane - base
            in_rows = ((on >= 0) & (on < 14)) | ((on >= 32) & (on < 46))
            in_cols = ((on >= 16) & (on < 30)) | ((on >= 48) & (on < 62))
            rel = jnp.where(in_rows, rel_rows, jnp.where(in_cols, rel_cols, 0.0))
            rough = rel.astype(BF).astype(F32)
            fine = jnp.where(on >= 32, rel - rough, rough)
            fine = jnp.where(on == 14, -1e30, fine)
            q_side = jnp.where(own, q * 0.125, fine).astype(BF)
            key_on = key_lane - base
            hot = jnp.where(
                key_on == 14,
                jnp.where(key_b >= 14, 1.0, 0.0),
                jnp.where(
                    (key_on % 32 < 14) & (key_a == key_on % 32),
                    1.0,
                    jnp.where((key_on % 32 >= 16) & (key_on % 32 < 30) & (key_b == key_on % 32 - 16), 1.0, 0.0),
                ),
            )
            k_side = jnp.where(own, k, hot).astype(BF)
            scores = lax.dot_general(q_side, k_side, (((1,), (1,)), ((), ())), preferred_element_type=F32)
            exponent = jnp.exp(scores - jnp.max(scores, axis=-1, keepdims=True))
            p = (exponent * (1.0 / jnp.sum(exponent, axis=-1, keepdims=True))).astype(BF)
            probs[window, 2 * pair_index + parity] = p
            outs.append(jnp.dot(p, v, preferred_element_type=F32))
        blended = jnp.where(lane < 64, outs[0], outs[1])
        out_lanes = pl.ds(pl.multiple_of(pair_index * 128, 128), 128)
        o_at = pl.ds(pl.multiple_of(start * 16, 16), 224)
        o[o_at, out_lanes] = jnp.where(alive, blended, 0.0).astype(BF)
        return 0

    lax.fori_loop(0, window_count(row, col) * 6, pair, 0)
    turn(n1, n1_turned)
    turn(o, o_turned)
    window_arrived(1)
    lax.fori_loop(0, 44, cut_c, 0)
    if weights:
        for n in range(2, len(CHUNKS)):
            last(n)
        for copy in sent:
            copy().wait_send()
    window_left(0)
    window_left(1)


def open_windows(x, c, shards, gain, shift, bias, tab):
    vm = pl.BlockSpec(memory_space=pltpu.VMEM)
    an = pl.BlockSpec(memory_space=pl.ANY)
    shape = jax.ShapeDtypeStruct
    dma = pltpu.SemaphoreType.DMA
    chunks = len(CHUNKS)
    weights = lax.axis_size("img") == 2
    if weights:
        given, wholes = list(shards), [(768, 2304), (768, 768), (768, 3072), (3072, 768)]
    else:
        widened = [lax.all_gather(w, "img", axis=1, tiled=True) for w in shards]
        gathered = [lax.all_gather(w, ("row", "col"), axis=0, tiled=True) for w in widened]
        given, wholes = gathered[:1], []
    raw = pltpu.VMEM((88, 3, 8, FEATURES), BF)
    outs = pl.pallas_call(
        functools.partial(open_kernel, weights),
        out_shape=[
            shape((ROWS, FEATURES), BF),
            shape((ROWS, FEATURES), BF),
            shape((FEATURES, ROWS), BF),
            shape((SPAN, 3 * FEATURES), BF),
            shape((4, 12, 224, 224), BF),
            shape((SPAN, FEATURES), BF),
            shape((FEATURES, ROWS), BF),
        ]
        + [shape(s, BF) for s in wholes],
        in_specs=[vm] * (6 + len(given)),
        out_specs=[vm] * 7 + ([vm, an, an, an] if weights else []),
        scratch_shapes=[raw, raw, pltpu.VMEM((ROWS, FEATURES), BF), dma((2, 2, 3)), dma((2, 4, 3)), dma((2, 2))]
        + ([dma((chunks, 16)), dma((chunks, 16)), dma((chunks,))] if weights else []),
        compiler_params=pltpu.CompilerParams(collective_id=0, has_side_effects=True, vmem_limit_bytes=67043328),
    )(x.reshape(2, 16, 2, 8, 768), c.reshape(2, 16, 2, 8, 768), gain, shift, bias, tab, *given)
    return list(outs) if weights else list(outs) + gathered


FF = 3072
CHUNK = 512
BLOCK = 176


def nt(a, b):
    return lax.dot_general(a, b, (((1,), (1,)), ((), ())), preferred_element_type=F32)


def norm_back(grad, unit, inverse, gain):
    scaled = grad * gain
    first_mean = jnp.mean(scaled, axis=-1, keepdims=True)
    second_mean = jnp.mean(scaled * unit, axis=-1, keepdims=True)
    return inverse * (scaled - first_mean - unit * second_mean)


def fold_rows(values):
    total = values[0:8]
    for i in range(1, values.shape[0] // 8):
        total = total + values[8 * i : 8 * i + 8]
    return total


def spread_rows(source, raw, row, col):
    def step(i, _):
        slot, raw_row, col_start, width = row_params(i, row, col)
        at = pl.ds(pl.multiple_of(i * 16, 16), 16)

        @pl.when(width > 0)
        def _():
            values = jnp.concatenate([source[at, :], jnp.zeros((8, FEATURES), F32)], axis=0)
            raw[slot * 22 + raw_row] = pltpu.roll(values, col_start, 0).astype(BF).reshape(3, 8, FEATURES)

        return 0

    lax.fori_loop(0, 44, step, 0)


def middle_kernel(
    o, xw, cw, wo, wu, wd, out_bias, up_bias, down_bias, gain, shift, raw_r, n2_turned, g_turned, dh, da, do, dm, sums, up_sum, n2, y_s, d_s, g_s
):
    step = pl.program_id(0)
    row, col = lax.axis_index("row"), lax.axis_index("col")
    blocks = [slice(i * BLOCK, (i + 1) * BLOCK) for i in range(ROWS // BLOCK)]

    def mid_of(at):
        return xw[at, :].astype(F32) + (jnp.dot(o[at, :], wo[...], preferred_element_type=F32) + out_bias[...])

    @pl.when(step == 0)
    def _():
        sums[...] = jnp.zeros_like(sums)
        d_s[...] = jnp.zeros_like(d_s)

        def begin(i, _):
            at = pl.ds(pl.multiple_of(i * BLOCK, 16), BLOCK)
            mid = mid_of(at)
            unit, _inverse = unit_of(mid)
            n2[at, :] = (unit * gain[...] + shift[...]).astype(BF)
            y_s[at, :] = mid + down_bias[...]
            dm[at, :] = mid
            return 0

        lax.fori_loop(0, ROWS // BLOCK, begin, 0)

        def turn(i, _):
            lanes = pl.ds(pl.multiple_of(i * 128, 128), 128)
            n2_turned[lanes, :] = n2[:, lanes].T
            return 0

        lax.fori_loop(0, FEATURES // 128, turn, 0)

    up_sum[...] = jnp.zeros_like(up_sum)
    for at in blocks:
        h = jnp.dot(n2[at, :], wu[...], preferred_element_type=F32) + up_bias[...]
        up = nt(cw[at, :], wd[...])
        phi = 0.5 * (1.0 + lax.erf(h * 0.7071067811865476))
        slope = phi + h * (jnp.exp(-0.5 * h * h) * 0.3989422804014327)
        active = (h * phi).astype(BF)
        back = (up * slope).astype(BF)
        g_s[at, :] = active
        dh[at, :] = back
        up_sum[...] += fold_rows(back.astype(F32))
        y_s[at, :] += jnp.dot(active, wd[...], preferred_element_type=F32)
        d_s[at, :] += nt(back, wu[...])
    for i in range(CHUNK // 128):
        g_turned[128 * i : 128 * i + 128, 0:ROWS] = g_s[:, 128 * i : 128 * i + 128].T

    @pl.when(step == FF // CHUNK - 1)
    def _():
        def end(i, _):
            at = pl.ds(pl.multiple_of(i * BLOCK, 16), BLOCK)
            unit, inverse = unit_of(dm[at, :])
            grad = d_s[at, :].astype(BF).astype(F32)
            up = cw[at, :].astype(F32)
            grad_mid = up + norm_back(grad, unit, inverse, gain[...])
            low_grad = grad_mid.astype(BF)
            dm[at, :] = grad_mid
            da[at, :] = low_grad
            do[at, :] = nt(low_grad, wo[...]).astype(BF)
            sums[0] += fold_rows(low_grad.astype(F32))
            sums[1] += fold_rows(up)
            sums[2] += fold_rows(grad * unit)
            sums[3] += fold_rows(grad)
            return 0

        lax.fori_loop(0, ROWS // BLOCK, end, 0)
        spread_rows(y_s, raw_r, row, col)


def middle(o, xw, cw, wo, wu, wd, out_bias, up_bias, down_bias, gain, shift):
    shape = jax.ShapeDtypeStruct
    once = lambda *s: pl.BlockSpec(s, lambda i: (0,) * len(s), pipeline_mode=pl.Buffered(1))
    return pl.pallas_call(
        middle_kernel,
        grid=(FF // CHUNK,),
        out_shape=[
            shape((88, 3, 8, FEATURES), BF),
            shape((FEATURES, ROWS), BF),
            shape((FF, FEATURES), BF),
            shape((ROWS, FF), BF),
            shape((ROWS, FEATURES), BF),
            shape((SPAN, FEATURES), BF),
            shape((ROWS, FEATURES), F32),
            shape((4, 8, FEATURES), F32),
            shape((8, FF), F32),
        ],
        in_specs=[
            once(SPAN, FEATURES),
            once(ROWS, FEATURES),
            once(ROWS, FEATURES),
            once(FEATURES, FEATURES),
            pl.BlockSpec((FEATURES, CHUNK), lambda i: (0, i)),
            pl.BlockSpec((CHUNK, FEATURES), lambda i: (i, 0)),
            once(1, FEATURES),
            pl.BlockSpec((1, CHUNK), lambda i: (0, i)),
            once(1, FEATURES),
            once(1, FEATURES),
            once(1, FEATURES),
        ],
        out_specs=[
            once(88, 3, 8, FEATURES),
            once(FEATURES, ROWS),
            pl.BlockSpec((CHUNK, FEATURES), lambda i: (i, 0)),
            pl.BlockSpec((ROWS, CHUNK), lambda i: (0, i)),
            once(ROWS, FEATURES),
            once(SPAN, FEATURES),
            once(ROWS, FEATURES),
            once(4, 8, FEATURES),
            pl.BlockSpec((8, CHUNK), lambda i: (0, i)),
        ],
        scratch_shapes=[
            pltpu.VMEM((ROWS, FEATURES), BF),
            pltpu.VMEM((ROWS, FEATURES), F32),
            pltpu.VMEM((ROWS, FEATURES), F32),
            pltpu.VMEM((ROWS, CHUNK), BF),
        ],
        compiler_params=pltpu.CompilerParams(vmem_limit_bytes=62 << 20),
    )(o, xw, cw, wo, wu, wd, out_bias, up_bias, down_bias, gain, shift)


def attention_back(window, pair_index, probs_of, do, qkv, o, tab, bias, bias_sums, table_sums, row, col):
    row_of = lax.broadcasted_iota(jnp.int32, (224, 1), 0)
    lane = lax.broadcasted_iota(jnp.int32, (1, 128), 1)
    key_place = lax.broadcasted_iota(jnp.int32, (224, 128), 0)
    key_lane = lax.broadcasted_iota(jnp.int32, (224, 128), 1)
    key_a, key_b = key_place // 16, key_place % 16
    start, tall, width = window_params(window, row, col)
    at = pl.ds(pl.multiple_of(start * 16, 16), 224)
    inside = row_of // 16 < tall
    alive = inside & (row_of % 16 < width)
    lanes = lambda third: pl.ds(pl.multiple_of(third * FEATURES + pair_index * 128, 128), 128)
    old = [qkv[at, lanes(third)].astype(F32) for third in range(3)]
    q = jnp.where(alive, old[0], 0.0)
    k = jnp.where(alive, old[1], 0.0)
    v = jnp.where(alive, old[2], bias[:, lanes(2)].astype(BF).astype(F32))
    grad = jnp.where(alive, do[at, lanes(0)].astype(F32), 0.0)
    product = grad * jnp.where(alive, o[at, lanes(0)].astype(F32), 0.0)
    q_turned = q.T.astype(BF)
    grad_turned = grad.T.astype(BF)
    value_parts, key_parts, query_parts, table_parts = [], [], [], []
    for parity in range(2):
        base = 64 if parity == 0 else 0
        own = (lane < 64) if parity == 0 else (lane >= 64)
        half = slice(64 * parity, 64 * parity + 64)
        inner = jnp.sum(jnp.where(own, product, 0.0), axis=-1, keepdims=True)
        rough = inner.astype(BF).astype(F32)
        on = lane - base
        grad_side = jnp.where(own, grad, jnp.where(on == 0, rough, jnp.where(on == 1, inner - rough, 0.0))).astype(BF)
        v_side = jnp.where(own, v, jnp.where((on == 0) | (on == 1), -1.0, 0.0)).astype(BF)
        centered = nt(grad_side, v_side)
        p = probs_of(parity)
        ds = (p.astype(F32) * centered).astype(BF)
        value_parts.append(jnp.dot(grad_turned[half], p, preferred_element_type=F32))
        key_parts.append(jnp.dot(q_turned[half], ds, preferred_element_type=F32))
        key_on = key_lane - base
        hot = jnp.where(
            (key_on >= 0) & (key_on < 14) & (key_a == key_on),
            1.0,
            jnp.where((key_on >= 16) & (key_on < 30) & (key_b == 29 - key_on), 1.0, 0.0),
        )
        k_side = jnp.where(own, k * 0.125, hot).astype(BF)
        wide = jnp.dot(ds, k_side, preferred_element_type=F32)
        query_parts.append(wide)
        by_rows = jnp.where((on >= 0) & (on < 14), wide, 0.0)
        by_cols = jnp.where((on >= 16) & (on < 30), wide, 0.0)
        table_parts.append(jnp.concatenate([pltpu.roll(by_rows[16 * a : 16 * a + 16], (128 - a) % 128, 1) for a in range(14)], axis=0))
        table_parts.append(
            jnp.concatenate([pltpu.roll(by_cols[16 * a : 16 * a + 16], 0, 1, stride=1, stride_axis=0) for a in range(14)], axis=0)
        )
    turned = jnp.concatenate(table_parts, axis=1).astype(BF)
    dq = jnp.where(lane < 64, query_parts[0], query_parts[1]) + nt(turned, tab[...])
    table_sums[...] += jnp.dot(q_turned, turned, preferred_element_type=F32)
    dk = jnp.concatenate(key_parts, axis=0).T * 0.125
    dv = jnp.concatenate(value_parts, axis=0).T.astype(BF).astype(F32)
    dq = jnp.where(alive, dq, 0.0).astype(BF).astype(F32)
    bias_sums[0, :, lanes(0)] += fold_rows(dq)
    bias_sums[1, :, lanes(0)] += fold_rows(dv)
    for third, new in enumerate((dq, dk, dv)):
        qkv[at, lanes(third)] = jnp.where(alive, new, jnp.where(inside, 0.0, old[third])).astype(BF)


def clear_idle(qkv, row, col):
    wide = row >= 2
    limit = jnp.where(wide, jnp.where(col == 3, 44, 36), 42)
    for a in range(36, 44):

        @pl.when(a >= limit)
        def _():
            qkv[16 * a : 16 * a + 16, :] = jnp.zeros((16, 3 * FEATURES), BF)


def plain_back_kernel(do, probs, qkv, o, tab, bias, dqkv, bias_sums, table_sums):
    row, col = lax.axis_index("row"), lax.axis_index("col")
    dqkv[...] = qkv[...]
    clear_idle(dqkv, row, col)
    bias_sums[...] = jnp.zeros_like(bias_sums)
    table_sums[...] = jnp.zeros_like(table_sums)

    def pair(index, _):
        window, pair_index = index // 6, index % 6
        attention_back(
            window,
            pair_index,
            lambda parity: probs[window, 2 * pair_index + parity],
            do,
            dqkv,
            o,
            tab,
            bias,
            bias_sums,
            table_sums,
            row,
            col,
        )
        return 0

    lax.fori_loop(0, window_count(row, col) * 6, pair, 0)


def plain_back(do, probs, qkv, o, tab, bias):
    vm = pl.BlockSpec(memory_space=pltpu.VMEM)
    shape = jax.ShapeDtypeStruct
    return pl.pallas_call(
        plain_back_kernel,
        out_shape=[shape((SPAN, 3 * FEATURES), BF), shape((2, 8, FEATURES), F32), shape((128, 512), F32)],
        in_specs=[vm] * 6,
        out_specs=[vm] * 3,
        compiler_params=pltpu.CompilerParams(vmem_limit_bytes=62 << 20),
    )(do, probs, qkv, o, tab, bias)


WHOLES = ((768, 2304), (768, 768), (768, 3072), (3072, 768))
SUM_CHUNKS = ((1, 0, 384), (3, 0, 128), (3, 128, 384), (2, 0, 768), (2, 768, 1536), (0, 0, 384), (0, 384, 768), (0, 768, 1152))


def pair_lanes(j, im):
    if im == 0:
        return (128 * j, FEATURES + 128 * j, 128 * (j + 3))
    return (2 * FEATURES + 128 * j, FEATURES + 128 * (j + 3), 2 * FEATURES + 128 * (j + 3))


def land_shapes(chunks):
    lands = []
    for w, lo, hi in chunks:
        kb, width = WHOLES[w][0] // 4, hi - lo
        lands += [
            pltpu.VMEM((2, 2, kb, width), BF),
            pltpu.VMEM((2, kb // 2, width), BF),
            pltpu.VMEM((2, kb // 2, width), BF),
            pltpu.VMEM((2, kb // 2, width), BF),
            pltpu.VMEM((3, kb // 4, width), BF),
        ]
    return lands


def reducers(chunks, full, left_turned, right_side, grads, land_refs, wsend, wrecv):
    img, row, col = place()
    y_row = lax.rem(row + 2, 4)
    core_row = row + 1 - 2 * lax.rem(row, 2)
    core_y = lax.rem(core_row + 2, 4)
    other = 1 - img
    lands = [land_refs[5 * n : 5 * n + 5] for n in range(len(chunks))]
    sent = []

    def size(n):
        w, lo, hi = chunks[n]
        return WHOLES[w][0] // 4, WHOLES[w][1] // 2, lo, hi - lo

    def block(n, rw, im, half=None):
        kb, nb, lo, width = size(n)
        cols = pl.ds(pl.multiple_of(im * nb + lo, 128), width)
        if half is None:
            return full[chunks[n][0]].at[pl.ds(pl.multiple_of(rw * kb, kb), kb), cols]
        return full[chunks[n][0]].at[pl.ds(pl.multiple_of(rw * kb + half * (kb // 2), kb // 2), kb // 2), cols]

    def shard(n, cl):
        kb, nb, lo, width = size(n)
        cols = pl.ds(pl.multiple_of(img * nb + lo, 128), width)
        return full[chunks[n][0]].at[pl.ds(pl.multiple_of(row * kb + cl * (kb // 4), kb // 4), kb // 4), cols]

    def push(n, k, src, dst, target):
        def copy():
            return pltpu.make_async_remote_copy(
                src_ref=src(), dst_ref=dst(), send_sem=wsend.at[n, k], recv_sem=wrecv.at[n, k], device_id=target(), device_id_type=MESH
            )

        copy().start()
        sent.append(copy)

    def arrive(n, k, ref):
        pltpu.make_async_copy(ref, ref, wrecv.at[n, k]).wait()

    def add(goal, part, rows):
        def step(i, _):
            at = pl.ds(pl.multiple_of(i * 48, 16), 48)
            goal[at, :] = (goal[at, :].astype(F32) + part[at, :].astype(F32)).astype(BF)
            return 0

        lax.fori_loop(0, rows // 48, step, 0)

    def product(n, rw):
        w = chunks[n][0]
        kb, nb, lo, width = size(n)
        rows = pl.ds(pl.multiple_of(rw * kb, kb), kb)
        for im in range(2):
            at = slice(im * nb + lo, im * nb + lo + width)
            if w == 0:
                right = jnp.concatenate([right_side[0][0:ROWS, p : p + 128] for p in pair_lanes(lo // 384, im)], axis=1)
            else:
                right = right_side[w][0:ROWS, at]
            full[w][rows, at] = jnp.dot(left_turned[w](rw, kb), right, preferred_element_type=F32).astype(BF)

    def pair_stage(n):
        land = lands[n][0]
        for j, rw in enumerate((core_row, core_y)):
            product(n, rw)
            for im in range(2):
                push(n, 2 * j + im, functools.partial(block, n, rw, im), lambda j=j, im=im: land.at[j, im], lambda: {"row": core_row})
        for rw in (row, y_row):
            product(n, rw)

    def first(n):
        kb, nb, lo, width = size(n)
        for j, rw in enumerate((row, y_row)):
            for im in range(2):
                arrive(n, 2 * j + im, lands[n][0].at[j, im])
                add(block(n, rw, im), lands[n][0].at[j, im], kb)
        for im in range(2):
            push(n, 4 + im, functools.partial(block, n, y_row, im, 0), lambda im=im: lands[n][1].at[im], lambda: {"row": y_row})
        push(n, 6, functools.partial(block, n, row, other, 1), lambda: lands[n][2].at[0], lambda: {"img": other})
        push(n, 7, functools.partial(block, n, y_row, other, 1), lambda: lands[n][2].at[1], lambda: {"img": other})

    def second(n):
        kb, nb, lo, width = size(n)
        for im in range(2):
            arrive(n, 4 + im, lands[n][1].at[im])
            add(block(n, row, im, 0), lands[n][1].at[im], kb // 2)
        push(n, 8, functools.partial(block, n, row, other, 0), lambda: lands[n][3].at[0], lambda: {"img": other})
        for j, rw in enumerate((row, y_row)):
            arrive(n, 6 + j, lands[n][2].at[j])
            add(block(n, rw, img, 1), lands[n][2].at[j], kb // 2)
        push(n, 9, functools.partial(block, n, y_row, img, 1), lambda: lands[n][3].at[1], lambda: {"row": y_row})

    def third(n):
        kb, nb, lo, width = size(n)
        for half in range(2):
            arrive(n, 8 + half, lands[n][3].at[half])
            add(block(n, row, img, half), lands[n][3].at[half], kb // 2)
        for d in range(1, 4):

            def src(d=d):
                return shard(n, lax.rem(col + d, 4))

            push(n, 9 + d, src, lambda d=d: lands[n][4].at[d - 1], lambda d=d: {"col": lax.rem(col + d, 4)})

    def fourth(n):
        w, lo, hi = chunks[n]
        for d in range(1, 4):
            arrive(n, 9 + d, lands[n][4].at[d - 1])
        mine = shard(n, col)

        def step(part, _):
            at = pl.ds(pl.multiple_of(part * 48, 16), 48)
            total = mine[at, :].astype(F32)
            for d in range(3):
                total = total + lands[n][4][d, at, :].astype(F32)
            if w > 0:
                grads[w][at, lo:hi] = total
            else:
                for im in range(2):

                    @pl.when(img == im)
                    def _():
                        for i, p in enumerate(pair_lanes(lo // 384, im)):
                            lane = p - 1152 * im
                            grads[0][at, lane : lane + 128] = total[:, 128 * i : 128 * i + 128]

            return 0

        lax.fori_loop(0, WHOLES[w][0] // 16 // 48, step, 0)

    return pair_stage, first, second, third, fourth, sent


def table_taker():
    take = relative_layout(True)
    out = np.zeros((4, 128, 128), np.float32)
    for parity in range(2):
        for which in range(2):
            out[2 * parity + which, :, 64 * which : 64 * which + 27] = take[parity, which].T
    return out


def source_tiles(row, col):
    wide = row >= 2
    side_row = row + 2 * (1 - col // 2)
    table = []
    for image in range(2):
        table.append((image, 0, image, row - 1, col, row > 0))
        table.append((image, 1, image, row, col - 1, col > 0))
        table.append((image, 2, image, row - 1, col - 1, (row > 0) & (col > 0)))
    third_image = jnp.where(wide, 3 - row, 1 - lax.rem(col, 2))
    table.append((2, 0, third_image, 3, col, wide))
    table.append((2, 1, third_image, side_row, 3, jnp.logical_not(wide)))
    table.append((2, 2, third_image, jnp.where(wide, 3, side_row - 1), jnp.where(wide, col - 1, 3), jnp.where(wide, col, side_row) > 0))
    table.append((3, 2, 3 - row, 3, 3, wide & (col == 3)))
    return table


def returns(raws, landing, send, recv, row, col):
    def each(t, act):
        for slot, kind, image, tile_row, tile_col, present in source_tiles(row, col):
            here = (tile_row == row) & (tile_col == col)
            act(slot, kind, image, tile_row, tile_col, present & here, present & jnp.logical_not(here))

    def start(t):
        def act(slot, kind, image, tile_row, tile_col, local, remote):
            @pl.when(local)
            def _():
                pltpu.make_async_copy(
                    window_part(raws[t], slot, kind), landing[t][kind].at[image], recv.at[t, image, kind]
                ).start()

            @pl.when(remote)
            def _():
                hop(t, slot, kind, image, tile_row, tile_col).start()

        each(t, act)

    def hop(t, slot, kind, image, tile_row, tile_col):
        return pltpu.make_async_remote_copy(
            src_ref=window_part(raws[t], slot, kind),
            dst_ref=landing[t][kind].at[image],
            send_sem=send.at[t, slot, kind],
            recv_sem=recv.at[t, image, kind],
            device_id={"row": jnp.maximum(tile_row, 0), "col": jnp.maximum(tile_col, 0)},
            device_id_type=MESH,
        )

    def arrived(t):
        for image in range(2):
            for kind in range(3):
                goal = landing[t][kind].at[image]
                pltpu.make_async_copy(goal, goal, recv.at[t, image, kind]).wait()

    def left(t):
        def act(slot, kind, image, tile_row, tile_col, local, remote):
            @pl.when(remote)
            def _():
                hop(t, slot, kind, image, tile_row, tile_col).wait_send()

        each(t, act)

    return start, arrived, left


def merge_tiles(owns, landing, goals, row, col):
    places = lax.broadcasted_iota(jnp.int32, (16, 1), 0)
    in_left = places < 14 - 2 * col

    def rows16(values):
        return values.reshape(16, FEATURES).astype(F32)

    def right_half(values):
        low = values.reshape(8, FEATURES).astype(F32)
        return jnp.concatenate([low, low], axis=0)

    for image in range(2):

        def merge(tile_row, _):
            top = tile_row < 14 - 2 * row
            upper = jnp.minimum(tile_row, 13)
            lower = jnp.maximum(tile_row - 8, 0)
            for own, (below, right, both), goal in zip(owns, landing, goals):
                stacked = jnp.where(top, rows16(own(image, upper)), rows16(below[image, lower]))
                beside = jnp.where(top, right_half(right[image, upper]), right_half(both[image, lower]))
                goal[image, tile_row] = jnp.where(in_left, stacked, beside).astype(goal.dtype)
            return 0

        lax.fori_loop(0, 16, merge, 0)


def input_grad(at, dqkv, wq, xw, image_grad, gain, norm_sums):
    grad = nt(dqkv[at, :], wq).astype(BF).astype(F32)
    unit, inverse = unit_of(xw[at, :].astype(F32))
    image_grad[at, :] += norm_back(grad, unit, inverse, gain[...])
    norm_sums[0] += fold_rows(grad * unit)
    norm_sums[1] += fold_rows(grad)


def plain_close_kernel(dqkv, xw, dm, raw_r, wq, gain, out, grad_out, norm_sums, image_grad, raw_g, *refs):
    img, row, col = place()
    landing, (send, recv) = (refs[:3], refs[3:6]), refs[6:]
    greet(img, row, col, False)
    start, arrived, left = returns((raw_r, raw_g), landing, send, recv, row, col)
    start(0)
    norm_sums[...] = jnp.zeros_like(norm_sums)
    image_grad[...] = dm[...]

    def step(i, _):
        input_grad(pl.ds(pl.multiple_of(i * BLOCK, 16), BLOCK), dqkv, wq[...], xw, image_grad, gain, norm_sums)
        return 0

    lax.fori_loop(0, ROWS // BLOCK, step, 0)
    spread_rows(image_grad, raw_g, row, col)
    start(1)
    for t in range(2):
        arrived(t)
    owns = [lambda image, upper, raw=raw: raw[image * 22 + 8 + upper, 1:3] for raw in (raw_r, raw_g)]
    merge_tiles(owns, landing, (out, grad_out), row, col)
    for t in range(2):
        left(t)


PIECES = [(2, 8, 2, 8, FEATURES), (2, 14, 1, 8, FEATURES), (2, 8, 1, 8, FEATURES)]


def plain_close(dqkv, xw, dm, raw_r, wq, gain):
    vm = pl.BlockSpec(memory_space=pltpu.VMEM)
    shape = jax.ShapeDtypeStruct
    dma = pltpu.SemaphoreType.DMA
    pieces = [pltpu.VMEM(s, BF) for s in PIECES]
    return pl.pallas_call(
        plain_close_kernel,
        out_shape=[shape((2, 16, 16, FEATURES), BF), shape((2, 16, 16, FEATURES), F32), shape((2, 8, FEATURES), F32)],
        in_specs=[vm] * 6,
        out_specs=[vm] * 3,
        scratch_shapes=[pltpu.VMEM((ROWS, FEATURES), F32), pltpu.VMEM((88, 3, 8, FEATURES), BF)]
        + pieces
        + pieces
        + [dma((2, 4, 3)), dma((2, 2, 3))],
        compiler_params=pltpu.CompilerParams(collective_id=2, has_side_effects=True, vmem_limit_bytes=67043328),
    )(dqkv, xw, dm, raw_r, wq, gain)


def back_kernel(
    do, o, tab, bias, o_turned, da, n2_turned, cw, xw, n1_turned, gain, sums, up_sum, taker, probs, qkv_in, dh_in, g_in, dm_in, wq_in, raw_r, *refs
):
    out, grad_out, gq, go, gu, gd, small_out, table_out = refs[:8]
    qkv, probs_s, image_grad, shared_h, shared_g, own_r = refs[8:14]
    bias_sums, table_sums, norm_sums = refs[14:17]
    landing = (refs[17:20], refs[20:23])
    full = refs[23:27]
    small, table, small_land, table_land, small_z, table_z = refs[27:33]
    count = len(SUM_CHUNKS)
    lands = refs[33 : 33 + 5 * count]
    send, recv, load_sem, probs_sem, wsend, wrecv, ssend, srecv = refs[33 + 5 * count :]
    img, row, col = place()
    y_row = lax.rem(row + 2, 4)
    core_row = row + 1 - 2 * lax.rem(row, 2)
    other = 1 - img
    copies = []

    def load(i):
        pairs = (
            (dh_in, shared_h.at[pl.ds(0, ROWS)]),
            (g_in, shared_g),
            (qkv_in, qkv),
            (dm_in, image_grad),
            (wq_in, shared_h.at[:, pl.ds(0, 3 * FEATURES)]),
            (raw_r.at[pl.ds(8, 14), pl.ds(1, 2)], own_r.at[0]),
            (raw_r.at[pl.ds(30, 14), pl.ds(1, 2)], own_r.at[1]),
        )
        return pltpu.make_async_copy(pairs[i][0], pairs[i][1], load_sem.at[i])

    for i in (2, 1, 0, 3, 5, 6):
        load(i).start()
    windows = window_count(row, col)

    def fetch(k, window, slot):
        pair_index = lax.rem(k, 2) * 3 + k // 2
        return pltpu.make_async_copy(probs.at[window, pl.ds(2 * pair_index, 2)], probs_s.at[slot], probs_sem.at[slot])

    fetch(0, 0, 0).start()
    greet(img, row, col)
    start, arrived, left = returns((raw_r, shared_g), landing, send, recv, row, col)
    start(0)

    def turned_rows(ref):
        return lambda rw, kb: ref[pl.ds(pl.multiple_of(rw * kb, kb), kb), :]

    def turned_g(rw, kb):
        return shared_g[pl.ds(pl.multiple_of(rw * 32, 32), 32)].reshape(FEATURES, FEATURES)[:, 0:ROWS]

    pair_stage, first, second, third, fourth, sent = reducers(
        SUM_CHUNKS,
        full,
        (turned_rows(n1_turned), turned_rows(o_turned), turned_rows(n2_turned), turned_g),
        (qkv, da, shared_h, cw),
        (gq, go, gu, gd),
        lands,
        wsend,
        wrecv,
    )
    bias_sums[...] = jnp.zeros_like(bias_sums)
    table_sums[...] = jnp.zeros_like(table_sums)
    norm_sums[...] = jnp.zeros_like(norm_sums)
    pair_stage(0)
    load(2).wait()
    clear_idle(qkv, row, col)
    load(1).wait()
    load(0).wait()
    steps = [
        (pair_stage, 1),
        (first, 0),
        (pair_stage, 2),
        (first, 1, second, 0),
        (pair_stage, 3),
        (first, 2, third, 0),
        (pair_stage, 5, second, 1),
        (first, 3),
        (pair_stage, 4),
        (third, 1, second, 2),
        (first, 5, fourth, 0),
        (second, 3),
        (pair_stage, 6, third, 2),
        (first, 4),
        (second, 5, fourth, 1),
        (third, 3),
        (first, 6, second, 4),
        (third, 5, fourth, 2),
    ]

    def head_pair(k, _):
        pair_index = lax.rem(k, 2) * 3 + k // 2

        def each(window, _):
            for i, act in enumerate(steps):
                pl.when((k == i // 3) & (window == i % 3))(functools.partial(run_all, act))
            turn_count = k * windows + window
            slot = lax.rem(turn_count, 2)
            fetch(k, window, slot).wait()
            wrap = window + 1 == windows
            next_k = jnp.where(wrap, k + 1, k)

            @pl.when(next_k < 6)
            def _():
                fetch(next_k, jnp.where(wrap, 0, window + 1), 1 - slot).start()

            attention_back(
                window,
                pair_index,
                lambda parity: probs_s[slot, parity],
                do,
                qkv,
                o,
                tab,
                bias,
                bias_sums,
                table_sums,
                row,
                col,
            )
            return 0

        lax.fori_loop(0, windows, each, 0)
        return 0

    lax.fori_loop(0, 6, head_pair, 0)
    load(4).start()
    pair_stage(7)
    load(3).wait()
    load(4).wait()

    def grad_rows(i):
        input_grad(pl.ds(i * BLOCK, BLOCK), qkv, shared_h[:, 0 : 3 * FEATURES], xw, image_grad, gain, norm_sums)

    grad_rows(0)
    first(7)
    grad_rows(1)
    second(6)
    third(4)
    grad_rows(2)
    fourth(3)
    second(7)
    grad_rows(3)
    spread_rows(image_grad, shared_g, row, col)
    start(1)
    third(6)
    def over_rows(values):
        return jnp.sum(values, axis=0, keepdims=True)

    small[0] = jnp.zeros((16, FEATURES), F32)
    lines = [bias_sums[0], bias_sums[1], sums[0], sums[1], norm_sums[0], norm_sums[1], sums[2], sums[3]]
    for i, values in enumerate(lines):
        small[0, i : i + 1, :] = over_rows(values)
    for i in range(4):
        small[0, 8 + i : 9 + i, :] = over_rows(up_sum[:, i * FEATURES : (i + 1) * FEATURES])
    exact = lax.Precision.HIGHEST
    total = jnp.zeros((64, 128), F32)
    for parity in range(2):
        for which in range(2):
            part = table_sums[64 * parity : 64 * parity + 64, 256 * parity + 128 * which : 256 * parity + 128 * which + 128]
            total = total + jnp.dot(part, taker[2 * parity + which], precision=exact, preferred_element_type=F32)
    table[0] = total
    hops = ({"row": core_row}, {"row": y_row}, {"img": other})

    def small_push(k, src, dst, target):
        c = pltpu.make_async_remote_copy(
            src_ref=src, dst_ref=dst, send_sem=ssend.at[k], recv_sem=srecv.at[k], device_id=target, device_id_type=MESH
        )
        c.start()
        copies.append(c)
        return c

    def small_step(i):
        if 0 < i <= 3:
            for k, (acc, land) in enumerate(((small, small_land), (table, table_land))):
                pltpu.make_async_copy(land.at[i - 1], land.at[i - 1], srecv.at[2 * (i - 1) + k]).wait()
                acc[i] = acc[i - 1] + land[i - 1]
        if i < 3:
            for k, (acc, land) in enumerate(((small, small_land), (table, table_land))):
                small_push(2 * i + k, acc.at[i], land.at[i], hops[i])
        if i == 3:
            small_z[col] = small[3]
            table_z[col] = table[3]
            for d in range(1, 4):
                cl = lax.rem(col + d, 4)
                small_push(4 + 2 * d, small.at[3], small_z.at[col], {"col": cl})
                small_push(5 + 2 * d, table.at[3], table_z.at[col], {"col": cl})
        if i == 4:
            for d in range(1, 4):
                cl = lax.rem(col + 4 - d, 4)
                pltpu.make_async_copy(small_z.at[cl], small_z.at[cl], srecv.at[4 + 2 * d]).wait()
                pltpu.make_async_copy(table_z.at[cl], table_z.at[cl], srecv.at[5 + 2 * d]).wait()
            small_out[...] = (small_z[0] + small_z[1]) + (small_z[2] + small_z[3])
            table_out[...] = (table_z[0] + table_z[1]) + (table_z[2] + table_z[3])

    small_step(0)
    third(7)
    fourth(4)
    small_step(1)
    fourth(5)
    small_step(2)
    arrived(0)
    load(5).wait()
    load(6).wait()
    merge_tiles([lambda image, upper: own_r[image, upper]], landing[:1], (out,), row, col)
    small_step(3)
    fourth(6)
    fourth(7)
    small_step(4)
    arrived(1)
    merge_tiles([lambda image, upper: shared_g[image * 22 + 8 + upper, 1:3]], landing[1:], (grad_out,), row, col)
    left(0)
    left(1)
    for c in copies:
        c.wait_send()
    for copy in sent:
        copy().wait_send()


def back(do, o, tab, bias, o_turned, da, n2_turned, cw, xw, n1_turned, gain, sums, up_sum, probs, qkv, dh, g, dm, wq, raw_r):
    vm = pl.BlockSpec(memory_space=pltpu.VMEM)
    an = pl.BlockSpec(memory_space=pl.ANY)
    shape = jax.ShapeDtypeStruct
    dma = pltpu.SemaphoreType.DMA
    pieces = [pltpu.VMEM(s, BF) for s in PIECES]
    count = len(SUM_CHUNKS)
    return pl.pallas_call(
        back_kernel,
        out_shape=[shape((2, 16, 16, FEATURES), BF), shape((2, 16, 16, FEATURES), F32)]
        + [shape((k // 16, n // 2), F32) for k, n in WHOLES]
        + [shape((16, FEATURES), F32), shape((64, 128), F32)],
        in_specs=[vm] * 14 + [an] * 7,
        out_specs=[vm] * 8,
        scratch_shapes=[
            pltpu.VMEM((SPAN, 3 * FEATURES), BF),
            pltpu.VMEM((2, 2, 224, 224), BF),
            pltpu.VMEM((ROWS, FEATURES), F32),
            pltpu.VMEM((FEATURES, 4 * FEATURES), BF),
            pltpu.VMEM((128, 3, 8, FEATURES), BF),
            pltpu.VMEM((2, 14, 2, 8, FEATURES), BF),
            pltpu.VMEM((2, 8, FEATURES), F32),
            pltpu.VMEM((128, 512), F32),
            pltpu.VMEM((2, 8, FEATURES), F32),
        ]
        + pieces
        + pieces
        + [pltpu.VMEM(s, BF) for s in WHOLES]
        + [
            pltpu.VMEM((4, 16, FEATURES), F32),
            pltpu.VMEM((4, 64, 128), F32),
            pltpu.VMEM((3, 16, FEATURES), F32),
            pltpu.VMEM((3, 64, 128), F32),
            pltpu.VMEM((4, 16, FEATURES), F32),
            pltpu.VMEM((4, 64, 128), F32),
        ]
        + land_shapes(SUM_CHUNKS)
        + [dma((2, 4, 3)), dma((2, 2, 3)), dma((7,)), dma((2,)), dma((count, 13)), dma((count, 13)), dma((12,)), dma((12,))],
        compiler_params=pltpu.CompilerParams(collective_id=1, has_side_effects=True, vmem_limit_bytes=67043328),
    )(
        do, o, tab, bias, o_turned, da, n2_turned, cw, xw, n1_turned, gain, sums, up_sum, jnp.asarray(table_taker()),
        probs, qkv, dh, g.reshape(128, 3, 8, FEATURES), dm, wq, raw_r,
    )


def on_device(
    image_in,
    cotangent,
    qkv_weight,
    out_weight,
    up_weight,
    down_weight,
    query_bias,
    value_bias,
    out_bias,
    up_bias,
    down_bias,
    first_gain,
    first_shift,
    second_gain,
    second_shift,
    rows_table,
    cols_table,
):
    line = lambda v: v.reshape(1, -1)
    bias_all = line(jnp.concatenate([query_bias, jnp.zeros_like(query_bias), value_bias]))
    tab = table_operand(rows_table, cols_table, False)
    tab_back = table_operand(rows_table, cols_table, True)
    xw, cw, n1_turned, qkv, probs, o, o_turned, wq, wo, wu, wd = open_windows(
        image_in, cotangent, (qkv_weight, out_weight, up_weight, down_weight), line(first_gain), line(first_shift), bias_all, tab
    )
    raw_r, n2_turned, g_turned, dh, da, do, dm, sums, up_sum = middle(
        o, xw, cw, wo, wu, wd, line(out_bias), line(up_bias), line(down_bias), line(second_gain), line(second_shift)
    )
    if lax.axis_size("img") == 2:
        *large, small, table = back(
            do, o, tab_back, bias_all, o_turned, da, n2_turned, cw, xw, n1_turned, line(first_gain), sums, up_sum,
            probs, qkv, dh, g_turned, dm, wq, raw_r,
        )
        return (
            *large,
            small[0],
            small[1],
            small[2],
            small[8:12].reshape(-1),
            *(small[i] for i in range(3, 8)),
            table[:, :27].T,
            table[:, 64:91].T,
        )
    dqkv, bias_sums, table_sums = plain_back(do, probs, qkv, o, tab_back, bias_all)
    image_out, image_grad, norm_sums = plain_close(dqkv, xw, dm, raw_r, wq, line(first_gain))
    dot = lambda a, b: jnp.dot(a, b, preferred_element_type=F32)
    totals = (dot(n1_turned, dqkv[:ROWS]), dot(o_turned, da), dot(n2_turned, dh), dot(g_turned[:, :ROWS], cw))
    shard_sums = []
    for total in totals:
        part = lax.psum_scatter(total.astype(BF), ("row", "col"), scatter_dimension=0, tiled=True)
        shard_sums.append(lax.psum_scatter(part, "img", scatter_dimension=1, tiled=True).astype(F32))
    rows_grad, cols_grad = table_grads(table_sums)
    small_sums = lax.psum(
        tuple(jnp.sum(bias_sums, axis=1))
        + (jnp.sum(sums[0], axis=0), jnp.sum(up_sum, axis=0), jnp.sum(sums[1], axis=0))
        + tuple(jnp.sum(norm_sums, axis=1))
        + (jnp.sum(sums[2], axis=0), jnp.sum(sums[3], axis=0), rows_grad, cols_grad),
        ("img", "row", "col"),
    )
    return (image_out, image_grad, *shard_sums, *small_sums)


def solution(mesh):
    tiles = P("img", "row", "col", None)
    shards = P(("row", "col"), "img")
    return jax.shard_map(
        on_device,
        mesh=mesh,
        in_specs=(tiles,) * 2 + (shards,) * 4 + (P(),) * 11,
        out_specs=(tiles,) * 2 + (shards,) * 4 + (P(),) * 11,
        check_vma=False,
    )
```

```python
import functools

import jax
import jax.numpy as jnp
import numpy as np
from jax import lax
from jax.experimental import pallas as pl
from jax.experimental.pallas import tpu as pltpu
from jax.sharding import PartitionSpec as P

MESH = pl.DeviceIdType.MESH


def place():
    return lax.axis_index("img"), lax.axis_index("row"), lax.axis_index("col")


def side_owner(window_row, image):
    return lax.rem(window_row, 2), 3 - image - 2 * (window_row // 2)


def piece_target(kind, image, row, col):
    last_row, last_col = row == 3, col == 3
    side_row, side_col = side_owner(row, image)
    next_row, next_col = side_owner(lax.rem(row + 1, 4), image)
    if kind == 0:
        return (jnp.where(last_row, 3 - image, row + 1), col, jnp.where(last_row, 2, image))
    if kind == 1:
        return (jnp.where(last_col, side_row, row), jnp.where(last_col, side_col, col + 1), jnp.where(last_col, 2, image))
    target_row = jnp.where(last_row, 3 - image, jnp.where(last_col, next_row, row + 1))
    target_col = jnp.where(last_col, jnp.where(last_row, 3, next_col), col + 1)
    slot = jnp.where(last_row & last_col, 3, jnp.where(last_row | last_col, 2, image))
    return (target_row, target_col, slot)


def arrivals(row, col):
    wide = row >= 2
    side_row = row + 2 * (1 - col // 2)
    table = []
    for image in range(2):
        table.append((image, 0, row > 0))
        table.append((image, 1, col > 0))
        table.append((image, 2, (row > 0) & (col > 0)))
    table.append((2, 0, wide))
    table.append((2, 1, jnp.logical_not(wide)))
    table.append((2, 2, jnp.where(wide, col, side_row) > 0))
    table.append((3, 2, wide & (col == 3)))
    return table


def tile_part(ref, image, kind):
    if kind == 0:
        return ref.at[image, pl.ds(8, 8), pl.ds(0, 2)]
    if kind == 1:
        return ref.at[image, pl.ds(0, 14), pl.ds(1, 1)]
    return ref.at[image, pl.ds(8, 8), pl.ds(1, 1)]


def window_part(ref, slot, kind):
    if kind == 0:
        return ref.at[pl.ds(slot * 22, 8), pl.ds(1, 2)]
    if kind == 1:
        return ref.at[pl.ds(slot * 22 + 8, 14), pl.ds(0, 1)]
    return ref.at[pl.ds(slot * 22, 8), pl.ds(0, 1)]


def greet(img, row, col, pairs=True):
    barrier = pltpu.get_barrier_semaphore()
    for row_step in range(4):
        for col_step in range(4):
            if row_step or col_step:
                pl.semaphore_signal(
                    barrier,
                    inc=1,
                    device_id={"row": lax.rem(row + row_step, 4), "col": lax.rem(col + col_step, 4)},
                    device_id_type=MESH,
                )
    if pairs:
        pl.semaphore_signal(barrier, inc=1, device_id={"img": 1 - img}, device_id_type=MESH)
    pl.semaphore_wait(barrier, 16 if pairs else 15)


CHUNKS = ((0, 0, 640), (0, 640, 1152), (1, 0, 384), (2, 0, 768), (2, 768, 1536), (3, 0, 128), (3, 128, 384))


def links(shards, fulls, wsend, wrecv, wloc):
    img, row, col = place()
    y_row = lax.rem(row + 2, 4)
    core_row = row + 1 - 2 * lax.rem(row, 2)
    other = 1 - img
    sent = []

    def rows_of(w, rw, half=None):
        kb = fulls[w].shape[0] // 4
        if half is None:
            return pl.ds(pl.multiple_of(rw * kb, kb), kb)
        return pl.ds(pl.multiple_of(rw * kb + half * (kb // 2), kb // 2), kb // 2)

    def cols_of(n, im):
        w, lo, hi = CHUNKS[n]
        nb = fulls[w].shape[1] // 2
        return pl.ds(pl.multiple_of(im * nb + lo, 128), hi - lo)

    def block(n, rw, im, half=None):
        w = CHUNKS[n][0]
        return fulls[w].at[rows_of(w, rw, half), cols_of(n, im)]

    def slot(n, cl):
        w = CHUNKS[n][0]
        k16 = fulls[w].shape[0] // 16
        return fulls[w].at[pl.ds(pl.multiple_of((row * 4 + cl) * k16, k16), k16), cols_of(n, img)]

    def source(n):
        w, lo, hi = CHUNKS[n]
        return shards[w].at[:, pl.ds(lo, hi - lo)]

    def push(n, k, where, target, start=None):
        def copy():
            ref = block(n, *where)
            return pltpu.make_async_remote_copy(
                src_ref=source(n) if start else ref,
                dst_ref=slot(n, col) if start else ref,
                send_sem=wsend.at[n, k],
                recv_sem=wrecv.at[n, k],
                device_id=target(),
                device_id_type=MESH,
            )

        copy().start()
        sent.append(copy)

    def arrive(n, k, ref):
        pltpu.make_async_copy(ref, ref, wrecv.at[n, k]).wait()

    def along_col(n):
        pltpu.make_async_copy(source(n), slot(n, col), wloc.at[n]).start()
        for d in range(1, 4):
            push(n, d - 1, (row, img), lambda d=d: {"col": lax.rem(col + d, 4)}, True)

    def first(n):
        pltpu.make_async_copy(source(n), slot(n, col), wloc.at[n]).wait()
        for d in range(1, 4):
            arrive(n, d - 1, slot(n, lax.rem(col + 4 - d, 4)))
        push(n, 3, (row, img, 0), lambda: {"img": other})
        push(n, 4, (row, img, 1), lambda: {"row": y_row})
        push(n, 5, (row, img), lambda: {"row": core_row})

    def second(n):
        arrive(n, 3, block(n, row, other, 0))
        arrive(n, 4, block(n, y_row, img, 1))
        push(n, 6, (row, img, 0), lambda: {"row": y_row})
        push(n, 7, (row, other, 0), lambda: {"row": y_row})
        push(n, 8, (row, img, 1), lambda: {"img": other})
        push(n, 9, (y_row, img, 1), lambda: {"img": other})
        push(n, 10, (row, other, 0), lambda: {"row": core_row})
        push(n, 11, (y_row, img, 1), lambda: {"row": core_row})

    def third(n):
        arrive(n, 6, block(n, y_row, img, 0))
        arrive(n, 7, block(n, y_row, other, 0))
        arrive(n, 8, block(n, row, other, 1))
        arrive(n, 9, block(n, y_row, other, 1))
        push(n, 12, (y_row, img, 0), lambda: {"row": core_row})
        push(n, 13, (y_row, other, 0), lambda: {"row": core_row})
        push(n, 14, (row, other, 1), lambda: {"row": core_row})
        push(n, 15, (y_row, other, 1), lambda: {"row": core_row})

    def last(n):
        core_y = lax.rem(core_row + 2, 4)
        arrive(n, 5, block(n, core_row, img))
        arrive(n, 10, block(n, core_row, other, 0))
        arrive(n, 11, block(n, core_y, img, 1))
        arrive(n, 12, block(n, core_y, img, 0))
        arrive(n, 13, block(n, core_y, other, 0))
        arrive(n, 14, block(n, core_row, other, 1))
        arrive(n, 15, block(n, core_y, other, 1))

    return along_col, first, second, third, last, sent


def window_moves(tiles, raws, send, recv, loc):
    img, row, col = place()

    def each(t, act):
        for image in range(2):
            for kind in range(3):
                target_row, target_col, target_slot = piece_target(kind, image, row, col)
                here = (target_row == row) & (target_col == col)
                part = tile_part(tiles[t], image, kind)
                goal = window_part(raws[t], target_slot, kind)
                act(here, part, goal, send.at[t, image, kind], recv.at[t, target_slot, kind], target_row, target_col)

    def remote(part, goal, leave, arrival, target_row, target_col):
        return pltpu.make_async_remote_copy(
            src_ref=part,
            dst_ref=goal,
            send_sem=leave,
            recv_sem=arrival,
            device_id={"row": target_row, "col": target_col},
            device_id_type=MESH,
        )

    def own(t, image):
        return pltpu.make_async_copy(tiles[t].at[image, pl.ds(0, 14)], raws[t].at[pl.ds(image * 22 + 8, 14), pl.ds(1, 2)], loc.at[t, image])

    def start(t):
        for image in range(2):
            own(t, image).start()

        def act(here, part, goal, leave, arrival, target_row, target_col):
            @pl.when(here)
            def _():
                pltpu.make_async_copy(part, goal, arrival).start()

            @pl.when(jnp.logical_not(here))
            def _():
                remote(part, goal, leave, arrival, target_row, target_col).start()

        each(t, act)

    def arrived(t):
        for image in range(2):
            own(t, image).wait()
        for slot_index, kind, present in arrivals(row, col):
            part = window_part(raws[t], slot_index, kind)

            @pl.when(present)
            def _():
                pltpu.make_async_copy(part, part, recv.at[t, slot_index, kind]).wait()

    def left(t):
        def act(here, part, goal, leave, arrival, target_row, target_col):
            @pl.when(jnp.logical_not(here))
            def _():
                remote(part, goal, leave, arrival, target_row, target_col).wait_send()

        each(t, act)

    return start, arrived, left


BF = jnp.bfloat16
F32 = jnp.float32
ROWS = 704
SPAN = 800
FEATURES = 768
EPS = 1e-06


def row_params(step, row, col):
    wide = row >= 2
    side_row = row + 2 * (1 - col // 2)
    third_step = step - 28
    in_corner = wide & (third_step >= 8)
    slot = jnp.where(step < 14, 0, jnp.where(step < 28, 1, jnp.where(in_corner, 3, 2)))
    place_row = jnp.where(step < 14, step, jnp.where(step < 28, step - 14, jnp.where(in_corner, third_step - 8, third_step)))
    full = step < 28
    row_start = jnp.where(full, 8 - 2 * row, jnp.where(wide, 0, 8 - 2 * side_row))
    col_start = jnp.where(full, 8 - 2 * col, jnp.where(wide & jnp.logical_not(in_corner), 8 - 2 * col, 0))
    width = jnp.where(full, 14, jnp.where(wide & jnp.logical_not(in_corner), 14, 8))
    alive = jnp.where(full, True, jnp.where(in_corner, col == 3, jnp.where(wide, True, third_step < 14)))
    return slot, jnp.minimum(place_row + row_start, 21), col_start, jnp.where(alive, width, 0)


def window_params(window, row, col):
    wide = row >= 2
    start = jnp.where(window < 2, 14 * window, jnp.where(window == 2, 28, 36))
    tall = jnp.where(window < 2, 14, jnp.where((window == 2) & jnp.logical_not(wide), 14, 8))
    width = jnp.where(window < 2, 14, jnp.where((window == 2) & wide, 14, 8))
    return start, tall, width


def window_count(row, col):
    return jnp.where((row >= 2) & (col == 3), 4, 3)


def unit_of(values):
    center = values - jnp.mean(values, axis=-1, keepdims=True)
    inverse = lax.rsqrt(jnp.mean(center * center, axis=-1, keepdims=True) + EPS)
    return center * inverse, inverse


def relative_layout(backward):
    take = np.zeros((2, 2, 27, 128), np.float32)
    for parity in range(2):
        base = 64 if parity == 0 else 0
        for j in range(27):
            for copy in (0,) if backward else (0, 32):
                take[parity, 0, 26 - j, (base - 13 + j + copy) % 128] = 1
                if backward:
                    take[parity, 1, j, base + 16 + j] = 1
                else:
                    take[parity, 1, 26 - j, (base + 3 + j + copy) % 128] = 1
    return take


def takers(backward):
    return jnp.asarray(relative_layout(backward).reshape(4, 27, 128), BF)


def build_table(tab, rows_table, cols_table, take):
    tab[...] = jnp.zeros_like(tab)
    for parity in range(2):
        for which, table in ((0, rows_table), (1, cols_table)):
            block = lax.dot_general(table[...], take[2 * parity + which], (((0,), (0,)), ((), ())), preferred_element_type=F32)
            lane = 256 * parity + 128 * which
            tab[64 * parity : 64 * parity + 64, lane : lane + 128] = block.astype(BF)


def as_row(ref):
    return ref[...].reshape(1, -1)


def run_all(acts):
    for act in acts:
        act[0](*act[1:])


def plan_slots(plan, acts):
    slots = [[]]
    for name in plan:
        if name == "|":
            slots.append([])
        elif name in acts:
            slots[-1].append((acts[name],))
        else:
            slots[-1].append((acts[name[0]], int(name[1:])))
    return slots


def table_grads(sums):
    take = jnp.asarray(relative_layout(True), F32)
    grads = []
    for which in range(2):
        total = 0.0
        for parity in range(2):
            part = sums[64 * parity : 64 * parity + 64, 256 * parity + 128 * which : 256 * parity + 128 * which + 128]
            total = total + lax.dot_general(take[parity, which], part, (((1,), (1,)), ((), ())), precision=lax.Precision.HIGHEST)
        grads.append(total)
    return grads


OPEN_PLAN = ("a0", "a1", "11", "a5", "a3", "10", "21", "20", "a6", "15", "13", "31", "25", "Wx", "30", "L0", "16", "23", "35", "a4", "X", "26", "L1", "P", "|", "|", "a2", "|", "|", "14", "|", "|", "|", "12", "|", "Wc", "L5", "|", "36", "|", "|", "|", "24", "|", "|", "L6", "|", "|", "33", "|", "|", "22", "T", "34", "32", "K", "L2", "L3", "L4")


def open_kernel(weights, x_ref, c_ref, gain, shift, query_bias, value_bias, rows_table, cols_table, take, *refs):
    img, row, col = place()
    greet(img, row, col, weights)
    if weights:
        shards, refs = refs[:4], refs[4:]
    else:
        wq, refs = refs[0], refs[1:]
    xw, cw, n1_turned, qkv_out, probs_out, o, o_turned = refs[:7]
    refs = refs[7:]
    if weights:
        fulls, refs = refs[:4], refs[4:]
    rawx, rawc, n1, tab, row_bias, qkv_s, probs, out_sem, probs_sem, send, recv, loc = refs[:12]
    refs = refs[12:]
    if weights:
        wq, wq_out = refs[0], fulls[0]
        along_col, first, second, third, last, sent = links(shards, (wq, *fulls[1:]), *refs[1:])
    window_start, window_arrived, window_left = window_moves((x_ref, c_ref), (rawx, rawc), send, recv, loc)
    places = lax.broadcasted_iota(jnp.int32, (16, 1), 0)

    def cut_one(raw, step):
        slot, raw_row, col_start, width = row_params(step, row, col)
        wide_rows = raw[slot * 22 + raw_row].reshape(24, FEATURES).astype(F32)
        keep = places < width
        return keep, jnp.where(keep, pltpu.roll(wide_rows, lax.rem(24 - col_start, 24), 0)[:16], 0.0)

    def cut_x(step, _):
        at = pl.ds(pl.multiple_of(step * 16, 16), 16)
        keep, x = cut_one(rawx, step)
        xw[at, :] = x.astype(BF)
        unit, _inverse = unit_of(x)
        n1[at, :] = jnp.where(keep, unit * as_row(gain) + as_row(shift), 0.0).astype(BF)
        return 0

    def cut_c(step, _):
        at = pl.ds(pl.multiple_of(step * 16, 16), 16)
        _keep, c = cut_one(rawc, step)
        cw[at, :] = c.astype(BF)
        return 0

    def project(step, _):
        at = pl.ds(pl.multiple_of(step * 352, 32), 352)
        for part_index in range(3):
            lanes = slice(part_index * FEATURES, (part_index + 1) * FEATURES)
            part = jnp.dot(n1[at, :], wq[:, lanes], preferred_element_type=F32)
            if part_index != 1:
                part = part + row_bias[part_index // 2]
            qkv_s[at, lanes] = part.astype(BF)
        return 0

    def turn(source, goal):
        def step(i, _):
            lanes = pl.ds(pl.multiple_of(i * 128, 128), 128)
            goal[lanes, :] = source[0:ROWS, lanes].T
            return 0

        lax.fori_loop(0, FEATURES // 128, step, 0)

    def cut_windows():
        window_arrived(0)
        lax.fori_loop(0, 44, cut_x, 0)

    def cut_cotangent():
        window_arrived(1)
        lax.fori_loop(0, 44, cut_c, 0)

    def project_all():
        lax.fori_loop(0, 2, project, 0)
        pltpu.make_async_copy(qkv_s, qkv_out, out_sem.at[0]).start()
        if weights:
            pltpu.make_async_copy(wq, wq_out, out_sem.at[1]).start()

    def turn_all():
        turn(n1, n1_turned)
        turn(o, o_turned)

    acts = {"X": cut_windows, "P": project_all, "T": turn_all, "K": cut_cotangent}
    acts["Wx"] = functools.partial(window_start, 0)
    acts["Wc"] = functools.partial(window_start, 1)
    if weights:
        acts.update({"a": along_col, "1": first, "2": second, "3": third, "L": last})
        slots = plan_slots(OPEN_PLAN, acts)
    else:
        slots = plan_slots(("Wx", "Wc", "X", "P", *("|",) * 18, "T", "K"), acts)
    o[...] = jnp.zeros_like(o)
    build_table(tab, rows_table, cols_table, take)
    row_bias[0] = as_row(query_bias)
    row_bias[1] = as_row(value_bias)
    run_all(slots[0])
    row_of = lax.broadcasted_iota(jnp.int32, (224, 1), 0)
    lane = lax.broadcasted_iota(jnp.int32, (1, 128), 1)
    key_place = lax.broadcasted_iota(jnp.int32, (224, 128), 0)
    key_lane = lax.broadcasted_iota(jnp.int32, (224, 128), 1)
    key_a, key_b = key_place // 16, key_place % 16

    def probs_copy(index):
        window, pair_index = index // 6, index % 6
        part = pl.ds(2 * pair_index, 2)
        return pltpu.make_async_copy(probs.at[window, part], probs_out.at[window, part], probs_sem.at[window, pair_index])

    def pair(index, _):
        for i, slot_acts in enumerate(slots[1:-1]):
            if slot_acts:
                pl.when(index == i + 1)(functools.partial(run_all, slot_acts))
        window, pair_index = index // 6, index % 6
        start, tall, width = window_params(window, row, col)
        at = pl.ds(pl.multiple_of(start * 16, 16), 224)
        alive = (row_of // 16 < tall) & (row_of % 16 < width)
        lanes = lambda third: pl.ds(pl.multiple_of(third * FEATURES + pair_index * 128, 128), 128)
        q = jnp.where(alive, qkv_s[at, lanes(0)].astype(F32), 0.0)
        k = jnp.where(alive, qkv_s[at, lanes(1)].astype(F32), 0.0)
        v = jnp.where(alive, qkv_s[at, lanes(2)].astype(F32), row_bias[1, :, lanes(0)].astype(BF).astype(F32)).astype(BF)
        terms = jnp.dot(q.astype(BF), tab[...], preferred_element_type=F32)
        outs = []
        for parity in range(2):
            base = 64 if parity == 0 else 0
            own = (lane < 64) if parity == 0 else (lane >= 64)
            rel_rows = jnp.concatenate(
                [pltpu.roll(terms[16 * a : 16 * a + 16, 256 * parity : 256 * parity + 128], a, 1) for a in range(14)], axis=0
            )
            rel_cols = jnp.concatenate(
                [
                    pltpu.roll(terms[16 * a : 16 * a + 16, 256 * parity + 128 : 256 * parity + 256], 0, 1, stride=1, stride_axis=0)
                    for a in range(14)
                ],
                axis=0,
            )
            on = lane - base
            in_rows = ((on >= 0) & (on < 14)) | ((on >= 32) & (on < 46))
            in_cols = ((on >= 16) & (on < 30)) | ((on >= 48) & (on < 62))
            rel = jnp.where(in_rows, rel_rows, jnp.where(in_cols, rel_cols, 0.0))
            rough = rel.astype(BF).astype(F32)
            fine = jnp.where(on >= 32, rel - rough, rough)
            fine = jnp.where(on == 14, -1e30, fine)
            q_side = jnp.where(own, q * 0.125, fine).astype(BF)
            key_on = key_lane - base
            hot = jnp.where(
                key_on == 14,
                jnp.where(key_b >= 14, 1.0, 0.0),
                jnp.where(
                    (key_on % 32 < 14) & (key_a == key_on % 32),
                    1.0,
                    jnp.where((key_on % 32 >= 16) & (key_on % 32 < 30) & (key_b == key_on % 32 - 16), 1.0, 0.0),
                ),
            )
            k_side = jnp.where(own, k, hot).astype(BF)
            scores = lax.dot_general(q_side, k_side, (((1,), (1,)), ((), ())), preferred_element_type=F32)
            exponent = jnp.exp(scores - jnp.max(scores, axis=-1, keepdims=True))
            p = (exponent * (1.0 / jnp.sum(exponent, axis=-1, keepdims=True))).astype(BF)
            probs[window, 2 * pair_index + parity] = p
            outs.append(jnp.dot(p, v, preferred_element_type=F32))
        blended = jnp.where(lane < 64, outs[0], outs[1])
        out_lanes = pl.ds(pl.multiple_of(pair_index * 128, 128), 128)
        o_at = pl.ds(pl.multiple_of(start * 16, 16), 224)
        o[o_at, out_lanes] = jnp.where(alive, blended, 0.0).astype(BF)
        probs_copy(index).start()
        return 0

    pairs = window_count(row, col) * 6
    lax.fori_loop(0, pairs, pair, 0)
    run_all(slots[-1])
    pltpu.make_async_copy(qkv_s, qkv_out, out_sem.at[0]).wait()
    if weights:
        pltpu.make_async_copy(wq, wq_out, out_sem.at[1]).wait()
        for copy in sent:
            copy().wait_send()
    lax.fori_loop(0, pairs, lambda index, _: (probs_copy(index).wait(), 0)[1], 0)
    window_left(0)
    window_left(1)


def open_windows(x, c, shards, gain, shift, query_bias, value_bias, rows_table, cols_table):
    vm = pl.BlockSpec(memory_space=pltpu.VMEM)
    an = pl.BlockSpec(memory_space=pl.ANY)
    shape = jax.ShapeDtypeStruct
    dma = pltpu.SemaphoreType.DMA
    chunks = len(CHUNKS)
    weights = lax.axis_size("img") == 2
    if weights:
        given, wholes = list(shards), [(768, 2304), (768, 768), (768, 3072), (3072, 768)]
    else:
        widened = [lax.all_gather(w, "img", axis=1, tiled=True) for w in shards]
        gathered = [lax.all_gather(w, ("row", "col"), axis=0, tiled=True) for w in widened]
        given, wholes = gathered[:1], []
    raw = pltpu.VMEM((88, 3, 8, FEATURES), BF)
    outs = pl.pallas_call(
        functools.partial(open_kernel, weights),
        out_shape=[
            shape((ROWS, FEATURES), BF),
            shape((ROWS, FEATURES), BF),
            shape((FEATURES, ROWS), BF),
            shape((SPAN, 3 * FEATURES), BF),
            shape((4, 12, 224, 224), BF),
            shape((SPAN, FEATURES), BF),
            shape((FEATURES, ROWS), BF),
        ]
        + [shape(s, BF) for s in wholes],
        in_specs=[vm] * (9 + len(given)),
        out_specs=[vm, vm, vm, an, an, vm, vm] + [an] * len(wholes),
        scratch_shapes=[
            raw,
            raw,
            pltpu.VMEM((ROWS, FEATURES), BF),
            pltpu.VMEM((128, 512), BF),
            pltpu.VMEM((2, 1, FEATURES), F32),
            pltpu.VMEM((SPAN, 3 * FEATURES), BF),
            pltpu.VMEM((4, 12, 224, 224), BF),
            dma((2,)),
            dma((4, 6)),
            dma((2, 2, 3)),
            dma((2, 4, 3)),
            dma((2, 2)),
        ]
        + ([pltpu.VMEM((768, 2304), BF), dma((chunks, 16)), dma((chunks, 16)), dma((chunks,))] if weights else []),
        compiler_params=pltpu.CompilerParams(collective_id=0, has_side_effects=True, vmem_limit_bytes=67043328),
    )(x.reshape(2, 16, 2, 8, 768), c.reshape(2, 16, 2, 8, 768), gain, shift, query_bias, value_bias, rows_table, cols_table, takers(False), *given)
    return list(outs) if weights else list(outs) + gathered


FF = 3072
CHUNK = 512
BLOCK = 176


def nt(a, b):
    return lax.dot_general(a, b, (((1,), (1,)), ((), ())), preferred_element_type=F32)


def norm_back(grad, unit, inverse, gain):
    scaled = grad * gain
    first_mean = jnp.mean(scaled, axis=-1, keepdims=True)
    second_mean = jnp.mean(scaled * unit, axis=-1, keepdims=True)
    return inverse * (scaled - first_mean - unit * second_mean)


def fold_rows(values):
    total = values[0:8]
    for i in range(1, values.shape[0] // 8):
        total = total + values[8 * i : 8 * i + 8]
    return total


def spread_rows(source, raw, row, col):
    def step(i, _):
        slot, raw_row, col_start, width = row_params(i, row, col)
        at = pl.ds(pl.multiple_of(i * 16, 16), 16)

        @pl.when(width > 0)
        def _():
            values = jnp.concatenate([source[at, :], jnp.zeros((8, FEATURES), F32)], axis=0)
            raw[slot * 22 + raw_row] = pltpu.roll(values, col_start, 0).astype(BF).reshape(3, 8, FEATURES)

        return 0

    lax.fori_loop(0, 44, step, 0)


def middle_kernel(
    o, xw, cw, wo, wu, wd, out_bias, up_bias, down_bias, gain, shift, raw_r, n2_turned, g_turned, dh, da, do, dm, sums, up_sum, n2, y_s, d_s, g_s
):
    step = pl.program_id(0)
    row, col = lax.axis_index("row"), lax.axis_index("col")
    blocks = [slice(i * BLOCK, (i + 1) * BLOCK) for i in range(ROWS // BLOCK)]

    def mid_of(at):
        return xw[at, :].astype(F32) + (jnp.dot(o[at, :], wo[...], preferred_element_type=F32) + as_row(out_bias))

    @pl.when(step == 0)
    def _():
        sums[...] = jnp.zeros_like(sums)
        d_s[...] = jnp.zeros_like(d_s)

        def begin(i, _):
            at = pl.ds(pl.multiple_of(i * BLOCK, 16), BLOCK)
            mid = mid_of(at)
            unit, _inverse = unit_of(mid)
            n2[at, :] = (unit * as_row(gain) + as_row(shift)).astype(BF)
            y_s[at, :] = mid + as_row(down_bias)
            dm[at, :] = mid
            return 0

        lax.fori_loop(0, ROWS // BLOCK, begin, 0)

        def turn(i, _):
            lanes = pl.ds(pl.multiple_of(i * 128, 128), 128)
            n2_turned[lanes, :] = n2[:, lanes].T
            return 0

        lax.fori_loop(0, FEATURES // 128, turn, 0)

    up_sum[...] = jnp.zeros_like(up_sum)
    for at in blocks:
        h = jnp.dot(n2[at, :], wu[...], preferred_element_type=F32) + up_bias[...]
        up = nt(cw[at, :], wd[...])
        phi = 0.5 * (1.0 + lax.erf(h * 0.7071067811865476))
        slope = phi + h * (jnp.exp(-0.5 * h * h) * 0.3989422804014327)
        active = (h * phi).astype(BF)
        back = (up * slope).astype(BF)
        g_s[at, :] = active
        dh[at, :] = back
        up_sum[...] += fold_rows(back.astype(F32))
        y_s[at, :] += jnp.dot(active, wd[...], preferred_element_type=F32)
        d_s[at, :] += nt(back, wu[...])
    for i in range(CHUNK // 128):
        g_turned[128 * i : 128 * i + 128, 0:ROWS] = g_s[:, 128 * i : 128 * i + 128].T

    @pl.when(step == FF // CHUNK - 1)
    def _():
        def end(i, _):
            at = pl.ds(pl.multiple_of(i * BLOCK, 16), BLOCK)
            unit, inverse = unit_of(dm[at, :])
            grad = d_s[at, :].astype(BF).astype(F32)
            up = cw[at, :].astype(F32)
            grad_mid = up + norm_back(grad, unit, inverse, as_row(gain))
            low_grad = grad_mid.astype(BF)
            dm[at, :] = grad_mid
            da[at, :] = low_grad
            do[at, :] = nt(low_grad, wo[...]).astype(BF)
            sums[0] += fold_rows(low_grad.astype(F32))
            sums[1] += fold_rows(up)
            sums[2] += fold_rows(grad * unit)
            sums[3] += fold_rows(grad)
            return 0

        lax.fori_loop(0, ROWS // BLOCK, end, 0)
        spread_rows(y_s, raw_r, row, col)


def middle(o, xw, cw, wo, wu, wd, out_bias, up_bias, down_bias, gain, shift):
    shape = jax.ShapeDtypeStruct
    once = lambda *s: pl.BlockSpec(s, lambda i: (0,) * len(s), pipeline_mode=pl.Buffered(1))
    return pl.pallas_call(
        middle_kernel,
        grid=(FF // CHUNK,),
        out_shape=[
            shape((88, 3, 8, FEATURES), BF),
            shape((FEATURES, ROWS), BF),
            shape((FF, FEATURES), BF),
            shape((ROWS, FF), BF),
            shape((ROWS, FEATURES), BF),
            shape((SPAN, FEATURES), BF),
            shape((ROWS, FEATURES), F32),
            shape((4, 8, FEATURES), F32),
            shape((8, FF), F32),
        ],
        in_specs=[
            once(SPAN, FEATURES),
            once(ROWS, FEATURES),
            once(ROWS, FEATURES),
            once(FEATURES, FEATURES),
            pl.BlockSpec((FEATURES, CHUNK), lambda i: (0, i)),
            pl.BlockSpec((CHUNK, FEATURES), lambda i: (i, 0)),
            once(FEATURES),
            pl.BlockSpec((1, CHUNK), lambda i: (0, i)),
            once(FEATURES),
            once(FEATURES),
            once(FEATURES),
        ],
        out_specs=[
            once(88, 3, 8, FEATURES),
            once(FEATURES, ROWS),
            pl.BlockSpec((CHUNK, FEATURES), lambda i: (i, 0)),
            pl.BlockSpec((ROWS, CHUNK), lambda i: (0, i)),
            once(ROWS, FEATURES),
            once(SPAN, FEATURES),
            once(ROWS, FEATURES),
            once(4, 8, FEATURES),
            pl.BlockSpec((8, CHUNK), lambda i: (0, i)),
        ],
        scratch_shapes=[
            pltpu.VMEM((ROWS, FEATURES), BF),
            pltpu.VMEM((ROWS, FEATURES), F32),
            pltpu.VMEM((ROWS, FEATURES), F32),
            pltpu.VMEM((ROWS, CHUNK), BF),
        ],
        compiler_params=pltpu.CompilerParams(vmem_limit_bytes=62 << 20),
    )(o, xw, cw, wo, wu, wd, out_bias, up_bias, down_bias, gain, shift)


def attention_back(window, pair_index, probs_of, do, qkv, o, tab, value_bias, bias_sums, table_sums, row, col):
    row_of = lax.broadcasted_iota(jnp.int32, (224, 1), 0)
    lane = lax.broadcasted_iota(jnp.int32, (1, 128), 1)
    key_place = lax.broadcasted_iota(jnp.int32, (224, 128), 0)
    key_lane = lax.broadcasted_iota(jnp.int32, (224, 128), 1)
    key_a, key_b = key_place // 16, key_place % 16
    start, tall, width = window_params(window, row, col)
    at = pl.ds(pl.multiple_of(start * 16, 16), 224)
    inside = row_of // 16 < tall
    alive = inside & (row_of % 16 < width)
    lanes = lambda third: pl.ds(pl.multiple_of(third * FEATURES + pair_index * 128, 128), 128)
    old = [qkv[at, lanes(third)].astype(F32) for third in range(3)]
    q = jnp.where(alive, old[0], 0.0)
    k = jnp.where(alive, old[1], 0.0)
    v = jnp.where(alive, old[2], value_bias[:, lanes(0)].astype(BF).astype(F32))
    grad = jnp.where(alive, do[at, lanes(0)].astype(F32), 0.0)
    product = grad * jnp.where(alive, o[at, lanes(0)].astype(F32), 0.0)
    q_turned = q.T.astype(BF)
    grad_turned = grad.T.astype(BF)
    value_parts, key_parts, query_parts, table_parts = [], [], [], []
    for parity in range(2):
        base = 64 if parity == 0 else 0
        own = (lane < 64) if parity == 0 else (lane >= 64)
        half = slice(64 * parity, 64 * parity + 64)
        inner = jnp.sum(jnp.where(own, product, 0.0), axis=-1, keepdims=True)
        rough = inner.astype(BF).astype(F32)
        on = lane - base
        grad_side = jnp.where(own, grad, jnp.where(on == 0, rough, jnp.where(on == 1, inner - rough, 0.0))).astype(BF)
        v_side = jnp.where(own, v, jnp.where((on == 0) | (on == 1), -1.0, 0.0)).astype(BF)
        centered = nt(grad_side, v_side)
        p = probs_of(parity)
        ds = (p.astype(F32) * centered).astype(BF)
        value_parts.append(jnp.dot(grad_turned[half], p, preferred_element_type=F32))
        key_parts.append(jnp.dot(q_turned[half], ds, preferred_element_type=F32))
        key_on = key_lane - base
        hot = jnp.where(
            (key_on >= 0) & (key_on < 14) & (key_a == key_on),
            1.0,
            jnp.where((key_on >= 16) & (key_on < 30) & (key_b == 29 - key_on), 1.0, 0.0),
        )
        k_side = jnp.where(own, k * 0.125, hot).astype(BF)
        wide = jnp.dot(ds, k_side, preferred_element_type=F32)
        query_parts.append(wide)
        by_rows = jnp.where((on >= 0) & (on < 14), wide, 0.0)
        by_cols = jnp.where((on >= 16) & (on < 30), wide, 0.0)
        table_parts.append(jnp.concatenate([pltpu.roll(by_rows[16 * a : 16 * a + 16], (128 - a) % 128, 1) for a in range(14)], axis=0))
        table_parts.append(
            jnp.concatenate([pltpu.roll(by_cols[16 * a : 16 * a + 16], 0, 1, stride=1, stride_axis=0) for a in range(14)], axis=0)
        )
    turned = jnp.concatenate(table_parts, axis=1).astype(BF)
    dq = jnp.where(lane < 64, query_parts[0], query_parts[1]) + nt(turned, tab[...])
    table_sums[...] += jnp.dot(q_turned, turned, preferred_element_type=F32)
    dk = jnp.concatenate(key_parts, axis=0).T * 0.125
    dv = jnp.concatenate(value_parts, axis=0).T.astype(BF).astype(F32)
    dq = jnp.where(alive, dq, 0.0).astype(BF).astype(F32)
    bias_sums[0, :, lanes(0)] += fold_rows(dq)
    bias_sums[1, :, lanes(0)] += fold_rows(dv)
    for third, new in enumerate((dq, dk, dv)):
        qkv[at, lanes(third)] = jnp.where(alive, new, jnp.where(inside, 0.0, old[third])).astype(BF)


def clear_idle(qkv, row, col):
    wide = row >= 2
    limit = jnp.where(wide, jnp.where(col == 3, 44, 36), 42)
    for a in range(36, 44):

        @pl.when(a >= limit)
        def _():
            qkv[16 * a : 16 * a + 16, :] = jnp.zeros((16, 3 * FEATURES), BF)


def plain_back_kernel(do, probs, qkv, o, value_bias, rows_table, cols_table, take, dqkv, bias_sums, table_sums, tab, row_bias):
    row, col = lax.axis_index("row"), lax.axis_index("col")
    build_table(tab, rows_table, cols_table, take)
    row_bias[...] = as_row(value_bias)
    dqkv[...] = qkv[...]
    clear_idle(dqkv, row, col)
    bias_sums[...] = jnp.zeros_like(bias_sums)
    table_sums[...] = jnp.zeros_like(table_sums)

    def pair(index, _):
        window, pair_index = index // 6, index % 6
        attention_back(
            window,
            pair_index,
            lambda parity: probs[window, 2 * pair_index + parity],
            do,
            dqkv,
            o,
            tab,
            row_bias,
            bias_sums,
            table_sums,
            row,
            col,
        )
        return 0

    lax.fori_loop(0, window_count(row, col) * 6, pair, 0)


def plain_back(do, probs, qkv, o, value_bias, rows_table, cols_table):
    vm = pl.BlockSpec(memory_space=pltpu.VMEM)
    shape = jax.ShapeDtypeStruct
    return pl.pallas_call(
        plain_back_kernel,
        out_shape=[shape((SPAN, 3 * FEATURES), BF), shape((2, 8, FEATURES), F32), shape((128, 512), F32)],
        in_specs=[vm] * 8,
        out_specs=[vm] * 3,
        scratch_shapes=[pltpu.VMEM((128, 512), BF), pltpu.VMEM((1, FEATURES), F32)],
        compiler_params=pltpu.CompilerParams(vmem_limit_bytes=62 << 20),
    )(do, probs, qkv, o, value_bias, rows_table, cols_table, takers(True))


WHOLES = ((768, 2304), (768, 768), (768, 3072), (3072, 768))
SUM_CHUNKS = ((1, 0, 384), (3, 0, 128), (3, 128, 384), (2, 0, 768), (2, 768, 1536), (0, 0, 384), (0, 384, 768), (0, 768, 1152))


def pair_lanes(j, im):
    if im == 0:
        return (128 * j, FEATURES + 128 * j, 128 * (j + 3))
    return (2 * FEATURES + 128 * j, FEATURES + 128 * (j + 3), 2 * FEATURES + 128 * (j + 3))


def land_shapes(chunks):
    lands = []
    for w, lo, hi in chunks:
        kb, width = WHOLES[w][0] // 4, hi - lo
        lands += [
            pltpu.VMEM((2, 2, kb, width), BF),
            pltpu.VMEM((2, kb // 2, width), BF),
            pltpu.VMEM((2, kb // 2, width), BF),
            pltpu.VMEM((2, kb // 2, width), BF),
            pltpu.VMEM((3, kb // 4, width), BF),
        ]
    return lands


def reducers(chunks, full, left_turned, right_side, grads, land_refs, wsend, wrecv):
    img, row, col = place()
    y_row = lax.rem(row + 2, 4)
    core_row = row + 1 - 2 * lax.rem(row, 2)
    core_y = lax.rem(core_row + 2, 4)
    other = 1 - img
    lands = [land_refs[5 * n : 5 * n + 5] for n in range(len(chunks))]
    sent = []

    def size(n):
        w, lo, hi = chunks[n]
        return WHOLES[w][0] // 4, WHOLES[w][1] // 2, lo, hi - lo

    def block(n, rw, im, half=None):
        kb, nb, lo, width = size(n)
        cols = pl.ds(pl.multiple_of(im * nb + lo, 128), width)
        if half is None:
            return full[chunks[n][0]].at[pl.ds(pl.multiple_of(rw * kb, kb), kb), cols]
        return full[chunks[n][0]].at[pl.ds(pl.multiple_of(rw * kb + half * (kb // 2), kb // 2), kb // 2), cols]

    def shard(n, cl):
        kb, nb, lo, width = size(n)
        cols = pl.ds(pl.multiple_of(img * nb + lo, 128), width)
        return full[chunks[n][0]].at[pl.ds(pl.multiple_of(row * kb + cl * (kb // 4), kb // 4), kb // 4), cols]

    def push(n, k, src, dst, target):
        def copy():
            return pltpu.make_async_remote_copy(
                src_ref=src(), dst_ref=dst(), send_sem=wsend.at[n, k], recv_sem=wrecv.at[n, k], device_id=target(), device_id_type=MESH
            )

        copy().start()
        sent.append(copy)

    def arrive(n, k, ref):
        pltpu.make_async_copy(ref, ref, wrecv.at[n, k]).wait()

    def add(goal, part, rows):
        def step(i, _):
            at = pl.ds(pl.multiple_of(i * 48, 16), 48)
            goal[at, :] = (goal[at, :].astype(F32) + part[at, :].astype(F32)).astype(BF)
            return 0

        lax.fori_loop(0, rows // 48, step, 0)

    def product(n, rw):
        w = chunks[n][0]
        kb, nb, lo, width = size(n)
        rows = pl.ds(pl.multiple_of(rw * kb, kb), kb)
        for im in range(2):
            at = slice(im * nb + lo, im * nb + lo + width)
            if w == 0:
                right = jnp.concatenate([right_side[0][0:ROWS, p : p + 128] for p in pair_lanes(lo // 384, im)], axis=1)
            else:
                right = right_side[w][0:ROWS, at]
            full[w][rows, at] = jnp.dot(left_turned[w](rw, kb), right, preferred_element_type=F32).astype(BF)

    def pair_stage(n):
        land = lands[n][0]
        for j, rw in enumerate((core_row, core_y)):
            product(n, rw)
            for im in range(2):
                push(n, 2 * j + im, functools.partial(block, n, rw, im), lambda j=j, im=im: land.at[j, im], lambda: {"row": core_row})
        for rw in (row, y_row):
            product(n, rw)

    def first(n):
        kb, nb, lo, width = size(n)
        for j, rw in enumerate((row, y_row)):
            for im in range(2):
                arrive(n, 2 * j + im, lands[n][0].at[j, im])
                add(block(n, rw, im), lands[n][0].at[j, im], kb)
        for im in range(2):
            push(n, 4 + im, functools.partial(block, n, y_row, im, 0), lambda im=im: lands[n][1].at[im], lambda: {"row": y_row})
        push(n, 6, functools.partial(block, n, row, other, 1), lambda: lands[n][2].at[0], lambda: {"img": other})
        push(n, 7, functools.partial(block, n, y_row, other, 1), lambda: lands[n][2].at[1], lambda: {"img": other})

    def second(n):
        kb, nb, lo, width = size(n)
        for im in range(2):
            arrive(n, 4 + im, lands[n][1].at[im])
            add(block(n, row, im, 0), lands[n][1].at[im], kb // 2)
        push(n, 8, functools.partial(block, n, row, other, 0), lambda: lands[n][3].at[0], lambda: {"img": other})
        for j, rw in enumerate((row, y_row)):
            arrive(n, 6 + j, lands[n][2].at[j])
            add(block(n, rw, img, 1), lands[n][2].at[j], kb // 2)
        push(n, 9, functools.partial(block, n, y_row, img, 1), lambda: lands[n][3].at[1], lambda: {"row": y_row})

    def third(n):
        kb, nb, lo, width = size(n)
        for half in range(2):
            arrive(n, 8 + half, lands[n][3].at[half])
            add(block(n, row, img, half), lands[n][3].at[half], kb // 2)
        for d in range(1, 4):

            def src(d=d):
                return shard(n, lax.rem(col + d, 4))

            push(n, 9 + d, src, lambda d=d: lands[n][4].at[d - 1], lambda d=d: {"col": lax.rem(col + d, 4)})

    def fourth(n):
        w, lo, hi = chunks[n]
        for d in range(1, 4):
            arrive(n, 9 + d, lands[n][4].at[d - 1])
        mine = shard(n, col)

        def step(part, _):
            at = pl.ds(pl.multiple_of(part * 48, 16), 48)
            total = mine[at, :].astype(F32)
            for d in range(3):
                total = total + lands[n][4][d, at, :].astype(F32)
            if w > 0:
                grads[w][at, lo:hi] = total
            else:
                for im in range(2):

                    @pl.when(img == im)
                    def _():
                        for i, p in enumerate(pair_lanes(lo // 384, im)):
                            lane = p - 1152 * im
                            grads[0][at, lane : lane + 128] = total[:, 128 * i : 128 * i + 128]

            return 0

        lax.fori_loop(0, WHOLES[w][0] // 16 // 48, step, 0)

    return pair_stage, first, second, third, fourth, sent


def table_taker():
    take = relative_layout(True)
    out = np.zeros((4, 128, 128), np.float32)
    for parity in range(2):
        for which in range(2):
            out[2 * parity + which, :, 64 * which : 64 * which + 27] = take[parity, which].T
    return out


def source_tiles(row, col):
    wide = row >= 2
    side_row = row + 2 * (1 - col // 2)
    table = []
    for image in range(2):
        table.append((image, 0, image, row - 1, col, row > 0))
        table.append((image, 1, image, row, col - 1, col > 0))
        table.append((image, 2, image, row - 1, col - 1, (row > 0) & (col > 0)))
    third_image = jnp.where(wide, 3 - row, 1 - lax.rem(col, 2))
    table.append((2, 0, third_image, 3, col, wide))
    table.append((2, 1, third_image, side_row, 3, jnp.logical_not(wide)))
    table.append((2, 2, third_image, jnp.where(wide, 3, side_row - 1), jnp.where(wide, col - 1, 3), jnp.where(wide, col, side_row) > 0))
    table.append((3, 2, 3 - row, 3, 3, wide & (col == 3)))
    return table


CLOSE_PLAN = ("p1", "|", "p0", "11", "p2", "10", "p3", "12", "|", "21", "20", "|", "|", "|", "|", "p4", "|", "13", "|", "|", "31", "22", "|", "|", "30", "p5", "|", "|", "|", "15", "|", "32", "|", "23", "|", "|", "25", "G0", "14", "33", "G1", "p7", "41", "G2", "35", "40", "17", "G3", "s0", "S", "24", "s1", "27", "37", "43", "34", "p6", "s2", "16", "42", "s3", "26", "36", "44", "46", "47", "45", "s4")


def returns(raws, landing, send, recv, row, col):
    def each(t, act):
        for slot, kind, image, tile_row, tile_col, present in source_tiles(row, col):
            here = (tile_row == row) & (tile_col == col)
            act(slot, kind, image, tile_row, tile_col, present & here, present & jnp.logical_not(here))

    def start(t):
        def act(slot, kind, image, tile_row, tile_col, local, remote):
            @pl.when(local)
            def _():
                pltpu.make_async_copy(
                    window_part(raws[t], slot, kind), landing[t][kind].at[image], recv.at[t, image, kind]
                ).start()

            @pl.when(remote)
            def _():
                hop(t, slot, kind, image, tile_row, tile_col).start()

        each(t, act)

    def hop(t, slot, kind, image, tile_row, tile_col):
        return pltpu.make_async_remote_copy(
            src_ref=window_part(raws[t], slot, kind),
            dst_ref=landing[t][kind].at[image],
            send_sem=send.at[t, slot, kind],
            recv_sem=recv.at[t, image, kind],
            device_id={"row": jnp.maximum(tile_row, 0), "col": jnp.maximum(tile_col, 0)},
            device_id_type=MESH,
        )

    def arrived(t):
        for image in range(2):
            for kind in range(3):
                goal = landing[t][kind].at[image]
                pltpu.make_async_copy(goal, goal, recv.at[t, image, kind]).wait()

    def left(t):
        def act(slot, kind, image, tile_row, tile_col, local, remote):
            @pl.when(remote)
            def _():
                hop(t, slot, kind, image, tile_row, tile_col).wait_send()

        each(t, act)

    return start, arrived, left


def merge_tiles(owns, landing, goals, row, col):
    places = lax.broadcasted_iota(jnp.int32, (16, 1), 0)
    in_left = places < 14 - 2 * col

    def rows16(values):
        return values.reshape(16, FEATURES).astype(F32)

    def right_half(values):
        low = values.reshape(8, FEATURES).astype(F32)
        return jnp.concatenate([low, low], axis=0)

    for image in range(2):

        def merge(tile_row, _):
            top = tile_row < 14 - 2 * row
            upper = jnp.minimum(tile_row, 13)
            lower = jnp.maximum(tile_row - 8, 0)
            for own, (below, right, both), goal in zip(owns, landing, goals):
                stacked = jnp.where(top, rows16(own(image, upper)), rows16(below[image, lower]))
                beside = jnp.where(top, right_half(right[image, upper]), right_half(both[image, lower]))
                goal[image, tile_row] = jnp.where(in_left, stacked, beside).astype(goal.dtype)
            return 0

        lax.fori_loop(0, 16, merge, 0)


def input_grad(at, dqkv, wq, xw, image_grad, gain, norm_sums):
    grad = nt(dqkv[at, :], wq).astype(BF).astype(F32)
    unit, inverse = unit_of(xw[at, :].astype(F32))
    image_grad[at, :] += norm_back(grad, unit, inverse, as_row(gain))
    norm_sums[0] += fold_rows(grad * unit)
    norm_sums[1] += fold_rows(grad)


def plain_close_kernel(dqkv, xw, dm, raw_r, wq, gain, out, grad_out, norm_sums, image_grad, raw_g, *refs):
    img, row, col = place()
    landing, (send, recv) = (refs[:3], refs[3:6]), refs[6:]
    greet(img, row, col, False)
    start, arrived, left = returns((raw_r, raw_g), landing, send, recv, row, col)
    start(0)
    norm_sums[...] = jnp.zeros_like(norm_sums)
    image_grad[...] = dm[...]

    def step(i, _):
        input_grad(pl.ds(pl.multiple_of(i * BLOCK, 16), BLOCK), dqkv, wq[...], xw, image_grad, gain, norm_sums)
        return 0

    lax.fori_loop(0, ROWS // BLOCK, step, 0)
    spread_rows(image_grad, raw_g, row, col)
    start(1)
    for t in range(2):
        arrived(t)
    owns = [lambda image, upper, raw=raw: raw[image * 22 + 8 + upper, 1:3] for raw in (raw_r, raw_g)]
    merge_tiles(owns, landing, (out, grad_out), row, col)
    for t in range(2):
        left(t)


PIECES = [(2, 8, 2, 8, FEATURES), (2, 14, 1, 8, FEATURES), (2, 8, 1, 8, FEATURES)]


def plain_close(dqkv, xw, dm, raw_r, wq, gain):
    vm = pl.BlockSpec(memory_space=pltpu.VMEM)
    shape = jax.ShapeDtypeStruct
    dma = pltpu.SemaphoreType.DMA
    pieces = [pltpu.VMEM(s, BF) for s in PIECES]
    return pl.pallas_call(
        plain_close_kernel,
        out_shape=[shape((2, 16, 16, FEATURES), BF), shape((2, 16, 16, FEATURES), F32), shape((2, 8, FEATURES), F32)],
        in_specs=[vm] * 6,
        out_specs=[vm] * 3,
        scratch_shapes=[pltpu.VMEM((ROWS, FEATURES), F32), pltpu.VMEM((88, 3, 8, FEATURES), BF)]
        + pieces
        + pieces
        + [dma((2, 4, 3)), dma((2, 2, 3))],
        compiler_params=pltpu.CompilerParams(collective_id=2, has_side_effects=True, vmem_limit_bytes=67043328),
    )(dqkv, xw, dm, raw_r, wq, gain)


def back_kernel(
    do, o, value_bias, rows_table, cols_table, take, o_turned, da, n2_turned, cw, xw, n1_turned, gain, sums, up_sum, taker, probs, qkv_in, dh_in, g_in, dm_in, wq_in, raw_r, *refs
):
    out, grad_out, gq, go, gu, gd, small_out, table_out = refs[:8]
    qkv, probs_s, image_grad, shared_h, shared_g, own_r = refs[8:14]
    bias_sums, table_sums, norm_sums, tab, row_bias = refs[14:19]
    landing = (refs[19:22], refs[22:25])
    full = refs[25:29]
    small, table, small_land, table_land, small_z, table_z = refs[29:35]
    count = len(SUM_CHUNKS)
    lands = refs[35 : 35 + 5 * count]
    send, recv, load_sem, probs_sem, wsend, wrecv, ssend, srecv = refs[35 + 5 * count :]
    img, row, col = place()
    y_row = lax.rem(row + 2, 4)
    core_row = row + 1 - 2 * lax.rem(row, 2)
    other = 1 - img
    copies = []

    def load(i):
        pairs = (
            (dh_in, shared_h.at[pl.ds(0, ROWS)]),
            (g_in, shared_g),
            (qkv_in, qkv),
            (dm_in, image_grad),
            (wq_in, shared_h.at[:, pl.ds(0, 3 * FEATURES)]),
            (raw_r.at[pl.ds(8, 14), pl.ds(1, 2)], own_r.at[0]),
            (raw_r.at[pl.ds(30, 14), pl.ds(1, 2)], own_r.at[1]),
        )
        return pltpu.make_async_copy(pairs[i][0], pairs[i][1], load_sem.at[i])

    for i in (2, 1, 0, 3, 5, 6):
        load(i).start()
    windows = window_count(row, col)

    def fetch(k, window, slot):
        pair_index = lax.rem(k, 2) * 3 + k // 2
        return pltpu.make_async_copy(probs.at[window, pl.ds(2 * pair_index, 2)], probs_s.at[slot], probs_sem.at[slot])

    fetch(0, 0, 0).start()
    greet(img, row, col)
    start, arrived, left = returns((raw_r, shared_g), landing, send, recv, row, col)
    start(0)

    def turned_rows(ref):
        return lambda rw, kb: ref[pl.ds(pl.multiple_of(rw * kb, kb), kb), :]

    def turned_g(rw, kb):
        return shared_g[pl.ds(pl.multiple_of(rw * 32, 32), 32)].reshape(FEATURES, FEATURES)[:, 0:ROWS]

    pair_stage, first, second, third, fourth, sent = reducers(
        SUM_CHUNKS,
        full,
        (turned_rows(n1_turned), turned_rows(o_turned), turned_rows(n2_turned), turned_g),
        (qkv, da, shared_h, cw),
        (gq, go, gu, gd),
        lands,
        wsend,
        wrecv,
    )
    bias_sums[...] = jnp.zeros_like(bias_sums)
    table_sums[...] = jnp.zeros_like(table_sums)
    norm_sums[...] = jnp.zeros_like(norm_sums)
    build_table(tab, rows_table, cols_table, take)
    row_bias[...] = as_row(value_bias)
    load(2).wait()
    clear_idle(qkv, row, col)
    load(1).wait()
    load(0).wait()

    def grad_rows(i):
        if i == 0:
            load(4).start()
            load(3).wait()
            load(4).wait()
        input_grad(pl.ds(i * BLOCK, BLOCK), qkv, shared_h[:, 0 : 3 * FEATURES], xw, image_grad, gain, norm_sums)

    def send_grad():
        spread_rows(image_grad, shared_g, row, col)
        start(1)

    def over_rows(values):
        return jnp.sum(values, axis=0, keepdims=True)

    def gather_small():
        small[0] = jnp.zeros((16, FEATURES), F32)
        lines = [bias_sums[0], bias_sums[1], sums[0], sums[1], norm_sums[0], norm_sums[1], sums[2], sums[3]]
        for i, values in enumerate(lines):
            small[0, i : i + 1, :] = over_rows(values)
        for i in range(4):
            small[0, 8 + i : 9 + i, :] = over_rows(up_sum[:, i * FEATURES : (i + 1) * FEATURES])
        exact = lax.Precision.HIGHEST
        total = jnp.zeros((64, 128), F32)
        for parity in range(2):
            for which in range(2):
                part = table_sums[64 * parity : 64 * parity + 64, 256 * parity + 128 * which : 256 * parity + 128 * which + 128]
                total = total + jnp.dot(part, taker[2 * parity + which], precision=exact, preferred_element_type=F32)
        table[0] = total

    hops = ({"row": core_row}, {"row": y_row}, {"img": other})

    def small_push(k, src, dst, target):
        c = pltpu.make_async_remote_copy(
            src_ref=src, dst_ref=dst, send_sem=ssend.at[k], recv_sem=srecv.at[k], device_id=target, device_id_type=MESH
        )
        c.start()
        copies.append(c)
        return c

    def small_step(i):
        if i == 0:
            gather_small()
        if 0 < i <= 3:
            for k, (acc, land) in enumerate(((small, small_land), (table, table_land))):
                pltpu.make_async_copy(land.at[i - 1], land.at[i - 1], srecv.at[2 * (i - 1) + k]).wait()
                acc[i] = acc[i - 1] + land[i - 1]
        if i < 3:
            for k, (acc, land) in enumerate(((small, small_land), (table, table_land))):
                small_push(2 * i + k, acc.at[i], land.at[i], hops[i])
        if i == 3:
            small_z[col] = small[3]
            table_z[col] = table[3]
            for d in range(1, 4):
                cl = lax.rem(col + d, 4)
                small_push(4 + 2 * d, small.at[3], small_z.at[col], {"col": cl})
                small_push(5 + 2 * d, table.at[3], table_z.at[col], {"col": cl})
        if i == 4:
            for d in range(1, 4):
                cl = lax.rem(col + 4 - d, 4)
                pltpu.make_async_copy(small_z.at[cl], small_z.at[cl], srecv.at[4 + 2 * d]).wait()
                pltpu.make_async_copy(table_z.at[cl], table_z.at[cl], srecv.at[5 + 2 * d]).wait()
            small_out[...] = (small_z[0] + small_z[1]) + (small_z[2] + small_z[3])
            table_out[...] = (table_z[0] + table_z[1]) + (table_z[2] + table_z[3])

    acts = {"p": pair_stage, "1": first, "2": second, "3": third, "4": fourth, "G": grad_rows, "s": small_step, "S": send_grad}
    slots = plan_slots(CLOSE_PLAN, acts)
    run_all(slots[0])

    def head_pair(k, _):
        pair_index = lax.rem(k, 2) * 3 + k // 2

        def each(window, _):
            for i, slot_acts in enumerate(slots[1:-1]):
                if slot_acts:
                    pl.when((k == (i + 1) // 3) & (window == (i + 1) % 3))(functools.partial(run_all, slot_acts))
            turn_count = k * windows + window
            slot = lax.rem(turn_count, 2)
            fetch(k, window, slot).wait()
            wrap = window + 1 == windows
            next_k = jnp.where(wrap, k + 1, k)

            @pl.when(next_k < 6)
            def _():
                fetch(next_k, jnp.where(wrap, 0, window + 1), 1 - slot).start()

            attention_back(
                window,
                pair_index,
                lambda parity: probs_s[slot, parity],
                do,
                qkv,
                o,
                tab,
                row_bias,
                bias_sums,
                table_sums,
                row,
                col,
            )
            return 0

        lax.fori_loop(0, windows, each, 0)
        return 0

    lax.fori_loop(0, 6, head_pair, 0)
    run_all(slots[-1])
    arrived(0)
    load(5).wait()
    load(6).wait()
    merge_tiles([lambda image, upper: own_r[image, upper]], landing[:1], (out,), row, col)
    arrived(1)
    merge_tiles([lambda image, upper: shared_g[image * 22 + 8 + upper, 1:3]], landing[1:], (grad_out,), row, col)
    left(0)
    left(1)
    for c in copies:
        c.wait_send()
    for copy in sent:
        copy().wait_send()


def back(do, o, value_bias, rows_table, cols_table, o_turned, da, n2_turned, cw, xw, n1_turned, gain, sums, up_sum, probs, qkv, dh, g, dm, wq, raw_r):
    vm = pl.BlockSpec(memory_space=pltpu.VMEM)
    an = pl.BlockSpec(memory_space=pl.ANY)
    shape = jax.ShapeDtypeStruct
    dma = pltpu.SemaphoreType.DMA
    pieces = [pltpu.VMEM(s, BF) for s in PIECES]
    count = len(SUM_CHUNKS)
    return pl.pallas_call(
        back_kernel,
        out_shape=[shape((2, 16, 16, FEATURES), BF), shape((2, 16, 16, FEATURES), BF)]
        + [shape((k // 16, n // 2), F32) for k, n in WHOLES]
        + [shape((16, FEATURES), F32), shape((64, 128), F32)],
        in_specs=[vm] * 16 + [an] * 7,
        out_specs=[vm] * 8,
        scratch_shapes=[
            pltpu.VMEM((SPAN, 3 * FEATURES), BF),
            pltpu.VMEM((2, 2, 224, 224), BF),
            pltpu.VMEM((ROWS, FEATURES), F32),
            pltpu.VMEM((FEATURES, 4 * FEATURES), BF),
            pltpu.VMEM((128, 3, 8, FEATURES), BF),
            pltpu.VMEM((2, 14, 2, 8, FEATURES), BF),
            pltpu.VMEM((2, 8, FEATURES), F32),
            pltpu.VMEM((128, 512), F32),
            pltpu.VMEM((2, 8, FEATURES), F32),
            pltpu.VMEM((128, 512), BF),
            pltpu.VMEM((1, FEATURES), F32),
        ]
        + pieces
        + pieces
        + [pltpu.VMEM(s, BF) for s in WHOLES]
        + [
            pltpu.VMEM((4, 16, FEATURES), F32),
            pltpu.VMEM((4, 64, 128), F32),
            pltpu.VMEM((3, 16, FEATURES), F32),
            pltpu.VMEM((3, 64, 128), F32),
            pltpu.VMEM((4, 16, FEATURES), F32),
            pltpu.VMEM((4, 64, 128), F32),
        ]
        + land_shapes(SUM_CHUNKS)
        + [dma((2, 4, 3)), dma((2, 2, 3)), dma((7,)), dma((2,)), dma((count, 13)), dma((count, 13)), dma((12,)), dma((12,))],
        compiler_params=pltpu.CompilerParams(collective_id=1, has_side_effects=True, vmem_limit_bytes=67043328),
    )(
        do, o, value_bias, rows_table, cols_table, takers(True), o_turned, da, n2_turned, cw, xw, n1_turned, gain, sums, up_sum, jnp.asarray(table_taker()),
        probs, qkv, dh, g.reshape(128, 3, 8, FEATURES), dm, wq, raw_r,
    )


def deliver_kernel(out_in, grad_in, *refs):
    sums_in, (small, table), outs = refs[:4], refs[4:6], refs[6:]
    outs[0][...] = out_in[...]

    def widen(i, _):
        outs[1][i // 16, i % 16] = grad_in[i // 16, i % 16].astype(F32)
        return 0

    lax.fori_loop(0, 32, widen, 0)
    for given, goal in zip(sums_in, outs[2:6]):
        goal[...] = given[...]
    for i, goal in zip((0, 1, 2, None, 3, 4, 5, 6, 7), outs[6:15]):
        if i is None:
            goal[...] = jnp.concatenate([small[8 + j : 9 + j, :] for j in range(4)], axis=1).reshape(4 * FEATURES)
        else:
            goal[...] = small[i : i + 1, :].reshape(FEATURES)
    turned = table[...].T
    outs[15][...] = turned[0:27, :]
    outs[16][...] = turned[64:91, :]


def deliver(*given):
    vm = pl.BlockSpec(memory_space=pltpu.VMEM)
    shape = jax.ShapeDtypeStruct
    lengths = [FEATURES] * 3 + [4 * FEATURES] + [FEATURES] * 5
    outs = [shape((2, 16, 16, FEATURES), BF), shape((2, 16, 16, FEATURES), F32)] + [shape((k // 16, n // 2), F32) for k, n in WHOLES]
    outs += [shape((n,), F32) for n in lengths] + [shape((27, 64), F32)] * 2
    return pl.pallas_call(deliver_kernel, out_shape=outs, in_specs=[vm] * 8, out_specs=[vm] * len(outs))(*given)


def on_device(
    image_in,
    cotangent,
    qkv_weight,
    out_weight,
    up_weight,
    down_weight,
    query_bias,
    value_bias,
    out_bias,
    up_bias,
    down_bias,
    first_gain,
    first_shift,
    second_gain,
    second_shift,
    rows_table,
    cols_table,
):
    line = lambda v: v.reshape(1, -1)
    xw, cw, n1_turned, qkv, probs, o, o_turned, wq, wo, wu, wd = open_windows(
        image_in, cotangent, (qkv_weight, out_weight, up_weight, down_weight), first_gain, first_shift, query_bias, value_bias, rows_table, cols_table
    )
    raw_r, n2_turned, g_turned, dh, da, do, dm, sums, up_sum = middle(
        o, xw, cw, wo, wu, wd, out_bias, line(up_bias), down_bias, second_gain, second_shift
    )
    if lax.axis_size("img") == 2:
        return tuple(
            deliver(
                *back(
                    do, o, value_bias, rows_table, cols_table, o_turned, da, n2_turned, cw, xw, n1_turned, first_gain, sums, up_sum,
                    probs, qkv, dh, g_turned, dm, wq, raw_r,
                )
            )
        )
    dqkv, bias_sums, table_sums = plain_back(do, probs, qkv, o, value_bias, rows_table, cols_table)
    image_out, image_grad, norm_sums = plain_close(dqkv, xw, dm, raw_r, wq, first_gain)
    dot = lambda a, b: jnp.dot(a, b, preferred_element_type=F32)
    totals = (dot(n1_turned, dqkv[:ROWS]), dot(o_turned, da), dot(n2_turned, dh), dot(g_turned[:, :ROWS], cw))
    shard_sums = []
    for total in totals:
        part = lax.psum_scatter(total.astype(BF), ("row", "col"), scatter_dimension=0, tiled=True)
        shard_sums.append(lax.psum_scatter(part, "img", scatter_dimension=1, tiled=True).astype(F32))
    rows_grad, cols_grad = table_grads(table_sums)
    small_sums = lax.psum(
        tuple(jnp.sum(bias_sums, axis=1))
        + (jnp.sum(sums[0], axis=0), jnp.sum(up_sum, axis=0), jnp.sum(sums[1], axis=0))
        + tuple(jnp.sum(norm_sums, axis=1))
        + (jnp.sum(sums[2], axis=0), jnp.sum(sums[3], axis=0), rows_grad, cols_grad),
        ("img", "row", "col"),
    )
    return (image_out, image_grad, *shard_sums, *small_sums)


def solution(mesh):
    tiles = P("img", "row", "col", None)
    shards = P(("row", "col"), "img")
    return jax.shard_map(
        on_device,
        mesh=mesh,
        in_specs=(tiles,) * 2 + (shards,) * 4 + (P(),) * 11,
        out_specs=(tiles,) * 2 + (shards,) * 4 + (P(),) * 11,
        check_vma=False,
    )
```

```python
import functools

import jax
import jax.numpy as jnp
import numpy as np
from jax import lax
from jax.experimental import pallas as pl
from jax.experimental.pallas import tpu as pltpu
from jax.sharding import PartitionSpec as P

MESH = pl.DeviceIdType.MESH


def place():
    return lax.axis_index("img"), lax.axis_index("row"), lax.axis_index("col")


def side_owner(window_row, image):
    return lax.rem(window_row, 2), 3 - image - 2 * (window_row // 2)


def piece_target(kind, image, row, col):
    last_row, last_col = row == 3, col == 3
    side_row, side_col = side_owner(row, image)
    next_row, next_col = side_owner(lax.rem(row + 1, 4), image)
    if kind == 0:
        return (jnp.where(last_row, 3 - image, row + 1), col, jnp.where(last_row, 2, image))
    if kind == 1:
        return (jnp.where(last_col, side_row, row), jnp.where(last_col, side_col, col + 1), jnp.where(last_col, 2, image))
    target_row = jnp.where(last_row, 3 - image, jnp.where(last_col, next_row, row + 1))
    target_col = jnp.where(last_col, jnp.where(last_row, 3, next_col), col + 1)
    slot = jnp.where(last_row & last_col, 3, jnp.where(last_row | last_col, 2, image))
    return (target_row, target_col, slot)


def arrivals(row, col):
    wide = row >= 2
    side_row = row + 2 * (1 - col // 2)
    table = []
    for image in range(2):
        table.append((image, 0, row > 0))
        table.append((image, 1, col > 0))
        table.append((image, 2, (row > 0) & (col > 0)))
    table.append((2, 0, wide))
    table.append((2, 1, jnp.logical_not(wide)))
    table.append((2, 2, jnp.where(wide, col, side_row) > 0))
    table.append((3, 2, wide & (col == 3)))
    return table


def tile_part(ref, image, kind):
    if kind == 0:
        return ref.at[image, pl.ds(8, 8), pl.ds(0, 2)]
    if kind == 1:
        return ref.at[image, pl.ds(0, 14), pl.ds(1, 1)]
    return ref.at[image, pl.ds(8, 8), pl.ds(1, 1)]


def window_part(ref, slot, kind):
    if kind == 0:
        return ref.at[pl.ds(slot * 22, 8), pl.ds(1, 2)]
    if kind == 1:
        return ref.at[pl.ds(slot * 22 + 8, 14), pl.ds(0, 1)]
    return ref.at[pl.ds(slot * 22, 8), pl.ds(0, 1)]


def greet(img, row, col, pairs=True):
    barrier = pltpu.get_barrier_semaphore()
    for row_step in range(4):
        for col_step in range(4):
            if row_step or col_step:
                pl.semaphore_signal(
                    barrier,
                    inc=1,
                    device_id={"row": lax.rem(row + row_step, 4), "col": lax.rem(col + col_step, 4)},
                    device_id_type=MESH,
                )
    if pairs:
        pl.semaphore_signal(barrier, inc=1, device_id={"img": 1 - img}, device_id_type=MESH)
    pl.semaphore_wait(barrier, 16 if pairs else 15)


CHUNKS = ((0, 0, 640), (0, 640, 1152), (1, 0, 384), (2, 0, 768), (2, 768, 1536), (3, 0, 128), (3, 128, 384))


def links(shards, fulls, wsend, wrecv, wloc):
    img, row, col = place()
    y_row = lax.rem(row + 2, 4)
    core_row = row + 1 - 2 * lax.rem(row, 2)
    other = 1 - img
    sent = []

    def rows_of(w, rw, half=None):
        kb = fulls[w].shape[0] // 4
        if half is None:
            return pl.ds(pl.multiple_of(rw * kb, kb), kb)
        return pl.ds(pl.multiple_of(rw * kb + half * (kb // 2), kb // 2), kb // 2)

    def cols_of(n, im):
        w, lo, hi = CHUNKS[n]
        nb = fulls[w].shape[1] // 2
        return pl.ds(pl.multiple_of(im * nb + lo, 128), hi - lo)

    def block(n, rw, im, half=None):
        w = CHUNKS[n][0]
        return fulls[w].at[rows_of(w, rw, half), cols_of(n, im)]

    def slot(n, cl):
        w = CHUNKS[n][0]
        k16 = fulls[w].shape[0] // 16
        return fulls[w].at[pl.ds(pl.multiple_of((row * 4 + cl) * k16, k16), k16), cols_of(n, img)]

    def source(n):
        w, lo, hi = CHUNKS[n]
        return shards[w].at[:, pl.ds(lo, hi - lo)]

    def push(n, k, where, target, start=None):
        def copy():
            ref = slot(n, where) if start else block(n, *where)
            return pltpu.make_async_remote_copy(
                src_ref=source(n) if start and where is col else ref,
                dst_ref=ref,
                send_sem=wsend.at[n, k],
                recv_sem=wrecv.at[n, k],
                device_id=target(),
                device_id_type=MESH,
            )

        copy().start()
        sent.append(copy)

    def arrive(n, k, ref):
        pltpu.make_async_copy(ref, ref, wrecv.at[n, k]).wait()

    far_col, near_col = lax.rem(col + 2, 4), col + 1 - 2 * lax.rem(col, 2)

    def along_col(n):
        pltpu.make_async_copy(source(n), slot(n, col), wloc.at[n]).start()
        push(n, 0, col, lambda: {"col": far_col}, True)

    def near_by(n):
        pltpu.make_async_copy(source(n), slot(n, col), wloc.at[n]).wait()
        push(n, 1, col, lambda: {"col": near_col}, True)
        arrive(n, 0, slot(n, far_col))
        push(n, 2, far_col, lambda: {"col": near_col}, True)

    def first(n):
        arrive(n, 1, slot(n, near_col))
        arrive(n, 2, slot(n, 3 - col))
        push(n, 3, (row, img, 0), lambda: {"img": other})
        push(n, 4, (row, img, 1), lambda: {"row": y_row})
        push(n, 5, (row, img), lambda: {"row": core_row})

    def second(n):
        arrive(n, 3, block(n, row, other, 0))
        arrive(n, 4, block(n, y_row, img, 1))
        push(n, 6, (row, img, 0), lambda: {"row": y_row})
        push(n, 7, (row, other, 0), lambda: {"row": y_row})
        push(n, 8, (row, img, 1), lambda: {"img": other})
        push(n, 9, (y_row, img, 1), lambda: {"img": other})
        push(n, 10, (row, other, 0), lambda: {"row": core_row})
        push(n, 11, (y_row, img, 1), lambda: {"row": core_row})

    def third(n):
        arrive(n, 6, block(n, y_row, img, 0))
        arrive(n, 7, block(n, y_row, other, 0))
        arrive(n, 8, block(n, row, other, 1))
        arrive(n, 9, block(n, y_row, other, 1))
        push(n, 12, (y_row, img, 0), lambda: {"row": core_row})
        push(n, 13, (y_row, other, 0), lambda: {"row": core_row})
        push(n, 14, (row, other, 1), lambda: {"row": core_row})
        push(n, 15, (y_row, other, 1), lambda: {"row": core_row})

    def last(n):
        core_y = lax.rem(core_row + 2, 4)
        arrive(n, 5, block(n, core_row, img))
        arrive(n, 10, block(n, core_row, other, 0))
        arrive(n, 11, block(n, core_y, img, 1))
        arrive(n, 12, block(n, core_y, img, 0))
        arrive(n, 13, block(n, core_y, other, 0))
        arrive(n, 14, block(n, core_row, other, 1))
        arrive(n, 15, block(n, core_y, other, 1))

    return along_col, near_by, first, second, third, last, sent


def window_moves(tiles, raws, send, recv, loc):
    img, row, col = place()

    def each(t, act):
        for image in range(2):
            for kind in range(3):
                target_row, target_col, target_slot = piece_target(kind, image, row, col)
                here = (target_row == row) & (target_col == col)
                part = tile_part(tiles[t], image, kind)
                goal = window_part(raws[t], target_slot, kind)
                act(here, part, goal, send.at[t, image, kind], recv.at[t, target_slot, kind], target_row, target_col)

    def remote(part, goal, leave, arrival, target_row, target_col):
        return pltpu.make_async_remote_copy(
            src_ref=part,
            dst_ref=goal,
            send_sem=leave,
            recv_sem=arrival,
            device_id={"row": target_row, "col": target_col},
            device_id_type=MESH,
        )

    def own(t, image):
        return pltpu.make_async_copy(tiles[t].at[image, pl.ds(0, 14)], raws[t].at[pl.ds(image * 22 + 8, 14), pl.ds(1, 2)], loc.at[t, image])

    def start(t):
        for image in range(2):
            own(t, image).start()

        def act(here, part, goal, leave, arrival, target_row, target_col):
            @pl.when(here)
            def _():
                pltpu.make_async_copy(part, goal, arrival).start()

            @pl.when(jnp.logical_not(here))
            def _():
                remote(part, goal, leave, arrival, target_row, target_col).start()

        each(t, act)

    def arrived(t):
        for image in range(2):
            own(t, image).wait()
        for slot_index, kind, present in arrivals(row, col):
            part = window_part(raws[t], slot_index, kind)

            @pl.when(present)
            def _():
                pltpu.make_async_copy(part, part, recv.at[t, slot_index, kind]).wait()

    def left(t):
        def act(here, part, goal, leave, arrival, target_row, target_col):
            @pl.when(jnp.logical_not(here))
            def _():
                remote(part, goal, leave, arrival, target_row, target_col).wait_send()

        each(t, act)

    return start, arrived, left


BF = jnp.bfloat16
F32 = jnp.float32
ROWS = 704
SPAN = 800
FEATURES = 768
EPS = 1e-06


def row_params(step, row, col):
    wide = row >= 2
    side_row = row + 2 * (1 - col // 2)
    third_step = step - 28
    in_corner = wide & (third_step >= 8)
    slot = jnp.where(step < 14, 0, jnp.where(step < 28, 1, jnp.where(in_corner, 3, 2)))
    place_row = jnp.where(step < 14, step, jnp.where(step < 28, step - 14, jnp.where(in_corner, third_step - 8, third_step)))
    full = step < 28
    row_start = jnp.where(full, 8 - 2 * row, jnp.where(wide, 0, 8 - 2 * side_row))
    col_start = jnp.where(full, 8 - 2 * col, jnp.where(wide & jnp.logical_not(in_corner), 8 - 2 * col, 0))
    width = jnp.where(full, 14, jnp.where(wide & jnp.logical_not(in_corner), 14, 8))
    alive = jnp.where(full, True, jnp.where(in_corner, col == 3, jnp.where(wide, True, third_step < 14)))
    return slot, jnp.minimum(place_row + row_start, 21), col_start, jnp.where(alive, width, 0)


def window_params(window, row, col):
    wide = row >= 2
    start = jnp.where(window < 2, 14 * window, jnp.where(window == 2, 28, 36))
    tall = jnp.where(window < 2, 14, jnp.where((window == 2) & jnp.logical_not(wide), 14, 8))
    width = jnp.where(window < 2, 14, jnp.where((window == 2) & wide, 14, 8))
    return start, tall, width


def window_count(row, col):
    return jnp.where((row >= 2) & (col == 3), 4, 3)


def unit_of(values):
    center = values - jnp.mean(values, axis=-1, keepdims=True)
    inverse = lax.rsqrt(jnp.mean(center * center, axis=-1, keepdims=True) + EPS)
    return center * inverse, inverse


def relative_layout(backward):
    take = np.zeros((2, 2, 27, 128), np.float32)
    for parity in range(2):
        base = 64 if parity == 0 else 0
        for j in range(27):
            for copy in (0,) if backward else (0, 32):
                take[parity, 0, 26 - j, (base - 13 + j + copy) % 128] = 1
                if backward:
                    take[parity, 1, j, base + 16 + j] = 1
                else:
                    take[parity, 1, 26 - j, (base + 3 + j + copy) % 128] = 1
    return take


def takers(backward):
    return jnp.asarray(relative_layout(backward).reshape(4, 27, 128), BF)


def build_table(tab, rows_table, cols_table, take):
    tab[...] = jnp.zeros_like(tab)
    for parity in range(2):
        for which, table in ((0, rows_table), (1, cols_table)):
            block = lax.dot_general(table[...], take[2 * parity + which], (((0,), (0,)), ((), ())), preferred_element_type=F32)
            lane = 256 * parity + 128 * which
            tab[64 * parity : 64 * parity + 64, lane : lane + 128] = block.astype(BF)


def as_row(ref):
    return ref[...].reshape(1, -1)


def run_all(acts):
    for act in acts:
        act[0](*act[1:])


def plan_slots(plan, acts):
    slots = [[]]
    for name in plan:
        if name == "|":
            slots.append([])
        elif name in acts:
            slots[-1].append((acts[name],))
        else:
            slots[-1].append((acts[name[0]], int(name[1:])))
    return slots


def table_grads(sums):
    take = jnp.asarray(relative_layout(True), F32)
    grads = []
    for which in range(2):
        total = 0.0
        for parity in range(2):
            part = sums[64 * parity : 64 * parity + 64, 256 * parity + 128 * which : 256 * parity + 128 * which + 128]
            total = total + lax.dot_general(take[parity, which], part, (((1,), (1,)), ((), ())), precision=lax.Precision.HIGHEST)
        grads.append(total)
    return grads


FF = 3072
CHUNK = 512
BLOCK = 176


def nt(a, b):
    return lax.dot_general(a, b, (((1,), (1,)), ((), ())), preferred_element_type=F32)


def norm_back(grad, unit, inverse, gain):
    scaled = grad * gain
    first_mean = jnp.mean(scaled, axis=-1, keepdims=True)
    second_mean = jnp.mean(scaled * unit, axis=-1, keepdims=True)
    return inverse * (scaled - first_mean - unit * second_mean)


def fold_rows(values):
    total = values[0:8]
    for i in range(1, values.shape[0] // 8):
        total = total + values[8 * i : 8 * i + 8]
    return total


def spread_rows(source, raw, row, col):
    def step(i, _):
        slot, raw_row, col_start, width = row_params(i, row, col)
        at = pl.ds(pl.multiple_of(i * 16, 16), 16)

        @pl.when(width > 0)
        def _():
            values = jnp.concatenate([source[at, :], jnp.zeros((8, FEATURES), F32)], axis=0)
            raw[slot * 22 + raw_row] = pltpu.roll(values, col_start, 0).astype(BF).reshape(3, 8, FEATURES)

        return 0

    lax.fori_loop(0, 44, step, 0)


OPEN_PLAN = ("a2", "a1", "a0", "a5", "b2", "b1", "a3", "12", "b0", "Wx", "11", "10", "21", "22", "b5", "20", "32", "b3", "a6", "31", "15", "13", "30", "b6", "a4", "25", "X", "L1", "Wc", "L2", "L0", "P", "|", "|", "|", "16", "35", "|", "|", "|", "23", "|", "|", "|", "|", "|", "b4", "26", "|", "|", "|", "|", "|", "|", "33", "|", "14", "L5", "T", "M", "36", "K", "24", "L6", "L3", "|", "34", "|", "L4", "|", "|")


def open_kernel(weights, x_ref, c_ref, gain, shift, query_bias, value_bias, rows_table, cols_table, take, out_bias, up_bias, down_bias, gain2, shift2, *refs):
    img, row, col = place()
    greet(img, row, col, weights)
    if weights:
        shards, refs = refs[:4], refs[4:]
    else:
        wq, wo, wu, wd = refs[:4]
        refs = refs[4:]
    xw, cw, n1_turned, qkv_out, probs_out, o, o_turned = refs[:7]
    raw_out, n2_turned, g_out, dh_out, da, do, dm, sums, up_sum = refs[7:16]
    refs = refs[16:]
    if weights:
        wq_out, refs = refs[0], refs[1:]
    rawx, rawc, n1, tab, row_bias, qkv_s, probs, y_s, d_s, g_s, g_chunk, dh_chunk, out_sem, probs_sem, send, recv, loc = refs[:17]
    refs = refs[17:]
    if weights:
        wq, wo, wu, wd = refs[:4]
        along_col, near_by, first, second, third, last, sent = links(shards, refs[:4], *refs[4:])
    window_start, window_arrived, window_left = window_moves((x_ref, c_ref), (rawx, rawc), send, recv, loc)
    places = lax.broadcasted_iota(jnp.int32, (16, 1), 0)

    def cut_one(raw, step):
        slot, raw_row, col_start, width = row_params(step, row, col)
        wide_rows = raw[slot * 22 + raw_row].reshape(24, FEATURES).astype(F32)
        keep = places < width
        return keep, jnp.where(keep, pltpu.roll(wide_rows, lax.rem(24 - col_start, 24), 0)[:16], 0.0)

    def cut_x(step, _):
        at = pl.ds(pl.multiple_of(step * 16, 16), 16)
        keep, x = cut_one(rawx, step)
        xw[at, :] = x.astype(BF)
        unit, _inverse = unit_of(x)
        n1[at, :] = jnp.where(keep, unit * as_row(gain) + as_row(shift), 0.0).astype(BF)
        return 0

    def cut_c(step, _):
        at = pl.ds(pl.multiple_of(step * 16, 16), 16)
        _keep, c = cut_one(rawc, step)
        cw[at, :] = c.astype(BF)
        return 0

    def project(step, _):
        at = pl.ds(pl.multiple_of(step * 352, 32), 352)
        for part_index in range(3):
            lanes = slice(part_index * FEATURES, (part_index + 1) * FEATURES)
            part = jnp.dot(n1[at, :], wq[:, lanes], preferred_element_type=F32)
            if part_index != 1:
                part = part + row_bias[part_index // 2]
            qkv_s[at, lanes] = part.astype(BF)
        return 0

    def turn(source, goal):
        def step(i, _):
            lanes = pl.ds(pl.multiple_of(i * 128, 128), 128)
            goal[lanes, :] = source[0:ROWS, lanes].T
            return 0

        lax.fori_loop(0, FEATURES // 128, step, 0)

    def cut_windows():
        window_arrived(0)
        lax.fori_loop(0, 44, cut_x, 0)

    def cut_cotangent():
        window_arrived(1)
        lax.fori_loop(0, 44, cut_c, 0)

    def project_all():
        lax.fori_loop(0, 2, project, 0)
        pltpu.make_async_copy(qkv_s, qkv_out, out_sem.at[0]).start()
        if weights:
            pltpu.make_async_copy(wq, wq_out, out_sem.at[1]).start()

    def turn_all():
        turn(n1, n1_turned)
        turn(o, o_turned)

    blocks = (slice(0, 352), slice(352, 704))

    def middle_begin():
        sums[...] = jnp.zeros_like(sums)
        up_sum[...] = jnp.zeros_like(up_sum)
        d_s[...] = jnp.zeros_like(d_s)

        def begin(i, _):
            at = pl.ds(pl.multiple_of(i * BLOCK, 16), BLOCK)
            mid = xw[at, :].astype(F32) + (jnp.dot(o[at, :], wo[...], preferred_element_type=F32) + as_row(out_bias))
            unit, _inverse = unit_of(mid)
            n1[at, :] = (unit * as_row(gain2) + as_row(shift2)).astype(BF)
            y_s[at, :] = mid + as_row(down_bias)
            dm[at, :] = mid
            return 0

        lax.fori_loop(0, ROWS // BLOCK, begin, 0)
        turn(n1, n2_turned)

    def chunk_out(which, step):
        lanes = pl.ds(pl.multiple_of(step * FEATURES, FEATURES), FEATURES)
        if which == 0:
            return pltpu.make_async_copy(g_chunk, g_out.at[lanes, :], out_sem.at[2])
        return pltpu.make_async_copy(dh_chunk, dh_out.at[:, lanes], out_sem.at[3])

    def middle_step(turn_index, _):
        for i, slot_acts in enumerate(middle_slots):
            if slot_acts:
                pl.when(turn_index == i)(functools.partial(run_all, slot_acts))
        step = lax.rem(turn_index, 2) * 2 + turn_index // 2
        lanes = pl.ds(pl.multiple_of(step * FEATURES, FEATURES), FEATURES)

        @pl.when(turn_index > 0)
        def _():
            chunk_out(0, 0).wait()
            chunk_out(1, 0).wait()

        for at in blocks:
            h = jnp.dot(n1[at, :], wu[:, lanes], preferred_element_type=F32) + up_bias[:, lanes]
            up = nt(cw[at, :], wd[lanes, :])
            phi = 0.5 * (1.0 + lax.erf(h * 0.7071067811865476))
            slope = phi + h * (jnp.exp(-0.5 * h * h) * 0.3989422804014327)
            active = (h * phi).astype(BF)
            back = (up * slope).astype(BF)
            g_s[at, :] = active
            dh_chunk[at, :] = back
            up_sum[:, lanes] += fold_rows(back.astype(F32))
            y_s[at, :] += jnp.dot(active, wd[lanes, :], preferred_element_type=F32)
            d_s[at, :] += nt(back, wu[:, lanes])
        for i in range(FEATURES // 128):
            g_chunk[128 * i : 128 * i + 128, 0:ROWS] = g_s[:, 128 * i : 128 * i + 128].T
        chunk_out(0, step).start()
        chunk_out(1, step).start()
        return 0

    def middle_end():
        def end(i, _):
            at = pl.ds(pl.multiple_of(i * BLOCK, 16), BLOCK)
            unit, inverse = unit_of(dm[at, :])
            grad = d_s[at, :].astype(BF).astype(F32)
            up = cw[at, :].astype(F32)
            grad_mid = up + norm_back(grad, unit, inverse, as_row(gain2))
            low_grad = grad_mid.astype(BF)
            dm[at, :] = grad_mid
            da[at, :] = low_grad
            do[at, :] = nt(low_grad, wo[...]).astype(BF)
            sums[0] += fold_rows(low_grad.astype(F32))
            sums[1] += fold_rows(up)
            sums[2] += fold_rows(grad * unit)
            sums[3] += fold_rows(grad)
            return 0

        spread_rows(y_s, rawx, row, col)
        raw_copy = pltpu.make_async_copy(rawx, raw_out, out_sem.at[4])
        raw_copy.start()
        lax.fori_loop(0, ROWS // BLOCK, end, 0)
        raw_copy.wait()

    acts = {"X": cut_windows, "P": project_all, "T": turn_all, "K": cut_cotangent, "M": middle_begin}
    acts["Wx"] = functools.partial(window_start, 0)
    acts["Wc"] = functools.partial(window_start, 1)
    if weights:
        acts.update({"a": along_col, "b": near_by, "1": first, "2": second, "3": third, "L": last})
        slots = plan_slots(OPEN_PLAN, acts)
    else:
        slots = plan_slots(("Wx", "Wc", "X", "P", *("|",) * 18, "T", "K", "M", *("|",) * 4), acts)
    o[...] = jnp.zeros_like(o)
    build_table(tab, rows_table, cols_table, take)
    row_bias[0] = as_row(query_bias)
    row_bias[1] = as_row(value_bias)
    run_all(slots[0])
    row_of = lax.broadcasted_iota(jnp.int32, (224, 1), 0)
    lane = lax.broadcasted_iota(jnp.int32, (1, 128), 1)
    key_place = lax.broadcasted_iota(jnp.int32, (224, 128), 0)
    key_lane = lax.broadcasted_iota(jnp.int32, (224, 128), 1)
    key_a, key_b = key_place // 16, key_place % 16

    def probs_copy(index):
        window, pair_index = index // 6, index % 6
        part = pl.ds(2 * pair_index, 2)
        return pltpu.make_async_copy(probs.at[window, part], probs_out.at[window, part], probs_sem.at[window, pair_index])

    def pair(index, _):
        for i, slot_acts in enumerate(slots[1:18]):
            if slot_acts:
                pl.when(index == i + 1)(functools.partial(run_all, slot_acts))
        window, pair_index = index // 6, index % 6
        start, tall, width = window_params(window, row, col)
        at = pl.ds(pl.multiple_of(start * 16, 16), 224)
        alive = (row_of // 16 < tall) & (row_of % 16 < width)
        lanes = lambda third: pl.ds(pl.multiple_of(third * FEATURES + pair_index * 128, 128), 128)
        q = jnp.where(alive, qkv_s[at, lanes(0)].astype(F32), 0.0)
        k = jnp.where(alive, qkv_s[at, lanes(1)].astype(F32), 0.0)
        v = jnp.where(alive, qkv_s[at, lanes(2)].astype(F32), row_bias[1, :, lanes(0)].astype(BF).astype(F32)).astype(BF)
        terms = jnp.dot(q.astype(BF), tab[...], preferred_element_type=F32)
        outs = []
        for parity in range(2):
            base = 64 if parity == 0 else 0
            own = (lane < 64) if parity == 0 else (lane >= 64)
            rel_rows = jnp.concatenate(
                [pltpu.roll(terms[16 * a : 16 * a + 16, 256 * parity : 256 * parity + 128], a, 1) for a in range(14)], axis=0
            )
            rel_cols = jnp.concatenate(
                [
                    pltpu.roll(terms[16 * a : 16 * a + 16, 256 * parity + 128 : 256 * parity + 256], 0, 1, stride=1, stride_axis=0)
                    for a in range(14)
                ],
                axis=0,
            )
            on = lane - base
            in_rows = ((on >= 0) & (on < 14)) | ((on >= 32) & (on < 46))
            in_cols = ((on >= 16) & (on < 30)) | ((on >= 48) & (on < 62))
            rel = jnp.where(in_rows, rel_rows, jnp.where(in_cols, rel_cols, 0.0))
            rough = rel.astype(BF).astype(F32)
            fine = jnp.where(on >= 32, rel - rough, rough)
            fine = jnp.where(on == 14, -1e30, fine)
            q_side = jnp.where(own, q * 0.125, fine).astype(BF)
            key_on = key_lane - base
            hot = jnp.where(
                key_on == 14,
                jnp.where(key_b >= 14, 1.0, 0.0),
                jnp.where(
                    (key_on % 32 < 14) & (key_a == key_on % 32),
                    1.0,
                    jnp.where((key_on % 32 >= 16) & (key_on % 32 < 30) & (key_b == key_on % 32 - 16), 1.0, 0.0),
                ),
            )
            k_side = jnp.where(own, k, hot).astype(BF)
            scores = lax.dot_general(q_side, k_side, (((1,), (1,)), ((), ())), preferred_element_type=F32)
            exponent = jnp.exp(scores - jnp.max(scores, axis=-1, keepdims=True))
            p = (exponent * (1.0 / jnp.sum(exponent, axis=-1, keepdims=True))).astype(BF)
            probs[window, 2 * pair_index + parity] = p
            outs.append(jnp.dot(p, v, preferred_element_type=F32))
        blended = jnp.where(lane < 64, outs[0], outs[1])
        out_lanes = pl.ds(pl.multiple_of(pair_index * 128, 128), 128)
        o_at = pl.ds(pl.multiple_of(start * 16, 16), 224)
        o[o_at, out_lanes] = jnp.where(alive, blended, 0.0).astype(BF)
        probs_copy(index).start()
        return 0

    pairs = window_count(row, col) * 6
    lax.fori_loop(0, pairs, pair, 0)
    run_all(slots[18])
    middle_slots = [[], *slots[19:22]]
    lax.fori_loop(0, 4, middle_step, 0)
    run_all(slots[22])
    middle_end()
    chunk_out(0, 0).wait()
    chunk_out(1, 0).wait()
    pltpu.make_async_copy(qkv_s, qkv_out, out_sem.at[0]).wait()
    if weights:
        pltpu.make_async_copy(wq, wq_out, out_sem.at[1]).wait()
        for copy in sent:
            copy().wait_send()
    lax.fori_loop(0, pairs, lambda index, _: (probs_copy(index).wait(), 0)[1], 0)
    window_left(0)
    window_left(1)


def open_windows(x, c, shards, gain, shift, query_bias, value_bias, rows_table, cols_table, out_bias, up_bias, down_bias, gain2, shift2):
    vm = pl.BlockSpec(memory_space=pltpu.VMEM)
    an = pl.BlockSpec(memory_space=pl.ANY)
    shape = jax.ShapeDtypeStruct
    dma = pltpu.SemaphoreType.DMA
    chunks = len(CHUNKS)
    weights = lax.axis_size("img") == 2
    if weights:
        given = list(shards)
    else:
        widened = [lax.all_gather(w, "img", axis=1, tiled=True) for w in shards]
        gathered = [lax.all_gather(w, ("row", "col"), axis=0, tiled=True) for w in widened]
        given = gathered
    raw = pltpu.VMEM((88, 3, 8, FEATURES), BF)
    outs = pl.pallas_call(
        functools.partial(open_kernel, weights),
        out_shape=[
            shape((ROWS, FEATURES), BF),
            shape((ROWS, FEATURES), BF),
            shape((FEATURES, ROWS), BF),
            shape((SPAN, 3 * FEATURES), BF),
            shape((4, 12, 224, 224), BF),
            shape((SPAN, FEATURES), BF),
            shape((FEATURES, ROWS), BF),
        ]
        + [
            shape((88, 3, 8, FEATURES), BF),
            shape((FEATURES, ROWS), BF),
            shape((FF, FEATURES), BF),
            shape((ROWS, FF), BF),
            shape((ROWS, FEATURES), BF),
            shape((SPAN, FEATURES), BF),
            shape((ROWS, FEATURES), F32),
            shape((4, 8, FEATURES), F32),
            shape((8, FF), F32),
        ]
        + ([shape((768, 2304), BF)] if weights else []),
        in_specs=[vm] * (14 + len(given)),
        out_specs=[vm, vm, vm, an, an, vm, vm, an, vm, an, an, vm, vm, vm, vm, vm] + ([an] if weights else []),
        scratch_shapes=[
            raw,
            raw,
            pltpu.VMEM((ROWS, FEATURES), BF),
            pltpu.VMEM((128, 512), BF),
            pltpu.VMEM((2, 1, FEATURES), F32),
            pltpu.VMEM((SPAN, 3 * FEATURES), BF),
            pltpu.VMEM((4, 12, 224, 224), BF),
            pltpu.VMEM((ROWS, FEATURES), F32),
            pltpu.VMEM((ROWS, FEATURES), F32),
            pltpu.VMEM((ROWS, FEATURES), BF),
            pltpu.VMEM((FEATURES, FEATURES), BF),
            pltpu.VMEM((ROWS, FEATURES), BF),
            dma((5,)),
            dma((4, 6)),
            dma((2, 2, 3)),
            dma((2, 4, 3)),
            dma((2, 2)),
        ]
        + ([pltpu.VMEM(s, BF) for s in WHOLES] + [dma((chunks, 16)), dma((chunks, 16)), dma((chunks,))] if weights else []),
        compiler_params=pltpu.CompilerParams(collective_id=0, has_side_effects=True, vmem_limit_bytes=67043328),
    )(x.reshape(2, 16, 2, 8, 768), c.reshape(2, 16, 2, 8, 768), gain, shift, query_bias, value_bias, rows_table, cols_table, takers(False), out_bias, up_bias, down_bias, gain2, shift2, *given)
    return list(outs) if weights else list(outs) + gathered[:1]


def attention_back(window, pair_index, probs_of, do, qkv, o, tab, value_bias, bias_sums, table_sums, row, col):
    row_of = lax.broadcasted_iota(jnp.int32, (224, 1), 0)
    lane = lax.broadcasted_iota(jnp.int32, (1, 128), 1)
    key_place = lax.broadcasted_iota(jnp.int32, (224, 128), 0)
    key_lane = lax.broadcasted_iota(jnp.int32, (224, 128), 1)
    key_a, key_b = key_place // 16, key_place % 16
    start, tall, width = window_params(window, row, col)
    at = pl.ds(pl.multiple_of(start * 16, 16), 224)
    inside = row_of // 16 < tall
    alive = inside & (row_of % 16 < width)
    lanes = lambda third: pl.ds(pl.multiple_of(third * FEATURES + pair_index * 128, 128), 128)
    old = [qkv[at, lanes(third)].astype(F32) for third in range(3)]
    q = jnp.where(alive, old[0], 0.0)
    k = jnp.where(alive, old[1], 0.0)
    v = jnp.where(alive, old[2], value_bias[:, lanes(0)].astype(BF).astype(F32))
    grad = jnp.where(alive, do[at, lanes(0)].astype(F32), 0.0)
    product = grad * jnp.where(alive, o[at, lanes(0)].astype(F32), 0.0)
    q_turned = q.T.astype(BF)
    grad_turned = grad.T.astype(BF)
    value_parts, key_parts, query_parts, table_parts = [], [], [], []
    for parity in range(2):
        base = 64 if parity == 0 else 0
        own = (lane < 64) if parity == 0 else (lane >= 64)
        half = slice(64 * parity, 64 * parity + 64)
        inner = jnp.sum(jnp.where(own, product, 0.0), axis=-1, keepdims=True)
        rough = inner.astype(BF).astype(F32)
        on = lane - base
        grad_side = jnp.where(own, grad, jnp.where(on == 0, rough, jnp.where(on == 1, inner - rough, 0.0))).astype(BF)
        v_side = jnp.where(own, v, jnp.where((on == 0) | (on == 1), -1.0, 0.0)).astype(BF)
        centered = nt(grad_side, v_side)
        p = probs_of(parity)
        ds = (p.astype(F32) * centered).astype(BF)
        value_parts.append(jnp.dot(grad_turned[half], p, preferred_element_type=F32))
        key_parts.append(jnp.dot(q_turned[half], ds, preferred_element_type=F32))
        key_on = key_lane - base
        hot = jnp.where(
            (key_on >= 0) & (key_on < 14) & (key_a == key_on),
            1.0,
            jnp.where((key_on >= 16) & (key_on < 30) & (key_b == 29 - key_on), 1.0, 0.0),
        )
        k_side = jnp.where(own, k * 0.125, hot).astype(BF)
        wide = jnp.dot(ds, k_side, preferred_element_type=F32)
        query_parts.append(wide)
        by_rows = jnp.where((on >= 0) & (on < 14), wide, 0.0)
        by_cols = jnp.where((on >= 16) & (on < 30), wide, 0.0)
        table_parts.append(jnp.concatenate([pltpu.roll(by_rows[16 * a : 16 * a + 16], (128 - a) % 128, 1) for a in range(14)], axis=0))
        table_parts.append(
            jnp.concatenate([pltpu.roll(by_cols[16 * a : 16 * a + 16], 0, 1, stride=1, stride_axis=0) for a in range(14)], axis=0)
        )
    turned = jnp.concatenate(table_parts, axis=1).astype(BF)
    dq = jnp.where(lane < 64, query_parts[0], query_parts[1]) + nt(turned, tab[...])
    table_sums[...] += jnp.dot(q_turned, turned, preferred_element_type=F32)
    dk = jnp.concatenate(key_parts, axis=0).T * 0.125
    dv = jnp.concatenate(value_parts, axis=0).T.astype(BF).astype(F32)
    dq = jnp.where(alive, dq, 0.0).astype(BF).astype(F32)
    bias_sums[0, :, lanes(0)] += fold_rows(dq)
    bias_sums[1, :, lanes(0)] += fold_rows(dv)
    for third, new in enumerate((dq, dk, dv)):
        qkv[at, lanes(third)] = jnp.where(alive, new, jnp.where(inside, 0.0, old[third])).astype(BF)


def clear_idle(qkv, row, col):
    wide = row >= 2
    limit = jnp.where(wide, jnp.where(col == 3, 44, 36), 42)
    for a in range(36, 44):

        @pl.when(a >= limit)
        def _():
            qkv[16 * a : 16 * a + 16, :] = jnp.zeros((16, 3 * FEATURES), BF)


def plain_back_kernel(do, probs, qkv, o, value_bias, rows_table, cols_table, take, dqkv, bias_sums, table_sums, tab, row_bias):
    row, col = lax.axis_index("row"), lax.axis_index("col")
    build_table(tab, rows_table, cols_table, take)
    row_bias[...] = as_row(value_bias)
    dqkv[...] = qkv[...]
    clear_idle(dqkv, row, col)
    bias_sums[...] = jnp.zeros_like(bias_sums)
    table_sums[...] = jnp.zeros_like(table_sums)

    def pair(index, _):
        window, pair_index = index // 6, index % 6
        attention_back(
            window,
            pair_index,
            lambda parity: probs[window, 2 * pair_index + parity],
            do,
            dqkv,
            o,
            tab,
            row_bias,
            bias_sums,
            table_sums,
            row,
            col,
        )
        return 0

    lax.fori_loop(0, window_count(row, col) * 6, pair, 0)


def plain_back(do, probs, qkv, o, value_bias, rows_table, cols_table):
    vm = pl.BlockSpec(memory_space=pltpu.VMEM)
    shape = jax.ShapeDtypeStruct
    return pl.pallas_call(
        plain_back_kernel,
        out_shape=[shape((SPAN, 3 * FEATURES), BF), shape((2, 8, FEATURES), F32), shape((128, 512), F32)],
        in_specs=[vm] * 8,
        out_specs=[vm] * 3,
        scratch_shapes=[pltpu.VMEM((128, 512), BF), pltpu.VMEM((1, FEATURES), F32)],
        compiler_params=pltpu.CompilerParams(vmem_limit_bytes=62 << 20),
    )(do, probs, qkv, o, value_bias, rows_table, cols_table, takers(True))


WHOLES = ((768, 2304), (768, 768), (768, 3072), (3072, 768))
SUM_CHUNKS = ((1, 0, 384), (3, 0, 128), (3, 128, 384), (2, 0, 768), (2, 768, 1536), (0, 0, 384), (0, 384, 768), (0, 768, 1152))


def pair_lanes(j, im):
    if im == 0:
        return (128 * j, FEATURES + 128 * j, 128 * (j + 3))
    return (2 * FEATURES + 128 * j, FEATURES + 128 * (j + 3), 2 * FEATURES + 128 * (j + 3))


def land_shapes(chunks):
    lands = []
    for w, lo, hi in chunks:
        kb, width = WHOLES[w][0] // 4, hi - lo
        lands += [
            pltpu.VMEM((2, 2, kb, width), BF),
            pltpu.VMEM((2, kb // 2, width), BF),
            pltpu.VMEM((2, kb // 2, width), BF),
            pltpu.VMEM((2, kb // 2, width), BF),
            pltpu.VMEM((3, kb // 4, width), BF),
        ]
    return lands


def reducers(chunks, full, left_turned, right_side, grads, land_refs, wsend, wrecv):
    img, row, col = place()
    y_row = lax.rem(row + 2, 4)
    core_row = row + 1 - 2 * lax.rem(row, 2)
    core_y = lax.rem(core_row + 2, 4)
    other = 1 - img
    far_col, near_col = lax.rem(col + 2, 4), col + 1 - 2 * lax.rem(col, 2)
    lands = [land_refs[5 * n : 5 * n + 5] for n in range(len(chunks))]
    sent = []

    def size(n):
        w, lo, hi = chunks[n]
        return WHOLES[w][0] // 4, WHOLES[w][1] // 2, lo, hi - lo

    def block(n, rw, im, half=None):
        kb, nb, lo, width = size(n)
        cols = pl.ds(pl.multiple_of(im * nb + lo, 128), width)
        if half is None:
            return full[chunks[n][0]].at[pl.ds(pl.multiple_of(rw * kb, kb), kb), cols]
        return full[chunks[n][0]].at[pl.ds(pl.multiple_of(rw * kb + half * (kb // 2), kb // 2), kb // 2), cols]

    def shard(n, cl):
        kb, nb, lo, width = size(n)
        cols = pl.ds(pl.multiple_of(img * nb + lo, 128), width)
        return full[chunks[n][0]].at[pl.ds(pl.multiple_of(row * kb + cl * (kb // 4), kb // 4), kb // 4), cols]

    def push(n, k, src, dst, target):
        def copy():
            return pltpu.make_async_remote_copy(
                src_ref=src(), dst_ref=dst(), send_sem=wsend.at[n, k], recv_sem=wrecv.at[n, k], device_id=target(), device_id_type=MESH
            )

        copy().start()
        sent.append(copy)

    def arrive(n, k, ref):
        pltpu.make_async_copy(ref, ref, wrecv.at[n, k]).wait()

    def add(goal, part, rows):
        def step(i, _):
            at = pl.ds(pl.multiple_of(i * 48, 16), 48)
            goal[at, :] = (goal[at, :].astype(F32) + part[at, :].astype(F32)).astype(BF)
            return 0

        lax.fori_loop(0, rows // 48, step, 0)

    def product(n, rw):
        w = chunks[n][0]
        kb, nb, lo, width = size(n)
        rows = pl.ds(pl.multiple_of(rw * kb, kb), kb)
        for im in range(2):
            at = slice(im * nb + lo, im * nb + lo + width)
            if w == 0:
                right = jnp.concatenate([right_side[0][0:ROWS, p : p + 128] for p in pair_lanes(lo // 384, im)], axis=1)
            else:
                right = right_side[w][0:ROWS, at]
            full[w][rows, at] = jnp.dot(left_turned[w](rw, kb), right, preferred_element_type=F32).astype(BF)

    def pair_stage(n):
        land = lands[n][0]
        for j, rw in enumerate((core_row, core_y)):
            product(n, rw)
            for im in range(2):
                push(n, 2 * j + im, functools.partial(block, n, rw, im), lambda j=j, im=im: land.at[j, im], lambda: {"row": core_row})
        for rw in (row, y_row):
            product(n, rw)

    def first(n):
        kb, nb, lo, width = size(n)
        for j, rw in enumerate((row, y_row)):
            for im in range(2):
                arrive(n, 2 * j + im, lands[n][0].at[j, im])
                add(block(n, rw, im), lands[n][0].at[j, im], kb)
        for im in range(2):
            push(n, 4 + im, functools.partial(block, n, y_row, im, 0), lambda im=im: lands[n][1].at[im], lambda: {"row": y_row})
        push(n, 6, functools.partial(block, n, row, other, 1), lambda: lands[n][2].at[0], lambda: {"img": other})
        push(n, 7, functools.partial(block, n, y_row, other, 1), lambda: lands[n][2].at[1], lambda: {"img": other})

    def second(n):
        kb, nb, lo, width = size(n)
        for im in range(2):
            arrive(n, 4 + im, lands[n][1].at[im])
            add(block(n, row, im, 0), lands[n][1].at[im], kb // 2)
        push(n, 8, functools.partial(block, n, row, other, 0), lambda: lands[n][3].at[0], lambda: {"img": other})
        for j, rw in enumerate((row, y_row)):
            arrive(n, 6 + j, lands[n][2].at[j])
            add(block(n, rw, img, 1), lands[n][2].at[j], kb // 2)
        push(n, 9, functools.partial(block, n, y_row, img, 1), lambda: lands[n][3].at[1], lambda: {"row": y_row})

    def third(n):
        kb, nb, lo, width = size(n)
        for half in range(2):
            arrive(n, 8 + half, lands[n][3].at[half])
            add(block(n, row, img, half), lands[n][3].at[half], kb // 2)
        push(n, 10, lambda: shard(n, near_col), lambda: lands[n][4].at[0], lambda: {"col": near_col})
        push(n, 11, lambda: shard(n, 3 - col), lambda: lands[n][4].at[1], lambda: {"col": near_col})

    def fourth(n):
        kb = size(n)[0]
        arrive(n, 11, lands[n][4].at[1])
        add(shard(n, far_col), lands[n][4].at[1], kb // 4)
        push(n, 12, lambda: shard(n, far_col), lambda: lands[n][4].at[2], lambda: {"col": far_col})

    def fifth(n):
        w, lo, hi = chunks[n]
        arrive(n, 10, lands[n][4].at[0])
        arrive(n, 12, lands[n][4].at[2])
        mine = shard(n, col)

        def step(part, _):
            at = pl.ds(pl.multiple_of(part * 48, 16), 48)
            total = mine[at, :].astype(F32) + lands[n][4][0, at, :].astype(F32) + lands[n][4][2, at, :].astype(F32)
            if w > 0:
                grads[w][at, lo:hi] = total
            else:
                for im in range(2):

                    @pl.when(img == im)
                    def _():
                        for i, p in enumerate(pair_lanes(lo // 384, im)):
                            lane = p - 1152 * im
                            grads[0][at, lane : lane + 128] = total[:, 128 * i : 128 * i + 128]

            return 0

        lax.fori_loop(0, WHOLES[w][0] // 16 // 48, step, 0)

    return pair_stage, first, second, third, fourth, fifth, sent


def table_taker():
    take = relative_layout(True)
    out = np.zeros((4, 128, 128), np.float32)
    for parity in range(2):
        for which in range(2):
            out[2 * parity + which, :, 64 * which : 64 * which + 27] = take[parity, which].T
    return out


def source_tiles(row, col):
    wide = row >= 2
    side_row = row + 2 * (1 - col // 2)
    table = []
    for image in range(2):
        table.append((image, 0, image, row - 1, col, row > 0))
        table.append((image, 1, image, row, col - 1, col > 0))
        table.append((image, 2, image, row - 1, col - 1, (row > 0) & (col > 0)))
    third_image = jnp.where(wide, 3 - row, 1 - lax.rem(col, 2))
    table.append((2, 0, third_image, 3, col, wide))
    table.append((2, 1, third_image, side_row, 3, jnp.logical_not(wide)))
    table.append((2, 2, third_image, jnp.where(wide, 3, side_row - 1), jnp.where(wide, col - 1, 3), jnp.where(wide, col, side_row) > 0))
    table.append((3, 2, 3 - row, 3, 3, wide & (col == 3)))
    return table


CLOSE_PLAN = ("p1", "p2", "11", "|", "|", "12", "p4", "|", "|", "14", "21", "|", "p0", "|", "|", "p3", "|", "22", "|", "p5", "24", "|", "10", "31", "|", "|", "|", "|", "|", "|", "|", "13", "|", "32", "41", "15", "34", "G0", "G1", "G2", "42", "p7", "G3", "S", "p6", "23", "s0", "25", "20", "17", "16", "30", "s1", "44", "35", "27", "40", "52", "33", "26", "s2", "45", "37", "51", "50", "36", "s3", "43", "54", "47", "46", "53", "57", "55", "56", "s4")


def returns(raws, landing, send, recv, row, col):
    def each(t, act):
        for slot, kind, image, tile_row, tile_col, present in source_tiles(row, col):
            here = (tile_row == row) & (tile_col == col)
            act(slot, kind, image, tile_row, tile_col, present & here, present & jnp.logical_not(here))

    def start(t):
        def act(slot, kind, image, tile_row, tile_col, local, remote):
            @pl.when(local)
            def _():
                pltpu.make_async_copy(
                    window_part(raws[t], slot, kind), landing[t][kind].at[image], recv.at[t, image, kind]
                ).start()

            @pl.when(remote)
            def _():
                hop(t, slot, kind, image, tile_row, tile_col).start()

        each(t, act)

    def hop(t, slot, kind, image, tile_row, tile_col):
        return pltpu.make_async_remote_copy(
            src_ref=window_part(raws[t], slot, kind),
            dst_ref=landing[t][kind].at[image],
            send_sem=send.at[t, slot, kind],
            recv_sem=recv.at[t, image, kind],
            device_id={"row": jnp.maximum(tile_row, 0), "col": jnp.maximum(tile_col, 0)},
            device_id_type=MESH,
        )

    def arrived(t):
        for image in range(2):
            for kind in range(3):
                goal = landing[t][kind].at[image]
                pltpu.make_async_copy(goal, goal, recv.at[t, image, kind]).wait()

    def left(t):
        def act(slot, kind, image, tile_row, tile_col, local, remote):
            @pl.when(remote)
            def _():
                hop(t, slot, kind, image, tile_row, tile_col).wait_send()

        each(t, act)

    return start, arrived, left


def merge_tiles(owns, landing, goals, row, col):
    places = lax.broadcasted_iota(jnp.int32, (16, 1), 0)
    in_left = places < 14 - 2 * col

    def rows16(values):
        return values.reshape(16, FEATURES).astype(F32)

    def right_half(values):
        low = values.reshape(8, FEATURES).astype(F32)
        return jnp.concatenate([low, low], axis=0)

    for image in range(2):

        def merge(tile_row, _):
            top = tile_row < 14 - 2 * row
            upper = jnp.minimum(tile_row, 13)
            lower = jnp.maximum(tile_row - 8, 0)
            for own, (below, right, both), goal in zip(owns, landing, goals):
                stacked = jnp.where(top, rows16(own(image, upper)), rows16(below[image, lower]))
                beside = jnp.where(top, right_half(right[image, upper]), right_half(both[image, lower]))
                goal[image, tile_row] = jnp.where(in_left, stacked, beside).astype(goal.dtype)
            return 0

        lax.fori_loop(0, 16, merge, 0)


def input_grad(at, dqkv, wq, xw, image_grad, gain, norm_sums):
    grad = nt(dqkv[at, :], wq).astype(BF).astype(F32)
    unit, inverse = unit_of(xw[at, :].astype(F32))
    image_grad[at, :] += norm_back(grad, unit, inverse, as_row(gain))
    norm_sums[0] += fold_rows(grad * unit)
    norm_sums[1] += fold_rows(grad)


def plain_close_kernel(dqkv, xw, dm, raw_r, wq, gain, out, grad_out, norm_sums, image_grad, raw_g, *refs):
    img, row, col = place()
    landing, (send, recv) = (refs[:3], refs[3:6]), refs[6:]
    greet(img, row, col, False)
    start, arrived, left = returns((raw_r, raw_g), landing, send, recv, row, col)
    start(0)
    norm_sums[...] = jnp.zeros_like(norm_sums)
    image_grad[...] = dm[...]

    def step(i, _):
        input_grad(pl.ds(pl.multiple_of(i * BLOCK, 16), BLOCK), dqkv, wq[...], xw, image_grad, gain, norm_sums)
        return 0

    lax.fori_loop(0, ROWS // BLOCK, step, 0)
    spread_rows(image_grad, raw_g, row, col)
    start(1)
    for t in range(2):
        arrived(t)
    owns = [lambda image, upper, raw=raw: raw[image * 22 + 8 + upper, 1:3] for raw in (raw_r, raw_g)]
    merge_tiles(owns, landing, (out, grad_out), row, col)
    for t in range(2):
        left(t)


PIECES = [(2, 8, 2, 8, FEATURES), (2, 14, 1, 8, FEATURES), (2, 8, 1, 8, FEATURES)]


def plain_close(dqkv, xw, dm, raw_r, wq, gain):
    vm = pl.BlockSpec(memory_space=pltpu.VMEM)
    shape = jax.ShapeDtypeStruct
    dma = pltpu.SemaphoreType.DMA
    pieces = [pltpu.VMEM(s, BF) for s in PIECES]
    return pl.pallas_call(
        plain_close_kernel,
        out_shape=[shape((2, 16, 16, FEATURES), BF), shape((2, 16, 16, FEATURES), F32), shape((2, 8, FEATURES), F32)],
        in_specs=[vm] * 6,
        out_specs=[vm] * 3,
        scratch_shapes=[pltpu.VMEM((ROWS, FEATURES), F32), pltpu.VMEM((88, 3, 8, FEATURES), BF)]
        + pieces
        + pieces
        + [dma((2, 4, 3)), dma((2, 2, 3))],
        compiler_params=pltpu.CompilerParams(collective_id=2, has_side_effects=True, vmem_limit_bytes=67043328),
    )(dqkv, xw, dm, raw_r, wq, gain)


def back_kernel(
    do, o, value_bias, rows_table, cols_table, take, o_turned, da, n2_turned, cw, xw, n1_turned, gain, sums, up_sum, taker, probs, qkv_in, dh_in, g_in, dm_in, wq_in, raw_r, *refs
):
    out, grad_out, gq, go, gu, gd, small_out, table_out = refs[:8]
    qkv, probs_s, image_grad, shared_h, shared_g, own_r = refs[8:14]
    bias_sums, table_sums, norm_sums, tab, row_bias = refs[14:19]
    landing = (refs[19:22], refs[22:25])
    full = refs[25:29]
    small, table, small_land, table_land, small_z, table_z = refs[29:35]
    count = len(SUM_CHUNKS)
    lands = refs[35 : 35 + 5 * count]
    send, recv, load_sem, probs_sem, wsend, wrecv, ssend, srecv = refs[35 + 5 * count :]
    img, row, col = place()
    y_row = lax.rem(row + 2, 4)
    core_row = row + 1 - 2 * lax.rem(row, 2)
    other = 1 - img
    copies = []

    def load(i):
        pairs = (
            (dh_in, shared_h.at[pl.ds(0, ROWS)]),
            (g_in, shared_g),
            (qkv_in, qkv),
            (dm_in, image_grad),
            (wq_in, shared_h.at[:, pl.ds(0, 3 * FEATURES)]),
            (raw_r.at[pl.ds(8, 14), pl.ds(1, 2)], own_r.at[0]),
            (raw_r.at[pl.ds(30, 14), pl.ds(1, 2)], own_r.at[1]),
        )
        return pltpu.make_async_copy(pairs[i][0], pairs[i][1], load_sem.at[i])

    for i in (1, 2, 0, 3, 5, 6):
        load(i).start()
    windows = window_count(row, col)

    def fetch(k, window, slot):
        pair_index = lax.rem(k, 2) * 3 + k // 2
        return pltpu.make_async_copy(probs.at[window, pl.ds(2 * pair_index, 2)], probs_s.at[slot], probs_sem.at[slot])

    fetch(0, 0, 0).start()
    greet(img, row, col)
    start, arrived, left = returns((raw_r, shared_g), landing, send, recv, row, col)
    start(0)

    def turned_rows(ref):
        return lambda rw, kb: ref[pl.ds(pl.multiple_of(rw * kb, kb), kb), :]

    def turned_g(rw, kb):
        return shared_g[pl.ds(pl.multiple_of(rw * 32, 32), 32)].reshape(FEATURES, FEATURES)[:, 0:ROWS]

    pair_stage, first, second, third, fourth, fifth, sent = reducers(
        SUM_CHUNKS,
        full,
        (turned_rows(n1_turned), turned_rows(o_turned), turned_rows(n2_turned), turned_g),
        (qkv, da, shared_h, cw),
        (gq, go, gu, gd),
        lands,
        wsend,
        wrecv,
    )
    bias_sums[...] = jnp.zeros_like(bias_sums)
    table_sums[...] = jnp.zeros_like(table_sums)
    norm_sums[...] = jnp.zeros_like(norm_sums)
    build_table(tab, rows_table, cols_table, take)
    row_bias[...] = as_row(value_bias)
    load(1).wait()

    def grad_rows(i):
        if i == 0:
            load(4).start()
            load(3).wait()
            load(4).wait()
        input_grad(pl.ds(i * BLOCK, BLOCK), qkv, shared_h[:, 0 : 3 * FEATURES], xw, image_grad, gain, norm_sums)

    def send_grad():
        spread_rows(image_grad, shared_g, row, col)
        start(1)

    def over_rows(values):
        return jnp.sum(values, axis=0, keepdims=True)

    def gather_small():
        small[0] = jnp.zeros((16, FEATURES), F32)
        lines = [bias_sums[0], bias_sums[1], sums[0], sums[1], norm_sums[0], norm_sums[1], sums[2], sums[3]]
        for i, values in enumerate(lines):
            small[0, i : i + 1, :] = over_rows(values)
        for i in range(4):
            small[0, 8 + i : 9 + i, :] = over_rows(up_sum[:, i * FEATURES : (i + 1) * FEATURES])
        exact = lax.Precision.HIGHEST
        total = jnp.zeros((64, 128), F32)
        for parity in range(2):
            for which in range(2):
                part = table_sums[64 * parity : 64 * parity + 64, 256 * parity + 128 * which : 256 * parity + 128 * which + 128]
                total = total + jnp.dot(part, taker[2 * parity + which], precision=exact, preferred_element_type=F32)
        table[0] = total

    hops = ({"row": core_row}, {"row": y_row}, {"img": other})

    def small_push(k, src, dst, target):
        c = pltpu.make_async_remote_copy(
            src_ref=src, dst_ref=dst, send_sem=ssend.at[k], recv_sem=srecv.at[k], device_id=target, device_id_type=MESH
        )
        c.start()
        copies.append(c)
        return c

    def small_step(i):
        if i == 0:
            gather_small()
        if 0 < i <= 3:
            for k, (acc, land) in enumerate(((small, small_land), (table, table_land))):
                pltpu.make_async_copy(land.at[i - 1], land.at[i - 1], srecv.at[2 * (i - 1) + k]).wait()
                acc[i] = acc[i - 1] + land[i - 1]
        if i < 3:
            for k, (acc, land) in enumerate(((small, small_land), (table, table_land))):
                small_push(2 * i + k, acc.at[i], land.at[i], hops[i])
        if i == 3:
            small_z[col] = small[3]
            table_z[col] = table[3]
            for d in range(1, 4):
                cl = lax.rem(col + d, 4)
                small_push(4 + 2 * d, small.at[3], small_z.at[col], {"col": cl})
                small_push(5 + 2 * d, table.at[3], table_z.at[col], {"col": cl})
        if i == 4:
            for d in range(1, 4):
                cl = lax.rem(col + 4 - d, 4)
                pltpu.make_async_copy(small_z.at[cl], small_z.at[cl], srecv.at[4 + 2 * d]).wait()
                pltpu.make_async_copy(table_z.at[cl], table_z.at[cl], srecv.at[5 + 2 * d]).wait()
            small_out[...] = (small_z[0] + small_z[1]) + (small_z[2] + small_z[3])
            table_out[...] = (table_z[0] + table_z[1]) + (table_z[2] + table_z[3])

    acts = {"p": pair_stage, "1": first, "2": second, "3": third, "4": fourth, "5": fifth, "G": grad_rows, "s": small_step, "S": send_grad}
    slots = plan_slots(CLOSE_PLAN, acts)
    run_all(slots[0])
    load(2).wait()
    clear_idle(qkv, row, col)
    load(0).wait()

    def head_pair(k, _):
        pair_index = lax.rem(k, 2) * 3 + k // 2

        def each(window, _):
            for i, slot_acts in enumerate(slots[1:-1]):
                if slot_acts:
                    pl.when((k == (i + 1) // 3) & (window == (i + 1) % 3))(functools.partial(run_all, slot_acts))
            turn_count = k * windows + window
            slot = lax.rem(turn_count, 2)
            fetch(k, window, slot).wait()
            wrap = window + 1 == windows
            next_k = jnp.where(wrap, k + 1, k)

            @pl.when(next_k < 6)
            def _():
                fetch(next_k, jnp.where(wrap, 0, window + 1), 1 - slot).start()

            attention_back(
                window,
                pair_index,
                lambda parity: probs_s[slot, parity],
                do,
                qkv,
                o,
                tab,
                row_bias,
                bias_sums,
                table_sums,
                row,
                col,
            )
            return 0

        lax.fori_loop(0, windows, each, 0)
        return 0

    lax.fori_loop(0, 6, head_pair, 0)
    run_all(slots[-1])
    arrived(0)
    load(5).wait()
    load(6).wait()
    merge_tiles([lambda image, upper: own_r[image, upper]], landing[:1], (out,), row, col)
    arrived(1)
    merge_tiles([lambda image, upper: shared_g[image * 22 + 8 + upper, 1:3]], landing[1:], (grad_out,), row, col)
    left(0)
    left(1)
    for c in copies:
        c.wait_send()
    for copy in sent:
        copy().wait_send()


def back(do, o, value_bias, rows_table, cols_table, o_turned, da, n2_turned, cw, xw, n1_turned, gain, sums, up_sum, probs, qkv, dh, g, dm, wq, raw_r):
    vm = pl.BlockSpec(memory_space=pltpu.VMEM)
    an = pl.BlockSpec(memory_space=pl.ANY)
    shape = jax.ShapeDtypeStruct
    dma = pltpu.SemaphoreType.DMA
    pieces = [pltpu.VMEM(s, BF) for s in PIECES]
    count = len(SUM_CHUNKS)
    return pl.pallas_call(
        back_kernel,
        out_shape=[shape((2, 16, 16, FEATURES), BF), shape((2, 16, 16, FEATURES), BF)]
        + [shape((k // 16, n // 2), F32) for k, n in WHOLES]
        + [shape((16, FEATURES), F32), shape((64, 128), F32)],
        in_specs=[vm] * 16 + [an] * 7,
        out_specs=[vm] * 8,
        scratch_shapes=[
            pltpu.VMEM((SPAN, 3 * FEATURES), BF),
            pltpu.VMEM((2, 2, 224, 224), BF),
            pltpu.VMEM((ROWS, FEATURES), F32),
            pltpu.VMEM((FEATURES, 4 * FEATURES), BF),
            pltpu.VMEM((128, 3, 8, FEATURES), BF),
            pltpu.VMEM((2, 14, 2, 8, FEATURES), BF),
            pltpu.VMEM((2, 8, FEATURES), F32),
            pltpu.VMEM((128, 512), F32),
            pltpu.VMEM((2, 8, FEATURES), F32),
            pltpu.VMEM((128, 512), BF),
            pltpu.VMEM((1, FEATURES), F32),
        ]
        + pieces
        + pieces
        + [pltpu.VMEM(s, BF) for s in WHOLES]
        + [
            pltpu.VMEM((4, 16, FEATURES), F32),
            pltpu.VMEM((4, 64, 128), F32),
            pltpu.VMEM((3, 16, FEATURES), F32),
            pltpu.VMEM((3, 64, 128), F32),
            pltpu.VMEM((4, 16, FEATURES), F32),
            pltpu.VMEM((4, 64, 128), F32),
        ]
        + land_shapes(SUM_CHUNKS)
        + [dma((2, 4, 3)), dma((2, 2, 3)), dma((7,)), dma((2,)), dma((count, 13)), dma((count, 13)), dma((12,)), dma((12,))],
        compiler_params=pltpu.CompilerParams(collective_id=1, has_side_effects=True, vmem_limit_bytes=67043328),
    )(
        do, o, value_bias, rows_table, cols_table, takers(True), o_turned, da, n2_turned, cw, xw, n1_turned, gain, sums, up_sum, jnp.asarray(table_taker()),
        probs, qkv, dh, g.reshape(128, 3, 8, FEATURES), dm, wq, raw_r,
    )


def deliver_kernel(out_in, grad_in, *refs):
    sums_in, (small, table), outs = refs[:4], refs[4:6], refs[6:]
    outs[0][...] = out_in[...]

    def widen(i, _):
        outs[1][i // 16, i % 16] = grad_in[i // 16, i % 16].astype(F32)
        return 0

    lax.fori_loop(0, 32, widen, 0)
    for given, goal in zip(sums_in, outs[2:6]):
        goal[...] = given[...]
    for i, goal in zip((0, 1, 2, None, 3, 4, 5, 6, 7), outs[6:15]):
        if i is None:
            goal[...] = jnp.concatenate([small[8 + j : 9 + j, :] for j in range(4)], axis=1).reshape(4 * FEATURES)
        else:
            goal[...] = small[i : i + 1, :].reshape(FEATURES)
    turned = table[...].T
    outs[15][...] = turned[0:27, :]
    outs[16][...] = turned[64:91, :]


def deliver(*given):
    vm = pl.BlockSpec(memory_space=pltpu.VMEM)
    shape = jax.ShapeDtypeStruct
    lengths = [FEATURES] * 3 + [4 * FEATURES] + [FEATURES] * 5
    outs = [shape((2, 16, 16, FEATURES), BF), shape((2, 16, 16, FEATURES), F32)] + [shape((k // 16, n // 2), F32) for k, n in WHOLES]
    outs += [shape((n,), F32) for n in lengths] + [shape((27, 64), F32)] * 2
    return pl.pallas_call(deliver_kernel, out_shape=outs, in_specs=[vm] * 8, out_specs=[vm] * len(outs))(*given)


def on_device(
    image_in,
    cotangent,
    qkv_weight,
    out_weight,
    up_weight,
    down_weight,
    query_bias,
    value_bias,
    out_bias,
    up_bias,
    down_bias,
    first_gain,
    first_shift,
    second_gain,
    second_shift,
    rows_table,
    cols_table,
):
    line = lambda v: v.reshape(1, -1)
    xw, cw, n1_turned, qkv, probs, o, o_turned, raw_r, n2_turned, g_turned, dh, da, do, dm, sums, up_sum, wq = open_windows(
        image_in,
        cotangent,
        (qkv_weight, out_weight, up_weight, down_weight),
        first_gain,
        first_shift,
        query_bias,
        value_bias,
        rows_table,
        cols_table,
        out_bias,
        line(up_bias),
        down_bias,
        second_gain,
        second_shift,
    )
    if lax.axis_size("img") == 2:
        return tuple(
            deliver(
                *back(
                    do, o, value_bias, rows_table, cols_table, o_turned, da, n2_turned, cw, xw, n1_turned, first_gain, sums, up_sum,
                    probs, qkv, dh, g_turned, dm, wq, raw_r,
                )
            )
        )
    dqkv, bias_sums, table_sums = plain_back(do, probs, qkv, o, value_bias, rows_table, cols_table)
    image_out, image_grad, norm_sums = plain_close(dqkv, xw, dm, raw_r, wq, first_gain)
    dot = lambda a, b: jnp.dot(a, b, preferred_element_type=F32)
    totals = (dot(n1_turned, dqkv[:ROWS]), dot(o_turned, da), dot(n2_turned, dh), dot(g_turned[:, :ROWS], cw))
    shard_sums = []
    for total in totals:
        part = lax.psum_scatter(total.astype(BF), ("row", "col"), scatter_dimension=0, tiled=True)
        shard_sums.append(lax.psum_scatter(part, "img", scatter_dimension=1, tiled=True).astype(F32))
    rows_grad, cols_grad = table_grads(table_sums)
    small_sums = lax.psum(
        tuple(jnp.sum(bias_sums, axis=1))
        + (jnp.sum(sums[0], axis=0), jnp.sum(up_sum, axis=0), jnp.sum(sums[1], axis=0))
        + tuple(jnp.sum(norm_sums, axis=1))
        + (jnp.sum(sums[2], axis=0), jnp.sum(sums[3], axis=0), rows_grad, cols_grad),
        ("img", "row", "col"),
    )
    return (image_out, image_grad, *shard_sums, *small_sums)


def solution(mesh):
    tiles = P("img", "row", "col", None)
    shards = P(("row", "col"), "img")
    return jax.shard_map(
        on_device,
        mesh=mesh,
        in_specs=(tiles,) * 2 + (shards,) * 4 + (P(),) * 11,
        out_specs=(tiles,) * 2 + (shards,) * 4 + (P(),) * 11,
        check_vma=False,
    )
```

```python
import functools

import jax
import jax.numpy as jnp
import numpy as np
from jax import lax
from jax.experimental import pallas as pl
from jax.experimental.pallas import tpu as pltpu
from jax.sharding import PartitionSpec as P

MESH = pl.DeviceIdType.MESH


def place():
    return lax.axis_index("img"), lax.axis_index("row"), lax.axis_index("col")


def side_owner(window_row, image):
    return lax.rem(window_row, 2), 3 - image - 2 * (window_row // 2)


def piece_target(kind, image, row, col):
    last_row, last_col = row == 3, col == 3
    side_row, side_col = side_owner(row, image)
    next_row, next_col = side_owner(lax.rem(row + 1, 4), image)
    if kind == 0:
        return (jnp.where(last_row, 3 - image, row + 1), col, jnp.where(last_row, 2, image))
    if kind == 1:
        return (jnp.where(last_col, side_row, row), jnp.where(last_col, side_col, col + 1), jnp.where(last_col, 2, image))
    target_row = jnp.where(last_row, 3 - image, jnp.where(last_col, next_row, row + 1))
    target_col = jnp.where(last_col, jnp.where(last_row, 3, next_col), col + 1)
    slot = jnp.where(last_row & last_col, 3, jnp.where(last_row | last_col, 2, image))
    return (target_row, target_col, slot)


def arrivals(row, col):
    wide = row >= 2
    side_row = row + 2 * (1 - col // 2)
    table = []
    for image in range(2):
        table.append((image, 0, row > 0))
        table.append((image, 1, col > 0))
        table.append((image, 2, (row > 0) & (col > 0)))
    table.append((2, 0, wide))
    table.append((2, 1, jnp.logical_not(wide)))
    table.append((2, 2, jnp.where(wide, col, side_row) > 0))
    table.append((3, 2, wide & (col == 3)))
    return table


def tile_part(ref, image, kind):
    if kind == 0:
        return ref.at[image, pl.ds(8, 8), pl.ds(0, 2)]
    if kind == 1:
        return ref.at[image, pl.ds(0, 14), pl.ds(1, 1)]
    return ref.at[image, pl.ds(8, 8), pl.ds(1, 1)]


def window_part(ref, slot, kind):
    if kind == 0:
        return ref.at[pl.ds(slot * 22, 8), pl.ds(1, 2)]
    if kind == 1:
        return ref.at[pl.ds(slot * 22 + 8, 14), pl.ds(0, 1)]
    return ref.at[pl.ds(slot * 22, 8), pl.ds(0, 1)]


def greet(img, row, col, pairs=True):
    barrier = pltpu.get_barrier_semaphore()
    for row_step in range(4):
        for col_step in range(4):
            if row_step or col_step:
                pl.semaphore_signal(
                    barrier,
                    inc=1,
                    device_id={"row": lax.rem(row + row_step, 4), "col": lax.rem(col + col_step, 4)},
                    device_id_type=MESH,
                )
    if pairs:
        pl.semaphore_signal(barrier, inc=1, device_id={"img": 1 - img}, device_id_type=MESH)
    pl.semaphore_wait(barrier, 16 if pairs else 15)


CHUNKS = ((0, 0, 640), (0, 640, 1152), (1, 0, 384), (2, 0, 768), (2, 768, 1536), (3, 0, 128), (3, 128, 384))


def links(shards, fulls, wsend, wrecv, wloc):
    img, row, col = place()
    y_row = lax.rem(row + 2, 4)
    core_row = row + 1 - 2 * lax.rem(row, 2)
    other = 1 - img
    sent = []

    def rows_of(w, rw, half=None):
        kb = fulls[w].shape[0] // 4
        if half is None:
            return pl.ds(pl.multiple_of(rw * kb, kb), kb)
        return pl.ds(pl.multiple_of(rw * kb + half * (kb // 2), kb // 2), kb // 2)

    def cols_of(n, im):
        w, lo, hi = CHUNKS[n]
        nb = fulls[w].shape[1] // 2
        return pl.ds(pl.multiple_of(im * nb + lo, 128), hi - lo)

    def block(n, rw, im, half=None):
        w = CHUNKS[n][0]
        return fulls[w].at[rows_of(w, rw, half), cols_of(n, im)]

    def slot(n, cl):
        w = CHUNKS[n][0]
        k16 = fulls[w].shape[0] // 16
        return fulls[w].at[pl.ds(pl.multiple_of((row * 4 + cl) * k16, k16), k16), cols_of(n, img)]

    def source(n):
        w, lo, hi = CHUNKS[n]
        return shards[w].at[:, pl.ds(lo, hi - lo)]

    def push(n, k, where, target, start=None):
        def copy():
            ref = slot(n, where) if start else block(n, *where)
            return pltpu.make_async_remote_copy(
                src_ref=source(n) if start and where is col else ref,
                dst_ref=ref,
                send_sem=wsend.at[n, k],
                recv_sem=wrecv.at[n, k],
                device_id=target(),
                device_id_type=MESH,
            )

        copy().start()
        sent.append(copy)

    def arrive(n, k, ref):
        pltpu.make_async_copy(ref, ref, wrecv.at[n, k]).wait()

    far_col, near_col = lax.rem(col + 2, 4), col + 1 - 2 * lax.rem(col, 2)

    def along_col(n):
        pltpu.make_async_copy(source(n), slot(n, col), wloc.at[n]).start()
        push(n, 0, col, lambda: {"col": far_col}, True)

    def near_by(n):
        pltpu.make_async_copy(source(n), slot(n, col), wloc.at[n]).wait()
        push(n, 1, col, lambda: {"col": near_col}, True)
        arrive(n, 0, slot(n, far_col))
        push(n, 2, far_col, lambda: {"col": near_col}, True)

    def first(n):
        arrive(n, 1, slot(n, near_col))
        arrive(n, 2, slot(n, 3 - col))
        push(n, 3, (row, img, 0), lambda: {"img": other})
        push(n, 4, (row, img, 1), lambda: {"row": y_row})
        push(n, 5, (row, img), lambda: {"row": core_row})

    def second(n):
        arrive(n, 3, block(n, row, other, 0))
        arrive(n, 4, block(n, y_row, img, 1))
        push(n, 6, (row, img, 0), lambda: {"row": y_row})
        push(n, 7, (row, other, 0), lambda: {"row": y_row})
        push(n, 8, (row, img, 1), lambda: {"img": other})
        push(n, 9, (y_row, img, 1), lambda: {"img": other})
        push(n, 10, (row, other, 0), lambda: {"row": core_row})
        push(n, 11, (y_row, img, 1), lambda: {"row": core_row})

    def third(n):
        arrive(n, 6, block(n, y_row, img, 0))
        arrive(n, 7, block(n, y_row, other, 0))
        arrive(n, 8, block(n, row, other, 1))
        arrive(n, 9, block(n, y_row, other, 1))
        push(n, 12, (y_row, img, 0), lambda: {"row": core_row})
        push(n, 13, (y_row, other, 0), lambda: {"row": core_row})
        push(n, 14, (row, other, 1), lambda: {"row": core_row})
        push(n, 15, (y_row, other, 1), lambda: {"row": core_row})

    def last(n):
        core_y = lax.rem(core_row + 2, 4)
        arrive(n, 5, block(n, core_row, img))
        arrive(n, 10, block(n, core_row, other, 0))
        arrive(n, 11, block(n, core_y, img, 1))
        arrive(n, 12, block(n, core_y, img, 0))
        arrive(n, 13, block(n, core_y, other, 0))
        arrive(n, 14, block(n, core_row, other, 1))
        arrive(n, 15, block(n, core_y, other, 1))

    return along_col, near_by, first, second, third, last, sent


def window_moves(tiles, raws, send, recv, loc):
    img, row, col = place()

    def each(t, act):
        for image in range(2):
            for kind in range(3):
                target_row, target_col, target_slot = piece_target(kind, image, row, col)
                here = (target_row == row) & (target_col == col)
                part = tile_part(tiles[t], image, kind)
                goal = window_part(raws[t], target_slot, kind)
                act(here, part, goal, send.at[t, image, kind], recv.at[t, target_slot, kind], target_row, target_col)

    def remote(part, goal, leave, arrival, target_row, target_col):
        return pltpu.make_async_remote_copy(
            src_ref=part,
            dst_ref=goal,
            send_sem=leave,
            recv_sem=arrival,
            device_id={"row": target_row, "col": target_col},
            device_id_type=MESH,
        )

    def own(t, image):
        return pltpu.make_async_copy(tiles[t].at[image, pl.ds(0, 14)], raws[t].at[pl.ds(image * 22 + 8, 14), pl.ds(1, 2)], loc.at[t, image])

    def start(t):
        for image in range(2):
            own(t, image).start()

        def act(here, part, goal, leave, arrival, target_row, target_col):
            @pl.when(here)
            def _():
                pltpu.make_async_copy(part, goal, arrival).start()

            @pl.when(jnp.logical_not(here))
            def _():
                remote(part, goal, leave, arrival, target_row, target_col).start()

        each(t, act)

    def arrived(t):
        for image in range(2):
            own(t, image).wait()
        for slot_index, kind, present in arrivals(row, col):
            part = window_part(raws[t], slot_index, kind)

            @pl.when(present)
            def _():
                pltpu.make_async_copy(part, part, recv.at[t, slot_index, kind]).wait()

    def left(t):
        def act(here, part, goal, leave, arrival, target_row, target_col):
            @pl.when(jnp.logical_not(here))
            def _():
                remote(part, goal, leave, arrival, target_row, target_col).wait_send()

        each(t, act)

    return start, arrived, left


BF = jnp.bfloat16
F32 = jnp.float32
ROWS = 704
SPAN = 800
FEATURES = 768
EPS = 1e-06


def row_params(step, row, col):
    wide = row >= 2
    side_row = row + 2 * (1 - col // 2)
    third_step = step - 28
    in_corner = wide & (third_step >= 8)
    slot = jnp.where(step < 14, 0, jnp.where(step < 28, 1, jnp.where(in_corner, 3, 2)))
    place_row = jnp.where(step < 14, step, jnp.where(step < 28, step - 14, jnp.where(in_corner, third_step - 8, third_step)))
    full = step < 28
    row_start = jnp.where(full, 8 - 2 * row, jnp.where(wide, 0, 8 - 2 * side_row))
    col_start = jnp.where(full, 8 - 2 * col, jnp.where(wide & jnp.logical_not(in_corner), 8 - 2 * col, 0))
    width = jnp.where(full, 14, jnp.where(wide & jnp.logical_not(in_corner), 14, 8))
    alive = jnp.where(full, True, jnp.where(in_corner, col == 3, jnp.where(wide, True, third_step < 14)))
    return slot, jnp.minimum(place_row + row_start, 21), col_start, jnp.where(alive, width, 0)


def window_params(window, row, col):
    wide = row >= 2
    start = jnp.where(window < 2, 14 * window, jnp.where(window == 2, 28, 36))
    tall = jnp.where(window < 2, 14, jnp.where((window == 2) & jnp.logical_not(wide), 14, 8))
    width = jnp.where(window < 2, 14, jnp.where((window == 2) & wide, 14, 8))
    return start, tall, width


def window_count(row, col):
    return jnp.where((row >= 2) & (col == 3), 4, 3)


def unit_of(values):
    center = values - jnp.mean(values, axis=-1, keepdims=True)
    inverse = lax.rsqrt(jnp.mean(center * center, axis=-1, keepdims=True) + EPS)
    return center * inverse, inverse


def relative_layout(backward):
    take = np.zeros((2, 2, 27, 128), np.float32)
    for parity in range(2):
        base = 64 if parity == 0 else 0
        for j in range(27):
            for copy in (0,) if backward else (0, 32):
                take[parity, 0, 26 - j, (base - 13 + j + copy) % 128] = 1
                if backward:
                    take[parity, 1, j, base + 16 + j] = 1
                else:
                    take[parity, 1, 26 - j, (base + 3 + j + copy) % 128] = 1
    return take


def takers(backward):
    return jnp.asarray(relative_layout(backward).reshape(4, 27, 128), BF)


def build_table(tab, rows_table, cols_table, take):
    tab[...] = jnp.zeros_like(tab)
    for parity in range(2):
        for which, table in ((0, rows_table), (1, cols_table)):
            block = lax.dot_general(table[...], take[2 * parity + which], (((0,), (0,)), ((), ())), preferred_element_type=F32)
            lane = 256 * parity + 128 * which
            tab[64 * parity : 64 * parity + 64, lane : lane + 128] = block.astype(BF)


def as_row(ref):
    return ref[...].reshape(1, -1)


def run_all(acts):
    for act in acts:
        act[0](*act[1:])


def plan_slots(plan, acts):
    slots = [[]]
    for name in plan:
        if name == "|":
            slots.append([])
        elif name in acts:
            slots[-1].append((acts[name],))
        else:
            slots[-1].append((acts[name[0]], int(name[1:])))
    return slots


def table_grads(sums):
    take = jnp.asarray(relative_layout(True), F32)
    grads = []
    for which in range(2):
        total = 0.0
        for parity in range(2):
            part = sums[64 * parity : 64 * parity + 64, 256 * parity + 128 * which : 256 * parity + 128 * which + 128]
            total = total + lax.dot_general(take[parity, which], part, (((1,), (1,)), ((), ())), precision=lax.Precision.HIGHEST)
        grads.append(total)
    return grads


FF = 3072
CHUNK = 512
BLOCK = 176


def nt(a, b):
    return lax.dot_general(a, b, (((1,), (1,)), ((), ())), preferred_element_type=F32)


def norm_back(grad, unit, inverse, gain):
    scaled = grad * gain
    first_mean = jnp.mean(scaled, axis=-1, keepdims=True)
    second_mean = jnp.mean(scaled * unit, axis=-1, keepdims=True)
    return inverse * (scaled - first_mean - unit * second_mean)


def fold_rows(values):
    total = values[0:8]
    for i in range(1, values.shape[0] // 8):
        total = total + values[8 * i : 8 * i + 8]
    return total


def spread_rows(source, raw, row, col):
    def step(i, _):
        slot, raw_row, col_start, width = row_params(i, row, col)
        at = pl.ds(pl.multiple_of(i * 16, 16), 16)

        @pl.when(width > 0)
        def _():
            values = jnp.concatenate([source[at, :], jnp.zeros((8, FEATURES), F32)], axis=0)
            raw[slot * 22 + raw_row] = pltpu.roll(values, col_start, 0).astype(BF).reshape(3, 8, FEATURES)

        return 0

    lax.fori_loop(0, 44, step, 0)


OPEN_PLAN = ("a0", "a2", "a1", "b0", "b2", "a6", "10", "b1", "a5", "Wx", "11", "b5", "b6", "12", "20", "22", "21", "15", "a3", "X", "16", "a4", "b3", "31", "30", "25", "L1", "L0", "P", "32", "13", "b4", "26", "|", "|", "L2", "|", "|", "Wc", "|", "|", "|", "|", "|", "|", "|", "35", "|", "|", "|", "|", "23", "14", "|", "36", "|", "U", "|", "M", "K", "T", "33", "24", "L3", "L5", "L6", "|", "34", "|", "L4", "|", "|")


def open_kernel(weights, x_ref, c_ref, gain, shift, query_bias, value_bias, rows_table, cols_table, take, out_bias, up_bias, down_bias, gain2, shift2, *refs):
    img, row, col = place()
    greet(img, row, col, weights)
    if weights:
        shards, refs = refs[:4], refs[4:]
    else:
        wq, wo, wu, wd = refs[:4]
        refs = refs[4:]
    xw_out, cw_out, n1_out, qkv_out, probs_out, o_out, o_turned_out = refs[:7]
    raw_out, n2_out, g_out, dh_out, da, do, dm, sums, up_sum = refs[7:16]
    refs = refs[16:]
    if weights:
        wq_out, refs = refs[0], refs[1:]
    rawx, rawc, n1, tab, row_bias, qkv_s, probs, y_s, d_s, g_s, g_chunk, dh_chunk, xw, cw, n1_turned, o, o_turned, n2_turned, hot, out_sem, probs_sem, send, recv, loc = refs[:24]
    refs = refs[24:]
    flushes = ((xw, xw_out), (cw, cw_out), (n1_turned, n1_out), (o, o_out), (o_turned, o_turned_out), (n2_turned, n2_out))

    def flush(i):
        return pltpu.make_async_copy(flushes[i][0], flushes[i][1], out_sem.at[5 + i])

    if weights:
        wq, wo, wu, wd = refs[:4]
        along_col, near_by, first, second, third, last, sent = links(shards, refs[:4], *refs[4:])
    window_start, window_arrived, window_left = window_moves((x_ref, c_ref), (rawx, rawc), send, recv, loc)
    places = lax.broadcasted_iota(jnp.int32, (16, 1), 0)

    def cut_one(raw, step):
        slot, raw_row, col_start, width = row_params(step, row, col)
        wide_rows = raw[slot * 22 + raw_row].reshape(24, FEATURES).astype(F32)
        keep = places < width
        return keep, jnp.where(keep, pltpu.roll(wide_rows, lax.rem(24 - col_start, 24), 0)[:16], 0.0)

    def cut_x(step, _):
        at = pl.ds(pl.multiple_of(step * 16, 16), 16)
        keep, x = cut_one(rawx, step)
        xw[at, :] = x.astype(BF)
        unit, _inverse = unit_of(x)
        n1[at, :] = jnp.where(keep, unit * as_row(gain) + as_row(shift), 0.0).astype(BF)
        return 0

    def cut_c(step, _):
        at = pl.ds(pl.multiple_of(step * 16, 16), 16)
        _keep, c = cut_one(rawc, step)
        cw[at, :] = c.astype(BF)
        return 0

    def project(step, _):
        at = pl.ds(pl.multiple_of(step * 352, 32), 352)
        for part_index in range(3):
            lanes = slice(part_index * FEATURES, (part_index + 1) * FEATURES)
            part = jnp.dot(n1[at, :], wq[:, lanes], preferred_element_type=F32)
            if part_index != 1:
                part = part + row_bias[part_index // 2]
            qkv_s[at, lanes] = part.astype(BF)
        return 0

    def turn(source, goal):
        def step(i, _):
            lanes = pl.ds(pl.multiple_of(i * 128, 128), 128)
            goal[lanes, :] = source[0:ROWS, lanes].T
            return 0

        lax.fori_loop(0, FEATURES // 128, step, 0)

    def cut_windows():
        window_arrived(0)
        lax.fori_loop(0, 44, cut_x, 0)
        flush(0).start()

    def cut_cotangent():
        window_arrived(1)
        lax.fori_loop(0, 44, cut_c, 0)
        flush(1).start()

    def project_all():
        lax.fori_loop(0, 2, project, 0)
        pltpu.make_async_copy(qkv_s, qkv_out, out_sem.at[0]).start()
        if weights:
            pltpu.make_async_copy(wq, wq_out, out_sem.at[1]).start()

    def turn_all():
        turn(o, o_turned)
        flush(3).start()
        flush(4).start()

    def turn_first():
        turn(n1, n1_turned)
        flush(2).start()

    blocks = (slice(0, 352), slice(352, 704))

    def middle_begin():
        sums[...] = jnp.zeros_like(sums)
        up_sum[...] = jnp.zeros_like(up_sum)
        d_s[...] = jnp.zeros_like(d_s)

        def begin(i, _):
            at = pl.ds(pl.multiple_of(i * BLOCK, 16), BLOCK)
            mid = xw[at, :].astype(F32) + (jnp.dot(o[at, :], wo[...], preferred_element_type=F32) + as_row(out_bias))
            unit, _inverse = unit_of(mid)
            n1[at, :] = (unit * as_row(gain2) + as_row(shift2)).astype(BF)
            y_s[at, :] = mid + as_row(down_bias)
            dm[at, :] = mid
            return 0

        lax.fori_loop(0, ROWS // BLOCK, begin, 0)
        turn(n1, n2_turned)
        flush(5).start()

    def chunk_out(which, step):
        lanes = pl.ds(pl.multiple_of(step * FEATURES, FEATURES), FEATURES)
        if which == 0:
            return pltpu.make_async_copy(g_chunk, g_out.at[lanes, :], out_sem.at[2])
        return pltpu.make_async_copy(dh_chunk, dh_out.at[:, lanes], out_sem.at[3])

    def middle_step(turn_index, _):
        for i, slot_acts in enumerate(middle_slots):
            if slot_acts:
                pl.when(turn_index == i)(functools.partial(run_all, slot_acts))
        step = lax.rem(turn_index, 2) * 2 + turn_index // 2
        lanes = pl.ds(pl.multiple_of(step * FEATURES, FEATURES), FEATURES)

        @pl.when(turn_index > 0)
        def _():
            chunk_out(0, 0).wait()
            chunk_out(1, 0).wait()

        for at in blocks:
            h = jnp.dot(n1[at, :], wu[:, lanes], preferred_element_type=F32) + up_bias[:, lanes]
            up = nt(cw[at, :], wd[lanes, :])
            phi = 0.5 * (1.0 + lax.erf(h * 0.7071067811865476))
            slope = phi + h * (jnp.exp(-0.5 * h * h) * 0.3989422804014327)
            active = (h * phi).astype(BF)
            back = (up * slope).astype(BF)
            g_s[at, :] = active
            dh_chunk[at, :] = back
            up_sum[:, lanes] += fold_rows(back.astype(F32))
            y_s[at, :] += jnp.dot(active, wd[lanes, :], preferred_element_type=F32)
            d_s[at, :] += nt(back, wu[:, lanes])
        for i in range(FEATURES // 128):
            g_chunk[128 * i : 128 * i + 128, 0:ROWS] = g_s[:, 128 * i : 128 * i + 128].T
        chunk_out(0, step).start()
        chunk_out(1, step).start()
        return 0

    def middle_end():
        def end(i, _):
            at = pl.ds(pl.multiple_of(i * BLOCK, 16), BLOCK)
            unit, inverse = unit_of(dm[at, :])
            grad = d_s[at, :].astype(BF).astype(F32)
            up = cw[at, :].astype(F32)
            grad_mid = up + norm_back(grad, unit, inverse, as_row(gain2))
            low_grad = grad_mid.astype(BF)
            dm[at, :] = grad_mid
            da[at, :] = low_grad
            do[at, :] = nt(low_grad, wo[...]).astype(BF)
            sums[0] += fold_rows(low_grad.astype(F32))
            sums[1] += fold_rows(up)
            sums[2] += fold_rows(grad * unit)
            sums[3] += fold_rows(grad)
            return 0

        spread_rows(y_s, rawx, row, col)
        raw_copy = pltpu.make_async_copy(rawx, raw_out, out_sem.at[4])
        raw_copy.start()
        lax.fori_loop(0, ROWS // BLOCK, end, 0)
        raw_copy.wait()

    acts = {"X": cut_windows, "P": project_all, "T": turn_all, "U": turn_first, "K": cut_cotangent, "M": middle_begin}
    acts["Wx"] = functools.partial(window_start, 0)
    acts["Wc"] = functools.partial(window_start, 1)
    if weights:
        acts.update({"a": along_col, "b": near_by, "1": first, "2": second, "3": third, "L": last})
        slots = plan_slots(OPEN_PLAN, acts)
    else:
        slots = plan_slots(("Wx", "Wc", "X", "P", *("|",) * 18, "T", "U", "K", "M", *("|",) * 4), acts)
    o[...] = jnp.zeros_like(o)
    build_table(tab, rows_table, cols_table, take)
    row_bias[0] = as_row(query_bias)
    row_bias[1] = as_row(value_bias)
    run_all(slots[0])
    row_of = lax.broadcasted_iota(jnp.int32, (224, 1), 0)
    lane = lax.broadcasted_iota(jnp.int32, (1, 128), 1)
    key_place = lax.broadcasted_iota(jnp.int32, (224, 128), 0)
    key_lane = lax.broadcasted_iota(jnp.int32, (224, 128), 1)
    key_a, key_b = key_place // 16, key_place % 16
    for parity in range(2):
        key_on = key_lane - (64 if parity == 0 else 0)
        hot[parity] = jnp.where(
            key_on == 14,
            jnp.where(key_b >= 14, 1.0, 0.0),
            jnp.where(
                (key_on % 32 < 14) & (key_a == key_on % 32),
                1.0,
                jnp.where((key_on % 32 >= 16) & (key_on % 32 < 30) & (key_b == key_on % 32 - 16), 1.0, 0.0),
            ),
        )

    def probs_copy(index):
        window, pair_index = index // 6, index % 6
        part = pl.ds(2 * pair_index, 2)
        return pltpu.make_async_copy(probs.at[window, part], probs_out.at[window, part], probs_sem.at[window, pair_index])

    def attend(window, pair_index, rows):
        start, tall, width = window_params(window, row, col)
        at = pl.ds(pl.multiple_of(start * 16, 16), 224)
        q_at = pl.ds(pl.multiple_of(start * 16, 16), rows)
        alive = (row_of // 16 < tall) & (row_of % 16 < width)
        lanes = lambda third: pl.ds(pl.multiple_of(third * FEATURES + pair_index * 128, 128), 128)
        q = jnp.where(alive[:rows], qkv_s[q_at, lanes(0)].astype(F32), 0.0)
        k = jnp.where(alive, qkv_s[at, lanes(1)].astype(F32), 0.0)
        v = jnp.where(alive, qkv_s[at, lanes(2)].astype(F32), row_bias[1, :, lanes(0)].astype(BF).astype(F32)).astype(BF)
        terms = jnp.dot(q.astype(BF), tab[...], preferred_element_type=F32)
        lines = [slice(16 * a, 16 * a + 16) for a in range(rows // 16)]
        outs = []
        for parity in range(2):
            own = (lane < 64) if parity == 0 else (lane >= 64)
            first_lane = 256 * parity
            rel_rows = jnp.concatenate(
                [pltpu.roll(terms[at_a, first_lane : first_lane + 128], a, 1) for a, at_a in enumerate(lines)], axis=0
            )
            rel_cols = jnp.concatenate(
                [pltpu.roll(terms[at_a, first_lane + 128 : first_lane + 256], 0, 1, stride=1, stride_axis=0) for at_a in lines], axis=0
            )
            on = lane - (64 if parity == 0 else 0)
            in_rows = ((on >= 0) & (on < 14)) | ((on >= 32) & (on < 46))
            in_cols = ((on >= 16) & (on < 30)) | ((on >= 48) & (on < 62))
            rel = jnp.where(in_rows, rel_rows, jnp.where(in_cols, rel_cols, 0.0))
            rough = rel.astype(BF).astype(F32)
            fine = jnp.where(on >= 32, rel - rough, rough)
            fine = jnp.where(on == 14, -1e30, fine)
            q_side = jnp.where(own, q * 0.125, fine).astype(BF)
            k_side = jnp.where(own, k, hot[parity]).astype(BF)
            scores = lax.dot_general(q_side, k_side, (((1,), (1,)), ((), ())), preferred_element_type=F32)
            exponent = jnp.exp(scores - jnp.max(scores, axis=-1, keepdims=True))
            p = (exponent * (1.0 / jnp.sum(exponent, axis=-1, keepdims=True))).astype(BF)
            probs[window, 2 * pair_index + parity, 0:rows, :] = p
            if rows < 224:
                probs[window, 2 * pair_index + parity, rows:224, :] = jnp.zeros((224 - rows, 224), BF)
            outs.append(jnp.dot(p, v, preferred_element_type=F32))
        blended = jnp.where(lane < 64, outs[0], outs[1])
        o[q_at, lanes(0)] = jnp.where(alive[:rows], blended, 0.0).astype(BF)

    def pair(index, _):
        for i, slot_acts in enumerate(slots[1:18]):
            if slot_acts:
                pl.when(index == i + 1)(functools.partial(run_all, slot_acts))
        window, pair_index = index // 6, index % 6
        short = (window >= 2) & (row >= 2)
        pl.when(short)(functools.partial(attend, window, pair_index, 128))
        pl.when(jnp.logical_not(short))(functools.partial(attend, window, pair_index, 224))
        probs_copy(index).start()
        return 0

    pairs = window_count(row, col) * 6
    lax.fori_loop(0, pairs, pair, 0)
    run_all(slots[18])
    middle_slots = [[], *slots[19:22]]
    lax.fori_loop(0, 4, middle_step, 0)
    run_all(slots[22])
    middle_end()
    chunk_out(0, 0).wait()
    chunk_out(1, 0).wait()
    pltpu.make_async_copy(qkv_s, qkv_out, out_sem.at[0]).wait()
    if weights:
        pltpu.make_async_copy(wq, wq_out, out_sem.at[1]).wait()
        for copy in sent:
            copy().wait_send()
    lax.fori_loop(0, pairs, lambda index, _: (probs_copy(index).wait(), 0)[1], 0)
    for i in range(6):
        flush(i).wait()
    window_left(0)
    window_left(1)


def open_windows(x, c, shards, gain, shift, query_bias, value_bias, rows_table, cols_table, out_bias, up_bias, down_bias, gain2, shift2):
    vm = pl.BlockSpec(memory_space=pltpu.VMEM)
    an = pl.BlockSpec(memory_space=pl.ANY)
    shape = jax.ShapeDtypeStruct
    dma = pltpu.SemaphoreType.DMA
    chunks = len(CHUNKS)
    weights = lax.axis_size("img") == 2
    if weights:
        given = list(shards)
    else:
        widened = [lax.all_gather(w, "img", axis=1, tiled=True) for w in shards]
        gathered = [lax.all_gather(w, ("row", "col"), axis=0, tiled=True) for w in widened]
        given = gathered
    raw = pltpu.VMEM((88, 3, 8, FEATURES), BF)
    outs = pl.pallas_call(
        functools.partial(open_kernel, weights),
        out_shape=[
            shape((ROWS, FEATURES), BF),
            shape((ROWS, FEATURES), BF),
            shape((FEATURES, ROWS), BF),
            shape((SPAN, 3 * FEATURES), BF),
            shape((4, 12, 224, 224), BF),
            shape((SPAN, FEATURES), BF),
            shape((FEATURES, ROWS), BF),
        ]
        + [
            shape((88, 3, 8, FEATURES), BF),
            shape((FEATURES, ROWS), BF),
            shape((FF, FEATURES), BF),
            shape((ROWS, FF), BF),
            shape((ROWS, FEATURES), BF),
            shape((SPAN, FEATURES), BF),
            shape((ROWS, FEATURES), F32),
            shape((4, 8, FEATURES), F32),
            shape((8, FF), F32),
        ]
        + ([shape((768, 2304), BF)] if weights else []),
        in_specs=[vm] * (14 + len(given)),
        out_specs=[an] * 11 + [vm] * 5 + ([an] if weights else []),
        scratch_shapes=[
            raw,
            raw,
            pltpu.VMEM((ROWS, FEATURES), BF),
            pltpu.VMEM((128, 512), BF),
            pltpu.VMEM((2, 1, FEATURES), F32),
            pltpu.VMEM((SPAN, 3 * FEATURES), BF),
            pltpu.VMEM((4, 12, 224, 224), BF),
            pltpu.VMEM((ROWS, FEATURES), F32),
            pltpu.VMEM((ROWS, FEATURES), F32),
            pltpu.VMEM((ROWS, FEATURES), BF),
            pltpu.VMEM((FEATURES, FEATURES), BF),
            pltpu.VMEM((ROWS, FEATURES), BF),
            pltpu.VMEM((ROWS, FEATURES), BF),
            pltpu.VMEM((ROWS, FEATURES), BF),
            pltpu.VMEM((FEATURES, ROWS), BF),
            pltpu.VMEM((SPAN, FEATURES), BF),
            pltpu.VMEM((FEATURES, ROWS), BF),
            pltpu.VMEM((FEATURES, ROWS), BF),
            pltpu.VMEM((2, 224, 128), F32),
            dma((11,)),
            dma((4, 6)),
            dma((2, 2, 3)),
            dma((2, 4, 3)),
            dma((2, 2)),
        ]
        + ([pltpu.VMEM(s, BF) for s in WHOLES] + [dma((chunks, 16)), dma((chunks, 16)), dma((chunks,))] if weights else []),
        compiler_params=pltpu.CompilerParams(collective_id=0, has_side_effects=True, vmem_limit_bytes=67043328),
    )(x.reshape(2, 16, 2, 8, 768), c.reshape(2, 16, 2, 8, 768), gain, shift, query_bias, value_bias, rows_table, cols_table, takers(False), out_bias, up_bias, down_bias, gain2, shift2, *given)
    return list(outs) if weights else list(outs) + gathered[:1]


def key_marks(hot):
    key_place = lax.broadcasted_iota(jnp.int32, (224, 128), 0)
    key_lane = lax.broadcasted_iota(jnp.int32, (224, 128), 1)
    key_a, key_b = key_place // 16, key_place % 16
    for parity in range(2):
        key_on = key_lane - (64 if parity == 0 else 0)
        hot[parity] = jnp.where(
            (key_on >= 0) & (key_on < 14) & (key_a == key_on),
            1.0,
            jnp.where((key_on >= 16) & (key_on < 30) & (key_b == 29 - key_on), 1.0, 0.0),
        )


def attention_back(window, pair_index, probs_of, do, qkv, o, tab, hot, value_bias, bias_sums, table_sums, row, col):
    row_of = lax.broadcasted_iota(jnp.int32, (224, 1), 0)
    lane = lax.broadcasted_iota(jnp.int32, (1, 128), 1)
    start, tall, width = window_params(window, row, col)
    at = pl.ds(pl.multiple_of(start * 16, 16), 224)
    inside = row_of // 16 < tall
    alive = inside & (row_of % 16 < width)
    lanes = lambda third: pl.ds(pl.multiple_of(third * FEATURES + pair_index * 128, 128), 128)
    old = [qkv[at, lanes(third)].astype(F32) for third in range(3)]
    q = jnp.where(alive, old[0], 0.0)
    k = jnp.where(alive, old[1], 0.0)
    v = jnp.where(alive, old[2], value_bias[:, lanes(0)].astype(BF).astype(F32))
    grad = jnp.where(alive, do[at, lanes(0)].astype(F32), 0.0)
    product = grad * jnp.where(alive, o[at, lanes(0)].astype(F32), 0.0)
    q_turned = q.T.astype(BF)
    grad_turned = grad.T.astype(BF)
    value_parts, key_parts, query_parts, table_parts = [], [], [], []
    for parity in range(2):
        base = 64 if parity == 0 else 0
        own = (lane < 64) if parity == 0 else (lane >= 64)
        half = slice(64 * parity, 64 * parity + 64)
        inner = jnp.sum(jnp.where(own, product, 0.0), axis=-1, keepdims=True)
        rough = inner.astype(BF).astype(F32)
        on = lane - base
        grad_side = jnp.where(own, grad, jnp.where(on == 0, rough, jnp.where(on == 1, inner - rough, 0.0))).astype(BF)
        v_side = jnp.where(own, v, jnp.where((on == 0) | (on == 1), -1.0, 0.0)).astype(BF)
        centered = nt(grad_side, v_side)
        p = probs_of(parity)
        ds = (p.astype(F32) * centered).astype(BF)
        value_parts.append(jnp.dot(grad_turned[half], p, preferred_element_type=F32))
        key_parts.append(jnp.dot(q_turned[half], ds, preferred_element_type=F32))
        k_side = jnp.where(own, k * 0.125, hot[parity]).astype(BF)
        wide = jnp.dot(ds, k_side, preferred_element_type=F32)
        query_parts.append(wide)
        by_rows = jnp.where((on >= 0) & (on < 14), wide, 0.0)
        by_cols = jnp.where((on >= 16) & (on < 30), wide, 0.0)
        table_parts.append(jnp.concatenate([pltpu.roll(by_rows[16 * a : 16 * a + 16], (128 - a) % 128, 1) for a in range(14)], axis=0))
        table_parts.append(
            jnp.concatenate([pltpu.roll(by_cols[16 * a : 16 * a + 16], 0, 1, stride=1, stride_axis=0) for a in range(14)], axis=0)
        )
    turned = jnp.concatenate(table_parts, axis=1).astype(BF)
    dq = jnp.where(lane < 64, query_parts[0], query_parts[1]) + nt(turned, tab[...])
    table_sums[...] += jnp.dot(q_turned, turned, preferred_element_type=F32)
    dk = jnp.concatenate(key_parts, axis=0).T * 0.125
    dv = jnp.concatenate(value_parts, axis=0).T.astype(BF).astype(F32)
    dq = jnp.where(alive, dq, 0.0).astype(BF).astype(F32)
    bias_sums[0, :, lanes(0)] += fold_rows(dq)
    bias_sums[1, :, lanes(0)] += fold_rows(dv)
    for third, new in enumerate((dq, dk, dv)):
        qkv[at, lanes(third)] = jnp.where(alive, new, jnp.where(inside, 0.0, old[third])).astype(BF)


def clear_idle(qkv, row, col):
    wide = row >= 2
    limit = jnp.where(wide, jnp.where(col == 3, 44, 36), 42)
    for a in range(36, 44):

        @pl.when(a >= limit)
        def _():
            qkv[16 * a : 16 * a + 16, :] = jnp.zeros((16, 3 * FEATURES), BF)


def plain_back_kernel(do, probs, qkv, o, value_bias, rows_table, cols_table, take, dqkv, bias_sums, table_sums, tab, row_bias, hot):
    row, col = lax.axis_index("row"), lax.axis_index("col")
    build_table(tab, rows_table, cols_table, take)
    row_bias[...] = as_row(value_bias)
    key_marks(hot)
    dqkv[...] = qkv[...]
    clear_idle(dqkv, row, col)
    bias_sums[...] = jnp.zeros_like(bias_sums)
    table_sums[...] = jnp.zeros_like(table_sums)

    def pair(index, _):
        window, pair_index = index // 6, index % 6
        attention_back(
            window,
            pair_index,
            lambda parity: probs[window, 2 * pair_index + parity],
            do,
            dqkv,
            o,
            tab,
            hot,
            row_bias,
            bias_sums,
            table_sums,
            row,
            col,
        )
        return 0

    lax.fori_loop(0, window_count(row, col) * 6, pair, 0)


def plain_back(do, probs, qkv, o, value_bias, rows_table, cols_table):
    vm = pl.BlockSpec(memory_space=pltpu.VMEM)
    shape = jax.ShapeDtypeStruct
    return pl.pallas_call(
        plain_back_kernel,
        out_shape=[shape((SPAN, 3 * FEATURES), BF), shape((2, 8, FEATURES), F32), shape((128, 512), F32)],
        in_specs=[vm] * 8,
        out_specs=[vm] * 3,
        scratch_shapes=[pltpu.VMEM((128, 512), BF), pltpu.VMEM((1, FEATURES), F32), pltpu.VMEM((2, 224, 128), F32)],
        compiler_params=pltpu.CompilerParams(vmem_limit_bytes=62 << 20),
    )(do, probs, qkv, o, value_bias, rows_table, cols_table, takers(True))


WHOLES = ((768, 2304), (768, 768), (768, 3072), (3072, 768))
SUM_CHUNKS = ((1, 0, 384), (3, 0, 128), (3, 128, 384), (2, 0, 768), (2, 768, 1536), (0, 0, 384), (0, 384, 768), (0, 768, 1152))


def pair_lanes(j, im):
    if im == 0:
        return (128 * j, FEATURES + 128 * j, 128 * (j + 3))
    return (2 * FEATURES + 128 * j, FEATURES + 128 * (j + 3), 2 * FEATURES + 128 * (j + 3))


def land_shapes(chunks):
    lands = []
    for w, lo, hi in chunks:
        kb, width = WHOLES[w][0] // 4, hi - lo
        lands += [
            pltpu.VMEM((2, 2, kb, width), BF),
            pltpu.VMEM((2, kb // 2, width), BF),
            pltpu.VMEM((2, kb // 2, width), BF),
            pltpu.VMEM((2, kb // 2, width), BF),
            pltpu.VMEM((3, kb // 4, width), BF),
        ]
    return lands


def reducers(chunks, full, left_turned, right_side, grads, land_refs, wsend, wrecv):
    img, row, col = place()
    y_row = lax.rem(row + 2, 4)
    core_row = row + 1 - 2 * lax.rem(row, 2)
    core_y = lax.rem(core_row + 2, 4)
    other = 1 - img
    far_col, near_col = lax.rem(col + 2, 4), col + 1 - 2 * lax.rem(col, 2)
    lands = [land_refs[5 * n : 5 * n + 5] for n in range(len(chunks))]
    sent = []

    def size(n):
        w, lo, hi = chunks[n]
        return WHOLES[w][0] // 4, WHOLES[w][1] // 2, lo, hi - lo

    def block(n, rw, im, half=None):
        kb, nb, lo, width = size(n)
        cols = pl.ds(pl.multiple_of(im * nb + lo, 128), width)
        if half is None:
            return full[chunks[n][0]].at[pl.ds(pl.multiple_of(rw * kb, kb), kb), cols]
        return full[chunks[n][0]].at[pl.ds(pl.multiple_of(rw * kb + half * (kb // 2), kb // 2), kb // 2), cols]

    def shard(n, cl):
        kb, nb, lo, width = size(n)
        cols = pl.ds(pl.multiple_of(img * nb + lo, 128), width)
        return full[chunks[n][0]].at[pl.ds(pl.multiple_of(row * kb + cl * (kb // 4), kb // 4), kb // 4), cols]

    def push(n, k, src, dst, target):
        def copy():
            return pltpu.make_async_remote_copy(
                src_ref=src(), dst_ref=dst(), send_sem=wsend.at[n, k], recv_sem=wrecv.at[n, k], device_id=target(), device_id_type=MESH
            )

        copy().start()
        sent.append(copy)

    def arrive(n, k, ref):
        pltpu.make_async_copy(ref, ref, wrecv.at[n, k]).wait()

    def add(goal, part, rows):
        def step(i, _):
            at = pl.ds(pl.multiple_of(i * 48, 16), 48)
            goal[at, :] = (goal[at, :].astype(F32) + part[at, :].astype(F32)).astype(BF)
            return 0

        lax.fori_loop(0, rows // 48, step, 0)

    def product(n, rw):
        w = chunks[n][0]
        kb, nb, lo, width = size(n)
        rows = pl.ds(pl.multiple_of(rw * kb, kb), kb)
        for im in range(2):
            at = slice(im * nb + lo, im * nb + lo + width)
            if w == 0:
                right = jnp.concatenate([right_side[0][0:ROWS, p : p + 128] for p in pair_lanes(lo // 384, im)], axis=1)
            else:
                right = right_side[w][0:ROWS, at]
            full[w][rows, at] = jnp.dot(left_turned[w](rw, kb), right, preferred_element_type=F32).astype(BF)

    def pair_stage(n):
        land = lands[n][0]
        for j, rw in enumerate((core_row, core_y)):
            product(n, rw)
            for im in range(2):
                push(n, 2 * j + im, functools.partial(block, n, rw, im), lambda j=j, im=im: land.at[j, im], lambda: {"row": core_row})
        for rw in (row, y_row):
            product(n, rw)

    def first(n):
        kb, nb, lo, width = size(n)
        for j, rw in enumerate((row, y_row)):
            for im in range(2):
                arrive(n, 2 * j + im, lands[n][0].at[j, im])
                add(block(n, rw, im), lands[n][0].at[j, im], kb)
        for im in range(2):
            push(n, 4 + im, functools.partial(block, n, y_row, im, 0), lambda im=im: lands[n][1].at[im], lambda: {"row": y_row})
        push(n, 6, functools.partial(block, n, row, other, 1), lambda: lands[n][2].at[0], lambda: {"img": other})
        push(n, 7, functools.partial(block, n, y_row, other, 1), lambda: lands[n][2].at[1], lambda: {"img": other})

    def second(n):
        kb, nb, lo, width = size(n)
        for im in range(2):
            arrive(n, 4 + im, lands[n][1].at[im])
            add(block(n, row, im, 0), lands[n][1].at[im], kb // 2)
        push(n, 8, functools.partial(block, n, row, other, 0), lambda: lands[n][3].at[0], lambda: {"img": other})
        for j, rw in enumerate((row, y_row)):
            arrive(n, 6 + j, lands[n][2].at[j])
            add(block(n, rw, img, 1), lands[n][2].at[j], kb // 2)
        push(n, 9, functools.partial(block, n, y_row, img, 1), lambda: lands[n][3].at[1], lambda: {"row": y_row})

    def third(n):
        kb, nb, lo, width = size(n)
        for half in range(2):
            arrive(n, 8 + half, lands[n][3].at[half])
            add(block(n, row, img, half), lands[n][3].at[half], kb // 2)
        push(n, 10, lambda: shard(n, near_col), lambda: lands[n][4].at[0], lambda: {"col": near_col})
        push(n, 11, lambda: shard(n, 3 - col), lambda: lands[n][4].at[1], lambda: {"col": near_col})

    def fourth(n):
        kb = size(n)[0]
        arrive(n, 11, lands[n][4].at[1])
        add(shard(n, far_col), lands[n][4].at[1], kb // 4)
        push(n, 12, lambda: shard(n, far_col), lambda: lands[n][4].at[2], lambda: {"col": far_col})

    def fifth(n):
        w, lo, hi = chunks[n]
        arrive(n, 10, lands[n][4].at[0])
        arrive(n, 12, lands[n][4].at[2])
        mine = shard(n, col)

        def step(part, _):
            at = pl.ds(pl.multiple_of(part * 48, 16), 48)
            total = mine[at, :].astype(F32) + lands[n][4][0, at, :].astype(F32) + lands[n][4][2, at, :].astype(F32)
            if w > 0:
                grads[w][at, lo:hi] = total
            else:
                for im in range(2):

                    @pl.when(img == im)
                    def _():
                        for i, p in enumerate(pair_lanes(lo // 384, im)):
                            lane = p - 1152 * im
                            grads[0][at, lane : lane + 128] = total[:, 128 * i : 128 * i + 128]

            return 0

        lax.fori_loop(0, WHOLES[w][0] // 16 // 48, step, 0)

    return pair_stage, first, second, third, fourth, fifth, sent


def table_taker():
    take = relative_layout(True)
    out = np.zeros((4, 128, 128), np.float32)
    for parity in range(2):
        for which in range(2):
            out[2 * parity + which, :, 64 * which : 64 * which + 27] = take[parity, which].T
    return out


def source_tiles(row, col):
    wide = row >= 2
    side_row = row + 2 * (1 - col // 2)
    table = []
    for image in range(2):
        table.append((image, 0, image, row - 1, col, row > 0))
        table.append((image, 1, image, row, col - 1, col > 0))
        table.append((image, 2, image, row - 1, col - 1, (row > 0) & (col > 0)))
    third_image = jnp.where(wide, 3 - row, 1 - lax.rem(col, 2))
    table.append((2, 0, third_image, 3, col, wide))
    table.append((2, 1, third_image, side_row, 3, jnp.logical_not(wide)))
    table.append((2, 2, third_image, jnp.where(wide, 3, side_row - 1), jnp.where(wide, col - 1, 3), jnp.where(wide, col, side_row) > 0))
    table.append((3, 2, 3 - row, 3, 3, wide & (col == 3)))
    return table


CLOSE_PLAN = ("p1", "p2", "11", "|", "|", "12", "p4", "|", "|", "14", "21", "|", "p0", "|", "|", "p3", "|", "22", "|", "p5", "24", "|", "10", "31", "|", "|", "|", "|", "|", "|", "|", "13", "|", "32", "41", "15", "34", "G0", "G1", "G2", "42", "p7", "G3", "S", "p6", "23", "s0", "25", "20", "17", "16", "30", "s1", "44", "35", "27", "40", "52", "33", "26", "s2", "45", "37", "51", "50", "36", "s3", "43", "54", "47", "46", "53", "57", "55", "56", "s4")


def returns(raws, landing, send, recv, row, col):
    def each(t, act):
        for slot, kind, image, tile_row, tile_col, present in source_tiles(row, col):
            here = (tile_row == row) & (tile_col == col)
            act(slot, kind, image, tile_row, tile_col, present & here, present & jnp.logical_not(here))

    def start(t):
        def act(slot, kind, image, tile_row, tile_col, local, remote):
            @pl.when(local)
            def _():
                pltpu.make_async_copy(
                    window_part(raws[t], slot, kind), landing[t][kind].at[image], recv.at[t, image, kind]
                ).start()

            @pl.when(remote)
            def _():
                hop(t, slot, kind, image, tile_row, tile_col).start()

        each(t, act)

    def hop(t, slot, kind, image, tile_row, tile_col):
        return pltpu.make_async_remote_copy(
            src_ref=window_part(raws[t], slot, kind),
            dst_ref=landing[t][kind].at[image],
            send_sem=send.at[t, slot, kind],
            recv_sem=recv.at[t, image, kind],
            device_id={"row": jnp.maximum(tile_row, 0), "col": jnp.maximum(tile_col, 0)},
            device_id_type=MESH,
        )

    def arrived(t):
        for image in range(2):
            for kind in range(3):
                goal = landing[t][kind].at[image]
                pltpu.make_async_copy(goal, goal, recv.at[t, image, kind]).wait()

    def left(t):
        def act(slot, kind, image, tile_row, tile_col, local, remote):
            @pl.when(remote)
            def _():
                hop(t, slot, kind, image, tile_row, tile_col).wait_send()

        each(t, act)

    return start, arrived, left


def merge_tiles(owns, landing, goals, row, col):
    places = lax.broadcasted_iota(jnp.int32, (16, 1), 0)
    in_left = places < 14 - 2 * col

    def rows16(values):
        return values.reshape(16, FEATURES).astype(F32)

    def right_half(values):
        low = values.reshape(8, FEATURES).astype(F32)
        return jnp.concatenate([low, low], axis=0)

    for image in range(2):

        def merge(tile_row, _):
            top = tile_row < 14 - 2 * row
            upper = jnp.minimum(tile_row, 13)
            lower = jnp.maximum(tile_row - 8, 0)
            for own, (below, right, both), goal in zip(owns, landing, goals):
                stacked = jnp.where(top, rows16(own(image, upper)), rows16(below[image, lower]))
                beside = jnp.where(top, right_half(right[image, upper]), right_half(both[image, lower]))
                goal[image, tile_row] = jnp.where(in_left, stacked, beside).astype(goal.dtype)
            return 0

        lax.fori_loop(0, 16, merge, 0)


def input_grad(at, dqkv, wq, xw, image_grad, gain, norm_sums):
    grad = nt(dqkv[at, :], wq).astype(BF).astype(F32)
    unit, inverse = unit_of(xw[at, :].astype(F32))
    image_grad[at, :] += norm_back(grad, unit, inverse, as_row(gain))
    norm_sums[0] += fold_rows(grad * unit)
    norm_sums[1] += fold_rows(grad)


def plain_close_kernel(dqkv, xw, dm, raw_r, wq, gain, out, grad_out, norm_sums, image_grad, raw_g, *refs):
    img, row, col = place()
    landing, (send, recv) = (refs[:3], refs[3:6]), refs[6:]
    greet(img, row, col, False)
    start, arrived, left = returns((raw_r, raw_g), landing, send, recv, row, col)
    start(0)
    norm_sums[...] = jnp.zeros_like(norm_sums)
    image_grad[...] = dm[...]

    def step(i, _):
        input_grad(pl.ds(pl.multiple_of(i * BLOCK, 16), BLOCK), dqkv, wq[...], xw, image_grad, gain, norm_sums)
        return 0

    lax.fori_loop(0, ROWS // BLOCK, step, 0)
    spread_rows(image_grad, raw_g, row, col)
    start(1)
    for t in range(2):
        arrived(t)
    owns = [lambda image, upper, raw=raw: raw[image * 22 + 8 + upper, 1:3] for raw in (raw_r, raw_g)]
    merge_tiles(owns, landing, (out, grad_out), row, col)
    for t in range(2):
        left(t)


PIECES = [(2, 8, 2, 8, FEATURES), (2, 14, 1, 8, FEATURES), (2, 8, 1, 8, FEATURES)]


def plain_close(dqkv, xw, dm, raw_r, wq, gain):
    vm = pl.BlockSpec(memory_space=pltpu.VMEM)
    shape = jax.ShapeDtypeStruct
    dma = pltpu.SemaphoreType.DMA
    pieces = [pltpu.VMEM(s, BF) for s in PIECES]
    return pl.pallas_call(
        plain_close_kernel,
        out_shape=[shape((2, 16, 16, FEATURES), BF), shape((2, 16, 16, FEATURES), F32), shape((2, 8, FEATURES), F32)],
        in_specs=[vm] * 6,
        out_specs=[vm] * 3,
        scratch_shapes=[pltpu.VMEM((ROWS, FEATURES), F32), pltpu.VMEM((88, 3, 8, FEATURES), BF)]
        + pieces
        + pieces
        + [dma((2, 4, 3)), dma((2, 2, 3))],
        compiler_params=pltpu.CompilerParams(collective_id=2, has_side_effects=True, vmem_limit_bytes=67043328),
    )(dqkv, xw, dm, raw_r, wq, gain)


def back_kernel(
    value_bias, rows_table, cols_table, take, o_turned, da, cw, gain, sums, up_sum, taker,
    do_in, o_in, n2_in, xw_in, n1_in, probs, qkv_in, dh_in, g_in, dm_in, wq_in, raw_r, *refs
):
    out, grad_out, gq, go, gu, gd, small_out, table_out = refs[:8]
    qkv, probs_s, image_grad, shared_h, shared_g, own_r = refs[8:14]
    bias_sums, table_sums, norm_sums, tab, row_bias = refs[14:19]
    landing = (refs[19:22], refs[22:25])
    full = refs[25:29]
    small, table, small_land, table_land, small_z, table_z = refs[29:35]
    count = len(SUM_CHUNKS)
    lands = refs[35 : 35 + 5 * count]
    do, o, n2_turned, xw, n1_turned, hot = refs[35 + 5 * count : 41 + 5 * count]
    send, recv, load_sem, probs_sem, wsend, wrecv, ssend, srecv = refs[41 + 5 * count :]
    img, row, col = place()
    y_row = lax.rem(row + 2, 4)
    core_row = row + 1 - 2 * lax.rem(row, 2)
    other = 1 - img
    copies = []

    def load(i):
        pairs = (
            (dh_in, shared_h.at[pl.ds(0, ROWS)]),
            (g_in, shared_g),
            (qkv_in, qkv),
            (dm_in, image_grad),
            (wq_in, shared_h.at[:, pl.ds(0, 3 * FEATURES)]),
            (raw_r.at[pl.ds(8, 14), pl.ds(1, 2)], own_r.at[0]),
            (raw_r.at[pl.ds(30, 14), pl.ds(1, 2)], own_r.at[1]),
            (do_in, do),
            (o_in, o),
            (n2_in, n2_turned),
            (xw_in, xw),
            (n1_in, n1_turned),
        )
        return pltpu.make_async_copy(pairs[i][0], pairs[i][1], load_sem.at[i])

    for i in (1, 2, 7, 8, 9, 0, 11, 10, 3, 5, 6):
        load(i).start()
    windows = window_count(row, col)

    def fetch(k, window, slot):
        pair_index = lax.rem(k, 2) * 3 + k // 2
        return pltpu.make_async_copy(probs.at[window, pl.ds(2 * pair_index, 2)], probs_s.at[slot], probs_sem.at[slot])

    fetch(0, 0, 0).start()
    greet(img, row, col)
    start, arrived, left = returns((raw_r, shared_g), landing, send, recv, row, col)
    start(0)

    def turned_rows(ref):
        return lambda rw, kb: ref[pl.ds(pl.multiple_of(rw * kb, kb), kb), :]

    def turned_g(rw, kb):
        return shared_g[pl.ds(pl.multiple_of(rw * 32, 32), 32)].reshape(FEATURES, FEATURES)[:, 0:ROWS]

    pair_stage, first, second, third, fourth, fifth, sent = reducers(
        SUM_CHUNKS,
        full,
        (turned_rows(n1_turned), turned_rows(o_turned), turned_rows(n2_turned), turned_g),
        (qkv, da, shared_h, cw),
        (gq, go, gu, gd),
        lands,
        wsend,
        wrecv,
    )
    bias_sums[...] = jnp.zeros_like(bias_sums)
    table_sums[...] = jnp.zeros_like(table_sums)
    norm_sums[...] = jnp.zeros_like(norm_sums)
    build_table(tab, rows_table, cols_table, take)
    row_bias[...] = as_row(value_bias)
    key_marks(hot)
    load(1).wait()

    def grad_rows(i):
        if i == 0:
            load(4).start()
            load(10).wait()
            load(3).wait()
            load(4).wait()
        input_grad(pl.ds(i * BLOCK, BLOCK), qkv, shared_h[:, 0 : 3 * FEATURES], xw, image_grad, gain, norm_sums)

    def send_grad():
        spread_rows(image_grad, shared_g, row, col)
        start(1)

    def over_rows(values):
        return jnp.sum(values, axis=0, keepdims=True)

    def gather_small():
        small[0] = jnp.zeros((16, FEATURES), F32)
        lines = [bias_sums[0], bias_sums[1], sums[0], sums[1], norm_sums[0], norm_sums[1], sums[2], sums[3]]
        for i, values in enumerate(lines):
            small[0, i : i + 1, :] = over_rows(values)
        for i in range(4):
            small[0, 8 + i : 9 + i, :] = over_rows(up_sum[:, i * FEATURES : (i + 1) * FEATURES])
        exact = lax.Precision.HIGHEST
        total = jnp.zeros((64, 128), F32)
        for parity in range(2):
            for which in range(2):
                part = table_sums[64 * parity : 64 * parity + 64, 256 * parity + 128 * which : 256 * parity + 128 * which + 128]
                total = total + jnp.dot(part, taker[2 * parity + which], precision=exact, preferred_element_type=F32)
        table[0] = total

    hops = ({"row": core_row}, {"row": y_row}, {"img": other})

    def small_push(k, src, dst, target):
        c = pltpu.make_async_remote_copy(
            src_ref=src, dst_ref=dst, send_sem=ssend.at[k], recv_sem=srecv.at[k], device_id=target, device_id_type=MESH
        )
        c.start()
        copies.append(c)
        return c

    def small_step(i):
        if i == 0:
            gather_small()
        if 0 < i <= 3:
            for k, (acc, land) in enumerate(((small, small_land), (table, table_land))):
                pltpu.make_async_copy(land.at[i - 1], land.at[i - 1], srecv.at[2 * (i - 1) + k]).wait()
                acc[i] = acc[i - 1] + land[i - 1]
        if i < 3:
            for k, (acc, land) in enumerate(((small, small_land), (table, table_land))):
                small_push(2 * i + k, acc.at[i], land.at[i], hops[i])
        if i == 3:
            small_z[col] = small[3]
            table_z[col] = table[3]
            for d in range(1, 4):
                cl = lax.rem(col + d, 4)
                small_push(4 + 2 * d, small.at[3], small_z.at[col], {"col": cl})
                small_push(5 + 2 * d, table.at[3], table_z.at[col], {"col": cl})
        if i == 4:
            for d in range(1, 4):
                cl = lax.rem(col + 4 - d, 4)
                pltpu.make_async_copy(small_z.at[cl], small_z.at[cl], srecv.at[4 + 2 * d]).wait()
                pltpu.make_async_copy(table_z.at[cl], table_z.at[cl], srecv.at[5 + 2 * d]).wait()
            small_out[...] = (small_z[0] + small_z[1]) + (small_z[2] + small_z[3])
            table_out[...] = (table_z[0] + table_z[1]) + (table_z[2] + table_z[3])

    acts = {"p": pair_stage, "1": first, "2": second, "3": third, "4": fourth, "5": fifth, "G": grad_rows, "s": small_step, "S": send_grad}
    slots = plan_slots(CLOSE_PLAN, acts)
    run_all(slots[0])
    load(2).wait()
    clear_idle(qkv, row, col)
    for i in (7, 8, 9, 0, 11):
        load(i).wait()

    def head_pair(k, _):
        pair_index = lax.rem(k, 2) * 3 + k // 2

        def each(window, _):
            for i, slot_acts in enumerate(slots[1:-1]):
                if slot_acts:
                    pl.when((k == (i + 1) // 3) & (window == (i + 1) % 3))(functools.partial(run_all, slot_acts))
            turn_count = k * windows + window
            slot = lax.rem(turn_count, 2)
            fetch(k, window, slot).wait()
            wrap = window + 1 == windows
            next_k = jnp.where(wrap, k + 1, k)

            @pl.when(next_k < 6)
            def _():
                fetch(next_k, jnp.where(wrap, 0, window + 1), 1 - slot).start()

            attention_back(
                window,
                pair_index,
                lambda parity: probs_s[slot, parity],
                do,
                qkv,
                o,
                tab,
                hot,
                row_bias,
                bias_sums,
                table_sums,
                row,
                col,
            )
            return 0

        lax.fori_loop(0, windows, each, 0)
        return 0

    lax.fori_loop(0, 6, head_pair, 0)
    run_all(slots[-1])
    arrived(0)
    load(5).wait()
    load(6).wait()
    merge_tiles([lambda image, upper: own_r[image, upper]], landing[:1], (out,), row, col)
    arrived(1)
    merge_tiles([lambda image, upper: shared_g[image * 22 + 8 + upper, 1:3]], landing[1:], (grad_out,), row, col)
    left(0)
    left(1)
    for c in copies:
        c.wait_send()
    for copy in sent:
        copy().wait_send()


def back(do, o, value_bias, rows_table, cols_table, o_turned, da, n2_turned, cw, xw, n1_turned, gain, sums, up_sum, probs, qkv, dh, g, dm, wq, raw_r):
    vm = pl.BlockSpec(memory_space=pltpu.VMEM)
    an = pl.BlockSpec(memory_space=pl.ANY)
    shape = jax.ShapeDtypeStruct
    dma = pltpu.SemaphoreType.DMA
    pieces = [pltpu.VMEM(s, BF) for s in PIECES]
    count = len(SUM_CHUNKS)
    return pl.pallas_call(
        back_kernel,
        out_shape=[shape((2, 16, 16, FEATURES), BF), shape((2, 16, 16, FEATURES), BF)]
        + [shape((k // 16, n // 2), F32) for k, n in WHOLES]
        + [shape((16, FEATURES), F32), shape((64, 128), F32)],
        in_specs=[vm] * 11 + [an] * 12,
        out_specs=[vm] * 8,
        scratch_shapes=[
            pltpu.VMEM((SPAN, 3 * FEATURES), BF),
            pltpu.VMEM((2, 2, 224, 224), BF),
            pltpu.VMEM((ROWS, FEATURES), F32),
            pltpu.VMEM((FEATURES, 4 * FEATURES), BF),
            pltpu.VMEM((128, 3, 8, FEATURES), BF),
            pltpu.VMEM((2, 14, 2, 8, FEATURES), BF),
            pltpu.VMEM((2, 8, FEATURES), F32),
            pltpu.VMEM((128, 512), F32),
            pltpu.VMEM((2, 8, FEATURES), F32),
            pltpu.VMEM((128, 512), BF),
            pltpu.VMEM((1, FEATURES), F32),
        ]
        + pieces
        + pieces
        + [pltpu.VMEM(s, BF) for s in WHOLES]
        + [
            pltpu.VMEM((4, 16, FEATURES), F32),
            pltpu.VMEM((4, 64, 128), F32),
            pltpu.VMEM((3, 16, FEATURES), F32),
            pltpu.VMEM((3, 64, 128), F32),
            pltpu.VMEM((4, 16, FEATURES), F32),
            pltpu.VMEM((4, 64, 128), F32),
        ]
        + land_shapes(SUM_CHUNKS)
        + [pltpu.VMEM(s, BF) for s in ((SPAN, FEATURES), (SPAN, FEATURES), (FEATURES, ROWS), (ROWS, FEATURES), (FEATURES, ROWS))]
        + [pltpu.VMEM((2, 224, 128), F32)]
        + [dma((2, 4, 3)), dma((2, 2, 3)), dma((12,)), dma((2,)), dma((count, 13)), dma((count, 13)), dma((12,)), dma((12,))],
        compiler_params=pltpu.CompilerParams(collective_id=1, has_side_effects=True, vmem_limit_bytes=67043328),
    )(
        value_bias, rows_table, cols_table, takers(True), o_turned, da, cw, gain, sums, up_sum, jnp.asarray(table_taker()),
        do, o, n2_turned, xw, n1_turned, probs, qkv, dh, g.reshape(128, 3, 8, FEATURES), dm, wq, raw_r,
    )


def deliver_kernel(out_in, grad_in, *refs):
    sums_in, (small, table), outs = refs[:4], refs[4:6], refs[6:]
    outs[0][...] = out_in[...]

    def widen(i, _):
        outs[1][i // 16, i % 16] = grad_in[i // 16, i % 16].astype(F32)
        return 0

    lax.fori_loop(0, 32, widen, 0)
    for given, goal in zip(sums_in, outs[2:6]):
        goal[...] = given[...]
    for i, goal in zip((0, 1, 2, None, 3, 4, 5, 6, 7), outs[6:15]):
        if i is None:
            goal[...] = jnp.concatenate([small[8 + j : 9 + j, :] for j in range(4)], axis=1).reshape(4 * FEATURES)
        else:
            goal[...] = small[i : i + 1, :].reshape(FEATURES)
    turned = table[...].T
    outs[15][...] = turned[0:27, :]
    outs[16][...] = turned[64:91, :]


def deliver(*given):
    vm = pl.BlockSpec(memory_space=pltpu.VMEM)
    shape = jax.ShapeDtypeStruct
    lengths = [FEATURES] * 3 + [4 * FEATURES] + [FEATURES] * 5
    outs = [shape((2, 16, 16, FEATURES), BF), shape((2, 16, 16, FEATURES), F32)] + [shape((k // 16, n // 2), F32) for k, n in WHOLES]
    outs += [shape((n,), F32) for n in lengths] + [shape((27, 64), F32)] * 2
    return pl.pallas_call(deliver_kernel, out_shape=outs, in_specs=[vm] * 8, out_specs=[vm] * len(outs))(*given)


def on_device(
    image_in,
    cotangent,
    qkv_weight,
    out_weight,
    up_weight,
    down_weight,
    query_bias,
    value_bias,
    out_bias,
    up_bias,
    down_bias,
    first_gain,
    first_shift,
    second_gain,
    second_shift,
    rows_table,
    cols_table,
):
    line = lambda v: v.reshape(1, -1)
    xw, cw, n1_turned, qkv, probs, o, o_turned, raw_r, n2_turned, g_turned, dh, da, do, dm, sums, up_sum, wq = open_windows(
        image_in,
        cotangent,
        (qkv_weight, out_weight, up_weight, down_weight),
        first_gain,
        first_shift,
        query_bias,
        value_bias,
        rows_table,
        cols_table,
        out_bias,
        line(up_bias),
        down_bias,
        second_gain,
        second_shift,
    )
    if lax.axis_size("img") == 2:
        return tuple(
            deliver(
                *back(
                    do, o, value_bias, rows_table, cols_table, o_turned, da, n2_turned, cw, xw, n1_turned, first_gain, sums, up_sum,
                    probs, qkv, dh, g_turned, dm, wq, raw_r,
                )
            )
        )
    dqkv, bias_sums, table_sums = plain_back(do, probs, qkv, o, value_bias, rows_table, cols_table)
    image_out, image_grad, norm_sums = plain_close(dqkv, xw, dm, raw_r, wq, first_gain)
    dot = lambda a, b: jnp.dot(a, b, preferred_element_type=F32)
    totals = (dot(n1_turned, dqkv[:ROWS]), dot(o_turned, da), dot(n2_turned, dh), dot(g_turned[:, :ROWS], cw))
    shard_sums = []
    for total in totals:
        part = lax.psum_scatter(total.astype(BF), ("row", "col"), scatter_dimension=0, tiled=True)
        shard_sums.append(lax.psum_scatter(part, "img", scatter_dimension=1, tiled=True).astype(F32))
    rows_grad, cols_grad = table_grads(table_sums)
    small_sums = lax.psum(
        tuple(jnp.sum(bias_sums, axis=1))
        + (jnp.sum(sums[0], axis=0), jnp.sum(up_sum, axis=0), jnp.sum(sums[1], axis=0))
        + tuple(jnp.sum(norm_sums, axis=1))
        + (jnp.sum(sums[2], axis=0), jnp.sum(sums[3], axis=0), rows_grad, cols_grad),
        ("img", "row", "col"),
    )
    return (image_out, image_grad, *shard_sums, *small_sums)


def solution(mesh):
    tiles = P("img", "row", "col", None)
    shards = P(("row", "col"), "img")
    return jax.shard_map(
        on_device,
        mesh=mesh,
        in_specs=(tiles,) * 2 + (shards,) * 4 + (P(),) * 11,
        out_specs=(tiles,) * 2 + (shards,) * 4 + (P(),) * 11,
        check_vma=False,
    )
```

```python
import functools

import jax
import jax.numpy as jnp
import numpy as np
from jax import lax
from jax.experimental import pallas as pl
from jax.experimental.pallas import tpu as pltpu
from jax.sharding import PartitionSpec as P

MESH = pl.DeviceIdType.MESH


def place():
    return lax.axis_index("img"), lax.axis_index("row"), lax.axis_index("col")


def side_owner(window_row, image):
    return lax.rem(window_row, 2), 3 - image - 2 * (window_row // 2)


def piece_target(kind, image, row, col):
    last_row, last_col = row == 3, col == 3
    side_row, side_col = side_owner(row, image)
    next_row, next_col = side_owner(lax.rem(row + 1, 4), image)
    if kind == 0:
        return (jnp.where(last_row, 3 - image, row + 1), col, jnp.where(last_row, 2, image))
    if kind == 1:
        return (jnp.where(last_col, side_row, row), jnp.where(last_col, side_col, col + 1), jnp.where(last_col, 2, image))
    target_row = jnp.where(last_row, 3 - image, jnp.where(last_col, next_row, row + 1))
    target_col = jnp.where(last_col, jnp.where(last_row, 3, next_col), col + 1)
    slot = jnp.where(last_row & last_col, 3, jnp.where(last_row | last_col, 2, image))
    return (target_row, target_col, slot)


def arrivals(row, col):
    wide = row >= 2
    side_row = row + 2 * (1 - col // 2)
    table = []
    for image in range(2):
        table.append((image, 0, row > 0))
        table.append((image, 1, col > 0))
        table.append((image, 2, (row > 0) & (col > 0)))
    table.append((2, 0, wide))
    table.append((2, 1, jnp.logical_not(wide)))
    table.append((2, 2, jnp.where(wide, col, side_row) > 0))
    table.append((3, 2, wide & (col == 3)))
    return table


def tile_part(ref, image, kind):
    if kind == 0:
        return ref.at[image, pl.ds(8, 8), pl.ds(0, 2)]
    if kind == 1:
        return ref.at[image, pl.ds(0, 14), pl.ds(1, 1)]
    return ref.at[image, pl.ds(8, 8), pl.ds(1, 1)]


def window_part(ref, slot, kind):
    if kind == 0:
        return ref.at[pl.ds(slot * 22, 8), pl.ds(1, 2)]
    if kind == 1:
        return ref.at[pl.ds(slot * 22 + 8, 14), pl.ds(0, 1)]
    return ref.at[pl.ds(slot * 22, 8), pl.ds(0, 1)]


def greet(img, row, col, pairs=True):
    barrier = pltpu.get_barrier_semaphore()
    for row_step in range(4):
        for col_step in range(4):
            if row_step or col_step:
                pl.semaphore_signal(
                    barrier,
                    inc=1,
                    device_id={"row": lax.rem(row + row_step, 4), "col": lax.rem(col + col_step, 4)},
                    device_id_type=MESH,
                )
    if pairs:
        pl.semaphore_signal(barrier, inc=1, device_id={"img": 1 - img}, device_id_type=MESH)
    pl.semaphore_wait(barrier, 16 if pairs else 15)


CHUNKS = ((0, 0, 640), (0, 640, 1152), (1, 0, 384), (2, 0, 768), (2, 768, 1536), (3, 0, 128), (3, 128, 384))


def links(shards, fulls, wsend, wrecv, wloc):
    img, row, col = place()
    y_row = lax.rem(row + 2, 4)
    core_row = row + 1 - 2 * lax.rem(row, 2)
    other = 1 - img
    sent = []

    def rows_of(w, rw, half=None):
        kb = fulls[w].shape[0] // 4
        if half is None:
            return pl.ds(pl.multiple_of(rw * kb, kb), kb)
        return pl.ds(pl.multiple_of(rw * kb + half * (kb // 2), kb // 2), kb // 2)

    def cols_of(n, im):
        w, lo, hi = CHUNKS[n]
        nb = fulls[w].shape[1] // 2
        return pl.ds(pl.multiple_of(im * nb + lo, 128), hi - lo)

    def block(n, rw, im, half=None):
        w = CHUNKS[n][0]
        return fulls[w].at[rows_of(w, rw, half), cols_of(n, im)]

    def slot(n, cl):
        w = CHUNKS[n][0]
        k16 = fulls[w].shape[0] // 16
        return fulls[w].at[pl.ds(pl.multiple_of((row * 4 + cl) * k16, k16), k16), cols_of(n, img)]

    def source(n):
        w, lo, hi = CHUNKS[n]
        return shards[w].at[:, pl.ds(lo, hi - lo)]

    def push(n, k, where, target, start=None):
        def copy():
            ref = slot(n, where) if start else block(n, *where)
            return pltpu.make_async_remote_copy(
                src_ref=source(n) if start and where is col else ref,
                dst_ref=ref,
                send_sem=wsend.at[n, k],
                recv_sem=wrecv.at[n, k],
                device_id=target(),
                device_id_type=MESH,
            )

        copy().start()
        sent.append(copy)

    def arrive(n, k, ref):
        pltpu.make_async_copy(ref, ref, wrecv.at[n, k]).wait()

    far_col, near_col = lax.rem(col + 2, 4), col + 1 - 2 * lax.rem(col, 2)

    def along_col(n):
        pltpu.make_async_copy(source(n), slot(n, col), wloc.at[n]).start()
        push(n, 0, col, lambda: {"col": far_col}, True)

    def near_by(n):
        pltpu.make_async_copy(source(n), slot(n, col), wloc.at[n]).wait()
        push(n, 1, col, lambda: {"col": near_col}, True)
        arrive(n, 0, slot(n, far_col))
        push(n, 2, far_col, lambda: {"col": near_col}, True)

    def first(n):
        arrive(n, 1, slot(n, near_col))
        arrive(n, 2, slot(n, 3 - col))
        push(n, 3, (row, img, 0), lambda: {"img": other})
        push(n, 4, (row, img, 1), lambda: {"row": y_row})
        push(n, 5, (row, img), lambda: {"row": core_row})

    def second(n):
        arrive(n, 3, block(n, row, other, 0))
        arrive(n, 4, block(n, y_row, img, 1))
        push(n, 6, (row, img, 0), lambda: {"row": y_row})
        push(n, 7, (row, other, 0), lambda: {"row": y_row})
        push(n, 8, (row, img, 1), lambda: {"img": other})
        push(n, 9, (y_row, img, 1), lambda: {"img": other})
        push(n, 10, (row, other, 0), lambda: {"row": core_row})
        push(n, 11, (y_row, img, 1), lambda: {"row": core_row})

    def third(n):
        arrive(n, 6, block(n, y_row, img, 0))
        arrive(n, 7, block(n, y_row, other, 0))
        arrive(n, 8, block(n, row, other, 1))
        arrive(n, 9, block(n, y_row, other, 1))
        push(n, 12, (y_row, img, 0), lambda: {"row": core_row})
        push(n, 13, (y_row, other, 0), lambda: {"row": core_row})
        push(n, 14, (row, other, 1), lambda: {"row": core_row})
        push(n, 15, (y_row, other, 1), lambda: {"row": core_row})

    def last(n):
        core_y = lax.rem(core_row + 2, 4)
        arrive(n, 5, block(n, core_row, img))
        arrive(n, 10, block(n, core_row, other, 0))
        arrive(n, 11, block(n, core_y, img, 1))
        arrive(n, 12, block(n, core_y, img, 0))
        arrive(n, 13, block(n, core_y, other, 0))
        arrive(n, 14, block(n, core_row, other, 1))
        arrive(n, 15, block(n, core_y, other, 1))

    return along_col, near_by, first, second, third, last, sent


def window_moves(tiles, raws, send, recv, loc):
    img, row, col = place()

    def each(t, act):
        for image in range(2):
            for kind in range(3):
                target_row, target_col, target_slot = piece_target(kind, image, row, col)
                here = (target_row == row) & (target_col == col)
                part = tile_part(tiles[t], image, kind)
                goal = window_part(raws[t], target_slot, kind)
                act(here, part, goal, send.at[t, image, kind], recv.at[t, target_slot, kind], target_row, target_col)

    def remote(part, goal, leave, arrival, target_row, target_col):
        return pltpu.make_async_remote_copy(
            src_ref=part,
            dst_ref=goal,
            send_sem=leave,
            recv_sem=arrival,
            device_id={"row": target_row, "col": target_col},
            device_id_type=MESH,
        )

    def own(t, image):
        return pltpu.make_async_copy(tiles[t].at[image, pl.ds(0, 14)], raws[t].at[pl.ds(image * 22 + 8, 14), pl.ds(1, 2)], loc.at[t, image])

    def start(t):
        for image in range(2):
            own(t, image).start()

        def act(here, part, goal, leave, arrival, target_row, target_col):
            @pl.when(here)
            def _():
                pltpu.make_async_copy(part, goal, arrival).start()

            @pl.when(jnp.logical_not(here))
            def _():
                remote(part, goal, leave, arrival, target_row, target_col).start()

        each(t, act)

    def arrived(t):
        for image in range(2):
            own(t, image).wait()
        for slot_index, kind, present in arrivals(row, col):
            part = window_part(raws[t], slot_index, kind)

            @pl.when(present)
            def _():
                pltpu.make_async_copy(part, part, recv.at[t, slot_index, kind]).wait()

    def left(t):
        def act(here, part, goal, leave, arrival, target_row, target_col):
            @pl.when(jnp.logical_not(here))
            def _():
                remote(part, goal, leave, arrival, target_row, target_col).wait_send()

        each(t, act)

    return start, arrived, left


BF = jnp.bfloat16
F32 = jnp.float32
ROWS = 704
SPAN = 800
FEATURES = 768
EPS = 1e-06


def row_params(step, row, col):
    wide = row >= 2
    side_row = row + 2 * (1 - col // 2)
    third_step = step - 28
    in_corner = wide & (third_step >= 8)
    slot = jnp.where(step < 14, 0, jnp.where(step < 28, 1, jnp.where(in_corner, 3, 2)))
    place_row = jnp.where(step < 14, step, jnp.where(step < 28, step - 14, jnp.where(in_corner, third_step - 8, third_step)))
    full = step < 28
    row_start = jnp.where(full, 8 - 2 * row, jnp.where(wide, 0, 8 - 2 * side_row))
    col_start = jnp.where(full, 8 - 2 * col, jnp.where(wide & jnp.logical_not(in_corner), 8 - 2 * col, 0))
    width = jnp.where(full, 14, jnp.where(wide & jnp.logical_not(in_corner), 14, 8))
    alive = jnp.where(full, True, jnp.where(in_corner, col == 3, jnp.where(wide, True, third_step < 14)))
    return slot, jnp.minimum(place_row + row_start, 21), col_start, jnp.where(alive, width, 0)


def window_params(window, row, col):
    wide = row >= 2
    start = jnp.where(window < 2, 14 * window, jnp.where(window == 2, 28, 36))
    tall = jnp.where(window < 2, 14, jnp.where((window == 2) & jnp.logical_not(wide), 14, 8))
    width = jnp.where(window < 2, 14, jnp.where((window == 2) & wide, 14, 8))
    return start, tall, width


def window_count(row, col):
    return jnp.where((row >= 2) & (col == 3), 4, 3)


def unit_of(values):
    center = values - jnp.mean(values, axis=-1, keepdims=True)
    inverse = lax.rsqrt(jnp.mean(center * center, axis=-1, keepdims=True) + EPS)
    return center * inverse, inverse


def relative_layout(backward):
    take = np.zeros((2, 2, 27, 128), np.float32)
    for parity in range(2):
        base = 64 if parity == 0 else 0
        for j in range(27):
            for copy in (0,) if backward else (0, 32):
                take[parity, 0, 26 - j, (base - 13 + j + copy) % 128] = 1
                if backward:
                    take[parity, 1, j, base + 16 + j] = 1
                else:
                    take[parity, 1, 26 - j, (base + 3 + j + copy) % 128] = 1
    return take


def takers(backward):
    return jnp.asarray(relative_layout(backward).reshape(4, 27, 128), BF)


def build_table(tab, rows_table, cols_table, take):
    tab[...] = jnp.zeros_like(tab)
    for parity in range(2):
        for which, table in ((0, rows_table), (1, cols_table)):
            block = lax.dot_general(table[...], take[2 * parity + which], (((0,), (0,)), ((), ())), preferred_element_type=F32)
            lane = 256 * parity + 128 * which
            tab[64 * parity : 64 * parity + 64, lane : lane + 128] = block.astype(BF)


def as_row(ref):
    return ref[...].reshape(1, -1)


def run_all(acts):
    for act in acts:
        act[0](*act[1:])


def plan_slots(plan, acts):
    slots = [[]]
    for name in plan:
        if name == "|":
            slots.append([])
        elif name in acts:
            slots[-1].append((acts[name],))
        else:
            slots[-1].append((acts[name[0]], int(name[1:])))
    return slots


def table_grads(sums):
    take = jnp.asarray(relative_layout(True), F32)
    grads = []
    for which in range(2):
        total = 0.0
        for parity in range(2):
            part = sums[64 * parity : 64 * parity + 64, 256 * parity + 128 * which : 256 * parity + 128 * which + 128]
            total = total + lax.dot_general(take[parity, which], part, (((1,), (1,)), ((), ())), precision=lax.Precision.HIGHEST)
        grads.append(total)
    return grads


FF = 3072
CHUNK = 512
BLOCK = 176


def nt(a, b):
    return lax.dot_general(a, b, (((1,), (1,)), ((), ())), preferred_element_type=F32)


def norm_back(grad, unit, inverse, gain):
    scaled = grad * gain
    first_mean = jnp.mean(scaled, axis=-1, keepdims=True)
    second_mean = jnp.mean(scaled * unit, axis=-1, keepdims=True)
    return inverse * (scaled - first_mean - unit * second_mean)


def fold_rows(values):
    total = values[0:8]
    for i in range(1, values.shape[0] // 8):
        total = total + values[8 * i : 8 * i + 8]
    return total


def spread_rows(source, raw, row, col):
    def step(i, _):
        slot, raw_row, col_start, width = row_params(i, row, col)
        at = pl.ds(pl.multiple_of(i * 16, 16), 16)

        @pl.when(width > 0)
        def _():
            values = jnp.concatenate([source[at, :], jnp.zeros((8, FEATURES), F32)], axis=0)
            raw[slot * 22 + raw_row] = pltpu.roll(values, col_start, 0).astype(BF).reshape(3, 8, FEATURES)

        return 0

    lax.fori_loop(0, 44, step, 0)


OPEN_PLAN = ("a0", "a2", "a1", "b0", "b2", "a6", "10", "b1", "a5", "Wx", "11", "b5", "b6", "12", "20", "22", "21", "15", "a3", "X", "16", "a4", "b3", "31", "30", "25", "L1", "L0", "P", "32", "13", "b4", "26", "|", "|", "L2", "|", "|", "Wc", "|", "|", "|", "|", "|", "|", "|", "35", "|", "|", "|", "|", "23", "14", "|", "36", "|", "U", "|", "M", "K", "T", "33", "24", "L3", "L5", "L6", "|", "34", "|", "L4", "|", "|")


def open_kernel(weights, x_ref, c_ref, gain, shift, query_bias, value_bias, rows_table, cols_table, take, out_bias, up_bias, down_bias, gain2, shift2, *refs):
    img, row, col = place()
    greet(img, row, col, weights)
    if weights:
        shards, refs = refs[:4], refs[4:]
    else:
        wq, wo, wu, wd = refs[:4]
        refs = refs[4:]
    xw_out, cw_out, n1_out, qkv_out, probs_out, o_out, o_turned_out = refs[:7]
    raw_out, n2_out, g_out, dh_out, da, do, dm, sums, up_sum = refs[7:16]
    refs = refs[16:]
    if weights:
        wq_out, refs = refs[0], refs[1:]
    rawx, rawc, n1, tab, row_bias, qkv_s, probs, y_s, d_s, g_s, g_chunk, dh_chunk, xw, cw, n1_turned, o, o_turned, n2_turned, hot, out_sem, probs_sem, send, recv, loc = refs[:24]
    refs = refs[24:]
    flushes = ((xw, xw_out), (cw, cw_out), (n1_turned, n1_out), (o, o_out), (o_turned, o_turned_out), (n2_turned, n2_out))

    def flush(i):
        return pltpu.make_async_copy(flushes[i][0], flushes[i][1], out_sem.at[5 + i])

    if weights:
        wq, wo, wu, wd = refs[:4]
        along_col, near_by, first, second, third, last, sent = links(shards, refs[:4], *refs[4:])
    window_start, window_arrived, window_left = window_moves((x_ref, c_ref), (rawx, rawc), send, recv, loc)
    places = lax.broadcasted_iota(jnp.int32, (16, 1), 0)

    def cut_one(raw, step):
        slot, raw_row, col_start, width = row_params(step, row, col)
        wide_rows = raw[slot * 22 + raw_row].reshape(24, FEATURES).astype(F32)
        keep = places < width
        return keep, jnp.where(keep, pltpu.roll(wide_rows, lax.rem(24 - col_start, 24), 0)[:16], 0.0)

    def cut_x(step, _):
        at = pl.ds(pl.multiple_of(step * 16, 16), 16)
        keep, x = cut_one(rawx, step)
        xw[at, :] = x.astype(BF)
        unit, _inverse = unit_of(x)
        n1[at, :] = jnp.where(keep, unit * as_row(gain) + as_row(shift), 0.0).astype(BF)
        return 0

    def cut_c(step, _):
        at = pl.ds(pl.multiple_of(step * 16, 16), 16)
        _keep, c = cut_one(rawc, step)
        cw[at, :] = c.astype(BF)
        return 0

    def project(step, _):
        at = pl.ds(pl.multiple_of(step * 352, 32), 352)
        for part_index in range(3):
            lanes = slice(part_index * FEATURES, (part_index + 1) * FEATURES)
            part = jnp.dot(n1[at, :], wq[:, lanes], preferred_element_type=F32)
            if part_index != 1:
                part = part + row_bias[part_index // 2]
            qkv_s[at, lanes] = part.astype(BF)
        return 0

    def turn(source, goal):
        def step(i, _):
            lanes = pl.ds(pl.multiple_of(i * 128, 128), 128)
            goal[lanes, :] = source[0:ROWS, lanes].T
            return 0

        lax.fori_loop(0, FEATURES // 128, step, 0)

    def cut_windows():
        window_arrived(0)
        lax.fori_loop(0, 44, cut_x, 0)
        flush(0).start()

    def cut_cotangent():
        window_arrived(1)
        lax.fori_loop(0, 44, cut_c, 0)
        flush(1).start()

    def project_all():
        lax.fori_loop(0, 2, project, 0)
        pltpu.make_async_copy(qkv_s, qkv_out, out_sem.at[0]).start()
        if weights:
            pltpu.make_async_copy(wq, wq_out, out_sem.at[1]).start()

    def turn_all():
        turn(o, o_turned)
        flush(3).start()
        flush(4).start()

    def turn_first():
        turn(n1, n1_turned)
        flush(2).start()

    blocks = (slice(0, 352), slice(352, 704))

    def middle_begin():
        sums[...] = jnp.zeros_like(sums)
        up_sum[...] = jnp.zeros_like(up_sum)
        d_s[...] = jnp.zeros_like(d_s)

        def begin(i, _):
            at = pl.ds(pl.multiple_of(i * BLOCK, 16), BLOCK)
            mid = xw[at, :].astype(F32) + (jnp.dot(o[at, :], wo[...], preferred_element_type=F32) + as_row(out_bias))
            unit, _inverse = unit_of(mid)
            n1[at, :] = (unit * as_row(gain2) + as_row(shift2)).astype(BF)
            y_s[at, :] = mid + as_row(down_bias)
            dm[at, :] = mid
            return 0

        lax.fori_loop(0, ROWS // BLOCK, begin, 0)
        turn(n1, n2_turned)
        flush(5).start()

    def chunk_out(which, step):
        lanes = pl.ds(pl.multiple_of(step * FEATURES, FEATURES), FEATURES)
        if which == 0:
            return pltpu.make_async_copy(g_chunk, g_out.at[lanes, :], out_sem.at[2])
        return pltpu.make_async_copy(dh_chunk, dh_out.at[:, lanes], out_sem.at[3])

    def middle_step(turn_index, _):
        for i, slot_acts in enumerate(middle_slots):
            if slot_acts:
                pl.when(turn_index == i)(functools.partial(run_all, slot_acts))
        step = lax.rem(turn_index, 2) * 2 + turn_index // 2
        lanes = pl.ds(pl.multiple_of(step * FEATURES, FEATURES), FEATURES)

        @pl.when(turn_index > 0)
        def _():
            chunk_out(0, 0).wait()
            chunk_out(1, 0).wait()

        for at in blocks:
            h = jnp.dot(n1[at, :], wu[:, lanes], preferred_element_type=F32) + up_bias[:, lanes]
            up = nt(cw[at, :], wd[lanes, :])
            phi = 0.5 * (1.0 + lax.erf(h * 0.7071067811865476))
            slope = phi + h * (jnp.exp(-0.5 * h * h) * 0.3989422804014327)
            active = (h * phi).astype(BF)
            back = (up * slope).astype(BF)
            g_s[at, :] = active
            dh_chunk[at, :] = back
            up_sum[:, lanes] += fold_rows(back.astype(F32))
            y_s[at, :] += jnp.dot(active, wd[lanes, :], preferred_element_type=F32)
            d_s[at, :] += nt(back, wu[:, lanes])
        for i in range(FEATURES // 128):
            g_chunk[128 * i : 128 * i + 128, 0:ROWS] = g_s[:, 128 * i : 128 * i + 128].T
        chunk_out(0, step).start()
        chunk_out(1, step).start()
        return 0

    def middle_end():
        def end(i, _):
            at = pl.ds(pl.multiple_of(i * BLOCK, 16), BLOCK)
            unit, inverse = unit_of(dm[at, :])
            grad = d_s[at, :].astype(BF).astype(F32)
            up = cw[at, :].astype(F32)
            grad_mid = up + norm_back(grad, unit, inverse, as_row(gain2))
            low_grad = grad_mid.astype(BF)
            dm[at, :] = grad_mid
            da[at, :] = low_grad
            do[at, :] = nt(low_grad, wo[...]).astype(BF)
            sums[0] += fold_rows(low_grad.astype(F32))
            sums[1] += fold_rows(up)
            sums[2] += fold_rows(grad * unit)
            sums[3] += fold_rows(grad)
            return 0

        spread_rows(y_s, rawx, row, col)
        raw_copy = pltpu.make_async_copy(rawx, raw_out, out_sem.at[4])
        raw_copy.start()
        lax.fori_loop(0, ROWS // BLOCK, end, 0)
        raw_copy.wait()

    acts = {"X": cut_windows, "P": project_all, "T": turn_all, "U": turn_first, "K": cut_cotangent, "M": middle_begin}
    acts["Wx"] = functools.partial(window_start, 0)
    acts["Wc"] = functools.partial(window_start, 1)
    if weights:
        acts.update({"a": along_col, "b": near_by, "1": first, "2": second, "3": third, "L": last})
        slots = plan_slots(OPEN_PLAN, acts)
    else:
        slots = plan_slots(("Wx", "Wc", "X", "P", *("|",) * 18, "T", "U", "K", "M", *("|",) * 4), acts)
    run_all(slots[0][:3])
    o[...] = jnp.zeros_like(o)
    build_table(tab, rows_table, cols_table, take)
    row_bias[0] = as_row(query_bias)
    row_bias[1] = as_row(value_bias)
    key_place = lax.broadcasted_iota(jnp.int32, (224, 128), 0)
    key_lane = lax.broadcasted_iota(jnp.int32, (224, 128), 1)
    key_a, key_b = key_place // 16, key_place % 16
    for parity in range(2):
        key_on = key_lane - (64 if parity == 0 else 0)
        hot[parity] = jnp.where(
            key_on == 14,
            jnp.where(key_b >= 14, 1.0, 0.0),
            jnp.where(
                (key_on % 32 < 14) & (key_a == key_on % 32),
                1.0,
                jnp.where((key_on % 32 >= 16) & (key_on % 32 < 30) & (key_b == key_on % 32 - 16), 1.0, 0.0),
            ),
        )
    run_all(slots[0][3:])
    row_of = lax.broadcasted_iota(jnp.int32, (224, 1), 0)
    lane = lax.broadcasted_iota(jnp.int32, (1, 128), 1)
    def probs_copy(index):
        window, pair_index = index // 6, index % 6
        part = pl.ds(2 * pair_index, 2)
        return pltpu.make_async_copy(probs.at[window, part], probs_out.at[window, part], probs_sem.at[window, pair_index])

    def attend(window, pair_index, rows):
        start, tall, width = window_params(window, row, col)
        at = pl.ds(pl.multiple_of(start * 16, 16), 224)
        q_at = pl.ds(pl.multiple_of(start * 16, 16), rows)
        alive = (row_of // 16 < tall) & (row_of % 16 < width)
        lanes = lambda third: pl.ds(pl.multiple_of(third * FEATURES + pair_index * 128, 128), 128)
        q = jnp.where(alive[:rows], qkv_s[q_at, lanes(0)].astype(F32), 0.0)
        k = jnp.where(alive, qkv_s[at, lanes(1)].astype(F32), 0.0)
        v = jnp.where(alive, qkv_s[at, lanes(2)].astype(F32), row_bias[1, :, lanes(0)].astype(BF).astype(F32)).astype(BF)
        terms = jnp.dot(q.astype(BF), tab[...], preferred_element_type=F32)
        lines = [slice(16 * a, 16 * a + 16) for a in range(rows // 16)]
        outs = []
        for parity in range(2):
            own = (lane < 64) if parity == 0 else (lane >= 64)
            first_lane = 256 * parity
            rel_rows = jnp.concatenate(
                [pltpu.roll(terms[at_a, first_lane : first_lane + 128], a, 1) for a, at_a in enumerate(lines)], axis=0
            )
            rel_cols = jnp.concatenate(
                [pltpu.roll(terms[at_a, first_lane + 128 : first_lane + 256], 0, 1, stride=1, stride_axis=0) for at_a in lines], axis=0
            )
            on = lane - (64 if parity == 0 else 0)
            in_rows = ((on >= 0) & (on < 14)) | ((on >= 32) & (on < 46))
            in_cols = ((on >= 16) & (on < 30)) | ((on >= 48) & (on < 62))
            rel = jnp.where(in_rows, rel_rows, jnp.where(in_cols, rel_cols, 0.0))
            rough = rel.astype(BF).astype(F32)
            fine = jnp.where(on >= 32, rel - rough, rough)
            fine = jnp.where(on == 14, -1e30, fine)
            q_side = jnp.where(own, q * 0.125, fine).astype(BF)
            k_side = jnp.where(own, k, hot[parity]).astype(BF)
            scores = lax.dot_general(q_side, k_side, (((1,), (1,)), ((), ())), preferred_element_type=F32)
            exponent = jnp.exp(scores - jnp.max(scores, axis=-1, keepdims=True))
            p = (exponent * (1.0 / jnp.sum(exponent, axis=-1, keepdims=True))).astype(BF)
            probs[window, 2 * pair_index + parity, 0:rows, :] = p
            if rows < 224:
                probs[window, 2 * pair_index + parity, rows:224, :] = jnp.zeros((224 - rows, 224), BF)
            outs.append(jnp.dot(p, v, preferred_element_type=F32))
        blended = jnp.where(lane < 64, outs[0], outs[1])
        o[q_at, lanes(0)] = jnp.where(alive[:rows], blended, 0.0).astype(BF)

    def pair(index, _):
        for i, slot_acts in enumerate(slots[1:18]):
            if slot_acts:
                pl.when(index == i + 1)(functools.partial(run_all, slot_acts))
        window, pair_index = index // 6, index % 6
        short = (window >= 2) & (row >= 2)
        pl.when(short)(functools.partial(attend, window, pair_index, 128))
        pl.when(jnp.logical_not(short))(functools.partial(attend, window, pair_index, 224))
        probs_copy(index).start()
        return 0

    pairs = window_count(row, col) * 6
    lax.fori_loop(0, pairs, pair, 0)
    run_all(slots[18])
    middle_slots = [[], *slots[19:22]]
    lax.fori_loop(0, 4, middle_step, 0)
    run_all(slots[22])
    middle_end()
    chunk_out(0, 0).wait()
    chunk_out(1, 0).wait()
    pltpu.make_async_copy(qkv_s, qkv_out, out_sem.at[0]).wait()
    if weights:
        pltpu.make_async_copy(wq, wq_out, out_sem.at[1]).wait()
        for copy in sent:
            copy().wait_send()
    lax.fori_loop(0, pairs, lambda index, _: (probs_copy(index).wait(), 0)[1], 0)
    for i in range(6):
        flush(i).wait()
    window_left(0)
    window_left(1)


def open_windows(x, c, shards, gain, shift, query_bias, value_bias, rows_table, cols_table, out_bias, up_bias, down_bias, gain2, shift2):
    vm = pl.BlockSpec(memory_space=pltpu.VMEM)
    an = pl.BlockSpec(memory_space=pl.ANY)
    shape = jax.ShapeDtypeStruct
    dma = pltpu.SemaphoreType.DMA
    chunks = len(CHUNKS)
    weights = lax.axis_size("img") == 2
    if weights:
        given = list(shards)
    else:
        widened = [lax.all_gather(w, "img", axis=1, tiled=True) for w in shards]
        gathered = [lax.all_gather(w, ("row", "col"), axis=0, tiled=True) for w in widened]
        given = gathered
    raw = pltpu.VMEM((88, 3, 8, FEATURES), BF)
    outs = pl.pallas_call(
        functools.partial(open_kernel, weights),
        out_shape=[
            shape((ROWS, FEATURES), BF),
            shape((ROWS, FEATURES), BF),
            shape((FEATURES, ROWS), BF),
            shape((SPAN, 3 * FEATURES), BF),
            shape((4, 12, 224, 224), BF),
            shape((SPAN, FEATURES), BF),
            shape((FEATURES, ROWS), BF),
        ]
        + [
            shape((88, 3, 8, FEATURES), BF),
            shape((FEATURES, ROWS), BF),
            shape((FF, FEATURES), BF),
            shape((ROWS, FF), BF),
            shape((ROWS, FEATURES), BF),
            shape((SPAN, FEATURES), BF),
            shape((ROWS, FEATURES), F32),
            shape((4, 8, FEATURES), F32),
            shape((8, FF), F32),
        ]
        + ([shape((768, 2304), BF)] if weights else []),
        in_specs=[vm] * (14 + len(given)),
        out_specs=[an] * 11 + [vm] * 5 + ([an] if weights else []),
        scratch_shapes=[
            raw,
            raw,
            pltpu.VMEM((ROWS, FEATURES), BF),
            pltpu.VMEM((128, 512), BF),
            pltpu.VMEM((2, 1, FEATURES), F32),
            pltpu.VMEM((SPAN, 3 * FEATURES), BF),
            pltpu.VMEM((4, 12, 224, 224), BF),
            pltpu.VMEM((ROWS, FEATURES), F32),
            pltpu.VMEM((ROWS, FEATURES), F32),
            pltpu.VMEM((ROWS, FEATURES), BF),
            pltpu.VMEM((FEATURES, FEATURES), BF),
            pltpu.VMEM((ROWS, FEATURES), BF),
            pltpu.VMEM((ROWS, FEATURES), BF),
            pltpu.VMEM((ROWS, FEATURES), BF),
            pltpu.VMEM((FEATURES, ROWS), BF),
            pltpu.VMEM((SPAN, FEATURES), BF),
            pltpu.VMEM((FEATURES, ROWS), BF),
            pltpu.VMEM((FEATURES, ROWS), BF),
            pltpu.VMEM((2, 224, 128), F32),
            dma((11,)),
            dma((4, 6)),
            dma((2, 2, 3)),
            dma((2, 4, 3)),
            dma((2, 2)),
        ]
        + ([pltpu.VMEM(s, BF) for s in WHOLES] + [dma((chunks, 16)), dma((chunks, 16)), dma((chunks,))] if weights else []),
        compiler_params=pltpu.CompilerParams(collective_id=0, has_side_effects=True, vmem_limit_bytes=67043328),
    )(x.reshape(2, 16, 2, 8, 768), c.reshape(2, 16, 2, 8, 768), gain, shift, query_bias, value_bias, rows_table, cols_table, takers(False), out_bias, up_bias, down_bias, gain2, shift2, *given)
    return list(outs) if weights else list(outs) + gathered[:1]


def key_marks(hot):
    key_place = lax.broadcasted_iota(jnp.int32, (224, 128), 0)
    key_lane = lax.broadcasted_iota(jnp.int32, (224, 128), 1)
    key_a, key_b = key_place // 16, key_place % 16
    for parity in range(2):
        key_on = key_lane - (64 if parity == 0 else 0)
        hot[parity] = jnp.where(
            (key_on >= 0) & (key_on < 14) & (key_a == key_on),
            1.0,
            jnp.where((key_on >= 16) & (key_on < 30) & (key_b == 29 - key_on), 1.0, 0.0),
        )


def attention_back(window, pair_index, probs_of, do, qkv, o, tab, hot, value_bias, bias_sums, table_sums, row, col):
    row_of = lax.broadcasted_iota(jnp.int32, (224, 1), 0)
    lane = lax.broadcasted_iota(jnp.int32, (1, 128), 1)
    start, tall, width = window_params(window, row, col)
    at = pl.ds(pl.multiple_of(start * 16, 16), 224)
    inside = row_of // 16 < tall
    alive = inside & (row_of % 16 < width)
    lanes = lambda third: pl.ds(pl.multiple_of(third * FEATURES + pair_index * 128, 128), 128)
    old = [qkv[at, lanes(third)].astype(F32) for third in range(3)]
    q = jnp.where(alive, old[0], 0.0)
    k = jnp.where(alive, old[1], 0.0)
    v = jnp.where(alive, old[2], value_bias[:, lanes(0)].astype(BF).astype(F32))
    grad = jnp.where(alive, do[at, lanes(0)].astype(F32), 0.0)
    product = grad * jnp.where(alive, o[at, lanes(0)].astype(F32), 0.0)
    q_turned = q.T.astype(BF)
    grad_turned = grad.T.astype(BF)
    value_parts, key_parts, query_parts, table_parts = [], [], [], []
    for parity in range(2):
        base = 64 if parity == 0 else 0
        own = (lane < 64) if parity == 0 else (lane >= 64)
        half = slice(64 * parity, 64 * parity + 64)
        inner = jnp.sum(jnp.where(own, product, 0.0), axis=-1, keepdims=True)
        rough = inner.astype(BF).astype(F32)
        on = lane - base
        grad_side = jnp.where(own, grad, jnp.where(on == 0, rough, jnp.where(on == 1, inner - rough, 0.0))).astype(BF)
        v_side = jnp.where(own, v, jnp.where((on == 0) | (on == 1), -1.0, 0.0)).astype(BF)
        centered = nt(grad_side, v_side)
        p = probs_of(parity)
        ds = (p.astype(F32) * centered).astype(BF)
        value_parts.append(jnp.dot(grad_turned[half], p, preferred_element_type=F32))
        key_parts.append(jnp.dot(q_turned[half], ds, preferred_element_type=F32))
        k_side = jnp.where(own, k * 0.125, hot[parity]).astype(BF)
        wide = jnp.dot(ds, k_side, preferred_element_type=F32)
        query_parts.append(wide)
        by_rows = jnp.where((on >= 0) & (on < 14), wide, 0.0)
        by_cols = jnp.where((on >= 16) & (on < 30), wide, 0.0)
        table_parts.append(jnp.concatenate([pltpu.roll(by_rows[16 * a : 16 * a + 16], (128 - a) % 128, 1) for a in range(14)], axis=0))
        table_parts.append(
            jnp.concatenate([pltpu.roll(by_cols[16 * a : 16 * a + 16], 0, 1, stride=1, stride_axis=0) for a in range(14)], axis=0)
        )
    turned = jnp.concatenate(table_parts, axis=1).astype(BF)
    dq = jnp.where(lane < 64, query_parts[0], query_parts[1]) + nt(turned, tab[...])
    table_sums[...] += jnp.dot(q_turned, turned, preferred_element_type=F32)
    dk = jnp.concatenate(key_parts, axis=0).T * 0.125
    dv = jnp.concatenate(value_parts, axis=0).T.astype(BF).astype(F32)
    dq = jnp.where(alive, dq, 0.0).astype(BF).astype(F32)
    bias_sums[0, :, lanes(0)] += fold_rows(dq)
    bias_sums[1, :, lanes(0)] += fold_rows(dv)
    for third, new in enumerate((dq, dk, dv)):
        qkv[at, lanes(third)] = jnp.where(alive, new, jnp.where(inside, 0.0, old[third])).astype(BF)


def clear_idle(qkv, row, col):
    wide = row >= 2
    limit = jnp.where(wide, jnp.where(col == 3, 44, 36), 42)
    for a in range(36, 44):

        @pl.when(a >= limit)
        def _():
            qkv[16 * a : 16 * a + 16, :] = jnp.zeros((16, 3 * FEATURES), BF)


def plain_back_kernel(do, probs, qkv, o, value_bias, rows_table, cols_table, take, dqkv, bias_sums, table_sums, tab, row_bias, hot):
    row, col = lax.axis_index("row"), lax.axis_index("col")
    build_table(tab, rows_table, cols_table, take)
    row_bias[...] = as_row(value_bias)
    key_marks(hot)
    dqkv[...] = qkv[...]
    clear_idle(dqkv, row, col)
    bias_sums[...] = jnp.zeros_like(bias_sums)
    table_sums[...] = jnp.zeros_like(table_sums)

    def pair(index, _):
        window, pair_index = index // 6, index % 6
        attention_back(
            window,
            pair_index,
            lambda parity: probs[window, 2 * pair_index + parity],
            do,
            dqkv,
            o,
            tab,
            hot,
            row_bias,
            bias_sums,
            table_sums,
            row,
            col,
        )
        return 0

    lax.fori_loop(0, window_count(row, col) * 6, pair, 0)


def plain_back(do, probs, qkv, o, value_bias, rows_table, cols_table):
    vm = pl.BlockSpec(memory_space=pltpu.VMEM)
    shape = jax.ShapeDtypeStruct
    return pl.pallas_call(
        plain_back_kernel,
        out_shape=[shape((SPAN, 3 * FEATURES), BF), shape((2, 8, FEATURES), F32), shape((128, 512), F32)],
        in_specs=[vm] * 8,
        out_specs=[vm] * 3,
        scratch_shapes=[pltpu.VMEM((128, 512), BF), pltpu.VMEM((1, FEATURES), F32), pltpu.VMEM((2, 224, 128), F32)],
        compiler_params=pltpu.CompilerParams(vmem_limit_bytes=62 << 20),
    )(do, probs, qkv, o, value_bias, rows_table, cols_table, takers(True))


WHOLES = ((768, 2304), (768, 768), (768, 3072), (3072, 768))
SUM_CHUNKS = ((1, 0, 384), (3, 0, 128), (3, 128, 384), (2, 0, 768), (2, 768, 1536), (0, 0, 384), (0, 384, 768), (0, 768, 1152))


def pair_lanes(j, im):
    if im == 0:
        return (128 * j, FEATURES + 128 * j, 128 * (j + 3))
    return (2 * FEATURES + 128 * j, FEATURES + 128 * (j + 3), 2 * FEATURES + 128 * (j + 3))


def land_shapes(chunks):
    lands = []
    for w, lo, hi in chunks:
        kb, width = WHOLES[w][0] // 4, hi - lo
        lands += [
            pltpu.VMEM((2, 2, kb, width), BF),
            pltpu.VMEM((2, kb // 2, width), BF),
            pltpu.VMEM((2, kb // 2, width), BF),
            pltpu.VMEM((2, kb // 2, width), BF),
            pltpu.VMEM((3, kb // 4, width), BF),
        ]
    return lands


def reducers(chunks, full, left_turned, right_side, grads, land_refs, wsend, wrecv):
    img, row, col = place()
    y_row = lax.rem(row + 2, 4)
    core_row = row + 1 - 2 * lax.rem(row, 2)
    core_y = lax.rem(core_row + 2, 4)
    other = 1 - img
    far_col, near_col = lax.rem(col + 2, 4), col + 1 - 2 * lax.rem(col, 2)
    lands = [land_refs[5 * n : 5 * n + 5] for n in range(len(chunks))]
    sent = []

    def size(n):
        w, lo, hi = chunks[n]
        return WHOLES[w][0] // 4, WHOLES[w][1] // 2, lo, hi - lo

    def block(n, rw, im, half=None):
        kb, nb, lo, width = size(n)
        cols = pl.ds(pl.multiple_of(im * nb + lo, 128), width)
        if half is None:
            return full[chunks[n][0]].at[pl.ds(pl.multiple_of(rw * kb, kb), kb), cols]
        return full[chunks[n][0]].at[pl.ds(pl.multiple_of(rw * kb + half * (kb // 2), kb // 2), kb // 2), cols]

    def shard(n, cl):
        kb, nb, lo, width = size(n)
        cols = pl.ds(pl.multiple_of(img * nb + lo, 128), width)
        return full[chunks[n][0]].at[pl.ds(pl.multiple_of(row * kb + cl * (kb // 4), kb // 4), kb // 4), cols]

    def push(n, k, src, dst, target):
        def copy():
            return pltpu.make_async_remote_copy(
                src_ref=src(), dst_ref=dst(), send_sem=wsend.at[n, k], recv_sem=wrecv.at[n, k], device_id=target(), device_id_type=MESH
            )

        copy().start()
        sent.append(copy)

    def arrive(n, k, ref):
        pltpu.make_async_copy(ref, ref, wrecv.at[n, k]).wait()

    def add(goal, part, rows):
        def step(i, _):
            at = pl.ds(pl.multiple_of(i * 48, 16), 48)
            goal[at, :] = (goal[at, :].astype(F32) + part[at, :].astype(F32)).astype(BF)
            return 0

        lax.fori_loop(0, rows // 48, step, 0)

    def product(n, rw):
        w = chunks[n][0]
        kb, nb, lo, width = size(n)
        rows = pl.ds(pl.multiple_of(rw * kb, kb), kb)
        for im in range(2):
            at = slice(im * nb + lo, im * nb + lo + width)
            if w == 0:
                right = jnp.concatenate([right_side[0][0:ROWS, p : p + 128] for p in pair_lanes(lo // 384, im)], axis=1)
            else:
                right = right_side[w][0:ROWS, at]
            full[w][rows, at] = jnp.dot(left_turned[w](rw, kb), right, preferred_element_type=F32).astype(BF)

    def pair_stage(n):
        land = lands[n][0]
        for j, rw in enumerate((core_row, core_y)):
            product(n, rw)
            for im in range(2):
                push(n, 2 * j + im, functools.partial(block, n, rw, im), lambda j=j, im=im: land.at[j, im], lambda: {"row": core_row})
        for rw in (row, y_row):
            product(n, rw)

    def first(n):
        kb, nb, lo, width = size(n)
        for j, rw in enumerate((row, y_row)):
            for im in range(2):
                arrive(n, 2 * j + im, lands[n][0].at[j, im])
                add(block(n, rw, im), lands[n][0].at[j, im], kb)
        for im in range(2):
            push(n, 4 + im, functools.partial(block, n, y_row, im, 0), lambda im=im: lands[n][1].at[im], lambda: {"row": y_row})
        push(n, 6, functools.partial(block, n, row, other, 1), lambda: lands[n][2].at[0], lambda: {"img": other})
        push(n, 7, functools.partial(block, n, y_row, other, 1), lambda: lands[n][2].at[1], lambda: {"img": other})

    def second(n):
        kb, nb, lo, width = size(n)
        for im in range(2):
            arrive(n, 4 + im, lands[n][1].at[im])
            add(block(n, row, im, 0), lands[n][1].at[im], kb // 2)
        push(n, 8, functools.partial(block, n, row, other, 0), lambda: lands[n][3].at[0], lambda: {"img": other})
        for j, rw in enumerate((row, y_row)):
            arrive(n, 6 + j, lands[n][2].at[j])
            add(block(n, rw, img, 1), lands[n][2].at[j], kb // 2)
        push(n, 9, functools.partial(block, n, y_row, img, 1), lambda: lands[n][3].at[1], lambda: {"row": y_row})

    def third(n):
        kb, nb, lo, width = size(n)
        for half in range(2):
            arrive(n, 8 + half, lands[n][3].at[half])
            add(block(n, row, img, half), lands[n][3].at[half], kb // 2)
        push(n, 10, lambda: shard(n, near_col), lambda: lands[n][4].at[0], lambda: {"col": near_col})
        push(n, 11, lambda: shard(n, 3 - col), lambda: lands[n][4].at[1], lambda: {"col": near_col})

    def fourth(n):
        kb = size(n)[0]
        arrive(n, 11, lands[n][4].at[1])
        add(shard(n, far_col), lands[n][4].at[1], kb // 4)
        push(n, 12, lambda: shard(n, far_col), lambda: lands[n][4].at[2], lambda: {"col": far_col})

    def fifth(n):
        w, lo, hi = chunks[n]
        arrive(n, 10, lands[n][4].at[0])
        arrive(n, 12, lands[n][4].at[2])
        mine = shard(n, col)

        def step(part, _):
            at = pl.ds(pl.multiple_of(part * 48, 16), 48)
            total = mine[at, :].astype(F32) + lands[n][4][0, at, :].astype(F32) + lands[n][4][2, at, :].astype(F32)
            if w > 0:
                grads[w][at, lo:hi] = total
            else:
                for im in range(2):

                    @pl.when(img == im)
                    def _():
                        for i, p in enumerate(pair_lanes(lo // 384, im)):
                            lane = p - 1152 * im
                            grads[0][at, lane : lane + 128] = total[:, 128 * i : 128 * i + 128]

            return 0

        lax.fori_loop(0, WHOLES[w][0] // 16 // 48, step, 0)

    return pair_stage, first, second, third, fourth, fifth, sent


def table_taker():
    take = relative_layout(True)
    out = np.zeros((4, 128, 128), np.float32)
    for parity in range(2):
        for which in range(2):
            out[2 * parity + which, :, 64 * which : 64 * which + 27] = take[parity, which].T
    return out


def source_tiles(row, col):
    wide = row >= 2
    side_row = row + 2 * (1 - col // 2)
    table = []
    for image in range(2):
        table.append((image, 0, image, row - 1, col, row > 0))
        table.append((image, 1, image, row, col - 1, col > 0))
        table.append((image, 2, image, row - 1, col - 1, (row > 0) & (col > 0)))
    third_image = jnp.where(wide, 3 - row, 1 - lax.rem(col, 2))
    table.append((2, 0, third_image, 3, col, wide))
    table.append((2, 1, third_image, side_row, 3, jnp.logical_not(wide)))
    table.append((2, 2, third_image, jnp.where(wide, 3, side_row - 1), jnp.where(wide, col - 1, 3), jnp.where(wide, col, side_row) > 0))
    table.append((3, 2, 3 - row, 3, 3, wide & (col == 3)))
    return table


CLOSE_PLAN = ("p1", "p2", "11", "|", "|", "12", "p4", "|", "|", "14", "21", "|", "p0", "|", "|", "p3", "|", "22", "|", "p5", "24", "|", "10", "31", "|", "|", "|", "|", "|", "|", "|", "13", "|", "32", "41", "15", "34", "G0", "G1", "G2", "42", "p7", "G3", "S", "p6", "23", "s0", "25", "20", "17", "16", "30", "s1", "44", "35", "27", "40", "52", "33", "26", "s2", "45", "37", "51", "50", "36", "s3", "43", "54", "47", "46", "53", "57", "55", "56", "s4")


def returns(raws, landing, send, recv, row, col):
    def each(t, act):
        for slot, kind, image, tile_row, tile_col, present in source_tiles(row, col):
            here = (tile_row == row) & (tile_col == col)
            act(slot, kind, image, tile_row, tile_col, present & here, present & jnp.logical_not(here))

    def start(t):
        def act(slot, kind, image, tile_row, tile_col, local, remote):
            @pl.when(local)
            def _():
                pltpu.make_async_copy(
                    window_part(raws[t], slot, kind), landing[t][kind].at[image], recv.at[t, image, kind]
                ).start()

            @pl.when(remote)
            def _():
                hop(t, slot, kind, image, tile_row, tile_col).start()

        each(t, act)

    def hop(t, slot, kind, image, tile_row, tile_col):
        return pltpu.make_async_remote_copy(
            src_ref=window_part(raws[t], slot, kind),
            dst_ref=landing[t][kind].at[image],
            send_sem=send.at[t, slot, kind],
            recv_sem=recv.at[t, image, kind],
            device_id={"row": jnp.maximum(tile_row, 0), "col": jnp.maximum(tile_col, 0)},
            device_id_type=MESH,
        )

    def arrived(t):
        for image in range(2):
            for kind in range(3):
                goal = landing[t][kind].at[image]
                pltpu.make_async_copy(goal, goal, recv.at[t, image, kind]).wait()

    def left(t):
        def act(slot, kind, image, tile_row, tile_col, local, remote):
            @pl.when(remote)
            def _():
                hop(t, slot, kind, image, tile_row, tile_col).wait_send()

        each(t, act)

    return start, arrived, left


def merge_tiles(owns, landing, goals, row, col):
    places = lax.broadcasted_iota(jnp.int32, (16, 1), 0)
    in_left = places < 14 - 2 * col

    def rows16(values):
        return values.reshape(16, FEATURES).astype(F32)

    def right_half(values):
        low = values.reshape(8, FEATURES).astype(F32)
        return jnp.concatenate([low, low], axis=0)

    for image in range(2):

        def merge(tile_row, _):
            top = tile_row < 14 - 2 * row
            upper = jnp.minimum(tile_row, 13)
            lower = jnp.maximum(tile_row - 8, 0)
            for own, (below, right, both), goal in zip(owns, landing, goals):
                stacked = jnp.where(top, rows16(own(image, upper)), rows16(below[image, lower]))
                beside = jnp.where(top, right_half(right[image, upper]), right_half(both[image, lower]))
                goal[image, tile_row] = jnp.where(in_left, stacked, beside).astype(goal.dtype)
            return 0

        lax.fori_loop(0, 16, merge, 0)


def input_grad(at, dqkv, wq, xw, image_grad, gain, norm_sums):
    grad = nt(dqkv[at, :], wq).astype(BF).astype(F32)
    unit, inverse = unit_of(xw[at, :].astype(F32))
    image_grad[at, :] += norm_back(grad, unit, inverse, as_row(gain))
    norm_sums[0] += fold_rows(grad * unit)
    norm_sums[1] += fold_rows(grad)


def plain_close_kernel(dqkv, xw, dm, raw_r, wq, gain, out, grad_out, norm_sums, image_grad, raw_g, *refs):
    img, row, col = place()
    landing, (send, recv) = (refs[:3], refs[3:6]), refs[6:]
    greet(img, row, col, False)
    start, arrived, left = returns((raw_r, raw_g), landing, send, recv, row, col)
    start(0)
    norm_sums[...] = jnp.zeros_like(norm_sums)
    image_grad[...] = dm[...]

    def step(i, _):
        input_grad(pl.ds(pl.multiple_of(i * BLOCK, 16), BLOCK), dqkv, wq[...], xw, image_grad, gain, norm_sums)
        return 0

    lax.fori_loop(0, ROWS // BLOCK, step, 0)
    spread_rows(image_grad, raw_g, row, col)
    start(1)
    for t in range(2):
        arrived(t)
    owns = [lambda image, upper, raw=raw: raw[image * 22 + 8 + upper, 1:3] for raw in (raw_r, raw_g)]
    merge_tiles(owns, landing, (out, grad_out), row, col)
    for t in range(2):
        left(t)


PIECES = [(2, 8, 2, 8, FEATURES), (2, 14, 1, 8, FEATURES), (2, 8, 1, 8, FEATURES)]


def plain_close(dqkv, xw, dm, raw_r, wq, gain):
    vm = pl.BlockSpec(memory_space=pltpu.VMEM)
    shape = jax.ShapeDtypeStruct
    dma = pltpu.SemaphoreType.DMA
    pieces = [pltpu.VMEM(s, BF) for s in PIECES]
    return pl.pallas_call(
        plain_close_kernel,
        out_shape=[shape((2, 16, 16, FEATURES), BF), shape((2, 16, 16, FEATURES), F32), shape((2, 8, FEATURES), F32)],
        in_specs=[vm] * 6,
        out_specs=[vm] * 3,
        scratch_shapes=[pltpu.VMEM((ROWS, FEATURES), F32), pltpu.VMEM((88, 3, 8, FEATURES), BF)]
        + pieces
        + pieces
        + [dma((2, 4, 3)), dma((2, 2, 3))],
        compiler_params=pltpu.CompilerParams(collective_id=2, has_side_effects=True, vmem_limit_bytes=67043328),
    )(dqkv, xw, dm, raw_r, wq, gain)


def back_kernel(
    value_bias, rows_table, cols_table, take, o_turned, da, cw, gain, sums, up_sum, taker,
    do_in, o_in, n2_in, xw_in, n1_in, probs, qkv_in, dh_in, g_in, dm_in, wq_in, raw_r, *refs
):
    out, grad_out, gq, go, gu, gd, small_out, table_out = refs[:8]
    qkv, probs_s, image_grad, shared_h, shared_g, own_r = refs[8:14]
    bias_sums, table_sums, norm_sums, tab, row_bias = refs[14:19]
    landing = (refs[19:22], refs[22:25])
    full = refs[25:29]
    small, table, small_land, table_land, small_z, table_z = refs[29:35]
    count = len(SUM_CHUNKS)
    lands = refs[35 : 35 + 5 * count]
    do, o, n2_turned, xw, n1_turned, hot = refs[35 + 5 * count : 41 + 5 * count]
    send, recv, load_sem, probs_sem, wsend, wrecv, ssend, srecv = refs[41 + 5 * count :]
    img, row, col = place()
    y_row = lax.rem(row + 2, 4)
    core_row = row + 1 - 2 * lax.rem(row, 2)
    other = 1 - img
    copies = []

    def load(i):
        pairs = (
            (dh_in, shared_h.at[pl.ds(0, ROWS)]),
            (g_in, shared_g),
            (qkv_in, qkv),
            (dm_in, image_grad),
            (wq_in, shared_h.at[:, pl.ds(0, 3 * FEATURES)]),
            (raw_r.at[pl.ds(8, 14), pl.ds(1, 2)], own_r.at[0]),
            (raw_r.at[pl.ds(30, 14), pl.ds(1, 2)], own_r.at[1]),
            (do_in, do),
            (o_in, o),
            (n2_in, n2_turned),
            (xw_in, xw),
            (n1_in, n1_turned),
        )
        return pltpu.make_async_copy(pairs[i][0], pairs[i][1], load_sem.at[i])

    for i in (1, 2, 7, 8, 9, 0, 11, 10, 3, 5, 6):
        load(i).start()
    windows = window_count(row, col)

    def fetch(k, window, slot):
        pair_index = lax.rem(k, 2) * 3 + k // 2
        return pltpu.make_async_copy(probs.at[window, pl.ds(2 * pair_index, 2)], probs_s.at[slot], probs_sem.at[slot])

    fetch(0, 0, 0).start()
    greet(img, row, col)
    start, arrived, left = returns((raw_r, shared_g), landing, send, recv, row, col)
    start(0)

    def turned_rows(ref):
        return lambda rw, kb: ref[pl.ds(pl.multiple_of(rw * kb, kb), kb), :]

    def turned_g(rw, kb):
        return shared_g[pl.ds(pl.multiple_of(rw * 32, 32), 32)].reshape(FEATURES, FEATURES)[:, 0:ROWS]

    pair_stage, first, second, third, fourth, fifth, sent = reducers(
        SUM_CHUNKS,
        full,
        (turned_rows(n1_turned), turned_rows(o_turned), turned_rows(n2_turned), turned_g),
        (qkv, da, shared_h, cw),
        (gq, go, gu, gd),
        lands,
        wsend,
        wrecv,
    )
    bias_sums[...] = jnp.zeros_like(bias_sums)
    table_sums[...] = jnp.zeros_like(table_sums)
    norm_sums[...] = jnp.zeros_like(norm_sums)
    load(1).wait()

    def grad_rows(i):
        if i == 0:
            load(4).start()
            load(10).wait()
            load(3).wait()
            load(4).wait()
        input_grad(pl.ds(i * BLOCK, BLOCK), qkv, shared_h[:, 0 : 3 * FEATURES], xw, image_grad, gain, norm_sums)

    def send_grad():
        spread_rows(image_grad, shared_g, row, col)
        start(1)

    def over_rows(values):
        return jnp.sum(values, axis=0, keepdims=True)

    def gather_small():
        small[0] = jnp.zeros((16, FEATURES), F32)
        lines = [bias_sums[0], bias_sums[1], sums[0], sums[1], norm_sums[0], norm_sums[1], sums[2], sums[3]]
        for i, values in enumerate(lines):
            small[0, i : i + 1, :] = over_rows(values)
        for i in range(4):
            small[0, 8 + i : 9 + i, :] = over_rows(up_sum[:, i * FEATURES : (i + 1) * FEATURES])
        exact = lax.Precision.HIGHEST
        total = jnp.zeros((64, 128), F32)
        for parity in range(2):
            for which in range(2):
                part = table_sums[64 * parity : 64 * parity + 64, 256 * parity + 128 * which : 256 * parity + 128 * which + 128]
                total = total + jnp.dot(part, taker[2 * parity + which], precision=exact, preferred_element_type=F32)
        table[0] = total

    hops = ({"row": core_row}, {"row": y_row}, {"img": other})

    def small_push(k, src, dst, target):
        c = pltpu.make_async_remote_copy(
            src_ref=src, dst_ref=dst, send_sem=ssend.at[k], recv_sem=srecv.at[k], device_id=target, device_id_type=MESH
        )
        c.start()
        copies.append(c)
        return c

    def small_step(i):
        if i == 0:
            gather_small()
        if 0 < i <= 3:
            for k, (acc, land) in enumerate(((small, small_land), (table, table_land))):
                pltpu.make_async_copy(land.at[i - 1], land.at[i - 1], srecv.at[2 * (i - 1) + k]).wait()
                acc[i] = acc[i - 1] + land[i - 1]
        if i < 3:
            for k, (acc, land) in enumerate(((small, small_land), (table, table_land))):
                small_push(2 * i + k, acc.at[i], land.at[i], hops[i])
        if i == 3:
            small_z[col] = small[3]
            table_z[col] = table[3]
            for d in range(1, 4):
                cl = lax.rem(col + d, 4)
                small_push(4 + 2 * d, small.at[3], small_z.at[col], {"col": cl})
                small_push(5 + 2 * d, table.at[3], table_z.at[col], {"col": cl})
        if i == 4:
            for d in range(1, 4):
                cl = lax.rem(col + 4 - d, 4)
                pltpu.make_async_copy(small_z.at[cl], small_z.at[cl], srecv.at[4 + 2 * d]).wait()
                pltpu.make_async_copy(table_z.at[cl], table_z.at[cl], srecv.at[5 + 2 * d]).wait()
            small_out[...] = (small_z[0] + small_z[1]) + (small_z[2] + small_z[3])
            table_out[...] = (table_z[0] + table_z[1]) + (table_z[2] + table_z[3])

    acts = {"p": pair_stage, "1": first, "2": second, "3": third, "4": fourth, "5": fifth, "G": grad_rows, "s": small_step, "S": send_grad}
    slots = plan_slots(CLOSE_PLAN, acts)
    run_all(slots[0])
    build_table(tab, rows_table, cols_table, take)
    row_bias[...] = as_row(value_bias)
    key_marks(hot)
    load(2).wait()
    clear_idle(qkv, row, col)
    for i in (7, 8, 9, 0, 11):
        load(i).wait()

    def head_pair(k, _):
        pair_index = lax.rem(k, 2) * 3 + k // 2

        def each(window, _):
            for i, slot_acts in enumerate(slots[1:-1]):
                if slot_acts:
                    pl.when((k == (i + 1) // 3) & (window == (i + 1) % 3))(functools.partial(run_all, slot_acts))
            turn_count = k * windows + window
            slot = lax.rem(turn_count, 2)
            fetch(k, window, slot).wait()
            wrap = window + 1 == windows
            next_k = jnp.where(wrap, k + 1, k)

            @pl.when(next_k < 6)
            def _():
                fetch(next_k, jnp.where(wrap, 0, window + 1), 1 - slot).start()

            attention_back(
                window,
                pair_index,
                lambda parity: probs_s[slot, parity],
                do,
                qkv,
                o,
                tab,
                hot,
                row_bias,
                bias_sums,
                table_sums,
                row,
                col,
            )
            return 0

        lax.fori_loop(0, windows, each, 0)
        return 0

    lax.fori_loop(0, 6, head_pair, 0)
    run_all(slots[-1])
    arrived(0)
    load(5).wait()
    load(6).wait()
    merge_tiles([lambda image, upper: own_r[image, upper]], landing[:1], (out,), row, col)
    arrived(1)
    merge_tiles([lambda image, upper: shared_g[image * 22 + 8 + upper, 1:3]], landing[1:], (grad_out,), row, col)
    left(0)
    left(1)
    for c in copies:
        c.wait_send()
    for copy in sent:
        copy().wait_send()


def back(do, o, value_bias, rows_table, cols_table, o_turned, da, n2_turned, cw, xw, n1_turned, gain, sums, up_sum, probs, qkv, dh, g, dm, wq, raw_r):
    vm = pl.BlockSpec(memory_space=pltpu.VMEM)
    an = pl.BlockSpec(memory_space=pl.ANY)
    shape = jax.ShapeDtypeStruct
    dma = pltpu.SemaphoreType.DMA
    pieces = [pltpu.VMEM(s, BF) for s in PIECES]
    count = len(SUM_CHUNKS)
    return pl.pallas_call(
        back_kernel,
        out_shape=[shape((2, 16, 16, FEATURES), BF), shape((2, 16, 16, FEATURES), BF)]
        + [shape((k // 16, n // 2), F32) for k, n in WHOLES]
        + [shape((16, FEATURES), F32), shape((64, 128), F32)],
        in_specs=[vm] * 11 + [an] * 12,
        out_specs=[vm] * 8,
        scratch_shapes=[
            pltpu.VMEM((SPAN, 3 * FEATURES), BF),
            pltpu.VMEM((2, 2, 224, 224), BF),
            pltpu.VMEM((ROWS, FEATURES), F32),
            pltpu.VMEM((FEATURES, 4 * FEATURES), BF),
            pltpu.VMEM((128, 3, 8, FEATURES), BF),
            pltpu.VMEM((2, 14, 2, 8, FEATURES), BF),
            pltpu.VMEM((2, 8, FEATURES), F32),
            pltpu.VMEM((128, 512), F32),
            pltpu.VMEM((2, 8, FEATURES), F32),
            pltpu.VMEM((128, 512), BF),
            pltpu.VMEM((1, FEATURES), F32),
        ]
        + pieces
        + pieces
        + [pltpu.VMEM(s, BF) for s in WHOLES]
        + [
            pltpu.VMEM((4, 16, FEATURES), F32),
            pltpu.VMEM((4, 64, 128), F32),
            pltpu.VMEM((3, 16, FEATURES), F32),
            pltpu.VMEM((3, 64, 128), F32),
            pltpu.VMEM((4, 16, FEATURES), F32),
            pltpu.VMEM((4, 64, 128), F32),
        ]
        + land_shapes(SUM_CHUNKS)
        + [pltpu.VMEM(s, BF) for s in ((SPAN, FEATURES), (SPAN, FEATURES), (FEATURES, ROWS), (ROWS, FEATURES), (FEATURES, ROWS))]
        + [pltpu.VMEM((2, 224, 128), F32)]
        + [dma((2, 4, 3)), dma((2, 2, 3)), dma((12,)), dma((2,)), dma((count, 13)), dma((count, 13)), dma((12,)), dma((12,))],
        compiler_params=pltpu.CompilerParams(collective_id=1, has_side_effects=True, vmem_limit_bytes=67043328),
    )(
        value_bias, rows_table, cols_table, takers(True), o_turned, da, cw, gain, sums, up_sum, jnp.asarray(table_taker()),
        do, o, n2_turned, xw, n1_turned, probs, qkv, dh, g.reshape(128, 3, 8, FEATURES), dm, wq, raw_r,
    )


def deliver_kernel(out_in, grad_in, *refs):
    sums_in, (small, table), outs = refs[:4], refs[4:6], refs[6:]
    outs[0][...] = out_in[...]

    def widen(i, _):
        outs[1][0, i] = grad_in[0, i].astype(F32)
        return 0

    lax.fori_loop(0, 16, widen, 0)

    @pl.when(pl.program_id(0) == 0)
    def _():
        for given, goal in zip(sums_in, outs[2:6]):
            goal[...] = given[...]
        for i, goal in zip((0, 1, 2, None, 3, 4, 5, 6, 7), outs[6:15]):
            if i is None:
                goal[...] = jnp.concatenate([small[8 + j : 9 + j, :] for j in range(4)], axis=1).reshape(4 * FEATURES)
            else:
                goal[...] = small[i : i + 1, :].reshape(FEATURES)
        turned = table[...].T
        outs[15][...] = turned[0:27, :]
        outs[16][...] = turned[64:91, :]


def deliver(*given):
    shape = jax.ShapeDtypeStruct
    lengths = [FEATURES] * 3 + [4 * FEATURES] + [FEATURES] * 5
    outs = [shape((2, 16, 16, FEATURES), BF), shape((2, 16, 16, FEATURES), F32)] + [shape((k // 16, n // 2), F32) for k, n in WHOLES]
    outs += [shape((n,), F32) for n in lengths] + [shape((27, 64), F32)] * 2
    image = pl.BlockSpec((1, 16, 16, FEATURES), lambda i: (i, 0, 0, 0))

    def spec(array):
        return pl.BlockSpec(array.shape, lambda i: (0,) * len(array.shape))

    return pl.pallas_call(
        deliver_kernel,
        grid=(2,),
        out_shape=outs,
        in_specs=[image] * 2 + [spec(v) for v in given[2:]],
        out_specs=[image] * 2 + [spec(v) for v in outs[2:]],
    )(*given)


def on_device(
    image_in,
    cotangent,
    qkv_weight,
    out_weight,
    up_weight,
    down_weight,
    query_bias,
    value_bias,
    out_bias,
    up_bias,
    down_bias,
    first_gain,
    first_shift,
    second_gain,
    second_shift,
    rows_table,
    cols_table,
):
    line = lambda v: v.reshape(1, -1)
    xw, cw, n1_turned, qkv, probs, o, o_turned, raw_r, n2_turned, g_turned, dh, da, do, dm, sums, up_sum, wq = open_windows(
        image_in,
        cotangent,
        (qkv_weight, out_weight, up_weight, down_weight),
        first_gain,
        first_shift,
        query_bias,
        value_bias,
        rows_table,
        cols_table,
        out_bias,
        line(up_bias),
        down_bias,
        second_gain,
        second_shift,
    )
    if lax.axis_size("img") == 2:
        return tuple(
            deliver(
                *back(
                    do, o, value_bias, rows_table, cols_table, o_turned, da, n2_turned, cw, xw, n1_turned, first_gain, sums, up_sum,
                    probs, qkv, dh, g_turned, dm, wq, raw_r,
                )
            )
        )
    dqkv, bias_sums, table_sums = plain_back(do, probs, qkv, o, value_bias, rows_table, cols_table)
    image_out, image_grad, norm_sums = plain_close(dqkv, xw, dm, raw_r, wq, first_gain)
    dot = lambda a, b: jnp.dot(a, b, preferred_element_type=F32)
    totals = (dot(n1_turned, dqkv[:ROWS]), dot(o_turned, da), dot(n2_turned, dh), dot(g_turned[:, :ROWS], cw))
    shard_sums = []
    for total in totals:
        part = lax.psum_scatter(total.astype(BF), ("row", "col"), scatter_dimension=0, tiled=True)
        shard_sums.append(lax.psum_scatter(part, "img", scatter_dimension=1, tiled=True).astype(F32))
    rows_grad, cols_grad = table_grads(table_sums)
    small_sums = lax.psum(
        tuple(jnp.sum(bias_sums, axis=1))
        + (jnp.sum(sums[0], axis=0), jnp.sum(up_sum, axis=0), jnp.sum(sums[1], axis=0))
        + tuple(jnp.sum(norm_sums, axis=1))
        + (jnp.sum(sums[2], axis=0), jnp.sum(sums[3], axis=0), rows_grad, cols_grad),
        ("img", "row", "col"),
    )
    return (image_out, image_grad, *shard_sums, *small_sums)


def solution(mesh):
    tiles = P("img", "row", "col", None)
    shards = P(("row", "col"), "img")
    return jax.shard_map(
        on_device,
        mesh=mesh,
        in_specs=(tiles,) * 2 + (shards,) * 4 + (P(),) * 11,
        out_specs=(tiles,) * 2 + (shards,) * 4 + (P(),) * 11,
        check_vma=False,
    )
```

```python
import functools

import jax
import jax.numpy as jnp
import numpy as np
from jax import lax
from jax.experimental import pallas as pl
from jax.experimental.pallas import tpu as pltpu
from jax.sharding import PartitionSpec as P

MESH = pl.DeviceIdType.MESH


def place():
    return lax.axis_index("img"), lax.axis_index("row"), lax.axis_index("col")


def side_owner(window_row, image):
    return lax.rem(window_row, 2), 3 - image - 2 * (window_row // 2)


def piece_target(kind, image, row, col):
    last_row, last_col = row == 3, col == 3
    side_row, side_col = side_owner(row, image)
    next_row, next_col = side_owner(lax.rem(row + 1, 4), image)
    if kind == 0:
        return (jnp.where(last_row, 3 - image, row + 1), col, jnp.where(last_row, 2, image))
    if kind == 1:
        return (jnp.where(last_col, side_row, row), jnp.where(last_col, side_col, col + 1), jnp.where(last_col, 2, image))
    target_row = jnp.where(last_row, 3 - image, jnp.where(last_col, next_row, row + 1))
    target_col = jnp.where(last_col, jnp.where(last_row, 3, next_col), col + 1)
    slot = jnp.where(last_row & last_col, 3, jnp.where(last_row | last_col, 2, image))
    return (target_row, target_col, slot)


def arrivals(row, col):
    wide = row >= 2
    side_row = row + 2 * (1 - col // 2)
    table = []
    for image in range(2):
        table.append((image, 0, row > 0))
        table.append((image, 1, col > 0))
        table.append((image, 2, (row > 0) & (col > 0)))
    table.append((2, 0, wide))
    table.append((2, 1, jnp.logical_not(wide)))
    table.append((2, 2, jnp.where(wide, col, side_row) > 0))
    table.append((3, 2, wide & (col == 3)))
    return table


def tile_part(ref, image, kind):
    if kind == 0:
        return ref.at[image, pl.ds(8, 8), pl.ds(0, 2)]
    if kind == 1:
        return ref.at[image, pl.ds(0, 14), pl.ds(1, 1)]
    return ref.at[image, pl.ds(8, 8), pl.ds(1, 1)]


def window_part(ref, slot, kind):
    if kind == 0:
        return ref.at[pl.ds(slot * 22, 8), pl.ds(1, 2)]
    if kind == 1:
        return ref.at[pl.ds(slot * 22 + 8, 14), pl.ds(0, 1)]
    return ref.at[pl.ds(slot * 22, 8), pl.ds(0, 1)]


def greet(img, row, col, pairs=True):
    barrier = pltpu.get_barrier_semaphore()
    for row_step in range(4):
        for col_step in range(4):
            if row_step or col_step:
                pl.semaphore_signal(
                    barrier,
                    inc=1,
                    device_id={"row": lax.rem(row + row_step, 4), "col": lax.rem(col + col_step, 4)},
                    device_id_type=MESH,
                )
    if pairs:
        pl.semaphore_signal(barrier, inc=1, device_id={"img": 1 - img}, device_id_type=MESH)
    pl.semaphore_wait(barrier, 16 if pairs else 15)


CHUNKS = ((0, 0, 640), (0, 640, 1152), (1, 0, 384), (2, 0, 768), (2, 768, 1536), (3, 0, 128), (3, 128, 384))


def links(shards, fulls, wsend, wrecv, wloc):
    img, row, col = place()
    y_row = lax.rem(row + 2, 4)
    core_row = row + 1 - 2 * lax.rem(row, 2)
    other = 1 - img
    sent = []

    def rows_of(w, rw, half=None):
        kb = fulls[w].shape[0] // 4
        if half is None:
            return pl.ds(pl.multiple_of(rw * kb, kb), kb)
        return pl.ds(pl.multiple_of(rw * kb + half * (kb // 2), kb // 2), kb // 2)

    def cols_of(n, im):
        w, lo, hi = CHUNKS[n]
        nb = fulls[w].shape[1] // 2
        return pl.ds(pl.multiple_of(im * nb + lo, 128), hi - lo)

    def block(n, rw, im, half=None):
        w = CHUNKS[n][0]
        return fulls[w].at[rows_of(w, rw, half), cols_of(n, im)]

    def slot(n, cl):
        w = CHUNKS[n][0]
        k16 = fulls[w].shape[0] // 16
        return fulls[w].at[pl.ds(pl.multiple_of((row * 4 + cl) * k16, k16), k16), cols_of(n, img)]

    def source(n):
        w, lo, hi = CHUNKS[n]
        return shards[w].at[:, pl.ds(lo, hi - lo)]

    def push(n, k, where, target, start=None):
        def copy():
            ref = slot(n, where) if start else block(n, *where)
            return pltpu.make_async_remote_copy(
                src_ref=source(n) if start and where is col else ref,
                dst_ref=ref,
                send_sem=wsend.at[n, k],
                recv_sem=wrecv.at[n, k],
                device_id=target(),
                device_id_type=MESH,
            )

        copy().start()
        sent.append(copy)

    def arrive(n, k, ref):
        pltpu.make_async_copy(ref, ref, wrecv.at[n, k]).wait()

    far_col, near_col = lax.rem(col + 2, 4), col + 1 - 2 * lax.rem(col, 2)

    def along_col(n):
        pltpu.make_async_copy(source(n), slot(n, col), wloc.at[n]).start()
        push(n, 0, col, lambda: {"col": far_col}, True)

    def near_by(n):
        pltpu.make_async_copy(source(n), slot(n, col), wloc.at[n]).wait()
        push(n, 1, col, lambda: {"col": near_col}, True)
        arrive(n, 0, slot(n, far_col))
        push(n, 2, far_col, lambda: {"col": near_col}, True)

    def first(n):
        arrive(n, 1, slot(n, near_col))
        arrive(n, 2, slot(n, 3 - col))
        push(n, 3, (row, img, 0), lambda: {"img": other})
        push(n, 4, (row, img, 1), lambda: {"row": y_row})
        push(n, 5, (row, img), lambda: {"row": core_row})

    def second(n):
        arrive(n, 3, block(n, row, other, 0))
        arrive(n, 4, block(n, y_row, img, 1))
        push(n, 6, (row, img, 0), lambda: {"row": y_row})
        push(n, 7, (row, other, 0), lambda: {"row": y_row})
        push(n, 8, (row, img, 1), lambda: {"img": other})
        push(n, 9, (y_row, img, 1), lambda: {"img": other})
        push(n, 10, (row, other, 0), lambda: {"row": core_row})
        push(n, 11, (y_row, img, 1), lambda: {"row": core_row})

    def third(n):
        arrive(n, 6, block(n, y_row, img, 0))
        arrive(n, 7, block(n, y_row, other, 0))
        arrive(n, 8, block(n, row, other, 1))
        arrive(n, 9, block(n, y_row, other, 1))
        push(n, 12, (y_row, img, 0), lambda: {"row": core_row})
        push(n, 13, (y_row, other, 0), lambda: {"row": core_row})
        push(n, 14, (row, other, 1), lambda: {"row": core_row})
        push(n, 15, (y_row, other, 1), lambda: {"row": core_row})

    def last(n):
        core_y = lax.rem(core_row + 2, 4)
        arrive(n, 5, block(n, core_row, img))
        arrive(n, 10, block(n, core_row, other, 0))
        arrive(n, 11, block(n, core_y, img, 1))
        arrive(n, 12, block(n, core_y, img, 0))
        arrive(n, 13, block(n, core_y, other, 0))
        arrive(n, 14, block(n, core_row, other, 1))
        arrive(n, 15, block(n, core_y, other, 1))

    return along_col, near_by, first, second, third, last, sent


def window_moves(tiles, raws, send, recv, loc):
    img, row, col = place()

    def each(t, act):
        for image in range(2):
            for kind in range(3):
                target_row, target_col, target_slot = piece_target(kind, image, row, col)
                here = (target_row == row) & (target_col == col)
                part = tile_part(tiles[t], image, kind)
                goal = window_part(raws[t], target_slot, kind)
                act(here, part, goal, send.at[t, image, kind], recv.at[t, target_slot, kind], target_row, target_col)

    def remote(part, goal, leave, arrival, target_row, target_col):
        return pltpu.make_async_remote_copy(
            src_ref=part,
            dst_ref=goal,
            send_sem=leave,
            recv_sem=arrival,
            device_id={"row": target_row, "col": target_col},
            device_id_type=MESH,
        )

    def own(t, image):
        return pltpu.make_async_copy(tiles[t].at[image, pl.ds(0, 14)], raws[t].at[pl.ds(image * 22 + 8, 14), pl.ds(1, 2)], loc.at[t, image])

    def start(t):
        for image in range(2):
            own(t, image).start()

        def act(here, part, goal, leave, arrival, target_row, target_col):
            @pl.when(here)
            def _():
                pltpu.make_async_copy(part, goal, arrival).start()

            @pl.when(jnp.logical_not(here))
            def _():
                remote(part, goal, leave, arrival, target_row, target_col).start()

        each(t, act)

    def arrived(t):
        for image in range(2):
            own(t, image).wait()
        for slot_index, kind, present in arrivals(row, col):
            part = window_part(raws[t], slot_index, kind)

            @pl.when(present)
            def _():
                pltpu.make_async_copy(part, part, recv.at[t, slot_index, kind]).wait()

    def left(t):
        def act(here, part, goal, leave, arrival, target_row, target_col):
            @pl.when(jnp.logical_not(here))
            def _():
                remote(part, goal, leave, arrival, target_row, target_col).wait_send()

        each(t, act)

    return start, arrived, left


BF = jnp.bfloat16
F32 = jnp.float32
ROWS = 704
SPAN = 800
FEATURES = 768
EPS = 1e-06


def row_params(step, row, col):
    wide = row >= 2
    side_row = row + 2 * (1 - col // 2)
    third_step = step - 28
    in_corner = wide & (third_step >= 8)
    slot = jnp.where(step < 14, 0, jnp.where(step < 28, 1, jnp.where(in_corner, 3, 2)))
    place_row = jnp.where(step < 14, step, jnp.where(step < 28, step - 14, jnp.where(in_corner, third_step - 8, third_step)))
    full = step < 28
    row_start = jnp.where(full, 8 - 2 * row, jnp.where(wide, 0, 8 - 2 * side_row))
    col_start = jnp.where(full, 8 - 2 * col, jnp.where(wide & jnp.logical_not(in_corner), 8 - 2 * col, 0))
    width = jnp.where(full, 14, jnp.where(wide & jnp.logical_not(in_corner), 14, 8))
    alive = jnp.where(full, True, jnp.where(in_corner, col == 3, jnp.where(wide, True, third_step < 14)))
    return slot, jnp.minimum(place_row + row_start, 21), col_start, jnp.where(alive, width, 0)


def window_params(window, row, col):
    wide = row >= 2
    start = jnp.where(window < 2, 14 * window, jnp.where(window == 2, 28, 36))
    tall = jnp.where(window < 2, 14, jnp.where((window == 2) & jnp.logical_not(wide), 14, 8))
    width = jnp.where(window < 2, 14, jnp.where((window == 2) & wide, 14, 8))
    return start, tall, width


def window_count(row, col):
    return jnp.where((row >= 2) & (col == 3), 4, 3)


def unit_of(values):
    center = values - jnp.mean(values, axis=-1, keepdims=True)
    inverse = lax.rsqrt(jnp.mean(center * center, axis=-1, keepdims=True) + EPS)
    return center * inverse, inverse


def relative_layout(backward):
    take = np.zeros((2, 2, 27, 128), np.float32)
    for parity in range(2):
        base = 64 if parity == 0 else 0
        for j in range(27):
            for copy in (0,) if backward else (0, 32):
                take[parity, 0, 26 - j, (base - 13 + j + copy) % 128] = 1
                if backward:
                    take[parity, 1, j, base + 16 + j] = 1
                else:
                    take[parity, 1, 26 - j, (base + 3 + j + copy) % 128] = 1
    return take


def takers(backward):
    return jnp.asarray(relative_layout(backward).reshape(4, 27, 128), BF)


def build_table(tab, rows_table, cols_table, take):
    tab[...] = jnp.zeros_like(tab)
    for parity in range(2):
        for which, table in ((0, rows_table), (1, cols_table)):
            block = lax.dot_general(table[...], take[2 * parity + which], (((0,), (0,)), ((), ())), preferred_element_type=F32)
            lane = 256 * parity + 128 * which
            tab[64 * parity : 64 * parity + 64, lane : lane + 128] = block.astype(BF)


def as_row(ref):
    return ref[...].reshape(1, -1)


def run_all(acts):
    for act in acts:
        act[0](*act[1:])


def plan_slots(plan, acts):
    slots = [[]]
    for name in plan:
        if name == "|":
            slots.append([])
        elif name in acts:
            slots[-1].append((acts[name],))
        else:
            slots[-1].append((acts[name[0]], int(name[1:])))
    return slots


def table_grads(sums):
    take = jnp.asarray(relative_layout(True), F32)
    grads = []
    for which in range(2):
        total = 0.0
        for parity in range(2):
            part = sums[64 * parity : 64 * parity + 64, 256 * parity + 128 * which : 256 * parity + 128 * which + 128]
            total = total + lax.dot_general(take[parity, which], part, (((1,), (1,)), ((), ())), precision=lax.Precision.HIGHEST)
        grads.append(total)
    return grads


FF = 3072
CHUNK = 512
BLOCK = 176


def nt(a, b):
    return lax.dot_general(a, b, (((1,), (1,)), ((), ())), preferred_element_type=F32)


def norm_back(grad, unit, inverse, gain):
    scaled = grad * gain
    first_mean = jnp.mean(scaled, axis=-1, keepdims=True)
    second_mean = jnp.mean(scaled * unit, axis=-1, keepdims=True)
    return inverse * (scaled - first_mean - unit * second_mean)


def fold_rows(values):
    total = values[0:8]
    for i in range(1, values.shape[0] // 8):
        total = total + values[8 * i : 8 * i + 8]
    return total


def spread_rows(source, raw, row, col):
    def step(i, _):
        slot, raw_row, col_start, width = row_params(i, row, col)
        at = pl.ds(pl.multiple_of(i * 16, 16), 16)

        @pl.when(width > 0)
        def _():
            values = jnp.concatenate([source[at, :], jnp.zeros((8, FEATURES), F32)], axis=0)
            raw[slot * 22 + raw_row] = pltpu.roll(values, col_start, 0).astype(BF).reshape(3, 8, FEATURES)

        return 0

    lax.fori_loop(0, 44, step, 0)


OPEN_PLAN = ("a0", "a2", "a1", "b0", "b2", "a6", "10", "b1", "a5", "Wx", "11", "b5", "b6", "12", "20", "22", "21", "15", "a3", "X", "16", "a4", "b3", "31", "30", "25", "L1", "L0", "P", "32", "13", "b4", "26", "|", "|", "L2", "|", "|", "Wc", "|", "|", "|", "|", "|", "|", "|", "35", "|", "|", "|", "|", "23", "14", "|", "36", "|", "U", "|", "M", "K", "33", "T", "24", "L3", "L5", "L6", "|", "34", "|", "L4", "|", "|")


def open_kernel(weights, x_ref, c_ref, gain, shift, query_bias, value_bias, rows_table, cols_table, take, out_bias, up_bias, down_bias, gain2, shift2, *refs):
    img, row, col = place()
    greet(img, row, col, weights)
    if weights:
        shards, refs = refs[:4], refs[4:]
    else:
        wq, wo, wu, wd = refs[:4]
        refs = refs[4:]
    xw_out, cw_out, n1_out, qkv_out, probs_out, o_out, o_turned_out = refs[:7]
    raw_out, n2_out, g_out, dh_out, da, do, dm, sums, up_sum = refs[7:16]
    refs = refs[16:]
    if weights:
        wq_out, refs = refs[0], refs[1:]
    rawx, rawc, n1, tab, row_bias, qkv_s, probs, y_s, d_s, g_s, g_chunk, dh_chunk, xw, cw, n1_turned, o, o_turned, n2_turned, hot, out_sem, probs_sem, send, recv, loc = refs[:24]
    refs = refs[24:]
    flushes = ((xw, xw_out), (cw, cw_out), (n1_turned, n1_out), (o, o_out), (o_turned, o_turned_out), (n2_turned, n2_out))

    def flush(i):
        return pltpu.make_async_copy(flushes[i][0], flushes[i][1], out_sem.at[5 + i])

    if weights:
        wq, wo, wu, wd = refs[:4]
        along_col, near_by, first, second, third, last, sent = links(shards, refs[:4], *refs[4:])
    window_start, window_arrived, window_left = window_moves((x_ref, c_ref), (rawx, rawc), send, recv, loc)
    places = lax.broadcasted_iota(jnp.int32, (16, 1), 0)

    def cut_one(raw, step):
        slot, raw_row, col_start, width = row_params(step, row, col)
        wide_rows = raw[slot * 22 + raw_row].reshape(24, FEATURES).astype(F32)
        keep = places < width
        return keep, jnp.where(keep, pltpu.roll(wide_rows, lax.rem(24 - col_start, 24), 0)[:16], 0.0)

    def cut_x(step, _):
        at = pl.ds(pl.multiple_of(step * 16, 16), 16)
        keep, x = cut_one(rawx, step)
        xw[at, :] = x.astype(BF)
        unit, _inverse = unit_of(x)
        n1[at, :] = jnp.where(keep, unit * as_row(gain) + as_row(shift), 0.0).astype(BF)
        return 0

    def cut_c(step, _):
        at = pl.ds(pl.multiple_of(step * 16, 16), 16)
        _keep, c = cut_one(rawc, step)
        cw[at, :] = c.astype(BF)
        return 0

    def project(step, _):
        at = pl.ds(pl.multiple_of(step * 352, 32), 352)
        for part_index in range(3):
            lanes = slice(part_index * FEATURES, (part_index + 1) * FEATURES)
            part = jnp.dot(n1[at, :], wq[:, lanes], preferred_element_type=F32)
            if part_index != 1:
                part = part + row_bias[part_index // 2]
            qkv_s[at, lanes] = part.astype(BF)
        return 0

    def turn(source, goal):
        def step(i, _):
            lanes = pl.ds(pl.multiple_of(i * 128, 128), 128)
            goal[lanes, :] = source[0:ROWS, lanes].T
            return 0

        lax.fori_loop(0, FEATURES // 128, step, 0)

    def cut_windows():
        window_arrived(0)
        lax.fori_loop(0, 44, cut_x, 0)
        flush(0).start()

    def cut_cotangent():
        window_arrived(1)
        lax.fori_loop(0, 44, cut_c, 0)
        flush(1).start()

    def project_all():
        lax.fori_loop(0, 2, project, 0)
        pltpu.make_async_copy(qkv_s, qkv_out, out_sem.at[0]).start()
        if weights:
            pltpu.make_async_copy(wq, wq_out, out_sem.at[1]).start()

    def turn_all():
        turn(o, o_turned)
        flush(3).start()
        flush(4).start()

    def turn_first():
        turn(n1, n1_turned)
        flush(2).start()

    blocks = (slice(0, 352), slice(352, 704))

    def middle_begin():
        sums[...] = jnp.zeros_like(sums)
        up_sum[...] = jnp.zeros_like(up_sum)
        d_s[...] = jnp.zeros_like(d_s)

        def begin(i, _):
            at = pl.ds(pl.multiple_of(i * BLOCK, 16), BLOCK)
            mid = xw[at, :].astype(F32) + (jnp.dot(o[at, :], wo[...], preferred_element_type=F32) + as_row(out_bias))
            unit, _inverse = unit_of(mid)
            n1[at, :] = (unit * as_row(gain2) + as_row(shift2)).astype(BF)
            y_s[at, :] = mid + as_row(down_bias)
            dm[at, :] = mid
            return 0

        lax.fori_loop(0, ROWS // BLOCK, begin, 0)
        turn(n1, n2_turned)
        flush(5).start()

    def chunk_out(which, step):
        lanes = pl.ds(pl.multiple_of(step * FEATURES, FEATURES), FEATURES)
        if which == 0:
            return pltpu.make_async_copy(g_chunk, g_out.at[lanes, :], out_sem.at[2])
        return pltpu.make_async_copy(dh_chunk, dh_out.at[:, lanes], out_sem.at[3])

    def middle_step(turn_index, _):
        for i, slot_acts in enumerate(middle_slots):
            if slot_acts:
                pl.when(turn_index == i)(functools.partial(run_all, slot_acts))
        step = lax.rem(turn_index, 2) * 2 + turn_index // 2
        lanes = pl.ds(pl.multiple_of(step * FEATURES, FEATURES), FEATURES)

        @pl.when(turn_index > 0)
        def _():
            chunk_out(0, 0).wait()
            chunk_out(1, 0).wait()

        for at in blocks:
            h = jnp.dot(n1[at, :], wu[:, lanes], preferred_element_type=F32) + up_bias[:, lanes]
            up = nt(cw[at, :], wd[lanes, :])
            phi = 0.5 * (1.0 + lax.erf(h * 0.7071067811865476))
            slope = phi + h * (jnp.exp(-0.5 * h * h) * 0.3989422804014327)
            active = (h * phi).astype(BF)
            back = (up * slope).astype(BF)
            g_s[at, :] = active
            dh_chunk[at, :] = back
            up_sum[:, lanes] += fold_rows(back.astype(F32))
            y_s[at, :] += jnp.dot(active, wd[lanes, :], preferred_element_type=F32)
            d_s[at, :] += nt(back, wu[:, lanes])
        for i in range(FEATURES // 128):
            g_chunk[128 * i : 128 * i + 128, 0:ROWS] = g_s[:, 128 * i : 128 * i + 128].T
        chunk_out(0, step).start()
        chunk_out(1, step).start()
        return 0

    def middle_end():
        def end(i, _):
            at = pl.ds(pl.multiple_of(i * BLOCK, 16), BLOCK)
            unit, inverse = unit_of(dm[at, :])
            grad = d_s[at, :].astype(BF).astype(F32)
            up = cw[at, :].astype(F32)
            grad_mid = up + norm_back(grad, unit, inverse, as_row(gain2))
            low_grad = grad_mid.astype(BF)
            dm[at, :] = grad_mid
            da[at, :] = low_grad
            do[at, :] = nt(low_grad, wo[...]).astype(BF)
            sums[0] += fold_rows(low_grad.astype(F32))
            sums[1] += fold_rows(up)
            sums[2] += fold_rows(grad * unit)
            sums[3] += fold_rows(grad)
            return 0

        spread_rows(y_s, rawx, row, col)
        raw_copy = pltpu.make_async_copy(rawx, raw_out, out_sem.at[4])
        raw_copy.start()
        lax.fori_loop(0, ROWS // BLOCK, end, 0)
        raw_copy.wait()

    acts = {"X": cut_windows, "P": project_all, "T": turn_all, "U": turn_first, "K": cut_cotangent, "M": middle_begin}
    acts["Wx"] = functools.partial(window_start, 0)
    acts["Wc"] = functools.partial(window_start, 1)
    if weights:
        acts.update({"a": along_col, "b": near_by, "1": first, "2": second, "3": third, "L": last})
        slots = plan_slots(OPEN_PLAN, acts)
    else:
        slots = plan_slots(("Wx", "Wc", "X", "P", *("|",) * 18, "T", "U", "K", "M", *("|",) * 4), acts)
    run_all(slots[0][:3])
    o[...] = jnp.zeros_like(o)
    build_table(tab, rows_table, cols_table, take)
    row_bias[0] = as_row(query_bias)
    row_bias[1] = as_row(value_bias)
    key_place = lax.broadcasted_iota(jnp.int32, (224, 128), 0)
    key_lane = lax.broadcasted_iota(jnp.int32, (224, 128), 1)
    key_a, key_b = key_place // 16, key_place % 16
    for parity in range(2):
        key_on = key_lane - (64 if parity == 0 else 0)
        hot[parity] = jnp.where(
            key_on == 14,
            jnp.where(key_b >= 14, 1.0, 0.0),
            jnp.where(
                (key_on % 32 < 14) & (key_a == key_on % 32),
                1.0,
                jnp.where((key_on % 32 >= 16) & (key_on % 32 < 30) & (key_b == key_on % 32 - 16), 1.0, 0.0),
            ),
        )
    run_all(slots[0][3:])
    row_of = lax.broadcasted_iota(jnp.int32, (224, 1), 0)
    lane = lax.broadcasted_iota(jnp.int32, (1, 128), 1)
    def probs_copy(index):
        window, pair_index = index // 6, index % 6
        part = pl.ds(2 * pair_index, 2)
        return pltpu.make_async_copy(probs.at[window, part], probs_out.at[window, part], probs_sem.at[window, pair_index])

    def attend(window, pair_index, rows):
        start, tall, width = window_params(window, row, col)
        at = pl.ds(pl.multiple_of(start * 16, 16), 224)
        q_at = pl.ds(pl.multiple_of(start * 16, 16), rows)
        alive = (row_of // 16 < tall) & (row_of % 16 < width)
        lanes = lambda third: pl.ds(pl.multiple_of(third * FEATURES + pair_index * 128, 128), 128)
        q = jnp.where(alive[:rows], qkv_s[q_at, lanes(0)].astype(F32), 0.0)
        k = jnp.where(alive, qkv_s[at, lanes(1)].astype(F32), 0.0)
        v = jnp.where(alive, qkv_s[at, lanes(2)].astype(F32), row_bias[1, :, lanes(0)].astype(BF).astype(F32)).astype(BF)
        terms = jnp.dot(q.astype(BF), tab[...], preferred_element_type=F32)
        lines = [slice(16 * a, 16 * a + 16) for a in range(rows // 16)]
        outs = []
        for parity in range(2):
            own = (lane < 64) if parity == 0 else (lane >= 64)
            first_lane = 256 * parity
            rel_rows = jnp.concatenate(
                [pltpu.roll(terms[at_a, first_lane : first_lane + 128], a, 1) for a, at_a in enumerate(lines)], axis=0
            )
            rel_cols = jnp.concatenate(
                [pltpu.roll(terms[at_a, first_lane + 128 : first_lane + 256], 0, 1, stride=1, stride_axis=0) for at_a in lines], axis=0
            )
            on = lane - (64 if parity == 0 else 0)
            in_rows = ((on >= 0) & (on < 14)) | ((on >= 32) & (on < 46))
            in_cols = ((on >= 16) & (on < 30)) | ((on >= 48) & (on < 62))
            rel = jnp.where(in_rows, rel_rows, jnp.where(in_cols, rel_cols, 0.0))
            rough = rel.astype(BF).astype(F32)
            fine = jnp.where(on >= 32, rel - rough, rough)
            fine = jnp.where(on == 14, -1e30, fine)
            q_side = jnp.where(own, q * 0.125, fine).astype(BF)
            k_side = jnp.where(own, k, hot[parity]).astype(BF)
            scores = lax.dot_general(q_side, k_side, (((1,), (1,)), ((), ())), preferred_element_type=F32)
            exponent = jnp.exp(scores - jnp.max(scores, axis=-1, keepdims=True))
            p = (exponent * (1.0 / jnp.sum(exponent, axis=-1, keepdims=True))).astype(BF)
            probs[window, 2 * pair_index + parity, 0:rows, :] = p
            if rows < 224:
                probs[window, 2 * pair_index + parity, rows:224, :] = jnp.zeros((224 - rows, 224), BF)
            outs.append(jnp.dot(p, v, preferred_element_type=F32))
        blended = jnp.where(lane < 64, outs[0], outs[1])
        o[q_at, lanes(0)] = jnp.where(alive[:rows], blended, 0.0).astype(BF)

    def pair(index, _):
        for i, slot_acts in enumerate(slots[1:18]):
            if slot_acts:
                pl.when(index == i + 1)(functools.partial(run_all, slot_acts))
        window, pair_index = index // 6, index % 6
        short = (window >= 2) & (row >= 2)
        pl.when(short)(functools.partial(attend, window, pair_index, 128))
        pl.when(jnp.logical_not(short))(functools.partial(attend, window, pair_index, 224))
        probs_copy(index).start()
        return 0

    pairs = window_count(row, col) * 6
    lax.fori_loop(0, pairs, pair, 0)
    run_all(slots[18])
    middle_slots = [[], *slots[19:22]]
    lax.fori_loop(0, 4, middle_step, 0)
    run_all(slots[22])
    middle_end()
    chunk_out(0, 0).wait()
    chunk_out(1, 0).wait()
    pltpu.make_async_copy(qkv_s, qkv_out, out_sem.at[0]).wait()
    if weights:
        pltpu.make_async_copy(wq, wq_out, out_sem.at[1]).wait()
        for copy in sent:
            copy().wait_send()
    lax.fori_loop(0, pairs, lambda index, _: (probs_copy(index).wait(), 0)[1], 0)
    for i in range(6):
        flush(i).wait()
    window_left(0)
    window_left(1)


def open_windows(x, c, shards, gain, shift, query_bias, value_bias, rows_table, cols_table, out_bias, up_bias, down_bias, gain2, shift2):
    vm = pl.BlockSpec(memory_space=pltpu.VMEM)
    an = pl.BlockSpec(memory_space=pl.ANY)
    shape = jax.ShapeDtypeStruct
    dma = pltpu.SemaphoreType.DMA
    chunks = len(CHUNKS)
    weights = lax.axis_size("img") == 2
    if weights:
        given = list(shards)
    else:
        widened = [lax.all_gather(w, "img", axis=1, tiled=True) for w in shards]
        gathered = [lax.all_gather(w, ("row", "col"), axis=0, tiled=True) for w in widened]
        given = gathered
    raw = pltpu.VMEM((88, 3, 8, FEATURES), BF)
    outs = pl.pallas_call(
        functools.partial(open_kernel, weights),
        out_shape=[
            shape((ROWS, FEATURES), BF),
            shape((ROWS, FEATURES), BF),
            shape((FEATURES, ROWS), BF),
            shape((SPAN, 3 * FEATURES), BF),
            shape((4, 12, 224, 224), BF),
            shape((SPAN, FEATURES), BF),
            shape((FEATURES, ROWS), BF),
        ]
        + [
            shape((88, 3, 8, FEATURES), BF),
            shape((FEATURES, ROWS), BF),
            shape((FF, FEATURES), BF),
            shape((ROWS, FF), BF),
            shape((ROWS, FEATURES), BF),
            shape((SPAN, FEATURES), BF),
            shape((ROWS, FEATURES), F32),
            shape((4, 8, FEATURES), F32),
            shape((8, FF), F32),
        ]
        + ([shape((768, 2304), BF)] if weights else []),
        in_specs=[vm] * (14 + len(given)),
        out_specs=[an] * 11 + [vm] * 5 + ([an] if weights else []),
        scratch_shapes=[
            raw,
            raw,
            pltpu.VMEM((ROWS, FEATURES), BF),
            pltpu.VMEM((128, 512), BF),
            pltpu.VMEM((2, 1, FEATURES), F32),
            pltpu.VMEM((SPAN, 3 * FEATURES), BF),
            pltpu.VMEM((4, 12, 224, 224), BF),
            pltpu.VMEM((ROWS, FEATURES), F32),
            pltpu.VMEM((ROWS, FEATURES), F32),
            pltpu.VMEM((ROWS, FEATURES), BF),
            pltpu.VMEM((FEATURES, FEATURES), BF),
            pltpu.VMEM((ROWS, FEATURES), BF),
            pltpu.VMEM((ROWS, FEATURES), BF),
            pltpu.VMEM((ROWS, FEATURES), BF),
            pltpu.VMEM((FEATURES, ROWS), BF),
            pltpu.VMEM((SPAN, FEATURES), BF),
            pltpu.VMEM((FEATURES, ROWS), BF),
            pltpu.VMEM((FEATURES, ROWS), BF),
            pltpu.VMEM((2, 224, 128), F32),
            dma((11,)),
            dma((4, 6)),
            dma((2, 2, 3)),
            dma((2, 4, 3)),
            dma((2, 2)),
        ]
        + ([pltpu.VMEM(s, BF) for s in WHOLES] + [dma((chunks, 16)), dma((chunks, 16)), dma((chunks,))] if weights else []),
        compiler_params=pltpu.CompilerParams(collective_id=0, has_side_effects=True, vmem_limit_bytes=67043328),
    )(x.reshape(2, 16, 2, 8, 768), c.reshape(2, 16, 2, 8, 768), gain, shift, query_bias, value_bias, rows_table, cols_table, takers(False), out_bias, up_bias, down_bias, gain2, shift2, *given)
    return list(outs) if weights else list(outs) + gathered[:1]


def key_marks(hot):
    key_place = lax.broadcasted_iota(jnp.int32, (224, 128), 0)
    key_lane = lax.broadcasted_iota(jnp.int32, (224, 128), 1)
    key_a, key_b = key_place // 16, key_place % 16
    for parity in range(2):
        key_on = key_lane - (64 if parity == 0 else 0)
        hot[parity] = jnp.where(
            (key_on >= 0) & (key_on < 14) & (key_a == key_on),
            1.0,
            jnp.where((key_on >= 16) & (key_on < 30) & (key_b == 29 - key_on), 1.0, 0.0),
        )


def attention_back(window, pair_index, probs_of, do, qkv, o, tab, hot, value_bias, bias_sums, table_sums, row, col):
    row_of = lax.broadcasted_iota(jnp.int32, (224, 1), 0)
    lane = lax.broadcasted_iota(jnp.int32, (1, 128), 1)
    start, tall, width = window_params(window, row, col)
    at = pl.ds(pl.multiple_of(start * 16, 16), 224)
    inside = row_of // 16 < tall
    alive = inside & (row_of % 16 < width)
    lanes = lambda third: pl.ds(pl.multiple_of(third * FEATURES + pair_index * 128, 128), 128)
    old = [qkv[at, lanes(third)].astype(F32) for third in range(3)]
    q = jnp.where(alive, old[0], 0.0)
    k = jnp.where(alive, old[1], 0.0)
    v = jnp.where(alive, old[2], value_bias[:, lanes(0)].astype(BF).astype(F32))
    grad = jnp.where(alive, do[at, lanes(0)].astype(F32), 0.0)
    product = grad * jnp.where(alive, o[at, lanes(0)].astype(F32), 0.0)
    q_turned = q.T.astype(BF)
    grad_turned = grad.T.astype(BF)
    value_parts, key_parts, query_parts, table_parts = [], [], [], []
    for parity in range(2):
        base = 64 if parity == 0 else 0
        own = (lane < 64) if parity == 0 else (lane >= 64)
        half = slice(64 * parity, 64 * parity + 64)
        inner = jnp.sum(jnp.where(own, product, 0.0), axis=-1, keepdims=True)
        rough = inner.astype(BF).astype(F32)
        on = lane - base
        grad_side = jnp.where(own, grad, jnp.where(on == 0, rough, jnp.where(on == 1, inner - rough, 0.0))).astype(BF)
        v_side = jnp.where(own, v, jnp.where((on == 0) | (on == 1), -1.0, 0.0)).astype(BF)
        centered = nt(grad_side, v_side)
        p = probs_of(parity)
        ds = (p.astype(F32) * centered).astype(BF)
        value_parts.append(jnp.dot(grad_turned[half], p, preferred_element_type=F32))
        key_parts.append(jnp.dot(q_turned[half], ds, preferred_element_type=F32))
        k_side = jnp.where(own, k * 0.125, hot[parity]).astype(BF)
        wide = jnp.dot(ds, k_side, preferred_element_type=F32)
        query_parts.append(wide)
        by_rows = jnp.where((on >= 0) & (on < 14), wide, 0.0)
        by_cols = jnp.where((on >= 16) & (on < 30), wide, 0.0)
        table_parts.append(jnp.concatenate([pltpu.roll(by_rows[16 * a : 16 * a + 16], (128 - a) % 128, 1) for a in range(14)], axis=0))
        table_parts.append(
            jnp.concatenate([pltpu.roll(by_cols[16 * a : 16 * a + 16], 0, 1, stride=1, stride_axis=0) for a in range(14)], axis=0)
        )
    turned = jnp.concatenate(table_parts, axis=1).astype(BF)
    dq = jnp.where(lane < 64, query_parts[0], query_parts[1]) + nt(turned, tab[...])
    table_sums[...] += jnp.dot(q_turned, turned, preferred_element_type=F32)
    dk = jnp.concatenate(key_parts, axis=0).T * 0.125
    dv = jnp.concatenate(value_parts, axis=0).T.astype(BF).astype(F32)
    dq = jnp.where(alive, dq, 0.0).astype(BF).astype(F32)
    bias_sums[0, :, lanes(0)] += fold_rows(dq)
    bias_sums[1, :, lanes(0)] += fold_rows(dv)
    for third, new in enumerate((dq, dk, dv)):
        qkv[at, lanes(third)] = jnp.where(alive, new, jnp.where(inside, 0.0, old[third])).astype(BF)


def clear_idle(qkv, row, col):
    wide = row >= 2
    limit = jnp.where(wide, jnp.where(col == 3, 44, 36), 42)
    for a in range(36, 44):

        @pl.when(a >= limit)
        def _():
            qkv[16 * a : 16 * a + 16, :] = jnp.zeros((16, 3 * FEATURES), BF)


def plain_back_kernel(do, probs, qkv, o, value_bias, rows_table, cols_table, take, dqkv, bias_sums, table_sums, tab, row_bias, hot):
    row, col = lax.axis_index("row"), lax.axis_index("col")
    build_table(tab, rows_table, cols_table, take)
    row_bias[...] = as_row(value_bias)
    key_marks(hot)
    dqkv[...] = qkv[...]
    clear_idle(dqkv, row, col)
    bias_sums[...] = jnp.zeros_like(bias_sums)
    table_sums[...] = jnp.zeros_like(table_sums)

    def pair(index, _):
        window, pair_index = index // 6, index % 6
        attention_back(
            window,
            pair_index,
            lambda parity: probs[window, 2 * pair_index + parity],
            do,
            dqkv,
            o,
            tab,
            hot,
            row_bias,
            bias_sums,
            table_sums,
            row,
            col,
        )
        return 0

    lax.fori_loop(0, window_count(row, col) * 6, pair, 0)


def plain_back(do, probs, qkv, o, value_bias, rows_table, cols_table):
    vm = pl.BlockSpec(memory_space=pltpu.VMEM)
    shape = jax.ShapeDtypeStruct
    return pl.pallas_call(
        plain_back_kernel,
        out_shape=[shape((SPAN, 3 * FEATURES), BF), shape((2, 8, FEATURES), F32), shape((128, 512), F32)],
        in_specs=[vm] * 8,
        out_specs=[vm] * 3,
        scratch_shapes=[pltpu.VMEM((128, 512), BF), pltpu.VMEM((1, FEATURES), F32), pltpu.VMEM((2, 224, 128), F32)],
        compiler_params=pltpu.CompilerParams(vmem_limit_bytes=62 << 20),
    )(do, probs, qkv, o, value_bias, rows_table, cols_table, takers(True))


WHOLES = ((768, 2304), (768, 768), (768, 3072), (3072, 768))
SUM_CHUNKS = ((1, 0, 384), (3, 0, 128), (3, 128, 384), (2, 0, 768), (2, 768, 1536), (0, 0, 384), (0, 384, 768), (0, 768, 1152))


def pair_lanes(j, im):
    if im == 0:
        return (128 * j, FEATURES + 128 * j, 128 * (j + 3))
    return (2 * FEATURES + 128 * j, FEATURES + 128 * (j + 3), 2 * FEATURES + 128 * (j + 3))


def land_shapes(chunks):
    lands = []
    for w, lo, hi in chunks:
        kb, width = WHOLES[w][0] // 4, hi - lo
        lands += [
            pltpu.VMEM((2, 2, kb, width), BF),
            pltpu.VMEM((2, kb // 2, width), BF),
            pltpu.VMEM((2, kb // 2, width), BF),
            pltpu.VMEM((2, kb // 2, width), BF),
            pltpu.VMEM((3, kb // 4, width), BF),
        ]
    return lands


def reducers(chunks, full, left_turned, right_side, grads, land_refs, wsend, wrecv):
    img, row, col = place()
    y_row = lax.rem(row + 2, 4)
    core_row = row + 1 - 2 * lax.rem(row, 2)
    core_y = lax.rem(core_row + 2, 4)
    other = 1 - img
    far_col, near_col = lax.rem(col + 2, 4), col + 1 - 2 * lax.rem(col, 2)
    lands = [land_refs[5 * n : 5 * n + 5] for n in range(len(chunks))]
    sent = []

    def size(n):
        w, lo, hi = chunks[n]
        return WHOLES[w][0] // 4, WHOLES[w][1] // 2, lo, hi - lo

    def block(n, rw, im, half=None):
        kb, nb, lo, width = size(n)
        cols = pl.ds(pl.multiple_of(im * nb + lo, 128), width)
        if half is None:
            return full[chunks[n][0]].at[pl.ds(pl.multiple_of(rw * kb, kb), kb), cols]
        return full[chunks[n][0]].at[pl.ds(pl.multiple_of(rw * kb + half * (kb // 2), kb // 2), kb // 2), cols]

    def shard(n, cl):
        kb, nb, lo, width = size(n)
        cols = pl.ds(pl.multiple_of(img * nb + lo, 128), width)
        return full[chunks[n][0]].at[pl.ds(pl.multiple_of(row * kb + cl * (kb // 4), kb // 4), kb // 4), cols]

    def push(n, k, src, dst, target):
        def copy():
            return pltpu.make_async_remote_copy(
                src_ref=src(), dst_ref=dst(), send_sem=wsend.at[n, k], recv_sem=wrecv.at[n, k], device_id=target(), device_id_type=MESH
            )

        copy().start()
        sent.append(copy)

    def arrive(n, k, ref):
        pltpu.make_async_copy(ref, ref, wrecv.at[n, k]).wait()

    def add(goal, part, rows):
        def step(i, _):
            at = pl.ds(pl.multiple_of(i * 48, 16), 48)
            goal[at, :] = (goal[at, :].astype(F32) + part[at, :].astype(F32)).astype(BF)
            return 0

        lax.fori_loop(0, rows // 48, step, 0)

    def product(n, rw):
        w = chunks[n][0]
        kb, nb, lo, width = size(n)
        rows = pl.ds(pl.multiple_of(rw * kb, kb), kb)
        for im in range(2):
            at = slice(im * nb + lo, im * nb + lo + width)
            if w == 0:
                right = jnp.concatenate([right_side[0][0:ROWS, p : p + 128] for p in pair_lanes(lo // 384, im)], axis=1)
            else:
                right = right_side[w][0:ROWS, at]
            full[w][rows, at] = jnp.dot(left_turned[w](rw, kb), right, preferred_element_type=F32).astype(BF)

    def pair_stage(n):
        land = lands[n][0]
        for j, rw in enumerate((core_row, core_y)):
            product(n, rw)
            for im in range(2):
                push(n, 2 * j + im, functools.partial(block, n, rw, im), lambda j=j, im=im: land.at[j, im], lambda: {"row": core_row})
        for rw in (row, y_row):
            product(n, rw)

    def first(n):
        kb, nb, lo, width = size(n)
        for j, rw in enumerate((row, y_row)):
            for im in range(2):
                arrive(n, 2 * j + im, lands[n][0].at[j, im])
                add(block(n, rw, im), lands[n][0].at[j, im], kb)
        for im in range(2):
            push(n, 4 + im, functools.partial(block, n, y_row, im, 0), lambda im=im: lands[n][1].at[im], lambda: {"row": y_row})
        push(n, 6, functools.partial(block, n, row, other, 1), lambda: lands[n][2].at[0], lambda: {"img": other})
        push(n, 7, functools.partial(block, n, y_row, other, 1), lambda: lands[n][2].at[1], lambda: {"img": other})

    def second(n):
        kb, nb, lo, width = size(n)
        for im in range(2):
            arrive(n, 4 + im, lands[n][1].at[im])
            add(block(n, row, im, 0), lands[n][1].at[im], kb // 2)
        push(n, 8, functools.partial(block, n, row, other, 0), lambda: lands[n][3].at[0], lambda: {"img": other})
        for j, rw in enumerate((row, y_row)):
            arrive(n, 6 + j, lands[n][2].at[j])
            add(block(n, rw, img, 1), lands[n][2].at[j], kb // 2)
        push(n, 9, functools.partial(block, n, y_row, img, 1), lambda: lands[n][3].at[1], lambda: {"row": y_row})

    def third(n):
        kb, nb, lo, width = size(n)
        for half in range(2):
            arrive(n, 8 + half, lands[n][3].at[half])
            add(block(n, row, img, half), lands[n][3].at[half], kb // 2)
        push(n, 10, lambda: shard(n, near_col), lambda: lands[n][4].at[0], lambda: {"col": near_col})
        push(n, 11, lambda: shard(n, 3 - col), lambda: lands[n][4].at[1], lambda: {"col": near_col})

    def fourth(n):
        kb = size(n)[0]
        arrive(n, 11, lands[n][4].at[1])
        add(shard(n, far_col), lands[n][4].at[1], kb // 4)
        push(n, 12, lambda: shard(n, far_col), lambda: lands[n][4].at[2], lambda: {"col": far_col})

    def fifth(n):
        w, lo, hi = chunks[n]
        arrive(n, 10, lands[n][4].at[0])
        arrive(n, 12, lands[n][4].at[2])
        mine = shard(n, col)

        def step(part, _):
            at = pl.ds(pl.multiple_of(part * 48, 16), 48)
            total = mine[at, :].astype(F32) + lands[n][4][0, at, :].astype(F32) + lands[n][4][2, at, :].astype(F32)
            if w > 0:
                grads[w][at, lo:hi] = total
            else:
                for im in range(2):

                    @pl.when(img == im)
                    def _():
                        for i, p in enumerate(pair_lanes(lo // 384, im)):
                            lane = p - 1152 * im
                            grads[0][at, lane : lane + 128] = total[:, 128 * i : 128 * i + 128]

            return 0

        lax.fori_loop(0, WHOLES[w][0] // 16 // 48, step, 0)

    return pair_stage, first, second, third, fourth, fifth, sent


def table_taker():
    take = relative_layout(True)
    out = np.zeros((4, 128, 128), np.float32)
    for parity in range(2):
        for which in range(2):
            out[2 * parity + which, :, 64 * which : 64 * which + 27] = take[parity, which].T
    return out


def source_tiles(row, col):
    wide = row >= 2
    side_row = row + 2 * (1 - col // 2)
    table = []
    for image in range(2):
        table.append((image, 0, image, row - 1, col, row > 0))
        table.append((image, 1, image, row, col - 1, col > 0))
        table.append((image, 2, image, row - 1, col - 1, (row > 0) & (col > 0)))
    third_image = jnp.where(wide, 3 - row, 1 - lax.rem(col, 2))
    table.append((2, 0, third_image, 3, col, wide))
    table.append((2, 1, third_image, side_row, 3, jnp.logical_not(wide)))
    table.append((2, 2, third_image, jnp.where(wide, 3, side_row - 1), jnp.where(wide, col - 1, 3), jnp.where(wide, col, side_row) > 0))
    table.append((3, 2, 3 - row, 3, 3, wide & (col == 3)))
    return table


CLOSE_PLAN = ("p1", "p2", "11", "|", "|", "12", "p4", "|", "|", "14", "21", "|", "p0", "|", "|", "p3", "|", "22", "|", "p5", "24", "|", "10", "31", "|", "|", "|", "|", "|", "|", "|", "13", "|", "32", "41", "15", "34", "G0", "G1", "G2", "42", "p7", "G3", "S", "p6", "23", "s0", "25", "20", "17", "16", "30", "s1", "44", "35", "27", "40", "52", "33", "26", "s2", "45", "37", "51", "50", "36", "s3", "43", "54", "47", "46", "53", "57", "55", "56", "s4")


def returns(raws, landing, send, recv, row, col):
    def each(t, act):
        for slot, kind, image, tile_row, tile_col, present in source_tiles(row, col):
            here = (tile_row == row) & (tile_col == col)
            act(slot, kind, image, tile_row, tile_col, present & here, present & jnp.logical_not(here))

    def start(t):
        def act(slot, kind, image, tile_row, tile_col, local, remote):
            @pl.when(local)
            def _():
                pltpu.make_async_copy(
                    window_part(raws[t], slot, kind), landing[t][kind].at[image], recv.at[t, image, kind]
                ).start()

            @pl.when(remote)
            def _():
                hop(t, slot, kind, image, tile_row, tile_col).start()

        each(t, act)

    def hop(t, slot, kind, image, tile_row, tile_col):
        return pltpu.make_async_remote_copy(
            src_ref=window_part(raws[t], slot, kind),
            dst_ref=landing[t][kind].at[image],
            send_sem=send.at[t, slot, kind],
            recv_sem=recv.at[t, image, kind],
            device_id={"row": jnp.maximum(tile_row, 0), "col": jnp.maximum(tile_col, 0)},
            device_id_type=MESH,
        )

    def arrived(t):
        for image in range(2):
            for kind in range(3):
                goal = landing[t][kind].at[image]
                pltpu.make_async_copy(goal, goal, recv.at[t, image, kind]).wait()

    def left(t):
        def act(slot, kind, image, tile_row, tile_col, local, remote):
            @pl.when(remote)
            def _():
                hop(t, slot, kind, image, tile_row, tile_col).wait_send()

        each(t, act)

    return start, arrived, left


def merge_tiles(owns, landing, goals, row, col):
    places = lax.broadcasted_iota(jnp.int32, (16, 1), 0)
    in_left = places < 14 - 2 * col

    def rows16(values):
        return values.reshape(16, FEATURES).astype(F32)

    def right_half(values):
        low = values.reshape(8, FEATURES).astype(F32)
        return jnp.concatenate([low, low], axis=0)

    for image in range(2):

        def merge(tile_row, _):
            top = tile_row < 14 - 2 * row
            upper = jnp.minimum(tile_row, 13)
            lower = jnp.maximum(tile_row - 8, 0)
            for own, (below, right, both), goal in zip(owns, landing, goals):
                stacked = jnp.where(top, rows16(own(image, upper)), rows16(below[image, lower]))
                beside = jnp.where(top, right_half(right[image, upper]), right_half(both[image, lower]))
                goal[image, tile_row] = jnp.where(in_left, stacked, beside).astype(goal.dtype)
            return 0

        lax.fori_loop(0, 16, merge, 0)


def input_grad(at, dqkv, wq, xw, image_grad, gain, norm_sums):
    grad = nt(dqkv[at, :], wq).astype(BF).astype(F32)
    unit, inverse = unit_of(xw[at, :].astype(F32))
    image_grad[at, :] += norm_back(grad, unit, inverse, as_row(gain))
    norm_sums[0] += fold_rows(grad * unit)
    norm_sums[1] += fold_rows(grad)


def plain_close_kernel(dqkv, xw, dm, raw_r, wq, gain, out, grad_out, norm_sums, image_grad, raw_g, *refs):
    img, row, col = place()
    landing, (send, recv) = (refs[:3], refs[3:6]), refs[6:]
    greet(img, row, col, False)
    start, arrived, left = returns((raw_r, raw_g), landing, send, recv, row, col)
    start(0)
    norm_sums[...] = jnp.zeros_like(norm_sums)
    image_grad[...] = dm[...]

    def step(i, _):
        input_grad(pl.ds(pl.multiple_of(i * BLOCK, 16), BLOCK), dqkv, wq[...], xw, image_grad, gain, norm_sums)
        return 0

    lax.fori_loop(0, ROWS // BLOCK, step, 0)
    spread_rows(image_grad, raw_g, row, col)
    start(1)
    for t in range(2):
        arrived(t)
    owns = [lambda image, upper, raw=raw: raw[image * 22 + 8 + upper, 1:3] for raw in (raw_r, raw_g)]
    merge_tiles(owns, landing, (out, grad_out), row, col)
    for t in range(2):
        left(t)


PIECES = [(2, 8, 2, 8, FEATURES), (2, 14, 1, 8, FEATURES), (2, 8, 1, 8, FEATURES)]


def plain_close(dqkv, xw, dm, raw_r, wq, gain):
    vm = pl.BlockSpec(memory_space=pltpu.VMEM)
    shape = jax.ShapeDtypeStruct
    dma = pltpu.SemaphoreType.DMA
    pieces = [pltpu.VMEM(s, BF) for s in PIECES]
    return pl.pallas_call(
        plain_close_kernel,
        out_shape=[shape((2, 16, 16, FEATURES), BF), shape((2, 16, 16, FEATURES), F32), shape((2, 8, FEATURES), F32)],
        in_specs=[vm] * 6,
        out_specs=[vm] * 3,
        scratch_shapes=[pltpu.VMEM((ROWS, FEATURES), F32), pltpu.VMEM((88, 3, 8, FEATURES), BF)]
        + pieces
        + pieces
        + [dma((2, 4, 3)), dma((2, 2, 3))],
        compiler_params=pltpu.CompilerParams(collective_id=2, has_side_effects=True, vmem_limit_bytes=67043328),
    )(dqkv, xw, dm, raw_r, wq, gain)


def back_kernel(
    value_bias, rows_table, cols_table, take, o_turned, da, cw, gain, sums, up_sum, taker,
    do_in, o_in, n2_in, xw_in, n1_in, probs, qkv_in, dh_in, g_in, dm_in, wq_in, raw_r, *refs
):
    out, grad_out, gq, go, gu, gd, small_out, table_out = refs[:8]
    qkv, probs_s, image_grad, shared_h, shared_g, own_r = refs[8:14]
    bias_sums, table_sums, norm_sums, tab, row_bias = refs[14:19]
    landing = (refs[19:22], refs[22:25])
    full = refs[25:29]
    small, table, small_land, table_land, small_z, table_z = refs[29:35]
    count = len(SUM_CHUNKS)
    lands = refs[35 : 35 + 5 * count]
    do, o, n2_turned, xw, n1_turned, hot = refs[35 + 5 * count : 41 + 5 * count]
    send, recv, load_sem, probs_sem, wsend, wrecv, ssend, srecv = refs[41 + 5 * count :]
    img, row, col = place()
    y_row = lax.rem(row + 2, 4)
    core_row = row + 1 - 2 * lax.rem(row, 2)
    other = 1 - img
    copies = []

    def load(i):
        pairs = (
            (dh_in, shared_h.at[pl.ds(0, ROWS)]),
            (g_in, shared_g),
            (qkv_in, qkv),
            (dm_in, image_grad),
            (wq_in, shared_h.at[:, pl.ds(0, 3 * FEATURES)]),
            (raw_r.at[pl.ds(8, 14), pl.ds(1, 2)], own_r.at[0]),
            (raw_r.at[pl.ds(30, 14), pl.ds(1, 2)], own_r.at[1]),
            (do_in, do),
            (o_in, o),
            (n2_in, n2_turned),
            (xw_in, xw),
            (n1_in, n1_turned),
        )
        return pltpu.make_async_copy(pairs[i][0], pairs[i][1], load_sem.at[i])

    for i in (1, 2, 7, 8, 9, 0, 11, 10, 3, 5, 6):
        load(i).start()
    windows = window_count(row, col)

    def fetch(k, window, slot):
        pair_index = lax.rem(k, 2) * 3 + k // 2
        return pltpu.make_async_copy(probs.at[window, pl.ds(2 * pair_index, 2)], probs_s.at[slot], probs_sem.at[slot])

    fetch(0, 0, 0).start()
    greet(img, row, col)
    start, arrived, left = returns((raw_r, shared_g), landing, send, recv, row, col)
    start(0)

    def turned_rows(ref):
        return lambda rw, kb: ref[pl.ds(pl.multiple_of(rw * kb, kb), kb), :]

    def turned_g(rw, kb):
        return shared_g[pl.ds(pl.multiple_of(rw * 32, 32), 32)].reshape(FEATURES, FEATURES)[:, 0:ROWS]

    pair_stage, first, second, third, fourth, fifth, sent = reducers(
        SUM_CHUNKS,
        full,
        (turned_rows(n1_turned), turned_rows(o_turned), turned_rows(n2_turned), turned_g),
        (qkv, da, shared_h, cw),
        (gq, go, gu, gd),
        lands,
        wsend,
        wrecv,
    )
    bias_sums[...] = jnp.zeros_like(bias_sums)
    table_sums[...] = jnp.zeros_like(table_sums)
    norm_sums[...] = jnp.zeros_like(norm_sums)
    load(1).wait()

    def grad_rows(i):
        if i == 0:
            load(4).start()
            load(10).wait()
            load(3).wait()
            load(4).wait()
        input_grad(pl.ds(i * BLOCK, BLOCK), qkv, shared_h[:, 0 : 3 * FEATURES], xw, image_grad, gain, norm_sums)

    def send_grad():
        spread_rows(image_grad, shared_g, row, col)
        start(1)

    def over_rows(values):
        return jnp.sum(values, axis=0, keepdims=True)

    def gather_small():
        small[0] = jnp.zeros((16, FEATURES), F32)
        lines = [bias_sums[0], bias_sums[1], sums[0], sums[1], norm_sums[0], norm_sums[1], sums[2], sums[3]]
        for i, values in enumerate(lines):
            small[0, i : i + 1, :] = over_rows(values)
        for i in range(4):
            small[0, 8 + i : 9 + i, :] = over_rows(up_sum[:, i * FEATURES : (i + 1) * FEATURES])
        exact = lax.Precision.HIGHEST
        total = jnp.zeros((64, 128), F32)
        for parity in range(2):
            for which in range(2):
                part = table_sums[64 * parity : 64 * parity + 64, 256 * parity + 128 * which : 256 * parity + 128 * which + 128]
                total = total + jnp.dot(part, taker[2 * parity + which], precision=exact, preferred_element_type=F32)
        table[0] = total

    hops = ({"row": core_row}, {"row": y_row}, {"img": other})

    def small_push(k, src, dst, target):
        c = pltpu.make_async_remote_copy(
            src_ref=src, dst_ref=dst, send_sem=ssend.at[k], recv_sem=srecv.at[k], device_id=target, device_id_type=MESH
        )
        c.start()
        copies.append(c)
        return c

    def small_step(i):
        if i == 0:
            gather_small()
        if 0 < i <= 3:
            for k, (acc, land) in enumerate(((small, small_land), (table, table_land))):
                pltpu.make_async_copy(land.at[i - 1], land.at[i - 1], srecv.at[2 * (i - 1) + k]).wait()
                acc[i] = acc[i - 1] + land[i - 1]
        if i < 3:
            for k, (acc, land) in enumerate(((small, small_land), (table, table_land))):
                small_push(2 * i + k, acc.at[i], land.at[i], hops[i])
        if i == 3:
            small_z[col] = small[3]
            table_z[col] = table[3]
            for d in range(1, 4):
                cl = lax.rem(col + d, 4)
                small_push(4 + 2 * d, small.at[3], small_z.at[col], {"col": cl})
                small_push(5 + 2 * d, table.at[3], table_z.at[col], {"col": cl})
        if i == 4:
            for d in range(1, 4):
                cl = lax.rem(col + 4 - d, 4)
                pltpu.make_async_copy(small_z.at[cl], small_z.at[cl], srecv.at[4 + 2 * d]).wait()
                pltpu.make_async_copy(table_z.at[cl], table_z.at[cl], srecv.at[5 + 2 * d]).wait()
            small_out[...] = (small_z[0] + small_z[1]) + (small_z[2] + small_z[3])
            table_out[...] = (table_z[0] + table_z[1]) + (table_z[2] + table_z[3])

    acts = {"p": pair_stage, "1": first, "2": second, "3": third, "4": fourth, "5": fifth, "G": grad_rows, "s": small_step, "S": send_grad}
    slots = plan_slots(CLOSE_PLAN, acts)
    run_all(slots[0])
    build_table(tab, rows_table, cols_table, take)
    row_bias[...] = as_row(value_bias)
    key_marks(hot)
    load(2).wait()
    clear_idle(qkv, row, col)
    for i in (7, 8, 9, 0, 11):
        load(i).wait()

    def head_pair(k, _):
        pair_index = lax.rem(k, 2) * 3 + k // 2

        def each(window, _):
            for i, slot_acts in enumerate(slots[1:-1]):
                if slot_acts:
                    pl.when((k == (i + 1) // 3) & (window == (i + 1) % 3))(functools.partial(run_all, slot_acts))
            turn_count = k * windows + window
            slot = lax.rem(turn_count, 2)
            fetch(k, window, slot).wait()
            wrap = window + 1 == windows
            next_k = jnp.where(wrap, k + 1, k)

            @pl.when(next_k < 6)
            def _():
                fetch(next_k, jnp.where(wrap, 0, window + 1), 1 - slot).start()

            attention_back(
                window,
                pair_index,
                lambda parity: probs_s[slot, parity],
                do,
                qkv,
                o,
                tab,
                hot,
                row_bias,
                bias_sums,
                table_sums,
                row,
                col,
            )
            return 0

        lax.fori_loop(0, windows, each, 0)
        return 0

    lax.fori_loop(0, 6, head_pair, 0)
    run_all(slots[-1])
    arrived(0)
    load(5).wait()
    load(6).wait()
    merge_tiles([lambda image, upper: own_r[image, upper]], landing[:1], (out,), row, col)
    arrived(1)
    merge_tiles([lambda image, upper: shared_g[image * 22 + 8 + upper, 1:3]], landing[1:], (grad_out,), row, col)
    left(0)
    left(1)
    for c in copies:
        c.wait_send()
    for copy in sent:
        copy().wait_send()


def back(do, o, value_bias, rows_table, cols_table, o_turned, da, n2_turned, cw, xw, n1_turned, gain, sums, up_sum, probs, qkv, dh, g, dm, wq, raw_r):
    vm = pl.BlockSpec(memory_space=pltpu.VMEM)
    an = pl.BlockSpec(memory_space=pl.ANY)
    shape = jax.ShapeDtypeStruct
    dma = pltpu.SemaphoreType.DMA
    pieces = [pltpu.VMEM(s, BF) for s in PIECES]
    count = len(SUM_CHUNKS)
    return pl.pallas_call(
        back_kernel,
        out_shape=[shape((2, 16, 16, FEATURES), BF), shape((2, 16, 16, FEATURES), BF)]
        + [shape((k // 16, n // 2), F32) for k, n in WHOLES]
        + [shape((16, FEATURES), F32), shape((64, 128), F32)],
        in_specs=[vm] * 11 + [an] * 12,
        out_specs=[vm] * 8,
        scratch_shapes=[
            pltpu.VMEM((SPAN, 3 * FEATURES), BF),
            pltpu.VMEM((2, 2, 224, 224), BF),
            pltpu.VMEM((ROWS, FEATURES), F32),
            pltpu.VMEM((FEATURES, 4 * FEATURES), BF),
            pltpu.VMEM((128, 3, 8, FEATURES), BF),
            pltpu.VMEM((2, 14, 2, 8, FEATURES), BF),
            pltpu.VMEM((2, 8, FEATURES), F32),
            pltpu.VMEM((128, 512), F32),
            pltpu.VMEM((2, 8, FEATURES), F32),
            pltpu.VMEM((128, 512), BF),
            pltpu.VMEM((1, FEATURES), F32),
        ]
        + pieces
        + pieces
        + [pltpu.VMEM(s, BF) for s in WHOLES]
        + [
            pltpu.VMEM((4, 16, FEATURES), F32),
            pltpu.VMEM((4, 64, 128), F32),
            pltpu.VMEM((3, 16, FEATURES), F32),
            pltpu.VMEM((3, 64, 128), F32),
            pltpu.VMEM((4, 16, FEATURES), F32),
            pltpu.VMEM((4, 64, 128), F32),
        ]
        + land_shapes(SUM_CHUNKS)
        + [pltpu.VMEM(s, BF) for s in ((SPAN, FEATURES), (SPAN, FEATURES), (FEATURES, ROWS), (ROWS, FEATURES), (FEATURES, ROWS))]
        + [pltpu.VMEM((2, 224, 128), F32)]
        + [dma((2, 4, 3)), dma((2, 2, 3)), dma((12,)), dma((2,)), dma((count, 13)), dma((count, 13)), dma((12,)), dma((12,))],
        compiler_params=pltpu.CompilerParams(collective_id=1, has_side_effects=True, vmem_limit_bytes=67043328),
    )(
        value_bias, rows_table, cols_table, takers(True), o_turned, da, cw, gain, sums, up_sum, jnp.asarray(table_taker()),
        do, o, n2_turned, xw, n1_turned, probs, qkv, dh, g.reshape(128, 3, 8, FEATURES), dm, wq, raw_r,
    )


def deliver_kernel(out_in, grad_in, *refs):
    sums_in, (small, table), outs = refs[:4], refs[4:6], refs[6:]
    outs[0][...] = out_in[...]

    def widen(i, _):
        outs[1][0, i] = grad_in[0, i].astype(F32)
        return 0

    lax.fori_loop(0, 16, widen, 0)

    @pl.when(pl.program_id(0) == 0)
    def _():
        for given, goal in zip(sums_in, outs[2:6]):
            goal[...] = given[...]
        for i, goal in zip((0, 1, 2, None, 3, 4, 5, 6, 7), outs[6:15]):
            if i is None:
                goal[...] = jnp.concatenate([small[8 + j : 9 + j, :] for j in range(4)], axis=1).reshape(4 * FEATURES)
            else:
                goal[...] = small[i : i + 1, :].reshape(FEATURES)
        turned = table[...].T
        outs[15][...] = turned[0:27, :]
        outs[16][...] = turned[64:91, :]


def deliver(*given):
    shape = jax.ShapeDtypeStruct
    lengths = [FEATURES] * 3 + [4 * FEATURES] + [FEATURES] * 5
    outs = [shape((2, 16, 16, FEATURES), BF), shape((2, 16, 16, FEATURES), F32)] + [shape((k // 16, n // 2), F32) for k, n in WHOLES]
    outs += [shape((n,), F32) for n in lengths] + [shape((27, 64), F32)] * 2
    image = pl.BlockSpec((1, 16, 16, FEATURES), lambda i: (i, 0, 0, 0))

    def spec(array):
        return pl.BlockSpec(array.shape, lambda i: (0,) * len(array.shape))

    return pl.pallas_call(
        deliver_kernel,
        grid=(2,),
        out_shape=outs,
        in_specs=[image] * 2 + [spec(v) for v in given[2:]],
        out_specs=[image] * 2 + [spec(v) for v in outs[2:]],
    )(*given)


def on_device(
    image_in,
    cotangent,
    qkv_weight,
    out_weight,
    up_weight,
    down_weight,
    query_bias,
    value_bias,
    out_bias,
    up_bias,
    down_bias,
    first_gain,
    first_shift,
    second_gain,
    second_shift,
    rows_table,
    cols_table,
):
    line = lambda v: v.reshape(1, -1)
    xw, cw, n1_turned, qkv, probs, o, o_turned, raw_r, n2_turned, g_turned, dh, da, do, dm, sums, up_sum, wq = open_windows(
        image_in,
        cotangent,
        (qkv_weight, out_weight, up_weight, down_weight),
        first_gain,
        first_shift,
        query_bias,
        value_bias,
        rows_table,
        cols_table,
        out_bias,
        line(up_bias),
        down_bias,
        second_gain,
        second_shift,
    )
    if lax.axis_size("img") == 2:
        return tuple(
            deliver(
                *back(
                    do, o, value_bias, rows_table, cols_table, o_turned, da, n2_turned, cw, xw, n1_turned, first_gain, sums, up_sum,
                    probs, qkv, dh, g_turned, dm, wq, raw_r,
                )
            )
        )
    dqkv, bias_sums, table_sums = plain_back(do, probs, qkv, o, value_bias, rows_table, cols_table)
    image_out, image_grad, norm_sums = plain_close(dqkv, xw, dm, raw_r, wq, first_gain)
    dot = lambda a, b: jnp.dot(a, b, preferred_element_type=F32)
    totals = (dot(n1_turned, dqkv[:ROWS]), dot(o_turned, da), dot(n2_turned, dh), dot(g_turned[:, :ROWS], cw))
    shard_sums = []
    for total in totals:
        part = lax.psum_scatter(total.astype(BF), ("row", "col"), scatter_dimension=0, tiled=True)
        shard_sums.append(lax.psum_scatter(part, "img", scatter_dimension=1, tiled=True).astype(F32))
    rows_grad, cols_grad = table_grads(table_sums)
    small_sums = lax.psum(
        tuple(jnp.sum(bias_sums, axis=1))
        + (jnp.sum(sums[0], axis=0), jnp.sum(up_sum, axis=0), jnp.sum(sums[1], axis=0))
        + tuple(jnp.sum(norm_sums, axis=1))
        + (jnp.sum(sums[2], axis=0), jnp.sum(sums[3], axis=0), rows_grad, cols_grad),
        ("img", "row", "col"),
    )
    return (image_out, image_grad, *shard_sums, *small_sums)


def solution(mesh):
    tiles = P("img", "row", "col", None)
    shards = P(("row", "col"), "img")
    return jax.shard_map(
        on_device,
        mesh=mesh,
        in_specs=(tiles,) * 2 + (shards,) * 4 + (P(),) * 11,
        out_specs=(tiles,) * 2 + (shards,) * 4 + (P(),) * 11,
        check_vma=False,
    )
```
